32 devices in a mesh: dp: 4 (over z), ctx: 8 (over y, x, core).
Axes of the slice: x: 2, y: 2, z: 4, core: 2. Of those that a mesh axis runs over, the one named last changes fastest.
Arguments:
- inputs: bfloat16 [4, 1024, 1024], P('dp', 'ctx'), may hold values from -6 to 6
- cotangent: bfloat16 [4, 1024, 1024], P('dp', 'ctx'), may hold values from -6 to 6
- mixer_params: float32 [4194304], P(('dp', 'ctx')), may hold values from -0.1875 to 0.1875
- mixer_first: float32 [4194304], P(('dp', 'ctx')), may hold values from -0.0014648438 to 0.0014648438
- mixer_second: float32 [4194304], P(('dp', 'ctx')), may hold values from 2.3434208e-11 to 2.3434207e-10
- ffn_params: float32 [4325376], P(('dp', 'ctx')), may hold values from -0.21320072 to 0.21320072
- ffn_first: float32 [4325376], P(('dp', 'ctx')), may hold values from -0.0014648438 to 0.0014648438
- ffn_second: float32 [4325376], P(('dp', 'ctx')), may hold values from 2.3434208e-11 to 2.3434207e-10
- small_params: float32 [14852], replicated, may hold values from -7 to 2.8
- small_first: float32 [14852], replicated, may hold values from -0.0014648438 to 0.0014648438
- small_second: float32 [14852], replicated, may hold values from 2.3434208e-11 to 2.3434208e-07
Outputs:
- outputs: bfloat16 [4, 1024, 1024], P('dp', 'ctx')
- grad_inputs: bfloat16 [4, 1024, 1024], P('dp', 'ctx')
- mixer_grad: float32 [4194304], P(('dp', 'ctx'))
- ffn_grad: float32 [4325376], P(('dp', 'ctx'))
- small_grad: float32 [14852], replicated
- mixer_new: float32 [4194304], P(('dp', 'ctx'))
- mixer_first_new: float32 [4194304], P(('dp', 'ctx'))
- mixer_second_new: float32 [4194304], P(('dp', 'ctx'))
- ffn_new: float32 [4325376], P(('dp', 'ctx'))
- ffn_first_new: float32 [4325376], P(('dp', 'ctx'))
- ffn_second_new: float32 [4325376], P(('dp', 'ctx'))
- small_new: float32 [14852], replicated
- small_first_new: float32 [14852], replicated
- small_second_new: float32 [14852], replicated
The draws below stay inside these ranges and needn't reach their ends.
All inputs are finite; a program needn't handle non-finite values.
Results may differ from the reference program's by a relative error of at most 0.013.
Values may be sent and summed in bfloat16 or wider, within the bound.
A program may use at most 320 MiB of HBM per device.

```python
import math
import jax
import jax.numpy as jnp
from jax import lax

D = 1024
H = 2
DK = 256
DV = 512
FF = 1408
CONV = 4
GROUP = 64
SEQS = 4
LEN = 1024
ROWS_MIX = 4096
ROWS_FFN = 4224
SMALL = 14852


def draw_mixer_params(key, part):
    total_rows = 2 * H * DK + 3 * H * DV
    row_index = jnp.arange(total_rows)[:, None]
    scales = jnp.where(row_index < 2 * H * DK + 2 * H * DV, D ** (-0.5), 1.5 * (H * DV) ** (-0.5))
    base = jax.random.truncated_normal(key, -4.0, 4.0, (total_rows, D), jnp.float32)
    return (base * scales).reshape(-1)


def draw_ffn_params(key, part):
    total_rows = 3 * FF
    row_index = jnp.arange(total_rows)[:, None]
    scales = jnp.where(row_index < 2 * FF, D ** (-0.5), 2.0 * FF ** (-0.5))
    base = jax.random.truncated_normal(key, -4.0, 4.0, (total_rows, D), jnp.float32)
    return (base * scales).reshape(-1)


def draw_small_params(key, part):
    width = 2 * H * DK + H * DV
    key_list = jax.random.split(key, 5)
    gain_values = 1.0 + 0.1 * jax.random.truncated_normal(key_list[0], -4.0, 4.0, (2 * D + DV,), jnp.float32)
    tap_values = 0.5 * jax.random.truncated_normal(key_list[1], -3.0, 3.0, (CONV * width,), jnp.float32)
    column = jnp.arange(2 * H)
    column_scale = jnp.where(column < H, 1.0, 1.5) * D ** (-0.5)
    gate_weights = jax.random.truncated_normal(key_list[2], -4.0, 4.0, (D, 2 * H), jnp.float32) * column_scale
    a_log = jax.random.uniform(key_list[3], (H,), jnp.float32, 0.0, 2.77)
    log_step = jax.random.uniform(key_list[4], (H,), jnp.float32, jnp.log(0.001), jnp.log(0.1))
    dt_bias = jnp.log(jnp.expm1(jnp.exp(log_step)))
    return jnp.concatenate([gain_values, tap_values, gate_weights.reshape(-1), a_log, dt_bias])


def shard_levels(stream_key, shape, cuts, low, largest):
    level, own = 1.0, jax.random.fold_in(stream_key, 6)
    for dim, blocks in cuts:
        heights = jnp.exp(jax.random.uniform(jax.random.fold_in(own, dim), (blocks,), jnp.float32, low / len(cuts), largest / len(cuts)))
        level = level * jnp.repeat(heights, shape[dim] // blocks).reshape([-1 if axis == dim else 1 for axis in range(len(shape))])
    return level


def noise(rng, extent, deviation, bound, shards=(), kind=jnp.bfloat16):
    values = jax.random.normal(rng, extent, jnp.float32) * deviation
    if len(shards) > 0:
        values = shard_levels(rng, extent, shards, -0.22, 0.18) * values
    return jnp.clip(values, min=-bound, max=bound).astype(kind)


def setup_inputs(seed: int = 0) -> dict:
    splits = jax.random.split(jax.random.key(seed), 12)
    inputs = noise(splits[0], (SEQS, LEN, D), 1.0, 6.0, ((0, 4), (1, 8)))
    cotangent = noise(splits[1], (SEQS, LEN, D), 1.0, 6.0, ((0, 4), (1, 8)))
    mixer_params = draw_mixer_params(jax.random.fold_in(splits[11], 71), 0)
    mixer_first = noise(splits[3], (ROWS_MIX * D,), (0.3 * ((ROWS_MIX + ROWS_FFN) * D + SMALL) ** -0.5), 0.0014648438, ((0, 32),), jnp.float32)
    mixer_second = jnp.clip(jnp.exp(math.log(2.343420735240187e-10) - 2.3025851 * jax.random.uniform(splits[4], (ROWS_MIX * D,), jnp.float32) ** shard_levels(splits[4], (ROWS_MIX * D,), ((0, 32),), -0.2, 0.2)), 2.3434207699346565e-11, 2.343420735240187e-10)
    ffn_params = draw_ffn_params(jax.random.fold_in(splits[11], 71), 0)
    ffn_first = noise(splits[6], (ROWS_FFN * D,), (0.3 * ((ROWS_MIX + ROWS_FFN) * D + SMALL) ** -0.5), 0.0014648438, ((0, 32),), jnp.float32)
    ffn_second = jnp.clip(jnp.exp(math.log(2.343420735240187e-10) - 2.3025851 * jax.random.uniform(splits[7], (ROWS_FFN * D,), jnp.float32) ** shard_levels(splits[7], (ROWS_FFN * D,), ((0, 32),), -0.2, 0.2)), 2.3434207699346565e-11, 2.343420735240187e-10)
    small_params = draw_small_params(jax.random.fold_in(splits[11], 71), 0)
    small_first = noise(splits[9], (SMALL,), (0.3 * ((ROWS_MIX + ROWS_FFN) * D + SMALL) ** -0.5), 0.0014648438, (), jnp.float32)
    small_second = jnp.clip(jnp.exp(jax.random.uniform(splits[10], (SMALL,), jnp.float32, math.log(2.3434207699346565e-11), math.log(2.3434208173966908e-07))), 2.3434207699346565e-11, 2.3434208173966908e-07)
    return {"inputs": inputs, "cotangent": cotangent, "mixer_params": mixer_params, "mixer_first": mixer_first, "mixer_second": mixer_second, "ffn_params": ffn_params, "ffn_first": ffn_first, "ffn_second": ffn_second, "small_params": small_params, "small_first": small_first, "small_second": small_second}


EPSILON = 1e-06
ADAM_EPS = 1e-08
LEARN_RATE = 0.02
BETA_ONE = 0.9
BETA_TWO = 0.999
DECAY_RATE = 0.1
CORRECT_ONE = 1.0 - 0.9 ** 3
CORRECT_TWO = 1.0 - 0.999 ** 3
MAX_NORM = 1.0
HIGHEST = lax.Precision.HIGHEST

def norm_scale(values, gain):
    return values * lax.rsqrt(lax.optimization_barrier(jnp.mean(values * values, axis=-1, keepdims=True)) + EPSILON) * gain

def swiglu(gate_part, up_part):
    return jax.nn.silu(gate_part) * up_part

def unpack_small(packed):
    width = 2 * H * DK + H * DV
    lengths = [D, D, DV, CONV * width, D * 2 * H, H, H]
    pieces = []
    offset = 0
    for length in lengths:
        pieces.append(packed[offset:offset + length])
        offset = offset + length
    return (pieces[0], pieces[1], pieces[2], pieces[3].reshape(CONV, width), pieces[4].reshape(D, 2 * H), pieces[5], pieces[6])

def split_weights(mix_whole, ffn_whole):
    mix_rows = mix_whole.reshape(-1, D)
    ffn_rows = ffn_whole.reshape(-1, D)
    edge = 2 * H * DK + 2 * H * DV
    return (mix_rows[:edge], mix_rows[edge:], ffn_rows[:2 * FF], ffn_rows[2 * FF:])

def features(extended, tap_values, gate_logits, a_log, dt_bias):
    count = extended.shape[0] - (CONV - 1)
    summed = tap_values[0] * extended[0:count]
    for tap_index in range(1, CONV):
        summed = summed + tap_values[tap_index] * extended[tap_index:tap_index + count]
    activated = jax.nn.silu(summed)
    query_part = activated[:, :H * DK].reshape(count, H, DK)
    key_part = activated[:, H * DK:2 * H * DK].reshape(count, H, DK)
    value_part = activated[:, 2 * H * DK:].reshape(count, H, DV)
    query = query_part * lax.rsqrt(lax.optimization_barrier(jnp.sum(query_part * query_part, axis=-1, keepdims=True)) + EPSILON) * DK ** (-0.5)
    keys = key_part * lax.rsqrt(lax.optimization_barrier(jnp.sum(key_part * key_part, axis=-1, keepdims=True)) + EPSILON)
    beta = jax.nn.sigmoid(gate_logits[:, :H])
    decay = -jnp.exp(a_log) * jax.nn.softplus(gate_logits[:, H:] + dt_bias)
    return (jnp.transpose(query, (1, 0, 2)), jnp.transpose(keys, (1, 0, 2)), jnp.transpose(value_part, (1, 0, 2)), beta.T, decay.T)

def split_groups(values):
    blocks = values.shape[1] // GROUP
    shaped = values.reshape((values.shape[0], blocks, GROUP) + values.shape[2:])
    return jnp.moveaxis(shaped, 1, 0)

def group_parts(key_block, value_block, beta_block, decay_block):
    size = decay_block.shape[-1]
    cumulative = jnp.cumsum(decay_block, axis=-1)
    row_index = lax.broadcasted_iota(jnp.int32, (size, size), 0)
    col_index = lax.broadcasted_iota(jnp.int32, (size, size), 1)
    lower = row_index >= col_index
    strict = row_index > col_index
    spread = jnp.where(lower, cumulative[:, :, None] - cumulative[:, None, :], 0.0)
    decay_matrix = jnp.where(lower, jnp.exp(spread), 0.0)
    key_gram = jnp.einsum('hid,hjd->hij', key_block, key_block, precision=HIGHEST)
    system = jnp.where(strict, beta_block[:, :, None] * key_gram * decay_matrix, 0.0) + jnp.eye(size, dtype=key_block.dtype)
    right_side = jnp.concatenate([key_block * (beta_block * jnp.exp(cumulative))[:, :, None], value_block * beta_block[:, :, None]], axis=-1)
    solved = jax.scipy.linalg.solve_triangular(system, right_side, lower=True, unit_diagonal=True)
    key_mix = solved[..., :DK]
    value_mix = solved[..., DK:]
    last_decay = cumulative[:, -1]
    keys_to_end = key_block * jnp.exp(last_decay[:, None] - cumulative)[:, :, None]
    return (cumulative, decay_matrix, key_mix, value_mix, last_decay, keys_to_end)

def group_run(state, pieces):
    query_block, key_block, value_block, beta_block, decay_block = pieces
    cumulative, decay_matrix, key_mix, value_mix, last_decay, keys_to_end = group_parts(key_block, value_block, beta_block, decay_block)
    pseudo_values = value_mix - jnp.einsum('hcd,hde->hce', key_mix, state, precision=HIGHEST)
    scores = jnp.einsum('hid,hjd->hij', query_block, key_block, precision=HIGHEST) * decay_matrix
    block_out = jnp.einsum('hcd,hde->hce', query_block * jnp.exp(cumulative)[:, :, None], state, precision=HIGHEST)
    block_out = block_out + jnp.einsum('hij,hje->hie', scores, pseudo_values, precision=HIGHEST)
    next_state = jnp.exp(last_decay)[:, None, None] * state + jnp.einsum('hcd,hce->hde', keys_to_end, pseudo_values, precision=HIGHEST)
    return (next_state, block_out)

def mixer_run(state, query, keys, values, beta, decay):
    pieces = (split_groups(query), split_groups(keys), split_groups(values), split_groups(beta), split_groups(decay))
    final_state, blocks_out = lax.scan(group_run, state, pieces)
    joined = jnp.moveaxis(blocks_out, 0, 1)
    return (joined.reshape(joined.shape[0], -1, joined.shape[-1]), final_state)

def gated_norm(mixed, out_gate, gain_head):
    count = out_gate.shape[0]
    heads = jnp.transpose(mixed, (1, 0, 2))
    normed = norm_scale(heads, gain_head)
    return (normed * jax.nn.silu(out_gate.reshape(count, H, DV))).reshape(count, H * DV)

def adam_step(weight, grad_full, first, second, clip):
    grad_clipped = grad_full * clip
    first_new = BETA_ONE * first + (1.0 - BETA_ONE) * grad_clipped
    second_new = BETA_TWO * second + (1.0 - BETA_TWO) * grad_clipped * grad_clipped
    update = first_new / CORRECT_ONE / (jnp.sqrt(second_new / CORRECT_TWO) + ADAM_EPS) + DECAY_RATE * weight
    return (weight - LEARN_RATE * update, first_new, second_new)

def sequence_pass(seq_in, seq_grad, weights, parts):
    w_in, w_out, w_ffn, w_down = weights
    gain_one, gain_two, gain_head, tap_values, w_gates, a_log, dt_bias = parts
    width = tap_values.shape[1]
    x_float = seq_in.astype(jnp.float32)
    normed_in = norm_scale(x_float, gain_one).astype(jnp.bfloat16)
    projected = jnp.dot(normed_in.astype(jnp.float32), w_in.T.astype(jnp.float32), preferred_element_type=jnp.float32)
    gate_logits = jnp.dot(normed_in.astype(jnp.float32), w_gates, precision=HIGHEST)
    extended = jnp.concatenate([jnp.zeros((CONV - 1, width), jnp.float32), projected[:, :width]], axis=0)
    out_gate = projected[:, width:]
    query, keys, values, beta, decay = features(extended, tap_values, gate_logits, a_log, dt_bias)
    start = jnp.zeros((H, DK, DV), jnp.float32)
    mixed, final_state = mixer_run(start, query, keys, values, beta, decay)
    head_out = gated_norm(mixed, out_gate, gain_head).astype(jnp.bfloat16)
    resid = x_float + jnp.dot(head_out.astype(jnp.float32), w_out.astype(jnp.float32), preferred_element_type=jnp.float32)
    normed_mid = norm_scale(resid, gain_two).astype(jnp.bfloat16)
    ffn_pre = jnp.dot(normed_mid.astype(jnp.float32), w_ffn.T.astype(jnp.float32), preferred_element_type=jnp.float32)
    gate_part = ffn_pre[:, :FF]
    up_part = ffn_pre[:, FF:]
    hidden_act = swiglu(gate_part, up_part).astype(jnp.bfloat16)
    result = (resid + jnp.dot(hidden_act.astype(jnp.float32), w_down.astype(jnp.float32), preferred_element_type=jnp.float32)).astype(jnp.bfloat16)
    grad_float = seq_grad.astype(jnp.float32)
    grad_down = jnp.dot(hidden_act.T.astype(jnp.float32), seq_grad.astype(jnp.float32), preferred_element_type=jnp.float32)
    grad_hidden = jnp.dot(seq_grad.astype(jnp.float32), w_down.T.astype(jnp.float32), preferred_element_type=jnp.float32)
    unused_one, pull_swiglu = jax.vjp(swiglu, gate_part, up_part)
    grad_gate, grad_up = pull_swiglu(grad_hidden)
    grad_pre = jnp.concatenate([grad_gate, grad_up], axis=1).astype(jnp.bfloat16)
    grad_ffn = jnp.dot(grad_pre.T.astype(jnp.float32), normed_mid.astype(jnp.float32), preferred_element_type=jnp.float32)
    grad_mid = jnp.dot(grad_pre.astype(jnp.float32), w_ffn.astype(jnp.float32), preferred_element_type=jnp.float32)
    unused_two, pull_mid = jax.vjp(norm_scale, resid, gain_two)
    grad_through, grad_gain_two = pull_mid(grad_mid)
    grad_resid = grad_float + grad_through
    resid_half = grad_resid.astype(jnp.bfloat16)
    grad_out = jnp.dot(head_out.T.astype(jnp.float32), resid_half.astype(jnp.float32), preferred_element_type=jnp.float32)
    grad_head = jnp.dot(resid_half.astype(jnp.float32), w_out.T.astype(jnp.float32), preferred_element_type=jnp.float32)
    unused_three, pull_gated = jax.vjp(gated_norm, mixed, out_gate, gain_head)
    grad_mixed, grad_gate_out, grad_gain_head = pull_gated(grad_head)
    unused_four, pull_mixer = jax.vjp(mixer_run, start, query, keys, values, beta, decay)
    mixer_grads = pull_mixer((grad_mixed, jnp.zeros_like(final_state)))
    unused_five, pull_feat = jax.vjp(features, extended, tap_values, gate_logits, a_log, dt_bias)
    grad_ext, grad_taps, grad_logits, grad_alog, grad_bias = pull_feat(mixer_grads[1:])
    grad_proj = jnp.concatenate([grad_ext[CONV - 1:], grad_gate_out], axis=1).astype(jnp.bfloat16)
    grad_in = jnp.dot(grad_proj.T.astype(jnp.float32), normed_in.astype(jnp.float32), preferred_element_type=jnp.float32)
    grad_normed = jnp.dot(grad_proj.astype(jnp.float32), w_in.astype(jnp.float32), preferred_element_type=jnp.float32) + jnp.dot(grad_logits, w_gates.T, precision=HIGHEST)
    grad_gates = jnp.dot(normed_in.astype(jnp.float32).T, grad_logits, precision=HIGHEST)
    unused_six, pull_in = jax.vjp(norm_scale, x_float, gain_one)
    grad_x, grad_gain_one = pull_in(grad_normed)
    grad_input = (grad_resid + grad_x).astype(jnp.bfloat16)
    grad_small = jnp.concatenate([grad_gain_one, grad_gain_two, grad_gain_head, grad_taps.reshape(-1), grad_gates.reshape(-1), grad_alog, grad_bias])
    return (result, grad_input, grad_in, grad_out, grad_ffn, grad_down, grad_small)

def reference(inputs, cotangent, mixer_params, mixer_first, mixer_second, ffn_params, ffn_first, ffn_second, small_params, small_first, small_second):
    weights = split_weights(mixer_params.astype(jnp.bfloat16), ffn_params.astype(jnp.bfloat16))
    parts = unpack_small(small_params)

    def one_sequence(carry, pair):
        seq_in, seq_grad = pair
        result, grad_input, grad_in, grad_out, grad_ffn, grad_down, grad_small = sequence_pass(seq_in, seq_grad, weights, parts)
        updated = (carry[0] + jnp.concatenate([grad_in, grad_out], axis=0), carry[1] + jnp.concatenate([grad_ffn, grad_down], axis=0), carry[2] + grad_small)
        return (updated, (result, grad_input))
    start = (jnp.zeros((2 * H * DK + 3 * H * DV, D), jnp.float32), jnp.zeros((3 * FF, D), jnp.float32), jnp.zeros(small_params.shape, jnp.float32))
    totals, stacked = lax.scan(one_sequence, start, (inputs, cotangent))
    mixer_grad = totals[0].reshape(-1)
    ffn_grad = totals[1].reshape(-1)
    small_grad = totals[2]
    squares = jnp.sum(mixer_grad * mixer_grad) + jnp.sum(ffn_grad * ffn_grad) + jnp.sum(small_grad * small_grad)
    clip = jnp.minimum(1.0, MAX_NORM / (jnp.sqrt(squares) + 1e-06))
    mixer_new, mixer_first_new, mixer_second_new = adam_step(mixer_params, mixer_grad, mixer_first, mixer_second, clip)
    ffn_new, ffn_first_new, ffn_second_new = adam_step(ffn_params, ffn_grad, ffn_first, ffn_second, clip)
    small_new, small_first_new, small_second_new = adam_step(small_params, small_grad, small_first, small_second, clip)
    return (stacked[0], stacked[1], mixer_grad, ffn_grad, small_grad, mixer_new, mixer_first_new, mixer_second_new, ffn_new, ffn_first_new, ffn_second_new, small_new, small_first_new, small_second_new)
```

```python
import functools
import math
import jax
import jax.numpy as jnp
from jax import lax
from jax.experimental import pallas as pl
from jax.experimental.pallas import tpu as pltpu
from jax.sharding import PartitionSpec as P

D = 1024
H = 2
DK = 256
DV = 512
FF = 1408
CONV = 4
GROUP = 64


EPSILON = 1e-06
ADAM_EPS = 1e-08
LEARN_RATE = 0.02
BETA_ONE = 0.9
BETA_TWO = 0.999
DECAY_RATE = 0.1
CORRECT_ONE = 1.0 - 0.9**3
CORRECT_TWO = 1.0 - 0.999**3
MAX_NORM = 1.0
HIGHEST = lax.Precision.HIGHEST


def from_behind(value, axis, steps):
    count = lax.axis_size(axis)
    initial, last = (max(0, -steps), min(count, count - steps))
    return lax.ppermute(value, axis, [(source, source + steps) for source in range(initial, last)])


def norm_scale(values, gain):
    return values * lax.rsqrt(jnp.mean(values * values, axis=-1, keepdims=True) + EPSILON) * gain


def swiglu(gate_part, up_part):
    return jax.nn.silu(gate_part) * up_part


def unpack_small(packed):
    width = 2 * H * DK + H * DV
    lengths = [D, D, DV, CONV * width, D * 2 * H, H, H]
    pieces = []
    offset = 0
    for length in lengths:
        pieces.append(packed[offset : offset + length])
        offset = offset + length
    return (
        pieces[0],
        pieces[1],
        pieces[2],
        pieces[3].reshape(CONV, width),
        pieces[4].reshape(D, 2 * H),
        pieces[5],
        pieces[6],
    )


def split_weights(mix_whole, ffn_whole):
    mix_rows = mix_whole.reshape(-1, D)
    ffn_rows = ffn_whole.reshape(-1, D)
    edge = 2 * H * DK + 2 * H * DV
    return (mix_rows[:edge], mix_rows[edge:], ffn_rows[: 2 * FF], ffn_rows[2 * FF :])


PAD = 16
HIGH = dict(precision=HIGHEST, preferred_element_type=jnp.float32)


def mm(a, b):
    return lax.dot_general(a, b, (((1,), (0,)), ((), ())), **HIGH)


def mm_nt(a, b):
    return lax.dot_general(a, b, (((1,), (1,)), ((), ())), **HIGH)


def mm_tn(a, b):
    return lax.dot_general(a, b, (((0,), (0,)), ((), ())), **HIGH)


def halves(a):
    high = a.astype(jnp.bfloat16)
    return high, (a - high.astype(jnp.float32)).astype(jnp.bfloat16)


def wire_mm(a, b, dims):
    high, low = halves(b)
    first = lax.dot_general(a, high, (dims, ((), ())), preferred_element_type=jnp.float32)
    return first + lax.dot_general(a, low, (dims, ((), ())), preferred_element_type=jnp.float32)


def iotas(size):
    shape = (size, size)
    return (
        lax.broadcasted_iota(jnp.int32, shape, 0),
        lax.broadcasted_iota(jnp.int32, shape, 1),
    )


def to_row(column, rows, cols):
    return jnp.sum(jnp.where(rows == cols, column, 0.0), axis=0, keepdims=True)


def unit_inverse(strict_part, rows, cols):
    size = strict_part.shape[0]
    inverse = jnp.where(rows == cols, 1.0, 0.0) - jnp.where(
        (rows // 2 == cols // 2), strict_part, 0.0
    )
    block = 2
    while block < size:
        joined = (rows // (2 * block) == cols // (2 * block)) & (rows // block != cols // block)
        off = jnp.where(joined, strict_part, 0.0)
        inverse = inverse - mm(mm(inverse, off), inverse)
        block = 2 * block
    return inverse


def silu_pair(x):
    gate = jax.nn.sigmoid(x)
    return x * gate, gate * (1.0 + x * (1.0 - gate))


def conv_sum(extended_ref, taps, count):
    total = None
    for tap in range(CONV):
        piece = taps[tap : tap + 1] * extended_ref[pl.ds(8 - (CONV - 1) + tap, count), :]
        total = piece if total is None else total + piece
    return total


def unit_rows(part):
    return lax.rsqrt(jnp.sum(part * part, axis=-1, keepdims=True) + EPSILON)


def decay_terms(decay_column, rows, cols):
    lower = rows >= cols
    size = rows.shape[0]
    spread_in = jnp.broadcast_to(decay_column, (size, 128))
    cumulative = mm(jnp.where(lower, 1.0, 0.0), spread_in)[:, :1]
    across = to_row(cumulative, rows, cols)
    matrix = jnp.where(lower, jnp.exp(jnp.where(lower, cumulative - across, 0.0)), 0.0)
    last = cumulative[size - 1 : size]
    return matrix, jnp.exp(cumulative), jnp.exp(last - cumulative), jnp.exp(last)


def forward_parts(
    projected_ref, border_ref, taps_ref, beta_ref, decay_ref,
    wire_ref, query_ref, keys_ref, values_ref, inverse_ref, extended_ref,
):
    count = projected_ref.shape[0]
    width = taps_ref.shape[1]
    extended_ref[0:8, :] = border_ref[...]
    extended_ref[pl.ds(8, count), :] = projected_ref[:, :width]
    summed = conv_sum(extended_ref, taps_ref[...], count)
    activated = summed * jax.nn.sigmoid(summed)
    rows, cols = iotas(count)
    for head in range(H):
        query_part = activated[:, head * DK : (head + 1) * DK]
        key_part = activated[:, (H + head) * DK : (H + head + 1) * DK]
        start = 2 * H * DK + head * DV
        values = activated[:, start : start + DV]
        query = query_part * unit_rows(query_part) * DK ** (-0.5)
        keys = key_part * unit_rows(key_part)
        beta = beta_ref[:, head : head + 1]
        matrix, grown, to_end, whole = decay_terms(decay_ref[:, head : head + 1], rows, cols)
        system = jnp.where(rows > cols, beta * mm_nt(keys, keys) * matrix, 0.0)
        inverse = unit_inverse(system, rows, cols)
        key_mix = mm(inverse, keys * (beta * grown))
        value_mix = mm(inverse, values * beta)
        base = head * (2 * DK + DV)
        wire_ref[0:count, base : base + DK] = (keys * to_end).astype(jnp.bfloat16)
        wire_ref[0:count, base + DK : base + 2 * DK] = key_mix.astype(jnp.bfloat16)
        wire_ref[0:count, base + 2 * DK : base + 2 * DK + DV] = value_mix.astype(jnp.bfloat16)
        high, low = halves(jnp.broadcast_to(whole, (PAD, 2 * DK + DV)))
        first = lax.broadcasted_iota(jnp.int32, (PAD, 2 * DK + DV), 0) < 8
        tail = jnp.where(first, high.astype(jnp.float32), low.astype(jnp.float32))
        wire_ref[pl.ds(count, PAD), base : base + 2 * DK + DV] = tail.astype(jnp.bfloat16)
        query_ref[:, head * DK : (head + 1) * DK] = query
        keys_ref[:, head * DK : (head + 1) * DK] = keys
        values_ref[:, head * DV : (head + 1) * DV] = values
        inverse_ref[head] = inverse


def wire_parts(wire_ref, index, head, count):
    base = head * (2 * DK + DV)
    to_end = wire_ref[index, 0:count, base : base + DK]
    key_mix = wire_ref[index, 0:count, base + DK : base + 2 * DK]
    value_mix = wire_ref[index, 0:count, base + 2 * DK : base + 2 * DK + DV]
    tail = wire_ref[index, pl.ds(count, PAD), base : base + 128].astype(jnp.float32)
    whole = tail[0:1, 0:1] + tail[8:9, 0:1]
    return to_end, key_mix, value_mix, whole


def own_mix(inverse, keys, values, beta, grown):
    return mm(inverse, keys * (beta * grown)), mm(inverse, values * beta)


def forward_chain(
    place_ref, wire_ref, query_ref, keys_ref, values_ref, inverse_ref, beta_ref, decay_ref,
    gate_ref, gain_ref, head_out_ref, mixed_ref, state_ref, pseudo_ref,
):
    count = query_ref.shape[0]
    state_ref[...] = jnp.zeros_like(state_ref)

    def lap(index, carry):
        for head in range(H):
            to_end, key_mix, value_mix, whole = wire_parts(wire_ref, index, head, count)
            state = state_ref[head]
            pseudo = value_mix.astype(jnp.float32) - wire_mm(key_mix, state, ((1,), (0,)))
            state_ref[head] = whole * state + wire_mm(to_end, pseudo, ((0,), (0,)))
        return carry

    lax.fori_loop(0, place_ref[0], lap, 0)
    rows, cols = iotas(count)
    for head in range(H):
        query = query_ref[:, head * DK : (head + 1) * DK]
        keys = keys_ref[:, head * DK : (head + 1) * DK]
        span = slice(head * DV, (head + 1) * DV)
        beta = beta_ref[:, head : head + 1]
        matrix, grown, to_end, whole = decay_terms(decay_ref[:, head : head + 1], rows, cols)
        key_mix, value_mix = own_mix(inverse_ref[head], keys, values_ref[:, span], beta, grown)
        state = state_ref[head]
        pseudo = value_mix - mm(key_mix, state)
        mixed = mm(query * grown, state) + mm(mm_nt(query, keys) * matrix, pseudo)
        scale = lax.rsqrt(jnp.mean(mixed * mixed, axis=-1, keepdims=True) + EPSILON)
        gated, unused = silu_pair(gate_ref[:, span])
        head_out_ref[:, span] = (mixed * scale * gain_ref[...] * gated).astype(jnp.bfloat16)
        mixed_ref[:, span] = mixed
        pseudo_ref[:, span] = pseudo


def backward_local(
    grad_ref, mixed_ref, query_ref, keys_ref, values_ref, inverse_ref, beta_ref, decay_ref,
    gate_ref, gain_ref, local_ref, grad_mixed_ref, grad_gate_ref, grad_gain_ref,
):
    count = query_ref.shape[0]
    rows, cols = iotas(count)
    gain_total = jnp.zeros((1, DV), jnp.float32)
    for head in range(H):
        query = query_ref[:, head * DK : (head + 1) * DK]
        keys = keys_ref[:, head * DK : (head + 1) * DK]
        span = slice(head * DV, (head + 1) * DV)
        mixed = mixed_ref[:, span]
        grad = grad_ref[:, span]
        scale = lax.rsqrt(jnp.mean(mixed * mixed, axis=-1, keepdims=True) + EPSILON)
        plain = mixed * scale
        gated, slope = silu_pair(gate_ref[:, span])
        grad_gate_ref[:, span] = grad * plain * gain_ref[...] * slope
        grad_normed = grad * gated
        gain_total = gain_total + jnp.sum(grad_normed * plain, axis=0, keepdims=True)
        pulled = grad_normed * gain_ref[...]
        grad_mixed = scale * (pulled - plain * jnp.mean(pulled * plain, axis=-1, keepdims=True))
        grad_mixed_ref[:, span] = grad_mixed
        beta = beta_ref[:, head : head + 1]
        matrix, grown, to_end, whole = decay_terms(decay_ref[:, head : head + 1], rows, cols)
        key_mix = mm(inverse_ref[head], keys * (beta * grown))
        grad_pseudo = mm_tn(mm_nt(query, keys) * matrix, grad_mixed)
        local = mm_tn(query * grown, grad_mixed) - mm_tn(key_mix, grad_pseudo)
        local_ref[head * DK : (head + 1) * DK, :] = local.astype(jnp.bfloat16)
    grad_gain_ref[...] = gain_total


def backward_chain(
    place_ref, wire_ref, local_ref, query_ref, keys_ref, values_ref, inverse_ref, beta_ref,
    decay_ref, state_ref, pseudo_ref, grad_mixed_ref, projected_ref, border_ref, taps_ref,
    grad_conv_ref, grad_border_ref, grad_taps_ref, grad_beta_ref, grad_decay_ref,
    after_ref, extended_ref, padded_ref,
):
    count = query_ref.shape[0]
    width = taps_ref.shape[1]
    devices = wire_ref.shape[0]
    after_ref[...] = jnp.zeros_like(after_ref)

    def lap(step, carry):
        index = devices - 1 - step
        for head in range(H):
            to_end, key_mix, value_mix, whole = wire_parts(wire_ref, index, head, count)
            after = after_ref[head]
            inner = wire_mm(to_end, after, ((1,), (0,)))
            local = local_ref[index, head * DK : (head + 1) * DK, :].astype(jnp.float32)
            after_ref[head] = whole * after - wire_mm(key_mix, inner, ((0,), (0,))) + local
        return carry

    lax.fori_loop(0, devices - 1 - place_ref[0], lap, 0)
    extended_ref[0:8, :] = border_ref[...]
    extended_ref[pl.ds(8, count), :] = projected_ref[:, :width]
    taps = taps_ref[...]
    summed = conv_sum(extended_ref, taps, count)
    activated, slope = silu_pair(summed)
    padded_ref[0:8, :] = jnp.zeros((8, width), jnp.float32)
    padded_ref[pl.ds(8 + count, 8), :] = jnp.zeros((8, width), jnp.float32)
    rows, cols = iotas(count)
    lower = rows >= cols
    strict = rows > cols
    lanes = lax.broadcasted_iota(jnp.int32, (count, 128), 1)
    beta_out = jnp.zeros((count, 128), jnp.float32)
    cumulative_out = jnp.zeros((count, 128), jnp.float32)
    row_column = lax.broadcasted_iota(jnp.int32, (count, 1), 0)
    for head in range(H):
        query = query_ref[:, head * DK : (head + 1) * DK]
        keys = keys_ref[:, head * DK : (head + 1) * DK]
        span = slice(head * DV, (head + 1) * DV)
        values = values_ref[:, span]
        beta = beta_ref[:, head : head + 1]
        matrix, grown, to_end, whole = decay_terms(decay_ref[:, head : head + 1], rows, cols)
        inverse = inverse_ref[head]
        state = state_ref[head]
        after = after_ref[head]
        pseudo = pseudo_ref[:, span]
        grad_mixed = grad_mixed_ref[:, span]
        keys_grown = keys * (beta * grown)
        key_mix = mm(inverse, keys_grown)
        value_mix = mm(inverse, values * beta)
        gram = mm_nt(keys, keys)
        system = jnp.where(strict, beta * gram * matrix, 0.0)
        scores = mm_nt(query, keys) * matrix
        keys_end = keys * to_end
        query_grown = query * grown
        grad_query_grown = mm_nt(grad_mixed, state)
        grad_scores = jnp.where(lower, mm_nt(grad_mixed, pseudo), 0.0)
        grad_pseudo = mm_tn(scores, grad_mixed) + mm(keys_end, after)
        grad_keys_end = mm_nt(pseudo, after)
        grad_whole = jnp.sum(jnp.sum(after * state, axis=1, keepdims=True), axis=0, keepdims=True)
        grad_value_in = mm_tn(inverse, grad_pseudo)
        grad_key_in = mm_tn(inverse, -mm_nt(grad_pseudo, state))
        grad_system = -jnp.where(
            strict, mm_nt(grad_value_in, value_mix) + mm_nt(grad_key_in, key_mix), 0.0
        )
        grad_raw = grad_scores * matrix
        grad_query = mm(grad_raw, keys) + grad_query_grown * grown
        grad_keys = mm_tn(grad_raw, query)
        weighted = grad_system * matrix
        grad_beta = jnp.sum(weighted * gram, axis=1, keepdims=True)
        grad_gram = weighted * beta
        grad_keys = grad_keys + mm(grad_gram, keys) + mm_tn(grad_gram, keys)
        spread = grad_scores * scores + grad_system * system
        grad_cumulative = jnp.sum(spread, axis=1, keepdims=True)
        across = jnp.sum(spread, axis=0, keepdims=True)
        grad_cumulative = grad_cumulative - jnp.sum(
            jnp.where(rows == cols, across, 0.0), axis=1, keepdims=True
        )
        grad_keys = grad_keys + grad_key_in * (beta * grown)
        through = jnp.sum(grad_key_in * keys, axis=1, keepdims=True) * grown
        grad_beta = grad_beta + through + jnp.sum(grad_value_in * values, axis=1, keepdims=True)
        grad_cumulative = grad_cumulative + through * beta
        grad_values = grad_value_in * beta
        grad_cumulative = grad_cumulative + jnp.sum(
            grad_query_grown * query_grown, axis=1, keepdims=True
        )
        grad_keys = grad_keys + grad_keys_end * to_end
        ending = jnp.sum(grad_keys_end * keys_end, axis=1, keepdims=True)
        final = jnp.sum(ending, axis=0, keepdims=True) + whole * grad_whole
        grad_cumulative = grad_cumulative - ending + jnp.where(row_column == count - 1, final, 0.0)
        beta_out = jnp.where(lanes == head, grad_beta, beta_out)
        cumulative_out = jnp.where(lanes == head, grad_cumulative, cumulative_out)
        key_part = activated[:, (H + head) * DK : (H + head + 1) * DK]
        key_scale = unit_rows(key_part)
        query_part = activated[:, head * DK : (head + 1) * DK]
        query_scale = unit_rows(query_part)
        factor = DK ** (-0.5)
        grad_query_part = (factor * query_scale) * (
            grad_query
            - query_part
            * (query_scale * query_scale)
            * jnp.sum(grad_query * query_part, axis=-1, keepdims=True)
        )
        grad_key_part = key_scale * (
            grad_keys
            - key_part
            * (key_scale * key_scale)
            * jnp.sum(grad_keys * key_part, axis=-1, keepdims=True)
        )
        spots = (head * DK, (H + head) * DK, 2 * H * DK + head * DV)
        for spot, grad in zip(spots, (grad_query_part, grad_key_part, grad_values)):
            size = grad.shape[1]
            padded_ref[pl.ds(8, count), spot : spot + size] = grad * slope[:, spot : spot + size]
    grad_beta_ref[...] = beta_out
    grad_decay_ref[...] = mm_tn(jnp.where(lower, 1.0, 0.0), cumulative_out)
    conv_total = jnp.zeros((count, width), jnp.float32)
    border_total = jnp.zeros((8, width), jnp.float32)
    summed_grad = padded_ref[pl.ds(8, count), :]
    tap_rows = lax.broadcasted_iota(jnp.int32, (8, width), 0)
    taps_total = jnp.zeros((8, width), jnp.float32)
    for tap in range(CONV):
        shift = CONV - 1 - tap
        conv_total = conv_total + taps[tap : tap + 1] * padded_ref[pl.ds(8 + shift, count), :]
        border_total = border_total + taps[tap : tap + 1] * padded_ref[pl.ds(shift, 8), :]
        piece = jnp.sum(
            summed_grad * extended_ref[pl.ds(8 - (CONV - 1) + tap, count), :],
            axis=0,
            keepdims=True,
        )
        taps_total = jnp.where(tap_rows == tap, piece, taps_total)
    grad_conv_ref[...] = conv_total
    grad_border_ref[...] = border_total
    grad_taps_ref[...] = taps_total


def fused(body, outputs, scratch=(), scalars=0, cost=(0, 0), label=None):
    def call(*args):
        vmem = pl.BlockSpec(memory_space=pltpu.VMEM)
        smem = pl.BlockSpec(memory_space=pltpu.SMEM)
        return pl.pallas_call(
            body,
            out_shape=outputs,
            in_specs=[smem] * scalars + [vmem] * (len(args) - scalars),
            out_specs=[vmem] * len(outputs),
            scratch_shapes=list(scratch),
            compiler_params=pltpu.CompilerParams(vmem_limit_bytes=60 * 2**20),
            cost_estimate=pl.CostEstimate(
                flops=cost[0], bytes_accessed=cost[1], transcendentals=0
            ),
            name=label,
        )(*args)

    return call


def gates(gate_logits, a_log, dt_bias):
    beta = jax.nn.sigmoid(gate_logits[:, :H])
    decay = -jnp.exp(a_log) * jax.nn.softplus(gate_logits[:, H:] + dt_bias)
    return beta, decay


def scatter_rows(pieces):
    outer, inner = lax.axis_size("dp"), lax.axis_size("ctx")
    whole = jnp.concatenate([piece.astype(jnp.bfloat16) for piece in pieces], axis=0)
    lane = math.gcd(whole.size // (outer * inner), D)
    blocks = whole.reshape(outer, inner, -1, lane)
    part = lax.psum_scatter(blocks, "ctx", scatter_dimension=1, tiled=False)
    own = lax.psum_scatter(part, "dp", scatter_dimension=0, tiled=False)
    return own.astype(jnp.float32).reshape(-1)


MESH = pl.DeviceIdType.MESH


class Place:
    def __init__(self, side):
        self.deep = lax.axis_size("dp")
        self.side = side
        self.ctx = lax.axis_size("ctx")
        self.z = lax.axis_index("dp")
        spot = lax.axis_index("ctx")
        self.c = lax.rem(spot, 2)
        chip = lax.div(spot, 2)
        self.x = lax.rem(chip, side)
        self.y = lax.div(chip, side)
        self.other_core = self.device(self.z, self.y, self.x, 1 - self.c)
        self.other_x = self.device(self.z, self.y, 1 - self.x, self.c)
        self.other_y = self.device(self.z, 1 - self.y, self.x, self.c)
        self.next_z = self.device(self.along(1), self.y, self.x, self.c)

    def along(self, step):
        return lax.rem(self.z + step + self.deep, self.deep)

    def device(self, z, y, x, c):
        return (z, (y * self.side + x) * 2 + c)

    def block(self, z, y, x, c):
        return z * self.ctx + (y * self.side + x) * 2 + c

    def enter(self, all_z=False):
        barrier = pltpu.get_barrier_semaphore()
        steps = range(1, self.deep) if all_z else (-1,)
        friends = [self.other_core, self.other_x, self.other_y]
        friends += [self.device(self.along(step), self.y, self.x, self.c) for step in steps]
        for friend in friends:
            pl.semaphore_signal(barrier, inc=1, device_id=friend, device_id_type=MESH)
        pl.semaphore_wait(barrier, len(friends))


class Copies:
    def __init__(self, send_sems, recv_sems, local_sems=None):
        self.send_sems, self.recv_sems, self.local_sems = send_sems, recv_sems, local_sems
        self.sent, self.locals = [], 0

    def push(self, source, target, device):
        index = len(self.sent)
        copy = pltpu.make_async_remote_copy(
            src_ref=source,
            dst_ref=target,
            send_sem=self.send_sems.at[index],
            recv_sem=self.recv_sems.at[index],
            device_id=device,
            device_id_type=MESH,
        )
        copy.start()
        self.sent.append(copy)
        return copy

    def local(self, source, target):
        copy = pltpu.make_async_copy(source, target, self.local_sems.at[self.locals])
        copy.start()
        self.locals += 1
        return copy

    def finish(self):
        for copy in self.sent:
            copy.wait_send()


def upper(rows):
    return rows // 2 // 16 * 16


def gather_steps(place, copies, shard_ref, out_ref):
    rows, deep = shard_ref.shape[0], place.deep
    top = upper(rows)
    spans = {None: (0, rows), 0: (0, top), 1: (top, rows - top)}
    ring, near, far, core = [], {}, {}, []

    def cut(ref, start, part):
        offset, size = spans[part]
        return ref.at[pl.ds(pl.multiple_of(start + offset, 16), size), :]

    def start_of(rel, dy, dx):
        y = 1 - place.y if dy else place.y
        x = 1 - place.x if dx else place.x
        return place.block(place.along(-rel), y, x, place.c) * rows

    def forward(rel, dy, dx, part, device):
        start = start_of(rel, dy, dx)
        own = rel == 0 and not dy and not dx
        source = cut(shard_ref, 0, part) if own else cut(out_ref, start, part)
        return copies.push(source, cut(out_ref, start, part), device)

    def spread(rel):
        if rel < deep - 1:
            ring.append(forward(rel, 0, 0, None, place.next_z))
        near[rel, "x0"] = forward(rel, 0, 0, 0, place.other_x)
        near[rel, "y1"] = forward(rel, 0, 0, 1, place.other_y)
        near[rel, "y0"] = forward(rel, 0, 0, 0, place.other_y)
        near[rel, "x1"] = forward(rel, 0, 0, 1, place.other_x)
        core.append(forward(rel, 0, 0, None, place.other_core))

    def second(rel):
        near[rel, "x0"].wait_recv()
        far[rel, 0] = forward(rel, 0, 1, 0, place.other_y)
        near[rel, "y1"].wait_recv()
        far[rel, 1] = forward(rel, 1, 0, 1, place.other_x)
        core.append(forward(rel, 0, 1, 0, place.other_core))
        core.append(forward(rel, 1, 0, 1, place.other_core))

    def third(rel):
        near[rel, "y0"].wait_recv()
        core.append(forward(rel, 1, 0, 0, place.other_core))
        near[rel, "x1"].wait_recv()
        core.append(forward(rel, 0, 1, 1, place.other_core))

    def fourth(rel):
        for part in (0, 1):
            far[rel, part].wait_recv()
            core.append(forward(rel, 1, 1, part, place.other_core))

    own_copy = []

    def first():
        own_copy.append(copies.local(shard_ref, cut(out_ref, start_of(0, 0, 0), None)))
        spread(0)

    def later(rel):
        ring[rel - 1].wait_recv()
        spread(rel)

    def last():
        for copy in core:
            copy.wait_recv()
        own_copy[0].wait()

    steps = [first]
    for rel in range(1, deep):
        steps.append(lambda rel=rel: later(rel))
        steps.append(lambda rel=rel: second(rel - 1))
        steps.append(lambda rel=rel: third(rel - 1))
    steps.append(lambda: second(deep - 1))
    steps.append(lambda: third(deep - 1))
    for rel in range(deep):
        steps.append(lambda rel=rel: fourth(rel))
    steps.append(last)
    return steps


def gather_kernel(side, count, *refs):
    shards, outs, (send_sems, recv_sems, local_sems) = refs[:count], refs[count : 2 * count], refs[2 * count :]
    place = Place(side)
    copies = Copies(send_sems, recv_sems, local_sems)
    place.enter()
    for group in zip(*[gather_steps(place, copies, *pair) for pair in zip(shards, outs)]):
        for step in group:
            step()
    copies.finish()


def gather_all(shards, side, tag):
    deep, ctx = lax.axis_size("dp"), lax.axis_size("ctx")
    each = (deep - 1) + 4 * deep + 2 * deep + deep + 2 * deep * 3
    any_space = pl.BlockSpec(memory_space=pl.ANY)
    return pl.pallas_call(
        functools.partial(gather_kernel, side, len(shards)),
        out_shape=[
            jax.ShapeDtypeStruct((deep * ctx * shard.shape[0], D), jnp.bfloat16) for shard in shards
        ],
        in_specs=[any_space] * len(shards),
        out_specs=[any_space] * len(shards),
        scratch_shapes=[
            pltpu.SemaphoreType.DMA((each * len(shards),)),
            pltpu.SemaphoreType.DMA((each * len(shards),)),
            pltpu.SemaphoreType.DMA((len(shards),)),
        ],
        compiler_params=pltpu.CompilerParams(collective_id=tag, has_side_effects=True),
        cost_estimate=pl.CostEstimate(flops=0, bytes_accessed=10**8, transcendentals=0),
        name="gather_parameters",
    )(*shards)


def wide(value):
    return value.astype(jnp.float32)


class Scatter:
    def __init__(self, place, copies, grad_ref, held, from_core, first_x, first_y, last_x, last_y, from_z):
        self.place, self.copies, self.grad = place, copies, grad_ref
        self.held, self.from_core, self.from_z = held, from_core, from_z
        self.first = {0: first_y, 1: first_x}
        self.last = {0: last_x, 1: last_y}
        self.rows = held.shape[1]
        self.top = upper(self.rows)
        self.loads, self.cores, self.near, self.far, self.ring = {}, {}, {}, {}, {}

    @staticmethod
    def scratch(deep, rows):
        top = upper(rows)
        low = rows - top
        return [
            pltpu.VMEM((4 * deep, rows, D), jnp.bfloat16),
            pltpu.VMEM((4 * deep, rows, D), jnp.bfloat16),
            pltpu.VMEM((2 * deep, low, D), jnp.bfloat16),
            pltpu.VMEM((2 * deep, top, D), jnp.bfloat16),
            pltpu.VMEM((deep, top, D), jnp.bfloat16),
            pltpu.VMEM((deep, low, D), jnp.bfloat16),
            pltpu.VMEM((deep - 1, rows, D), jnp.bfloat16),
        ]

    @staticmethod
    def copies_of(deep):
        return 4 * deep + 4 * deep + 2 * deep + deep - 1

    def slot(self, rel, dy, dx):
        return (rel - 1) * 4 + dy * 2 + dx

    def span(self, part):
        return pl.ds(0, self.top) if part == 0 else pl.ds(self.top, self.rows - self.top)

    def load(self):
        place = self.place
        for rel in range(1, place.deep + 1):
            for dy, dx in ((1, 1), (1, 0), (0, 1), (0, 0)):
                y = 1 - place.y if dy else place.y
                x = 1 - place.x if dx else place.x
                slot = self.slot(rel, dy, dx)

                def rows_of(core):
                    start = place.block(place.along(-rel), y, x, core) * self.rows
                    return self.grad.at[pl.ds(pl.multiple_of(start, 16), self.rows), :]

                self.cores[slot] = self.copies.push(
                    rows_of(1 - place.c), self.from_core.at[slot], place.other_core
                )
                self.loads[slot] = self.copies.local(rows_of(place.c), self.held.at[slot])

    def stage_one(self, rel):
        place = self.place
        for dy, dx in ((1, 1), (1, 0), (0, 1), (0, 0)):
            slot = self.slot(rel, dy, dx)
            self.loads[slot].wait()
            self.cores[slot].wait_recv()
            self.held[slot] = (wide(self.held[slot]) + wide(self.from_core[slot])).astype(jnp.bfloat16)
            if dy:
                self.near[rel, 0, dx] = self.copies.push(
                    self.held.at[slot, self.span(0), :],
                    self.first[0].at[(rel - 1) * 2 + dx],
                    place.other_y,
                )
            if dx:
                self.near[rel, 1, dy] = self.copies.push(
                    self.held.at[slot, self.span(1), :],
                    self.first[1].at[(rel - 1) * 2 + dy],
                    place.other_x,
                )

    def add(self, slot, part, piece):
        self.held[slot, self.span(part), :] = (
            wide(self.held[slot, self.span(part), :]) + wide(piece)
        ).astype(jnp.bfloat16)

    def stage_two(self, rel):
        place = self.place
        for part in (0, 1):
            for away in (1, 0):
                self.near[rel, part, away].wait_recv()
                slot = self.slot(rel, away, 0) if part else self.slot(rel, 0, away)
                self.add(slot, part, self.first[part][(rel - 1) * 2 + away])
                if away:
                    self.far[rel, part] = self.copies.push(
                        self.held.at[slot, self.span(part), :],
                        self.last[part].at[rel - 1],
                        place.other_y if part else place.other_x,
                    )

    def stage_three(self, rel, total_ref=None):
        slot = self.slot(rel, 0, 0)
        for part in (0, 1):
            self.far[rel, part].wait_recv()
            self.add(slot, part, self.last[part][rel - 1])
        if rel >= 2:
            self.ring[rel - 1].wait_recv()
            total = wide(self.held[slot]) + wide(self.from_z[rel - 2])
            if rel == self.place.deep:
                total_ref[...] = total
                return
            self.held[slot] = total.astype(jnp.bfloat16)
        self.ring[rel] = self.copies.push(
            self.held.at[slot], self.from_z.at[rel - 1], self.place.next_z
        )

    def steps(self, total_ref):
        deep = self.place.deep
        out = [self.load]
        for turn in range(1, deep + 3):
            if turn <= deep:
                out.append(lambda rel=turn: self.stage_one(rel))
            if 1 <= turn - 1 <= deep:
                out.append(lambda rel=turn - 1: self.stage_two(rel))
            if 1 <= turn - 2 <= deep:
                out.append(lambda rel=turn - 2: self.stage_three(rel, total_ref))
        return out


class Everywhere:
    def __init__(self, place, copies, total, slots, stack):
        self.place, self.copies = place, copies
        self.total, self.slots, self.stack = total, slots, stack
        self.turns = (place.other_core, place.other_x, place.other_y)
        self.pending = []

    @staticmethod
    def scratch(deep, rows):
        return [pltpu.VMEM((3, rows, 128), jnp.float32), pltpu.VMEM((deep, rows, 128), jnp.float32),
                pltpu.VMEM((4, rows, 128), jnp.float32)]

    def send(self, turn):
        self.pending = [
            self.copies.push(self.total.at[turn], self.slots.at[turn], self.turns[turn])
        ]

    def take(self, turn):
        self.pending[0].wait_recv()
        self.total[turn + 1] = self.total[turn] + self.slots[turn]

    def send_z(self):
        place = self.place
        self.pending = [
            self.copies.push(
                self.total.at[3],
                self.stack.at[place.z],
                place.device(place.along(step), place.y, place.x, place.c),
            )
            for step in range(1, place.deep)
        ]
        self.stack[place.z] = self.total[3]

    def take_z(self):
        for copy in self.pending:
            copy.wait_recv()
        result = self.stack[0]
        for index in range(1, self.place.deep):
            result = result + self.stack[index]
        return result

    def run(self):
        for turn in range(3):
            self.send(turn)
            self.take(turn)
        self.send_z()
        return self.take_z()


def scatter_kernel(side, counts, *refs):
    refs = list(refs)
    take = lambda number: [refs.pop(0) for unused in range(number)]
    grads = take(counts)
    small_ref, = take(1)
    totals = take(counts)
    small_out, squares_out = take(2)
    scratch = [take(7) for unused in range(counts)]
    small_scratch, square_scratch = take(3), take(3)
    send_sems, recv_sems, local_sems = refs
    place = Place(side)
    copies = Copies(send_sems, recv_sems, local_sems)
    place.enter(all_z=True)
    scatters = [Scatter(place, copies, grad, *own) for grad, own in zip(grads, scratch)]
    small = Everywhere(place, copies, small_scratch[2], *small_scratch[:2])
    small.total[0] = small_ref[...]
    lists = [scatter.steps(total) for scatter, total in zip(scatters, totals)]
    extra = [lambda: small.send(0)]
    for turn in range(3):
        extra.append(lambda turn=turn: small.take(turn))
        extra.append(lambda turn=turn: small.send(turn + 1) if turn < 2 else small.send_z())
    for index, group in enumerate(zip(*lists)):
        for step in group:
            step()
        if index < len(extra):
            extra[index]()
    for step in extra[len(lists[0]) :]:
        step()
    small_total = small.take_z()
    small_out[...] = small_total
    squares = jnp.zeros((8, 128), jnp.float32)
    for total in totals:
        value = total[...]
        line = jnp.sum(value * value, axis=0, keepdims=True)
        for start in range(0, D, 128):
            squares = squares + line[:, start : start + 128] * 0.125
    square = Everywhere(place, copies, square_scratch[2], *square_scratch[:2])
    square.total[0] = squares
    squares_out[...] = square.run()
    copies.finish()


def scatter_all(grads, small, side, tag):
    deep, ctx = lax.axis_size("dp"), lax.axis_size("ctx")
    rows = [grad.shape[0] // (deep * ctx) for grad in grads]
    number = len(grads) * Scatter.copies_of(deep) + 2 * (3 + deep - 1)
    vmem = pl.BlockSpec(memory_space=pltpu.VMEM)
    scratch = []
    for size in rows:
        scratch += Scatter.scratch(deep, size)
    scratch += Everywhere.scratch(deep, small.shape[0]) + Everywhere.scratch(deep, 8)
    return pl.pallas_call(
        functools.partial(scatter_kernel, side, len(grads)),
        out_shape=[jax.ShapeDtypeStruct((size, D), jnp.float32) for size in rows]
        + [jax.ShapeDtypeStruct(small.shape, jnp.float32), jax.ShapeDtypeStruct((8, 128), jnp.float32)],
        in_specs=[pl.BlockSpec(memory_space=pl.ANY)] * len(grads) + [vmem],
        out_specs=[vmem] * (len(grads) + 2),
        scratch_shapes=scratch
        + [
            pltpu.SemaphoreType.DMA((number,)),
            pltpu.SemaphoreType.DMA((number,)),
            pltpu.SemaphoreType.DMA((4 * deep * len(grads),)),
        ],
        compiler_params=pltpu.CompilerParams(
            collective_id=tag, has_side_effects=True, vmem_limit_bytes=60 * 2**20
        ),
        cost_estimate=pl.CostEstimate(flops=0, bytes_accessed=10**8, transcendentals=0),
        name="scatter_gradients",
    )(*grads, small)


def chip_side():
    half = lax.axis_size("ctx") // 2
    side = math.isqrt(half)
    return side if side == 2 and 2 * side * side == lax.axis_size("ctx") else 0


def adam_step(weight, grad_full, first, second, clip):
    grad_clipped = grad_full * clip
    first_new = BETA_ONE * first + (1.0 - BETA_ONE) * grad_clipped
    second_new = BETA_TWO * second + (1.0 - BETA_TWO) * grad_clipped * grad_clipped
    update = (
        first_new / CORRECT_ONE / (jnp.sqrt(second_new / CORRECT_TWO) + ADAM_EPS)
        + DECAY_RATE * weight
    )
    return (weight - LEARN_RATE * update, first_new, second_new)


def body(
    inputs,
    cotangent,
    mixer_params,
    mixer_first,
    mixer_second,
    ffn_params,
    ffn_first,
    ffn_second,
    small_params,
    small_first,
    small_second,
):
    gain_one, gain_two, gain_head, tap_values, w_gates, a_log, dt_bias = unpack_small(small_params)
    width = tap_values.shape[1]
    mix_part = mixer_params.astype(jnp.bfloat16)
    ffn_part = ffn_params.astype(jnp.bfloat16)
    everyone = lax.axis_size("dp") * lax.axis_size("ctx")
    mix_rows, ffn_rows = mix_part.size // D, ffn_part.size // D
    side = chip_side() if mix_rows % 32 == 0 and ffn_part.size % D == 0 else 0
    padding = -ffn_rows % 16
    if side:
        mix_whole, ffn_whole = gather_all(
            (
                mix_part.reshape(mix_rows, D),
                jnp.pad(ffn_part.reshape(ffn_rows, D), ((0, padding), (0, 0))),
            ),
            side,
            1,
        )
        ffn_whole = ffn_whole.reshape(everyone, ffn_rows + padding, D)[:, :ffn_rows]
    else:
        mix_whole, ffn_whole = (
            lax.all_gather(mix_part, ("dp", "ctx"), axis=0, tiled=True),
            lax.all_gather(ffn_part, ("dp", "ctx"), axis=0, tiled=True),
        )
    w_in, w_out, w_ffn, w_down = split_weights(mix_whole, ffn_whole)
    x_float = inputs[0].astype(jnp.float32)
    count = x_float.shape[0]
    normed_in = norm_scale(x_float, gain_one).astype(jnp.bfloat16)
    projected = jnp.dot(normed_in, w_in.T, preferred_element_type=jnp.float32)
    gate_logits = jnp.dot(normed_in.astype(jnp.float32), w_gates, precision=HIGHEST)
    f32 = jnp.float32
    devices = lax.axis_size("ctx")
    place = lax.axis_index("ctx").astype(jnp.int32).reshape(1)
    out_gate = projected[:, width:]
    edge = from_behind(projected[count - 8 :, :width], "ctx", 1)
    border = jnp.where(lax.broadcasted_iota(jnp.int32, (8, 1), 0) >= 8 - (CONV - 1), edge, 0.0)
    (beta, decay), pull_gates = jax.vjp(gates, gate_logits, a_log, dt_bias)
    wire, query, keys, values, inverse = fused(
        forward_parts,
        (
            jax.ShapeDtypeStruct((count + PAD, H * (2 * DK + DV)), jnp.bfloat16),
            jax.ShapeDtypeStruct((count, H * DK), f32),
            jax.ShapeDtypeStruct((count, H * DK), f32),
            jax.ShapeDtypeStruct((count, H * DV), f32),
            jax.ShapeDtypeStruct((H, count, count), f32),
        ),
        scratch=(pltpu.VMEM((count + 8, width), f32),),
        label="forward_parts",
    )(projected, border, tap_values, beta, decay)
    wires = lax.all_gather(wire, "ctx")
    gain_row = gain_head.reshape(1, DV)
    head_out, mixed, state, pseudo = fused(
        forward_chain,
        (
            jax.ShapeDtypeStruct((count, H * DV), jnp.bfloat16),
            jax.ShapeDtypeStruct((count, H * DV), f32),
            jax.ShapeDtypeStruct((H, DK, DV), f32),
            jax.ShapeDtypeStruct((count, H * DV), f32),
        ),
        scalars=1,
        label="forward_chain",
    )(place, wires, query, keys, values, inverse, beta, decay, out_gate, gain_row)
    resid = x_float + jnp.dot(head_out, w_out, preferred_element_type=jnp.float32)
    normed_mid = norm_scale(resid, gain_two).astype(jnp.bfloat16)
    ffn_pre = jnp.dot(normed_mid, w_ffn.T, preferred_element_type=jnp.float32)
    gate_part = ffn_pre[:, :FF]
    up_part = ffn_pre[:, FF:]
    hidden_act = swiglu(gate_part, up_part).astype(jnp.bfloat16)
    result = (resid + jnp.dot(hidden_act, w_down, preferred_element_type=jnp.float32)).astype(
        jnp.bfloat16
    )
    seq_grad = cotangent[0]
    grad_float = seq_grad.astype(jnp.float32)
    grad_down = jnp.dot(hidden_act.T, seq_grad, preferred_element_type=jnp.float32)
    grad_hidden = jnp.dot(seq_grad, w_down.T, preferred_element_type=jnp.float32)
    unused_one, pull_swiglu = jax.vjp(swiglu, gate_part, up_part)
    grad_gate, grad_up = pull_swiglu(grad_hidden)
    grad_pre = jnp.concatenate([grad_gate, grad_up], axis=1).astype(jnp.bfloat16)
    grad_ffn = jnp.dot(grad_pre.T, normed_mid, preferred_element_type=jnp.float32)
    grad_mid = jnp.dot(grad_pre, w_ffn, preferred_element_type=jnp.float32)
    unused_two, pull_mid = jax.vjp(norm_scale, resid, gain_two)
    grad_through, grad_gain_two = pull_mid(grad_mid)
    grad_resid = grad_float + grad_through
    resid_half = grad_resid.astype(jnp.bfloat16)
    grad_out = jnp.dot(head_out.T, resid_half, preferred_element_type=jnp.float32)
    grad_head = jnp.dot(resid_half, w_out.T, preferred_element_type=jnp.float32)
    local, grad_mixed, grad_gate_out, grad_gain_head = fused(
        backward_local,
        (
            jax.ShapeDtypeStruct((H * DK, DV), jnp.bfloat16),
            jax.ShapeDtypeStruct((count, H * DV), f32),
            jax.ShapeDtypeStruct((count, H * DV), f32),
            jax.ShapeDtypeStruct((1, DV), f32),
        ),
        label="backward_local",
    )(grad_head, mixed, query, keys, values, inverse, beta, decay, out_gate, gain_row)
    locals_all = lax.all_gather(local, "ctx")
    if not side:
        locals_all, grad_ffn, grad_down = lax.optimization_barrier((locals_all, grad_ffn, grad_down))
        ffn_shard = scatter_rows((grad_ffn, grad_down))
    grad_conv, grad_border, grad_taps, grad_beta, grad_decay = fused(
        backward_chain,
        (
            jax.ShapeDtypeStruct((count, width), f32),
            jax.ShapeDtypeStruct((8, width), f32),
            jax.ShapeDtypeStruct((8, width), f32),
            jax.ShapeDtypeStruct((count, 128), f32),
            jax.ShapeDtypeStruct((count, 128), f32),
        ),
        scratch=(
            pltpu.VMEM((H, DK, DV), f32),
            pltpu.VMEM((count + 8, width), f32),
            pltpu.VMEM((count + 16, width), f32),
        ),
        scalars=1,
        label="backward_chain",
    )(
        place, wires, locals_all, query, keys, values, inverse, beta, decay, state, pseudo,
        grad_mixed, projected, border, tap_values,
    )
    grad_logits, grad_alog, grad_bias = pull_gates((grad_beta[:, :H], grad_decay[:, :H]))
    returned = from_behind(grad_border, "ctx", -1)[8 - (CONV - 1) :]
    grad_conv = grad_conv.at[count - (CONV - 1) :].add(returned)
    grad_proj = jnp.concatenate([grad_conv, grad_gate_out], axis=1).astype(jnp.bfloat16)
    grad_in = jnp.dot(grad_proj.T, normed_in, preferred_element_type=jnp.float32)
    grad_normed = jnp.dot(grad_proj, w_in, preferred_element_type=jnp.float32) + jnp.dot(
        grad_logits, w_gates.T, precision=HIGHEST
    )
    grad_gates = jnp.dot(normed_in.astype(jnp.float32).T, grad_logits, precision=HIGHEST)
    unused_six, pull_in = jax.vjp(norm_scale, x_float, gain_one)
    grad_x, grad_gain_one = pull_in(grad_normed)
    grad_input = (grad_resid + grad_x).astype(jnp.bfloat16)
    small_local = jnp.concatenate(
        [
            grad_gain_one,
            grad_gain_two,
            grad_gain_head.reshape(-1),
            grad_taps[:CONV].reshape(-1),
            grad_gates.reshape(-1),
            grad_alog,
            grad_bias,
        ]
    )
    if side:
        half = lambda value: value.astype(jnp.bfloat16)
        mix_all = jnp.concatenate([half(grad_in), half(grad_out)], axis=0)
        ffn_all = jnp.concatenate([half(grad_ffn), half(grad_down)], axis=0)
        ffn_all = jnp.pad(ffn_all.reshape(everyone, ffn_rows, D), ((0, 0), (0, padding), (0, 0)))
        short = -small_local.size % 1024
        mix_shard, ffn_shard, small_grad, total_squares = scatter_all(
            (mix_all, ffn_all.reshape(-1, D)),
            jnp.pad(small_local, (0, short)).reshape(-1, 128),
            side,
            2,
        )
        mix_shard = mix_shard.reshape(-1)
        ffn_shard = ffn_shard[:ffn_rows].reshape(-1)
        small_grad = small_grad.reshape(-1)[: small_local.size]
        total_squares = jnp.sum(total_squares)
    else:
        small_grad = lax.psum(small_local, ("dp", "ctx"))
        ffn_shard, grad_in, grad_out = lax.optimization_barrier((ffn_shard, grad_in, grad_out))
        mix_shard = scatter_rows((grad_in, grad_out))
        small_grad, mix_shard = lax.optimization_barrier((small_grad, mix_shard))
        shard_squares = jnp.sum(mix_shard * mix_shard) + jnp.sum(ffn_shard * ffn_shard)
        total_squares = lax.psum(shard_squares, ("dp", "ctx"))
    squares = total_squares + jnp.sum(small_grad * small_grad)
    clip = jnp.minimum(1.0, MAX_NORM / (jnp.sqrt(squares) + 1e-06))
    mixer_new, mixer_first_new, mixer_second_new = adam_step(
        mixer_params, mix_shard, mixer_first, mixer_second, clip
    )
    ffn_new, ffn_first_new, ffn_second_new = adam_step(
        ffn_params, ffn_shard, ffn_first, ffn_second, clip
    )
    small_new, small_first_new, small_second_new = adam_step(
        small_params, small_grad, small_first, small_second, clip
    )
    return (
        result[None],
        grad_input[None],
        mix_shard,
        ffn_shard,
        small_grad,
        mixer_new,
        mixer_first_new,
        mixer_second_new,
        ffn_new,
        ffn_first_new,
        ffn_second_new,
        small_new,
        small_first_new,
        small_second_new,
    )


def solution(mesh):
    return jax.shard_map(
        body,
        mesh=mesh,
        in_specs=(
            P("dp", "ctx", None),
            P("dp", "ctx", None),
            P(("dp", "ctx")),
            P(("dp", "ctx")),
            P(("dp", "ctx")),
            P(("dp", "ctx")),
            P(("dp", "ctx")),
            P(("dp", "ctx")),
            P(),
            P(),
            P(),
        ),
        out_specs=(
            P("dp", "ctx", None),
            P("dp", "ctx", None),
            P(("dp", "ctx")),
            P(("dp", "ctx")),
            P(),
            P(("dp", "ctx")),
            P(("dp", "ctx")),
            P(("dp", "ctx")),
            P(("dp", "ctx")),
            P(("dp", "ctx")),
            P(("dp", "ctx")),
            P(),
            P(),
            P(),
        ),
        check_vma=False,
    )
```

```python
import functools
import math
import jax
import jax.numpy as jnp
from jax import lax
from jax.experimental import pallas as pl
from jax.experimental.pallas import tpu as pltpu
from jax.sharding import PartitionSpec as P

D = 1024
H = 2
DK = 256
DV = 512
FF = 1408
CONV = 4
GROUP = 64


EPSILON = 1e-06
ADAM_EPS = 1e-08
LEARN_RATE = 0.02
BETA_ONE = 0.9
BETA_TWO = 0.999
DECAY_RATE = 0.1
CORRECT_ONE = 1.0 - 0.9**3
CORRECT_TWO = 1.0 - 0.999**3
MAX_NORM = 1.0
HIGHEST = lax.Precision.HIGHEST


def from_behind(value, axis, steps):
    count = lax.axis_size(axis)
    initial, last = (max(0, -steps), min(count, count - steps))
    return lax.ppermute(value, axis, [(source, source + steps) for source in range(initial, last)])


def norm_scale(values, gain):
    return values * lax.rsqrt(jnp.mean(values * values, axis=-1, keepdims=True) + EPSILON) * gain


def swiglu(gate_part, up_part):
    return jax.nn.silu(gate_part) * up_part


def unpack_small(packed):
    width = 2 * H * DK + H * DV
    lengths = [D, D, DV, CONV * width, D * 2 * H, H, H]
    pieces = []
    offset = 0
    for length in lengths:
        pieces.append(packed[offset : offset + length])
        offset = offset + length
    return (
        pieces[0],
        pieces[1],
        pieces[2],
        pieces[3].reshape(CONV, width),
        pieces[4].reshape(D, 2 * H),
        pieces[5],
        pieces[6],
    )


def split_weights(mix_whole, ffn_whole):
    mix_rows = mix_whole.reshape(-1, D)
    ffn_rows = ffn_whole.reshape(-1, D)
    edge = 2 * H * DK + 2 * H * DV
    return (mix_rows[:edge], mix_rows[edge:], ffn_rows[: 2 * FF], ffn_rows[2 * FF :])


PAD = 16
HIGH = dict(precision=HIGHEST, preferred_element_type=jnp.float32)


def mm(a, b):
    return lax.dot_general(a, b, (((1,), (0,)), ((), ())), **HIGH)


def mm_nt(a, b):
    return lax.dot_general(a, b, (((1,), (1,)), ((), ())), **HIGH)


def mm_tn(a, b):
    return lax.dot_general(a, b, (((0,), (0,)), ((), ())), **HIGH)


def halves(a):
    high = a.astype(jnp.bfloat16)
    return high, (a - high.astype(jnp.float32)).astype(jnp.bfloat16)


def wire_mm(a, b, dims):
    high, low = halves(b)
    first = lax.dot_general(a, high, (dims, ((), ())), preferred_element_type=jnp.float32)
    return first + lax.dot_general(a, low, (dims, ((), ())), preferred_element_type=jnp.float32)


def iotas(size):
    shape = (size, size)
    return (
        lax.broadcasted_iota(jnp.int32, shape, 0),
        lax.broadcasted_iota(jnp.int32, shape, 1),
    )


def to_row(column, rows, cols):
    return jnp.sum(jnp.where(rows == cols, column, 0.0), axis=0, keepdims=True)


def unit_inverse(strict_part, rows, cols):
    size = strict_part.shape[0]
    inverse = jnp.where(rows == cols, 1.0, 0.0) - jnp.where(
        (rows // 2 == cols // 2), strict_part, 0.0
    )
    block = 2
    while block < size:
        joined = (rows // (2 * block) == cols // (2 * block)) & (rows // block != cols // block)
        off = jnp.where(joined, strict_part, 0.0)
        inverse = inverse - mm(mm(inverse, off), inverse)
        block = 2 * block
    return inverse


def silu_pair(x):
    gate = jax.nn.sigmoid(x)
    return x * gate, gate * (1.0 + x * (1.0 - gate))


def conv_sum(extended_ref, taps, count):
    total = None
    for tap in range(CONV):
        piece = taps[tap : tap + 1] * extended_ref[pl.ds(8 - (CONV - 1) + tap, count), :]
        total = piece if total is None else total + piece
    return total


def unit_rows(part):
    return lax.rsqrt(jnp.sum(part * part, axis=-1, keepdims=True) + EPSILON)


def decay_terms(decay_column, rows, cols):
    lower = rows >= cols
    size = rows.shape[0]
    spread_in = jnp.broadcast_to(decay_column, (size, 128))
    cumulative = mm(jnp.where(lower, 1.0, 0.0), spread_in)[:, :1]
    across = to_row(cumulative, rows, cols)
    matrix = jnp.where(lower, jnp.exp(jnp.where(lower, cumulative - across, 0.0)), 0.0)
    last = cumulative[size - 1 : size]
    return matrix, jnp.exp(cumulative), jnp.exp(last - cumulative), jnp.exp(last)


def forward_parts(
    projected_ref, border_ref, taps_ref, beta_ref, decay_ref,
    wire_ref, query_ref, keys_ref, values_ref, inverse_ref, extended_ref,
):
    count = projected_ref.shape[0]
    width = taps_ref.shape[1]
    extended_ref[0:8, :] = border_ref[...]
    extended_ref[pl.ds(8, count), :] = projected_ref[:, :width]
    summed = conv_sum(extended_ref, taps_ref[...], count)
    activated = summed * jax.nn.sigmoid(summed)
    rows, cols = iotas(count)
    for head in range(H):
        query_part = activated[:, head * DK : (head + 1) * DK]
        key_part = activated[:, (H + head) * DK : (H + head + 1) * DK]
        start = 2 * H * DK + head * DV
        values = activated[:, start : start + DV]
        query = query_part * unit_rows(query_part) * DK ** (-0.5)
        keys = key_part * unit_rows(key_part)
        beta = beta_ref[:, head : head + 1]
        matrix, grown, to_end, whole = decay_terms(decay_ref[:, head : head + 1], rows, cols)
        system = jnp.where(rows > cols, beta * mm_nt(keys, keys) * matrix, 0.0)
        inverse = unit_inverse(system, rows, cols)
        key_mix = mm(inverse, keys * (beta * grown))
        value_mix = mm(inverse, values * beta)
        base = head * (2 * DK + DV)
        wire_ref[0:count, base : base + DK] = (keys * to_end).astype(jnp.bfloat16)
        wire_ref[0:count, base + DK : base + 2 * DK] = key_mix.astype(jnp.bfloat16)
        wire_ref[0:count, base + 2 * DK : base + 2 * DK + DV] = value_mix.astype(jnp.bfloat16)
        high, low = halves(jnp.broadcast_to(whole, (PAD, 2 * DK + DV)))
        first = lax.broadcasted_iota(jnp.int32, (PAD, 2 * DK + DV), 0) < 8
        tail = jnp.where(first, high.astype(jnp.float32), low.astype(jnp.float32))
        wire_ref[pl.ds(count, PAD), base : base + 2 * DK + DV] = tail.astype(jnp.bfloat16)
        query_ref[:, head * DK : (head + 1) * DK] = query
        keys_ref[:, head * DK : (head + 1) * DK] = keys
        values_ref[:, head * DV : (head + 1) * DV] = values
        inverse_ref[head] = inverse


def wire_parts(wire_ref, index, head, count):
    base = head * (2 * DK + DV)
    to_end = wire_ref[index, 0:count, base : base + DK]
    key_mix = wire_ref[index, 0:count, base + DK : base + 2 * DK]
    value_mix = wire_ref[index, 0:count, base + 2 * DK : base + 2 * DK + DV]
    tail = wire_ref[index, pl.ds(count, PAD), base : base + 128].astype(jnp.float32)
    whole = tail[0:1, 0:1] + tail[8:9, 0:1]
    return to_end, key_mix, value_mix, whole


def own_mix(inverse, keys, values, beta, grown):
    return mm(inverse, keys * (beta * grown)), mm(inverse, values * beta)


def forward_chain(
    place_ref, wire_ref, query_ref, keys_ref, values_ref, inverse_ref, beta_ref, decay_ref,
    gate_ref, gain_ref, head_out_ref, mixed_ref, state_ref, pseudo_ref,
):
    count = query_ref.shape[0]
    state_ref[...] = jnp.zeros_like(state_ref)

    def lap(index, carry):
        for head in range(H):
            to_end, key_mix, value_mix, whole = wire_parts(wire_ref, index, head, count)
            state = state_ref[head]
            pseudo = value_mix.astype(jnp.float32) - wire_mm(key_mix, state, ((1,), (0,)))
            state_ref[head] = whole * state + wire_mm(to_end, pseudo, ((0,), (0,)))
        return carry

    lax.fori_loop(0, place_ref[0], lap, 0)
    rows, cols = iotas(count)
    for head in range(H):
        query = query_ref[:, head * DK : (head + 1) * DK]
        keys = keys_ref[:, head * DK : (head + 1) * DK]
        span = slice(head * DV, (head + 1) * DV)
        beta = beta_ref[:, head : head + 1]
        matrix, grown, to_end, whole = decay_terms(decay_ref[:, head : head + 1], rows, cols)
        key_mix, value_mix = own_mix(inverse_ref[head], keys, values_ref[:, span], beta, grown)
        state = state_ref[head]
        pseudo = value_mix - mm(key_mix, state)
        mixed = mm(query * grown, state) + mm(mm_nt(query, keys) * matrix, pseudo)
        scale = lax.rsqrt(jnp.mean(mixed * mixed, axis=-1, keepdims=True) + EPSILON)
        gated, unused = silu_pair(gate_ref(span) if callable(gate_ref) else gate_ref[:, span])
        head_out_ref[:, span] = (mixed * scale * gain_ref[...] * gated).astype(jnp.bfloat16)
        mixed_ref[:, span] = mixed
        pseudo_ref[:, span] = pseudo


def backward_local(
    grad_ref, mixed_ref, query_ref, keys_ref, values_ref, inverse_ref, beta_ref, decay_ref,
    gate_ref, gain_ref, local_ref, grad_mixed_ref, grad_gate_ref, grad_gain_ref,
):
    count = query_ref.shape[0]
    rows, cols = iotas(count)
    gain_total = jnp.zeros((1, DV), jnp.float32)
    for head in range(H):
        query = query_ref[:, head * DK : (head + 1) * DK]
        keys = keys_ref[:, head * DK : (head + 1) * DK]
        span = slice(head * DV, (head + 1) * DV)
        mixed = mixed_ref[:, span]
        grad = grad_ref[:, span]
        scale = lax.rsqrt(jnp.mean(mixed * mixed, axis=-1, keepdims=True) + EPSILON)
        plain = mixed * scale
        gated, slope = silu_pair(gate_ref(span) if callable(gate_ref) else gate_ref[:, span])
        grad_gate_ref[:, span] = grad * plain * gain_ref[...] * slope
        grad_normed = grad * gated
        gain_total = gain_total + jnp.sum(grad_normed * plain, axis=0, keepdims=True)
        pulled = grad_normed * gain_ref[...]
        grad_mixed = scale * (pulled - plain * jnp.mean(pulled * plain, axis=-1, keepdims=True))
        grad_mixed_ref[:, span] = grad_mixed
        beta = beta_ref[:, head : head + 1]
        matrix, grown, to_end, whole = decay_terms(decay_ref[:, head : head + 1], rows, cols)
        key_mix = mm(inverse_ref[head], keys * (beta * grown))
        grad_pseudo = mm_tn(mm_nt(query, keys) * matrix, grad_mixed)
        local = mm_tn(query * grown, grad_mixed) - mm_tn(key_mix, grad_pseudo)
        local_ref[head * DK : (head + 1) * DK, :] = local.astype(jnp.bfloat16)
    grad_gain_ref[...] = gain_total


def backward_chain(
    place_ref, wire_ref, local_ref, query_ref, keys_ref, values_ref, inverse_ref, beta_ref,
    decay_ref, state_ref, pseudo_ref, grad_mixed_ref, projected_ref, border_ref, taps_ref,
    grad_conv_ref, grad_border_ref, grad_taps_ref, grad_beta_ref, grad_decay_ref,
    after_ref, extended_ref, padded_ref,
):
    count = query_ref.shape[0]
    width = taps_ref.shape[1]
    devices = wire_ref.shape[0]
    after_ref[...] = jnp.zeros_like(after_ref)

    def lap(step, carry):
        index = devices - 1 - step
        for head in range(H):
            to_end, key_mix, value_mix, whole = wire_parts(wire_ref, index, head, count)
            after = after_ref[head]
            inner = wire_mm(to_end, after, ((1,), (0,)))
            local = local_ref[index, head * DK : (head + 1) * DK, :].astype(jnp.float32)
            after_ref[head] = whole * after - wire_mm(key_mix, inner, ((0,), (0,))) + local
        return carry

    lax.fori_loop(0, devices - 1 - place_ref[0], lap, 0)
    extended_ref[0:8, :] = border_ref[...]
    extended_ref[pl.ds(8, count), :] = projected_ref[:, :width]
    taps = taps_ref[...]
    summed = conv_sum(extended_ref, taps, count)
    activated, slope = silu_pair(summed)
    padded_ref[0:8, :] = jnp.zeros((8, width), jnp.float32)
    padded_ref[pl.ds(8 + count, 8), :] = jnp.zeros((8, width), jnp.float32)
    rows, cols = iotas(count)
    lower = rows >= cols
    strict = rows > cols
    lanes = lax.broadcasted_iota(jnp.int32, (count, 128), 1)
    beta_out = jnp.zeros((count, 128), jnp.float32)
    cumulative_out = jnp.zeros((count, 128), jnp.float32)
    row_column = lax.broadcasted_iota(jnp.int32, (count, 1), 0)
    for head in range(H):
        query = query_ref[:, head * DK : (head + 1) * DK]
        keys = keys_ref[:, head * DK : (head + 1) * DK]
        span = slice(head * DV, (head + 1) * DV)
        values = values_ref[:, span]
        beta = beta_ref[:, head : head + 1]
        matrix, grown, to_end, whole = decay_terms(decay_ref[:, head : head + 1], rows, cols)
        inverse = inverse_ref[head]
        state = state_ref[head]
        after = after_ref[head]
        pseudo = pseudo_ref[:, span]
        grad_mixed = grad_mixed_ref[:, span]
        keys_grown = keys * (beta * grown)
        key_mix = mm(inverse, keys_grown)
        value_mix = mm(inverse, values * beta)
        gram = mm_nt(keys, keys)
        system = jnp.where(strict, beta * gram * matrix, 0.0)
        scores = mm_nt(query, keys) * matrix
        keys_end = keys * to_end
        query_grown = query * grown
        grad_query_grown = mm_nt(grad_mixed, state)
        grad_scores = jnp.where(lower, mm_nt(grad_mixed, pseudo), 0.0)
        grad_pseudo = mm_tn(scores, grad_mixed) + mm(keys_end, after)
        grad_keys_end = mm_nt(pseudo, after)
        grad_whole = jnp.sum(jnp.sum(after * state, axis=1, keepdims=True), axis=0, keepdims=True)
        grad_value_in = mm_tn(inverse, grad_pseudo)
        grad_key_in = mm_tn(inverse, -mm_nt(grad_pseudo, state))
        grad_system = -jnp.where(
            strict, mm_nt(grad_value_in, value_mix) + mm_nt(grad_key_in, key_mix), 0.0
        )
        grad_raw = grad_scores * matrix
        grad_query = mm(grad_raw, keys) + grad_query_grown * grown
        grad_keys = mm_tn(grad_raw, query)
        weighted = grad_system * matrix
        grad_beta = jnp.sum(weighted * gram, axis=1, keepdims=True)
        grad_gram = weighted * beta
        grad_keys = grad_keys + mm(grad_gram, keys) + mm_tn(grad_gram, keys)
        spread = grad_scores * scores + grad_system * system
        grad_cumulative = jnp.sum(spread, axis=1, keepdims=True)
        across = jnp.sum(spread, axis=0, keepdims=True)
        grad_cumulative = grad_cumulative - jnp.sum(
            jnp.where(rows == cols, across, 0.0), axis=1, keepdims=True
        )
        grad_keys = grad_keys + grad_key_in * (beta * grown)
        through = jnp.sum(grad_key_in * keys, axis=1, keepdims=True) * grown
        grad_beta = grad_beta + through + jnp.sum(grad_value_in * values, axis=1, keepdims=True)
        grad_cumulative = grad_cumulative + through * beta
        grad_values = grad_value_in * beta
        grad_cumulative = grad_cumulative + jnp.sum(
            grad_query_grown * query_grown, axis=1, keepdims=True
        )
        grad_keys = grad_keys + grad_keys_end * to_end
        ending = jnp.sum(grad_keys_end * keys_end, axis=1, keepdims=True)
        final = jnp.sum(ending, axis=0, keepdims=True) + whole * grad_whole
        grad_cumulative = grad_cumulative - ending + jnp.where(row_column == count - 1, final, 0.0)
        beta_out = jnp.where(lanes == head, grad_beta, beta_out)
        cumulative_out = jnp.where(lanes == head, grad_cumulative, cumulative_out)
        key_part = activated[:, (H + head) * DK : (H + head + 1) * DK]
        key_scale = unit_rows(key_part)
        query_part = activated[:, head * DK : (head + 1) * DK]
        query_scale = unit_rows(query_part)
        factor = DK ** (-0.5)
        grad_query_part = (factor * query_scale) * (
            grad_query
            - query_part
            * (query_scale * query_scale)
            * jnp.sum(grad_query * query_part, axis=-1, keepdims=True)
        )
        grad_key_part = key_scale * (
            grad_keys
            - key_part
            * (key_scale * key_scale)
            * jnp.sum(grad_keys * key_part, axis=-1, keepdims=True)
        )
        spots = (head * DK, (H + head) * DK, 2 * H * DK + head * DV)
        for spot, grad in zip(spots, (grad_query_part, grad_key_part, grad_values)):
            size = grad.shape[1]
            padded_ref[pl.ds(8, count), spot : spot + size] = grad * slope[:, spot : spot + size]
    grad_beta_ref[...] = beta_out
    grad_decay_ref[...] = mm_tn(jnp.where(lower, 1.0, 0.0), cumulative_out)
    conv_total = jnp.zeros((count, width), jnp.float32)
    border_total = jnp.zeros((8, width), jnp.float32)
    summed_grad = padded_ref[pl.ds(8, count), :]
    tap_rows = lax.broadcasted_iota(jnp.int32, (8, width), 0)
    taps_total = jnp.zeros((8, width), jnp.float32)
    for tap in range(CONV):
        shift = CONV - 1 - tap
        conv_total = conv_total + taps[tap : tap + 1] * padded_ref[pl.ds(8 + shift, count), :]
        border_total = border_total + taps[tap : tap + 1] * padded_ref[pl.ds(shift, 8), :]
        piece = jnp.sum(
            summed_grad * extended_ref[pl.ds(8 - (CONV - 1) + tap, count), :],
            axis=0,
            keepdims=True,
        )
        taps_total = jnp.where(tap_rows == tap, piece, taps_total)
    grad_conv_ref[...] = conv_total
    grad_border_ref[...] = border_total
    grad_taps_ref[...] = taps_total


def fused(body, outputs, scratch=(), scalars=0, cost=(0, 0), label=None):
    def call(*args):
        vmem = pl.BlockSpec(memory_space=pltpu.VMEM)
        smem = pl.BlockSpec(memory_space=pltpu.SMEM)
        return pl.pallas_call(
            body,
            out_shape=outputs,
            in_specs=[smem] * scalars + [vmem] * (len(args) - scalars),
            out_specs=[vmem] * len(outputs),
            scratch_shapes=list(scratch),
            compiler_params=pltpu.CompilerParams(vmem_limit_bytes=60 * 2**20),
            cost_estimate=pl.CostEstimate(
                flops=cost[0], bytes_accessed=cost[1], transcendentals=0
            ),
            name=label,
        )(*args)

    return call


def gates(gate_logits, a_log, dt_bias):
    beta = jax.nn.sigmoid(gate_logits[:, :H])
    decay = -jnp.exp(a_log) * jax.nn.softplus(gate_logits[:, H:] + dt_bias)
    return beta, decay


def scatter_rows(pieces):
    outer, inner = lax.axis_size("dp"), lax.axis_size("ctx")
    whole = jnp.concatenate([piece.astype(jnp.bfloat16) for piece in pieces], axis=0)
    lane = math.gcd(whole.size // (outer * inner), D)
    blocks = whole.reshape(outer, inner, -1, lane)
    part = lax.psum_scatter(blocks, "ctx", scatter_dimension=1, tiled=False)
    own = lax.psum_scatter(part, "dp", scatter_dimension=0, tiled=False)
    return own.astype(jnp.float32).reshape(-1)


MESH = pl.DeviceIdType.MESH


class Place:
    def __init__(self, side):
        self.deep = lax.axis_size("dp")
        self.side = side
        self.ctx = lax.axis_size("ctx")
        self.z = lax.axis_index("dp")
        spot = lax.axis_index("ctx")
        self.c = lax.rem(spot, 2)
        chip = lax.div(spot, 2)
        self.x = lax.rem(chip, side)
        self.y = lax.div(chip, side)
        self.other_core = self.device(self.z, self.y, self.x, 1 - self.c)
        self.other_x = self.device(self.z, self.y, 1 - self.x, self.c)
        self.other_y = self.device(self.z, 1 - self.y, self.x, self.c)
        self.next_z = self.device(self.along(1), self.y, self.x, self.c)

    def along(self, step):
        return lax.rem(self.z + step + self.deep, self.deep)

    def device(self, z, y, x, c):
        return (z, (y * self.side + x) * 2 + c)

    def block(self, z, y, x, c):
        return z * self.ctx + (y * self.side + x) * 2 + c

    def enter(self, all_z=False):
        barrier = pltpu.get_barrier_semaphore()
        steps = range(1, self.deep) if all_z else (-1,)
        friends = [self.other_core, self.other_x, self.other_y]
        friends += [self.device(self.along(step), self.y, self.x, self.c) for step in steps]
        for friend in friends:
            pl.semaphore_signal(barrier, inc=1, device_id=friend, device_id_type=MESH)
        pl.semaphore_wait(barrier, len(friends))


class Copies:
    def __init__(self, send_sems, recv_sems, local_sems=None):
        self.send_sems, self.recv_sems, self.local_sems = send_sems, recv_sems, local_sems
        self.sent, self.locals = [], 0

    def push(self, source, target, device):
        index = len(self.sent)
        copy = pltpu.make_async_remote_copy(
            src_ref=source,
            dst_ref=target,
            send_sem=self.send_sems.at[index],
            recv_sem=self.recv_sems.at[index],
            device_id=device,
            device_id_type=MESH,
        )
        copy.start()
        self.sent.append(copy)
        return copy

    def local(self, source, target):
        copy = pltpu.make_async_copy(source, target, self.local_sems.at[self.locals])
        copy.start()
        self.locals += 1
        return copy

    def finish(self):
        for copy in self.sent:
            copy.wait_send()


def upper(rows):
    return rows // 2 // 16 * 16


def gather_steps(place, copies, shard_ref, out_ref, plane=False):
    rows, deep = shard_ref.shape[0], 1 if plane else place.deep
    top = upper(rows)
    spans = {None: (0, rows), 0: (0, top), 1: (top, rows - top)}
    ring, near, far, core = [], {}, {}, []

    def cut(ref, start, part):
        offset, size = spans[part]
        return ref.at[pl.ds(pl.multiple_of(start + offset, 16), size), :]

    def start_of(rel, dy, dx):
        y = 1 - place.y if dy else place.y
        x = 1 - place.x if dx else place.x
        z = 0 if plane else place.along(-rel)
        return place.block(z, y, x, place.c) * rows

    def forward(rel, dy, dx, part, device):
        start = start_of(rel, dy, dx)
        own = rel == 0 and not dy and not dx
        source = cut(shard_ref, 0, part) if own else cut(out_ref, start, part)
        return copies.push(source, cut(out_ref, start, part), device)

    def spread(rel):
        if rel < deep - 1:
            ring.append(forward(rel, 0, 0, None, place.next_z))
        near[rel, "x0"] = forward(rel, 0, 0, 0, place.other_x)
        near[rel, "y1"] = forward(rel, 0, 0, 1, place.other_y)
        near[rel, "y0"] = forward(rel, 0, 0, 0, place.other_y)
        near[rel, "x1"] = forward(rel, 0, 0, 1, place.other_x)
        core.append(forward(rel, 0, 0, None, place.other_core))

    def second(rel):
        near[rel, "x0"].wait_recv()
        far[rel, 0] = forward(rel, 0, 1, 0, place.other_y)
        near[rel, "y1"].wait_recv()
        far[rel, 1] = forward(rel, 1, 0, 1, place.other_x)
        core.append(forward(rel, 0, 1, 0, place.other_core))
        core.append(forward(rel, 1, 0, 1, place.other_core))

    def third(rel):
        near[rel, "y0"].wait_recv()
        core.append(forward(rel, 1, 0, 0, place.other_core))
        near[rel, "x1"].wait_recv()
        core.append(forward(rel, 0, 1, 1, place.other_core))

    def fourth(rel):
        for part in (0, 1):
            far[rel, part].wait_recv()
            core.append(forward(rel, 1, 1, part, place.other_core))

    own_copy = []

    def first():
        own_copy.append(copies.local(shard_ref, cut(out_ref, start_of(0, 0, 0), None)))
        spread(0)

    def later(rel):
        ring[rel - 1].wait_recv()
        spread(rel)

    def last():
        for copy in core:
            copy.wait_recv()
        own_copy[0].wait()

    steps = [first]
    for rel in range(1, deep):
        steps.append(lambda rel=rel: later(rel))
        steps.append(lambda rel=rel: second(rel - 1))
        steps.append(lambda rel=rel: third(rel - 1))
    steps.append(lambda: second(deep - 1))
    steps.append(lambda: third(deep - 1))
    for rel in range(deep):
        steps.append(lambda rel=rel: fourth(rel))
    steps.append(last)
    return steps


def wide(value):
    return value.astype(jnp.float32)


class Scatter:
    def __init__(self, place, copies, grad_ref, held, from_core, first_x, first_y, last_x, last_y, from_z):
        self.place, self.copies, self.grad = place, copies, grad_ref
        self.held, self.from_core, self.from_z = held, from_core, from_z
        self.first = {0: first_y, 1: first_x}
        self.last = {0: last_x, 1: last_y}
        self.rows = held.shape[1]
        self.top = upper(self.rows)
        self.loads, self.cores, self.near, self.far, self.ring = {}, {}, {}, {}, {}

    @staticmethod
    def scratch(deep, rows):
        top = upper(rows)
        low = rows - top
        return [
            pltpu.VMEM((4 * deep, rows, D), jnp.bfloat16),
            pltpu.VMEM((4 * deep, rows, D), jnp.bfloat16),
            pltpu.VMEM((2 * deep, low, D), jnp.bfloat16),
            pltpu.VMEM((2 * deep, top, D), jnp.bfloat16),
            pltpu.VMEM((deep, top, D), jnp.bfloat16),
            pltpu.VMEM((deep, low, D), jnp.bfloat16),
            pltpu.VMEM((deep - 1, rows, D), jnp.bfloat16),
        ]

    @staticmethod
    def copies_of(deep):
        return 4 * deep + 4 * deep + 2 * deep + deep - 1

    def slot(self, rel, dy, dx):
        return (rel - 1) * 4 + dy * 2 + dx

    def span(self, part):
        return pl.ds(0, self.top) if part == 0 else pl.ds(self.top, self.rows - self.top)

    def load(self):
        place = self.place
        for rel in range(1, place.deep + 1):
            for dy, dx in ((1, 1), (1, 0), (0, 1), (0, 0)):
                y = 1 - place.y if dy else place.y
                x = 1 - place.x if dx else place.x
                slot = self.slot(rel, dy, dx)

                def rows_of(core):
                    start = place.block(place.along(-rel), y, x, core) * self.rows
                    return self.grad.at[pl.ds(pl.multiple_of(start, 16), self.rows), :]

                self.cores[slot] = self.copies.push(
                    rows_of(1 - place.c), self.from_core.at[slot], place.other_core
                )
                self.loads[slot] = self.copies.local(rows_of(place.c), self.held.at[slot])

    def stage_one(self, rel):
        place = self.place
        for dy, dx in ((1, 1), (1, 0), (0, 1), (0, 0)):
            slot = self.slot(rel, dy, dx)
            self.loads[slot].wait()
            self.cores[slot].wait_recv()
            self.held[slot] = (wide(self.held[slot]) + wide(self.from_core[slot])).astype(jnp.bfloat16)
            if dy:
                self.near[rel, 0, dx] = self.copies.push(
                    self.held.at[slot, self.span(0), :],
                    self.first[0].at[(rel - 1) * 2 + dx],
                    place.other_y,
                )
            if dx:
                self.near[rel, 1, dy] = self.copies.push(
                    self.held.at[slot, self.span(1), :],
                    self.first[1].at[(rel - 1) * 2 + dy],
                    place.other_x,
                )

    def add(self, slot, part, piece):
        self.held[slot, self.span(part), :] = (
            wide(self.held[slot, self.span(part), :]) + wide(piece)
        ).astype(jnp.bfloat16)

    def stage_two(self, rel):
        place = self.place
        for part in (0, 1):
            for away in (1, 0):
                self.near[rel, part, away].wait_recv()
                slot = self.slot(rel, away, 0) if part else self.slot(rel, 0, away)
                self.add(slot, part, self.first[part][(rel - 1) * 2 + away])
                if away:
                    self.far[rel, part] = self.copies.push(
                        self.held.at[slot, self.span(part), :],
                        self.last[part].at[rel - 1],
                        place.other_y if part else place.other_x,
                    )

    def stage_three(self, rel, total_ref=None):
        slot = self.slot(rel, 0, 0)
        for part in (0, 1):
            self.far[rel, part].wait_recv()
            self.add(slot, part, self.last[part][rel - 1])
        if rel >= 2:
            self.ring[rel - 1].wait_recv()
            total = wide(self.held[slot]) + wide(self.from_z[rel - 2])
            if rel == self.place.deep:
                total_ref[...] = total
                return
            self.held[slot] = total.astype(jnp.bfloat16)
        self.ring[rel] = self.copies.push(
            self.held.at[slot], self.from_z.at[rel - 1], self.place.next_z
        )

    def steps(self, total_ref):
        deep = self.place.deep
        out = [self.load]
        for turn in range(1, deep + 3):
            if turn <= deep:
                out.append(lambda rel=turn: self.stage_one(rel))
            if 1 <= turn - 1 <= deep:
                out.append(lambda rel=turn - 1: self.stage_two(rel))
            if 1 <= turn - 2 <= deep:
                out.append(lambda rel=turn - 2: self.stage_three(rel, total_ref))
        return out


class Everywhere:
    def __init__(self, place, copies, total, slots, stack):
        self.place, self.copies = place, copies
        self.total, self.slots, self.stack = total, slots, stack
        self.turns = (place.other_core, place.other_x, place.other_y)
        self.pending = []

    @staticmethod
    def scratch(deep, rows):
        return [pltpu.VMEM((3, rows, 128), jnp.float32), pltpu.VMEM((deep, rows, 128), jnp.float32),
                pltpu.VMEM((4, rows, 128), jnp.float32)]

    def send(self, turn):
        self.pending = [
            self.copies.push(self.total.at[turn], self.slots.at[turn], self.turns[turn])
        ]

    def take(self, turn):
        self.pending[0].wait_recv()
        self.total[turn + 1] = self.total[turn] + self.slots[turn]

    def send_z(self):
        place = self.place
        self.pending = [
            self.copies.push(
                self.total.at[3],
                self.stack.at[place.z],
                place.device(place.along(step), place.y, place.x, place.c),
            )
            for step in range(1, place.deep)
        ]
        self.stack[place.z] = self.total[3]

    def take_z(self):
        for copy in self.pending:
            copy.wait_recv()
        result = self.stack[0]
        for index in range(1, self.place.deep):
            result = result + self.stack[index]
        return result

    def run(self):
        for turn in range(3):
            self.send(turn)
            self.take(turn)
        self.send_z()
        return self.take_z()


def scatter_kernel(side, counts, *refs):
    refs = list(refs)
    take = lambda number: [refs.pop(0) for unused in range(number)]
    grads = take(counts)
    small_ref, other_ref = take(2)
    totals = take(counts)
    small_out, squares_out = take(2)
    scratch = [take(7) for unused in range(counts)]
    small_scratch, square_scratch = take(3), take(3)
    send_sems, recv_sems, local_sems = refs
    place = Place(side)
    copies = Copies(send_sems, recv_sems, local_sems)
    place.enter(all_z=True)
    scatters = [Scatter(place, copies, grad, *own) for grad, own in zip(grads, scratch)]
    small = Everywhere(place, copies, small_scratch[2], *small_scratch[:2])
    small.total[0] = small_ref[...]
    lists = [scatter.steps(total) for scatter, total in zip(scatters, totals)]
    extra = [lambda: small.send(0)]
    for turn in range(3):
        extra.append(lambda turn=turn: small.take(turn))
        extra.append(lambda turn=turn: small.send(turn + 1) if turn < 2 else small.send_z())
    for index, group in enumerate(zip(*lists)):
        for step in group:
            step()
        if index < len(extra):
            extra[index]()
    for step in extra[len(lists[0]) :]:
        step()
    small_total = small.take_z()
    small_out[...] = small_total
    squares = jnp.zeros((8, 128), jnp.float32)
    for total in totals + [other_ref]:
        value = total[...]
        line = jnp.sum(value * value, axis=0, keepdims=True)
        for start in range(0, D, 128):
            squares = squares + line[:, start : start + 128] * 0.125
    square = Everywhere(place, copies, square_scratch[2], *square_scratch[:2])
    square.total[0] = squares
    squares_out[...] = square.run()
    copies.finish()


def scatter_all(grads, small, other, side, tag):
    deep, ctx = lax.axis_size("dp"), lax.axis_size("ctx")
    rows = [grad.shape[0] // (deep * ctx) for grad in grads]
    number = len(grads) * Scatter.copies_of(deep) + 2 * (3 + deep - 1)
    vmem = pl.BlockSpec(memory_space=pltpu.VMEM)
    scratch = []
    for size in rows:
        scratch += Scatter.scratch(deep, size)
    scratch += Everywhere.scratch(deep, small.shape[0]) + Everywhere.scratch(deep, 8)
    return pl.pallas_call(
        functools.partial(scatter_kernel, side, len(grads)),
        out_shape=[jax.ShapeDtypeStruct((size, D), jnp.float32) for size in rows]
        + [jax.ShapeDtypeStruct(small.shape, jnp.float32), jax.ShapeDtypeStruct((8, 128), jnp.float32)],
        in_specs=[pl.BlockSpec(memory_space=pl.ANY)] * len(grads) + [vmem] * 2,
        out_specs=[vmem] * (len(grads) + 2),
        scratch_shapes=scratch
        + [
            pltpu.SemaphoreType.DMA((number,)),
            pltpu.SemaphoreType.DMA((number,)),
            pltpu.SemaphoreType.DMA((4 * deep * len(grads),)),
        ],
        compiler_params=pltpu.CompilerParams(
            collective_id=tag, has_side_effects=True, vmem_limit_bytes=60 * 2**20
        ),
        cost_estimate=pl.CostEstimate(flops=0, bytes_accessed=10**8, transcendentals=0),
        name="scatter_gradients",
    )(*grads, small, other)


def gather_copies(deep):
    return (deep - 1) + 4 * deep + 2 * deep + deep + 2 * deep * 3


def front_parts(ext_ref, taps_ref, beta_ref, decay_ref, wire_ref, query_ref, keys_ref, values_ref, inverse_ref):
    count = query_ref.shape[0]
    width = taps_ref.shape[1]
    summed = ext_sum(ext_ref, taps_ref[...], count, 0, width)
    activated = summed * jax.nn.sigmoid(summed)
    rows, cols = iotas(count)
    for head in range(H):
        query_part = activated[:, head * DK : (head + 1) * DK]
        key_part = activated[:, (H + head) * DK : (H + head + 1) * DK]
        start = 2 * H * DK + head * DV
        values = activated[:, start : start + DV]
        query = query_part * unit_rows(query_part) * DK ** (-0.5)
        keys = key_part * unit_rows(key_part)
        beta = beta_ref[:, head : head + 1]
        matrix, grown, to_end, whole = decay_terms(decay_ref[:, head : head + 1], rows, cols)
        system = jnp.where(rows > cols, beta * mm_nt(keys, keys) * matrix, 0.0)
        inverse = unit_inverse(system, rows, cols)
        key_mix = mm(inverse, keys * (beta * grown))
        value_mix = mm(inverse, values * beta)
        base = head * (2 * DK + DV)
        wire_ref[0:count, base : base + DK] = (keys * to_end).astype(jnp.bfloat16)
        wire_ref[0:count, base + DK : base + 2 * DK] = key_mix.astype(jnp.bfloat16)
        wire_ref[0:count, base + 2 * DK : base + 2 * DK + DV] = value_mix.astype(jnp.bfloat16)
        high, low = halves(jnp.broadcast_to(whole, (PAD, 2 * DK + DV)))
        first = lax.broadcasted_iota(jnp.int32, (PAD, 2 * DK + DV), 0) < 8
        tail = jnp.where(first, high.astype(jnp.float32), low.astype(jnp.float32))
        wire_ref[pl.ds(count, PAD), base : base + 2 * DK + DV] = tail.astype(jnp.bfloat16)
        query_ref[:, head * DK : (head + 1) * DK] = query
        keys_ref[:, head * DK : (head + 1) * DK] = keys
        values_ref[:, head * DV : (head + 1) * DV] = values
        inverse_ref[head] = inverse
        yield


def ext_sum(ext_ref, taps, count, start, size):
    total = None
    for tap in range(CONV):
        piece = (
            taps[tap : tap + 1, start : start + size]
            * ext_ref[pl.ds(8 - (CONV - 1) + tap, count), start : start + size]
        )
        total = piece if total is None else total + piece
    return total


def front_kernel(
    side, mix_shard, ffn_shard, normed_ref, taps_ref, beta_ref, decay_ref,
    mix_out, ffn_out, wires_out, ext_ref, query_ref, keys_ref, values_ref, inverse_ref,
    weight_ref, wire_ref, send_sems, recv_sems, local_sems,
):
    place = Place(side)
    copies = Copies(send_sems, recv_sems, local_sems)
    place.enter()
    mix = gather_steps(place, copies, mix_shard, mix_out)
    ffn = gather_steps(place, copies, ffn_shard, ffn_out)
    early = 3 * (place.deep - 1) + 2
    for step in mix[:early]:
        step()
    ffn.pop(0)()
    for step in mix[early:]:
        step()
    depth = weight_ref.shape[0]
    chunk = DV
    loads = [
        copies.local(mix_out.at[pl.ds(start, chunk), :], weight_ref.at[pl.ds(start, chunk), :])
        for start in range(0, depth, chunk)
    ]
    for index, load in enumerate(loads):
        load.wait()
        span = pl.ds(index * chunk, chunk)
        piece = lax.dot_general(
            normed_ref[...], weight_ref[span, :], (((1,), (1,)), ((), ())),
            preferred_element_type=jnp.float32,
        )
        ext_ref[:, index * chunk : (index + 1) * chunk] = piece[8:]
        if index % 2 == 1:
            ffn.pop(0)()
    parts = front_parts(
        ext_ref, taps_ref, beta_ref, decay_ref, wire_ref, query_ref, keys_ref, values_ref, inverse_ref
    )
    for unused in parts:
        for again in range(3):
            ffn.pop(0)()
    wires = gather_steps(place, copies, wire_ref, wires_out, plane=True)
    wires.pop(0)()
    ffn.pop(0)()
    while wires[1:]:
        wires.pop(0)()
        if len(ffn) > 1:
            ffn.pop(0)()
    for step in ffn + wires:
        step()
    copies.finish()


def front(mix_shard, ffn_shard, normed, taps, beta, decay, side, tag):
    f32 = jnp.float32
    deep, ctx = lax.axis_size("dp"), lax.axis_size("ctx")
    count = beta.shape[0]
    everyone = deep * ctx
    number = 2 * gather_copies(deep) + gather_copies(1)
    anywhere = pl.BlockSpec(memory_space=pl.ANY)
    vmem = pl.BlockSpec(memory_space=pltpu.VMEM)
    depth = 2 * H * DK + 2 * H * DV
    return pl.pallas_call(
        functools.partial(front_kernel, side),
        out_shape=[
            jax.ShapeDtypeStruct((everyone * mix_shard.shape[0], D), jnp.bfloat16),
            jax.ShapeDtypeStruct((everyone * ffn_shard.shape[0], D), jnp.bfloat16),
            jax.ShapeDtypeStruct((ctx * (count + PAD), H * (2 * DK + DV)), jnp.bfloat16),
            jax.ShapeDtypeStruct((count + 8, depth), f32),
            jax.ShapeDtypeStruct((count, H * DK), f32),
            jax.ShapeDtypeStruct((count, H * DK), f32),
            jax.ShapeDtypeStruct((count, H * DV), f32),
            jax.ShapeDtypeStruct((H, count, count), f32),
        ],
        in_specs=[anywhere] * 2 + [vmem] * 4,
        out_specs=[anywhere] * 3 + [vmem] * 5,
        scratch_shapes=[
            pltpu.VMEM((depth, D), jnp.bfloat16),
            pltpu.VMEM((count + PAD, H * (2 * DK + DV)), jnp.bfloat16),
            pltpu.SemaphoreType.DMA((number,)),
            pltpu.SemaphoreType.DMA((number,)),
            pltpu.SemaphoreType.DMA((3 + depth // DV,)),
        ],
        compiler_params=pltpu.CompilerParams(
            collective_id=tag, has_side_effects=True, vmem_limit_bytes=60 * 2**20
        ),
        cost_estimate=pl.CostEstimate(flops=0, bytes_accessed=10**8, transcendentals=0),
        name="front",
    )(mix_shard, ffn_shard, normed, taps, beta, decay)


def dot_nn(a, b):
    return lax.dot_general(a, b, (((1,), (0,)), ((), ())), preferred_element_type=jnp.float32)


def dot_nt(a, b):
    return lax.dot_general(a, b, (((1,), (1,)), ((), ())), preferred_element_type=jnp.float32)


def dot_tn(a, b):
    return lax.dot_general(a, b, (((0,), (0,)), ((), ())), preferred_element_type=jnp.float32)


def chunk_of(rows):
    return max(size for size in range(16, 577, 16) if rows % size == 0)


def by_chunks(rows, body):
    size = chunk_of(rows)

    def turn(index, carry):
        body(pl.ds(pl.multiple_of(index * size, 16), size), index * size, size)
        return carry

    lax.fori_loop(0, rows // size, turn, 0)


def norm_back(grad, values, scale, gain):
    plain = values * scale
    pulled = grad * gain
    through = scale * (pulled - plain * jnp.mean(pulled * plain, axis=-1, keepdims=True))
    return through, jnp.sum(grad * plain, axis=0, keepdims=True)


def middle_kernel(
    rows, place_ref, wires_ref, query_ref, keys_ref, values_ref, inverse_ref, beta_ref, decay_ref,
    ext_ref, gain_head_ref, x_ref, cot_ref, gain_two_ref, mix_hbm, ffn_hbm,
    result_ref, grad_resid_ref, grad_out_ref, ffn_grad_ref, gain_two_grad_ref, state_ref, pseudo_ref,
    local_ref, grad_mixed_ref, grad_gate_ref, gain_head_grad_ref,
    w_out, w_ffn, mixed_ref, head_out_ref, pre_ref, compact_ref, down_ref, hidden_ref, total_ref,
    grad_head_ref, sems,
):
    count = query_ref.shape[0]
    padded = -(-rows // 16) * 16
    width = ext_ref.shape[1] - H * DV
    own_gate = lambda span: ext_ref[8:, width + span.start : width + span.stop]
    out_rows = w_out.shape[0]
    load_out = pltpu.make_async_copy(
        mix_hbm.at[pl.ds(mix_hbm.shape[0] - out_rows, out_rows), :], w_out, sems.at[0]
    )
    load_ffn = pltpu.make_async_copy(ffn_hbm, w_ffn, sems.at[1])
    load_out.start()
    load_ffn.start()
    forward_chain(
        place_ref, wires_ref, query_ref, keys_ref, values_ref, inverse_ref, beta_ref, decay_ref,
        own_gate, gain_head_ref, head_out_ref, mixed_ref, state_ref, pseudo_ref,
    )
    load_out.wait()
    resid = x_ref[...].astype(jnp.float32) + dot_nn(head_out_ref[...], w_out[...])
    scale = lax.rsqrt(jnp.mean(resid * resid, axis=-1, keepdims=True) + EPSILON)
    normed = (resid * scale * gain_two_ref[...]).astype(jnp.bfloat16)
    load_ffn.wait()
    pairs = 2 * FF
    blocks = ffn_hbm.shape[0] // padded
    used = -(-pairs // rows)
    split = pairs // rows
    inside = pairs - split * rows
    upper_rows = used * padded
    down_start = split * padded
    down_rows = (blocks - split) * padded
    bf16 = jnp.bfloat16

    def pre(span, start, size):
        pre_ref[span, :] = dot_nt(w_ffn[span, :], normed)

    by_chunks(upper_rows, pre)
    for block in range(used):
        size = min(rows, pairs - block * rows)
        compact_ref[pl.ds(block * rows, size), :] = pre_ref[pl.ds(block * padded, size), :]
    down_ref[...] = jnp.zeros_like(down_ref)

    def pieces():
        done = 0
        for block in range(blocks - split):
            offset = inside if block == 0 else 0
            size = rows - offset
            yield done, block * padded + offset, size
            done += size

    gate = compact_ref[0:FF, :]
    up = compact_ref[FF:pairs, :]
    hidden_ref[...] = gate * jax.nn.sigmoid(gate) * up
    for done, spot, size in pieces():
        down_ref[pl.ds(spot, size), :] = hidden_ref[pl.ds(done, size), :]
    total_ref[...] = resid

    def out_chunk(span, start, size):
        here = pl.ds(pl.multiple_of(down_start + start, 16), size)
        total_ref[...] += dot_tn(down_ref[span, :].astype(bf16), w_ffn[here, :])

    by_chunks(down_rows, out_chunk)
    result_ref[...] = total_ref[...].astype(bf16)
    cot = cot_ref[...]

    def hidden_chunk(span, start, size):
        here = pl.ds(pl.multiple_of(down_start + start, 16), size)
        pre_ref[span, :] = dot_nt(w_ffn[here, :], cot)

    by_chunks(down_rows, hidden_chunk)
    for done, spot, size in pieces():
        hidden_ref[pl.ds(done, size), :] = pre_ref[pl.ds(spot, size), :]
    gate = compact_ref[0:FF, :]
    up = compact_ref[FF:pairs, :]
    active, slope = silu_pair(gate)
    grad_hidden = hidden_ref[...]
    compact_ref[0:FF, :] = grad_hidden * up * slope
    compact_ref[FF:pairs, :] = grad_hidden * active
    pre_ref[...] = jnp.zeros_like(pre_ref)
    for block in range(used):
        size = min(rows, pairs - block * rows)
        pre_ref[pl.ds(block * padded, size), :] = compact_ref[pl.ds(block * rows, size), :]
    total_ref[...] = jnp.zeros_like(total_ref)

    def mid_chunk(span, start, size):
        piece = pre_ref[span, :].astype(bf16)
        total_ref[...] += dot_tn(piece, w_ffn[span, :])
        ffn_grad_ref[span, :] = dot_nn(piece, normed).astype(bf16)

    by_chunks(upper_rows, mid_chunk)
    shared = upper_rows - down_start
    if shared:
        both = jnp.concatenate(
            [pre_ref[pl.ds(down_start, shared), :], down_ref[pl.ds(0, shared), :]], axis=1
        ).astype(bf16)
        against = jnp.concatenate([normed, cot], axis=0)
        ffn_grad_ref[pl.ds(down_start, shared), :] = dot_nn(both, against).astype(bf16)

    def down_chunk(span, start, size):
        here = pl.ds(pl.multiple_of(shared + start, 16), size)
        there = pl.ds(pl.multiple_of(upper_rows + start, 16), size)
        ffn_grad_ref[there, :] = dot_nn(down_ref[here, :].astype(bf16), cot).astype(bf16)

    by_chunks(down_rows - shared, down_chunk)
    resid = x_ref[...].astype(jnp.float32) + dot_nn(head_out_ref[...], w_out[...])
    through, gain_two_grad_ref[...] = norm_back(total_ref[...], resid, scale, gain_two_ref[...])
    grad_resid = cot.astype(jnp.float32) + through
    grad_resid_ref[...] = grad_resid
    resid_half = grad_resid.astype(bf16)
    grad_out_ref[...] = dot_tn(head_out_ref[...], resid_half).astype(bf16)
    grad_head_ref[...] = dot_nt(resid_half, w_out[...])
    backward_local(
        grad_head_ref, mixed_ref, query_ref, keys_ref, values_ref, inverse_ref, beta_ref, decay_ref,
        own_gate, gain_head_ref, local_ref, grad_mixed_ref, grad_gate_ref, gain_head_grad_ref,
    )


def middle(rows, place, wires, query, keys, values, inverse, beta, decay, ext, gain_head, x, cot, gain_two, mix, ffn):
    f32, bf16 = jnp.float32, jnp.bfloat16
    count = query.shape[0]
    padded = -(-rows // 16) * 16
    blocks = ffn.shape[0] // padded
    used, split = -(-2 * FF // rows), 2 * FF // rows
    out_rows = H * DV
    vmem = pl.BlockSpec(memory_space=pltpu.VMEM)
    anywhere = pl.BlockSpec(memory_space=pl.ANY)
    return pl.pallas_call(
        functools.partial(middle_kernel, rows),
        out_shape=[
            jax.ShapeDtypeStruct((count, D), bf16),
            jax.ShapeDtypeStruct((count, D), f32),
            jax.ShapeDtypeStruct((out_rows, D), bf16),
            jax.ShapeDtypeStruct(ffn.shape, bf16),
            jax.ShapeDtypeStruct((1, D), f32),
            jax.ShapeDtypeStruct((H, DK, DV), f32),
            jax.ShapeDtypeStruct((count, H * DV), f32),
            jax.ShapeDtypeStruct((H * DK, DV), bf16),
            jax.ShapeDtypeStruct((count, H * DV), f32),
            jax.ShapeDtypeStruct((count, H * DV), f32),
            jax.ShapeDtypeStruct((1, DV), f32),
        ],
        in_specs=[pl.BlockSpec(memory_space=pltpu.SMEM)] + [vmem] * 12 + [anywhere] * 2,
        out_specs=[vmem] * 11,
        scratch_shapes=[
            pltpu.VMEM((out_rows, D), bf16),
            pltpu.VMEM(ffn.shape, bf16),
            pltpu.VMEM((count, H * DV), f32),
            pltpu.VMEM((count, H * DV), bf16),
            pltpu.VMEM((used * padded, count), f32),
            pltpu.VMEM((2 * FF, count), f32),
            pltpu.VMEM(((blocks - split) * padded, count), f32),
            pltpu.VMEM((FF, count), f32),
            pltpu.VMEM((count, D), f32),
            pltpu.VMEM((count, H * DV), f32),
            pltpu.SemaphoreType.DMA((2,)),
        ],
        compiler_params=pltpu.CompilerParams(vmem_limit_bytes=60 * 2**20),
        cost_estimate=pl.CostEstimate(flops=10**10, bytes_accessed=5 * 10**7, transcendentals=0),
        name="middle",
    )(place, wires, query, keys, values, inverse, beta, decay, ext, gain_head, x, cot, gain_two, mix, ffn)


def back_kernel(
    side, wires_ref, local_ref, query_ref, keys_ref, values_ref, inverse_ref, beta_ref, decay_ref,
    state_ref, pseudo_ref, grad_mixed_ref, ext_ref, taps_ref, ffn_grad,
    shard_out, grad_conv_ref, grad_border_ref, grad_taps_ref, grad_beta_ref, grad_decay_ref,
    *scratch,
):
    after_ref, padded_ref, locals_ref = scratch[:3]
    send_sems, recv_sems, local_sems = scratch[-3:]
    place = Place(side)
    copies = Copies(send_sems, recv_sems, local_sems)
    place.enter()
    scatter = Scatter(place, copies, ffn_grad, *scratch[3:-3])
    ffn = scatter.steps(shard_out)
    states = gather_steps(place, copies, local_ref, locals_ref, plane=True)
    states.pop(0)()
    ffn.pop(0)()
    for step in states:
        step()
        ffn.pop(0)()
    work = back_chain(
        wires_ref, locals_ref, query_ref, keys_ref, values_ref, inverse_ref, beta_ref,
        decay_ref, state_ref, pseudo_ref, grad_mixed_ref, ext_ref, taps_ref,
        grad_conv_ref, grad_border_ref, grad_taps_ref, grad_beta_ref, grad_decay_ref,
        after_ref, padded_ref,
    )
    for unused in work:
        if ffn:
            ffn.pop(0)()
    for step in ffn:
        step()
    copies.finish()


def back(side, tag, wires, local, query, keys, values, inverse, beta, decay, state, pseudo, grad_mixed, ext, taps, ffn_grad):
    f32 = jnp.float32
    deep, ctx = lax.axis_size("dp"), lax.axis_size("ctx")
    count, width = query.shape[0], taps.shape[1]
    rows = ffn_grad.shape[0] // (deep * ctx)
    number = Scatter.copies_of(deep) + gather_copies(1)
    vmem = pl.BlockSpec(memory_space=pltpu.VMEM)
    anywhere = pl.BlockSpec(memory_space=pl.ANY)
    return pl.pallas_call(
        functools.partial(back_kernel, side),
        out_shape=[
            jax.ShapeDtypeStruct((rows, D), f32),
            jax.ShapeDtypeStruct((count, width), f32),
            jax.ShapeDtypeStruct((8, width), f32),
            jax.ShapeDtypeStruct((8, width), f32),
            jax.ShapeDtypeStruct((count, 128), f32),
            jax.ShapeDtypeStruct((count, 128), f32),
        ],
        in_specs=[vmem] * 13 + [anywhere],
        out_specs=[vmem] * 6,
        scratch_shapes=[
            pltpu.VMEM((H, DK, DV), f32),
            pltpu.VMEM((count + 16, width), f32),
            pltpu.VMEM((ctx * H * DK, DV), jnp.bfloat16),
        ]
        + Scatter.scratch(deep, rows)
        + [
            pltpu.SemaphoreType.DMA((number,)),
            pltpu.SemaphoreType.DMA((number,)),
            pltpu.SemaphoreType.DMA((4 * deep + 1,)),
        ],
        compiler_params=pltpu.CompilerParams(
            collective_id=tag, has_side_effects=True, vmem_limit_bytes=60 * 2**20
        ),
        cost_estimate=pl.CostEstimate(flops=10**10, bytes_accessed=10**8, transcendentals=0),
        name="back",
    )(wires, local, query, keys, values, inverse, beta, decay, state, pseudo, grad_mixed, ext, taps, ffn_grad)


def back_chain(
    wire_ref, local_ref, query_ref, keys_ref, values_ref, inverse_ref, beta_ref,
    decay_ref, state_ref, pseudo_ref, grad_mixed_ref, ext_ref, taps_ref,
    grad_conv_ref, grad_border_ref, grad_taps_ref, grad_beta_ref, grad_decay_ref,
    after_ref, padded_ref,
):
    count = query_ref.shape[0]
    width = taps_ref.shape[1]
    devices = wire_ref.shape[0]
    after_ref[...] = jnp.zeros_like(after_ref)

    def lap(step, carry):
        index = devices - 1 - step
        for head in range(H):
            to_end, key_mix, value_mix, whole = wire_parts(wire_ref, index, head, count)
            after = after_ref[head]
            inner = wire_mm(to_end, after, ((1,), (0,)))
            spot = pl.multiple_of((index * H + head) * DK, DK)
            local = local_ref[pl.ds(spot, DK), :].astype(jnp.float32)
            after_ref[head] = whole * after - wire_mm(key_mix, inner, ((0,), (0,))) + local
        return carry

    lax.fori_loop(0, devices - 1 - lax.axis_index("ctx"), lap, 0)
    yield
    taps = taps_ref[...]
    summed = ext_sum(ext_ref, taps, count, 0, width)
    activated, slope = silu_pair(summed)
    padded_ref[0:8, :] = jnp.zeros((8, width), jnp.float32)
    padded_ref[pl.ds(8 + count, 8), :] = jnp.zeros((8, width), jnp.float32)
    rows, cols = iotas(count)
    lower = rows >= cols
    strict = rows > cols
    lanes = lax.broadcasted_iota(jnp.int32, (count, 128), 1)
    beta_out = jnp.zeros((count, 128), jnp.float32)
    cumulative_out = jnp.zeros((count, 128), jnp.float32)
    row_column = lax.broadcasted_iota(jnp.int32, (count, 1), 0)
    for head in range(H):
        query = query_ref[:, head * DK : (head + 1) * DK]
        keys = keys_ref[:, head * DK : (head + 1) * DK]
        span = slice(head * DV, (head + 1) * DV)
        values = values_ref[:, span]
        beta = beta_ref[:, head : head + 1]
        matrix, grown, to_end, whole = decay_terms(decay_ref[:, head : head + 1], rows, cols)
        inverse = inverse_ref[head]
        state = state_ref[head]
        after = after_ref[head]
        pseudo = pseudo_ref[:, span]
        grad_mixed = grad_mixed_ref[:, span]
        keys_grown = keys * (beta * grown)
        key_mix = mm(inverse, keys_grown)
        value_mix = mm(inverse, values * beta)
        gram = mm_nt(keys, keys)
        system = jnp.where(strict, beta * gram * matrix, 0.0)
        scores = mm_nt(query, keys) * matrix
        keys_end = keys * to_end
        query_grown = query * grown
        grad_query_grown = mm_nt(grad_mixed, state)
        grad_scores = jnp.where(lower, mm_nt(grad_mixed, pseudo), 0.0)
        grad_pseudo = mm_tn(scores, grad_mixed) + mm(keys_end, after)
        grad_keys_end = mm_nt(pseudo, after)
        grad_whole = jnp.sum(jnp.sum(after * state, axis=1, keepdims=True), axis=0, keepdims=True)
        grad_value_in = mm_tn(inverse, grad_pseudo)
        grad_key_in = mm_tn(inverse, -mm_nt(grad_pseudo, state))
        grad_system = -jnp.where(
            strict, mm_nt(grad_value_in, value_mix) + mm_nt(grad_key_in, key_mix), 0.0
        )
        grad_raw = grad_scores * matrix
        grad_query = mm(grad_raw, keys) + grad_query_grown * grown
        grad_keys = mm_tn(grad_raw, query)
        weighted = grad_system * matrix
        grad_beta = jnp.sum(weighted * gram, axis=1, keepdims=True)
        grad_gram = weighted * beta
        grad_keys = grad_keys + mm(grad_gram, keys) + mm_tn(grad_gram, keys)
        spread = grad_scores * scores + grad_system * system
        grad_cumulative = jnp.sum(spread, axis=1, keepdims=True)
        across = jnp.sum(spread, axis=0, keepdims=True)
        grad_cumulative = grad_cumulative - jnp.sum(
            jnp.where(rows == cols, across, 0.0), axis=1, keepdims=True
        )
        grad_keys = grad_keys + grad_key_in * (beta * grown)
        through = jnp.sum(grad_key_in * keys, axis=1, keepdims=True) * grown
        grad_beta = grad_beta + through + jnp.sum(grad_value_in * values, axis=1, keepdims=True)
        grad_cumulative = grad_cumulative + through * beta
        grad_values = grad_value_in * beta
        grad_cumulative = grad_cumulative + jnp.sum(
            grad_query_grown * query_grown, axis=1, keepdims=True
        )
        grad_keys = grad_keys + grad_keys_end * to_end
        ending = jnp.sum(grad_keys_end * keys_end, axis=1, keepdims=True)
        final = jnp.sum(ending, axis=0, keepdims=True) + whole * grad_whole
        grad_cumulative = grad_cumulative - ending + jnp.where(row_column == count - 1, final, 0.0)
        beta_out = jnp.where(lanes == head, grad_beta, beta_out)
        cumulative_out = jnp.where(lanes == head, grad_cumulative, cumulative_out)
        key_part = activated[:, (H + head) * DK : (H + head + 1) * DK]
        key_scale = unit_rows(key_part)
        query_part = activated[:, head * DK : (head + 1) * DK]
        query_scale = unit_rows(query_part)
        factor = DK ** (-0.5)
        grad_query_part = (factor * query_scale) * (
            grad_query
            - query_part
            * (query_scale * query_scale)
            * jnp.sum(grad_query * query_part, axis=-1, keepdims=True)
        )
        grad_key_part = key_scale * (
            grad_keys
            - key_part
            * (key_scale * key_scale)
            * jnp.sum(grad_keys * key_part, axis=-1, keepdims=True)
        )
        spots = (head * DK, (H + head) * DK, 2 * H * DK + head * DV)
        for spot, grad in zip(spots, (grad_query_part, grad_key_part, grad_values)):
            size = grad.shape[1]
            padded_ref[pl.ds(8, count), spot : spot + size] = grad * slope[:, spot : spot + size]
        yield
    grad_beta_ref[...] = beta_out
    grad_decay_ref[...] = mm_tn(jnp.where(lower, 1.0, 0.0), cumulative_out)
    conv_total = jnp.zeros((count, width), jnp.float32)
    border_total = jnp.zeros((8, width), jnp.float32)
    summed_grad = padded_ref[pl.ds(8, count), :]
    tap_rows = lax.broadcasted_iota(jnp.int32, (8, width), 0)
    taps_total = jnp.zeros((8, width), jnp.float32)
    for tap in range(CONV):
        shift = CONV - 1 - tap
        conv_total = conv_total + taps[tap : tap + 1] * padded_ref[pl.ds(8 + shift, count), :]
        border_total = border_total + taps[tap : tap + 1] * padded_ref[pl.ds(shift, 8), :]
        piece = jnp.sum(
            summed_grad * ext_ref[pl.ds(8 - (CONV - 1) + tap, count), :width],
            axis=0,
            keepdims=True,
        )
        taps_total = jnp.where(tap_rows == tap, piece, taps_total)
    grad_conv_ref[...] = conv_total
    grad_border_ref[...] = border_total
    grad_taps_ref[...] = taps_total
    yield


def chip_side():
    half = lax.axis_size("ctx") // 2
    side = math.isqrt(half)
    return side if side == 2 and 2 * side * side == lax.axis_size("ctx") else 0


def adam_step(weight, grad_full, first, second, clip):
    grad_clipped = grad_full * clip
    first_new = BETA_ONE * first + (1.0 - BETA_ONE) * grad_clipped
    second_new = BETA_TWO * second + (1.0 - BETA_TWO) * grad_clipped * grad_clipped
    update = (
        first_new / CORRECT_ONE / (jnp.sqrt(second_new / CORRECT_TWO) + ADAM_EPS)
        + DECAY_RATE * weight
    )
    return (weight - LEARN_RATE * update, first_new, second_new)


def plain(
    inputs,
    cotangent,
    mixer_params,
    mixer_first,
    mixer_second,
    ffn_params,
    ffn_first,
    ffn_second,
    small_params,
    small_first,
    small_second,
):
    gain_one, gain_two, gain_head, tap_values, w_gates, a_log, dt_bias = unpack_small(small_params)
    width = tap_values.shape[1]
    mix_part = mixer_params.astype(jnp.bfloat16)
    ffn_part = ffn_params.astype(jnp.bfloat16)
    mix_whole, ffn_whole = (
        lax.all_gather(mix_part, ("dp", "ctx"), axis=0, tiled=True),
        lax.all_gather(ffn_part, ("dp", "ctx"), axis=0, tiled=True),
    )
    w_in, w_out, w_ffn, w_down = split_weights(mix_whole, ffn_whole)
    x_float = inputs[0].astype(jnp.float32)
    count = x_float.shape[0]
    normed_in = norm_scale(x_float, gain_one).astype(jnp.bfloat16)
    projected = jnp.dot(normed_in, w_in.T, preferred_element_type=jnp.float32)
    gate_logits = jnp.dot(normed_in.astype(jnp.float32), w_gates, precision=HIGHEST)
    f32 = jnp.float32
    devices = lax.axis_size("ctx")
    place = lax.axis_index("ctx").astype(jnp.int32).reshape(1)
    out_gate = projected[:, width:]
    edge = from_behind(projected[count - 8 :, :width], "ctx", 1)
    border = jnp.where(lax.broadcasted_iota(jnp.int32, (8, 1), 0) >= 8 - (CONV - 1), edge, 0.0)
    (beta, decay), pull_gates = jax.vjp(gates, gate_logits, a_log, dt_bias)
    wire, query, keys, values, inverse = fused(
        forward_parts,
        (
            jax.ShapeDtypeStruct((count + PAD, H * (2 * DK + DV)), jnp.bfloat16),
            jax.ShapeDtypeStruct((count, H * DK), f32),
            jax.ShapeDtypeStruct((count, H * DK), f32),
            jax.ShapeDtypeStruct((count, H * DV), f32),
            jax.ShapeDtypeStruct((H, count, count), f32),
        ),
        scratch=(pltpu.VMEM((count + 8, width), f32),),
        label="forward_parts",
    )(projected, border, tap_values, beta, decay)
    wires = lax.all_gather(wire, "ctx")
    gain_row = gain_head.reshape(1, DV)
    head_out, mixed, state, pseudo = fused(
        forward_chain,
        (
            jax.ShapeDtypeStruct((count, H * DV), jnp.bfloat16),
            jax.ShapeDtypeStruct((count, H * DV), f32),
            jax.ShapeDtypeStruct((H, DK, DV), f32),
            jax.ShapeDtypeStruct((count, H * DV), f32),
        ),
        scalars=1,
        label="forward_chain",
    )(place, wires, query, keys, values, inverse, beta, decay, out_gate, gain_row)
    resid = x_float + jnp.dot(head_out, w_out, preferred_element_type=jnp.float32)
    normed_mid = norm_scale(resid, gain_two).astype(jnp.bfloat16)
    ffn_pre = jnp.dot(normed_mid, w_ffn.T, preferred_element_type=jnp.float32)
    gate_part = ffn_pre[:, :FF]
    up_part = ffn_pre[:, FF:]
    hidden_act = swiglu(gate_part, up_part).astype(jnp.bfloat16)
    result = (resid + jnp.dot(hidden_act, w_down, preferred_element_type=jnp.float32)).astype(
        jnp.bfloat16
    )
    seq_grad = cotangent[0]
    grad_float = seq_grad.astype(jnp.float32)
    grad_down = jnp.dot(hidden_act.T, seq_grad, preferred_element_type=jnp.float32)
    grad_hidden = jnp.dot(seq_grad, w_down.T, preferred_element_type=jnp.float32)
    unused_one, pull_swiglu = jax.vjp(swiglu, gate_part, up_part)
    grad_gate, grad_up = pull_swiglu(grad_hidden)
    grad_pre = jnp.concatenate([grad_gate, grad_up], axis=1).astype(jnp.bfloat16)
    grad_ffn = jnp.dot(grad_pre.T, normed_mid, preferred_element_type=jnp.float32)
    grad_mid = jnp.dot(grad_pre, w_ffn, preferred_element_type=jnp.float32)
    unused_two, pull_mid = jax.vjp(norm_scale, resid, gain_two)
    grad_through, grad_gain_two = pull_mid(grad_mid)
    grad_resid = grad_float + grad_through
    resid_half = grad_resid.astype(jnp.bfloat16)
    grad_out = jnp.dot(head_out.T, resid_half, preferred_element_type=jnp.float32)
    grad_head = jnp.dot(resid_half, w_out.T, preferred_element_type=jnp.float32)
    local, grad_mixed, grad_gate_out, grad_gain_head = fused(
        backward_local,
        (
            jax.ShapeDtypeStruct((H * DK, DV), jnp.bfloat16),
            jax.ShapeDtypeStruct((count, H * DV), f32),
            jax.ShapeDtypeStruct((count, H * DV), f32),
            jax.ShapeDtypeStruct((1, DV), f32),
        ),
        label="backward_local",
    )(grad_head, mixed, query, keys, values, inverse, beta, decay, out_gate, gain_row)
    locals_all = lax.all_gather(local, "ctx")
    locals_all, grad_ffn, grad_down = lax.optimization_barrier((locals_all, grad_ffn, grad_down))
    ffn_shard = scatter_rows((grad_ffn, grad_down))
    grad_conv, grad_border, grad_taps, grad_beta, grad_decay = fused(
        backward_chain,
        (
            jax.ShapeDtypeStruct((count, width), f32),
            jax.ShapeDtypeStruct((8, width), f32),
            jax.ShapeDtypeStruct((8, width), f32),
            jax.ShapeDtypeStruct((count, 128), f32),
            jax.ShapeDtypeStruct((count, 128), f32),
        ),
        scratch=(
            pltpu.VMEM((H, DK, DV), f32),
            pltpu.VMEM((count + 8, width), f32),
            pltpu.VMEM((count + 16, width), f32),
        ),
        scalars=1,
        label="backward_chain",
    )(
        place, wires, locals_all, query, keys, values, inverse, beta, decay, state, pseudo,
        grad_mixed, projected, border, tap_values,
    )
    grad_logits, grad_alog, grad_bias = pull_gates((grad_beta[:, :H], grad_decay[:, :H]))
    returned = from_behind(grad_border, "ctx", -1)[8 - (CONV - 1) :]
    grad_conv = grad_conv.at[count - (CONV - 1) :].add(returned)
    grad_proj = jnp.concatenate([grad_conv, grad_gate_out], axis=1).astype(jnp.bfloat16)
    grad_in = jnp.dot(grad_proj.T, normed_in, preferred_element_type=jnp.float32)
    grad_normed = jnp.dot(grad_proj, w_in, preferred_element_type=jnp.float32) + jnp.dot(
        grad_logits, w_gates.T, precision=HIGHEST
    )
    grad_gates = jnp.dot(normed_in.astype(jnp.float32).T, grad_logits, precision=HIGHEST)
    unused_six, pull_in = jax.vjp(norm_scale, x_float, gain_one)
    grad_x, grad_gain_one = pull_in(grad_normed)
    grad_input = (grad_resid + grad_x).astype(jnp.bfloat16)
    small_local = jnp.concatenate(
        [
            grad_gain_one,
            grad_gain_two,
            grad_gain_head.reshape(-1),
            grad_taps[:CONV].reshape(-1),
            grad_gates.reshape(-1),
            grad_alog,
            grad_bias,
        ]
    )
    small_grad = lax.psum(small_local, ("dp", "ctx"))
    ffn_shard, grad_in, grad_out = lax.optimization_barrier((ffn_shard, grad_in, grad_out))
    mix_shard = scatter_rows((grad_in, grad_out))
    small_grad, mix_shard = lax.optimization_barrier((small_grad, mix_shard))
    shard_squares = jnp.sum(mix_shard * mix_shard) + jnp.sum(ffn_shard * ffn_shard)
    total_squares = lax.psum(shard_squares, ("dp", "ctx"))
    squares = total_squares + jnp.sum(small_grad * small_grad)
    clip = jnp.minimum(1.0, MAX_NORM / (jnp.sqrt(squares) + 1e-06))
    mixer_new, mixer_first_new, mixer_second_new = adam_step(
        mixer_params, mix_shard, mixer_first, mixer_second, clip
    )
    ffn_new, ffn_first_new, ffn_second_new = adam_step(
        ffn_params, ffn_shard, ffn_first, ffn_second, clip
    )
    small_new, small_first_new, small_second_new = adam_step(
        small_params, small_grad, small_first, small_second, clip
    )
    return (
        result[None],
        grad_input[None],
        mix_shard,
        ffn_shard,
        small_grad,
        mixer_new,
        mixer_first_new,
        mixer_second_new,
        ffn_new,
        ffn_first_new,
        ffn_second_new,
        small_new,
        small_first_new,
        small_second_new,
    )


def fast(
    side, inputs, cotangent, mixer_params, mixer_first, mixer_second, ffn_params, ffn_first, ffn_second, small_params, small_first, small_second,
):
    gain_one, gain_two, gain_head, tap_values, w_gates, a_log, dt_bias = unpack_small(small_params)
    width = tap_values.shape[1]
    f32, bf16 = jnp.float32, jnp.bfloat16
    everyone = lax.axis_size("dp") * lax.axis_size("ctx")
    mix_rows, ffn_rows = mixer_params.size // D, ffn_params.size // D
    padding = -ffn_rows % 16
    mix_part = mixer_params.reshape(mix_rows, D).astype(bf16)
    ffn_part = jnp.pad(ffn_params.reshape(ffn_rows, D).astype(bf16), ((0, padding), (0, 0)))
    x_float = inputs[0].astype(f32)
    count = x_float.shape[0]
    normed_in = norm_scale(x_float, gain_one).astype(bf16)
    gate_logits = jnp.dot(normed_in.astype(f32), w_gates, precision=HIGHEST)
    (beta, decay), pull_gates = jax.vjp(gates, gate_logits, a_log, dt_bias)
    before = from_behind(normed_in[count - 16 :], "ctx", 1)
    mix_whole, ffn_whole, wires, ext, query, keys, values, inverse = front(
        mix_part, ffn_part, jnp.concatenate([before, normed_in], axis=0), tap_values, beta, decay, side, 1
    )
    wires = wires.reshape(-1, count + PAD, wires.shape[1])
    place = lax.axis_index("ctx").astype(jnp.int32).reshape(1)
    (
        result, grad_resid, grad_out, ffn_grad, grad_gain_two, state, pseudo, local, grad_mixed,
        grad_gate_out, grad_gain_head,
    ) = middle(
        ffn_rows, place, wires, query, keys, values, inverse, beta, decay, ext,
        gain_head.reshape(1, DV), inputs[0], cotangent[0], gain_two.reshape(1, D), mix_whole, ffn_whole,
    )
    ffn_shard, grad_conv, grad_border, grad_taps, grad_beta, grad_decay = back(
        side, 2, wires, local, query, keys, values, inverse, beta, decay, state, pseudo, grad_mixed,
        ext, tap_values, ffn_grad,
    )
    grad_logits, grad_alog, grad_bias = pull_gates((grad_beta[:, :H], grad_decay[:, :H]))
    returned = from_behind(grad_border, "ctx", -1)[8 - (CONV - 1) :]
    grad_conv = grad_conv.at[count - (CONV - 1) :].add(returned)
    grad_proj = jnp.concatenate([grad_conv, grad_gate_out], axis=1).astype(bf16)
    grad_in = jnp.dot(grad_proj.T, normed_in, preferred_element_type=f32).astype(bf16)
    w_in = mix_whole[: grad_proj.shape[1]]
    grad_normed = jnp.dot(grad_proj, w_in, preferred_element_type=f32) + jnp.dot(
        grad_logits, w_gates.T, precision=HIGHEST
    )
    grad_gates = jnp.dot(normed_in.astype(f32).T, grad_logits, precision=HIGHEST)
    unused_six, pull_in = jax.vjp(norm_scale, x_float, gain_one)
    grad_x, grad_gain_one = pull_in(grad_normed)
    grad_input = (grad_resid + grad_x).astype(bf16)
    small_local = jnp.concatenate(
        [
            grad_gain_one,
            grad_gain_two.reshape(-1),
            grad_gain_head.reshape(-1),
            grad_taps[:CONV].reshape(-1),
            grad_gates.reshape(-1),
            grad_alog,
            grad_bias,
        ]
    )
    short = -small_local.size % 1024
    mix_shard, small_grad, total_squares = scatter_all(
        (jnp.concatenate([grad_in, grad_out], axis=0),),
        jnp.pad(small_local, (0, short)).reshape(-1, 128),
        ffn_shard,
        side,
        3,
    )
    mix_shard = mix_shard.reshape(-1)
    ffn_shard = ffn_shard[:ffn_rows].reshape(-1)
    small_grad = small_grad.reshape(-1)[: small_local.size]
    squares = jnp.sum(total_squares) + jnp.sum(small_grad * small_grad)
    clip = jnp.minimum(1.0, MAX_NORM / (jnp.sqrt(squares) + 1e-06))
    mixer_new, mixer_first_new, mixer_second_new = adam_step(
        mixer_params, mix_shard, mixer_first, mixer_second, clip
    )
    ffn_new, ffn_first_new, ffn_second_new = adam_step(
        ffn_params, ffn_shard, ffn_first, ffn_second, clip
    )
    small_new, small_first_new, small_second_new = adam_step(
        small_params, small_grad, small_first, small_second, clip
    )
    return (
        result[None],
        grad_input[None],
        mix_shard,
        ffn_shard,
        small_grad,
        mixer_new,
        mixer_first_new,
        mixer_second_new,
        ffn_new,
        ffn_first_new,
        ffn_second_new,
        small_new,
        small_first_new,
        small_second_new,
    )


def body(*args):
    rows, left = divmod(args[5].size, D)
    side = chip_side() if left == 0 and args[2].size % (32 * D) == 0 else 0
    return fast(side, *args) if side else plain(*args)


def solution(mesh):
    return jax.shard_map(
        body,
        mesh=mesh,
        in_specs=(
            P("dp", "ctx", None),
            P("dp", "ctx", None),
            P(("dp", "ctx")),
            P(("dp", "ctx")),
            P(("dp", "ctx")),
            P(("dp", "ctx")),
            P(("dp", "ctx")),
            P(("dp", "ctx")),
            P(),
            P(),
            P(),
        ),
        out_specs=(
            P("dp", "ctx", None),
            P("dp", "ctx", None),
            P(("dp", "ctx")),
            P(("dp", "ctx")),
            P(),
            P(("dp", "ctx")),
            P(("dp", "ctx")),
            P(("dp", "ctx")),
            P(("dp", "ctx")),
            P(("dp", "ctx")),
            P(("dp", "ctx")),
            P(),
            P(),
            P(),
        ),
        check_vma=False,
    )
```

```python
import functools
import math
import jax
import jax.numpy as jnp
from jax import lax
from jax.experimental import pallas as pl
from jax.experimental.pallas import tpu as pltpu
from jax.sharding import PartitionSpec as P

D = 1024
H = 2
DK = 256
DV = 512
FF = 1408
CONV = 4
GROUP = 64


EPSILON = 1e-06
ADAM_EPS = 1e-08
LEARN_RATE = 0.02
BETA_ONE = 0.9
BETA_TWO = 0.999
DECAY_RATE = 0.1
CORRECT_ONE = 1.0 - 0.9**3
CORRECT_TWO = 1.0 - 0.999**3
MAX_NORM = 1.0
HIGHEST = lax.Precision.HIGHEST


def from_behind(value, axis, steps):
    count = lax.axis_size(axis)
    initial, last = (max(0, -steps), min(count, count - steps))
    return lax.ppermute(value, axis, [(source, source + steps) for source in range(initial, last)])


def norm_scale(values, gain):
    return values * lax.rsqrt(jnp.mean(values * values, axis=-1, keepdims=True) + EPSILON) * gain


def swiglu(gate_part, up_part):
    return jax.nn.silu(gate_part) * up_part


def unpack_small(packed):
    width = 2 * H * DK + H * DV
    lengths = [D, D, DV, CONV * width, D * 2 * H, H, H]
    pieces = []
    offset = 0
    for length in lengths:
        pieces.append(packed[offset : offset + length])
        offset = offset + length
    return (
        pieces[0],
        pieces[1],
        pieces[2],
        pieces[3].reshape(CONV, width),
        pieces[4].reshape(D, 2 * H),
        pieces[5],
        pieces[6],
    )


def split_weights(mix_whole, ffn_whole):
    mix_rows = mix_whole.reshape(-1, D)
    ffn_rows = ffn_whole.reshape(-1, D)
    edge = 2 * H * DK + 2 * H * DV
    return (mix_rows[:edge], mix_rows[edge:], ffn_rows[: 2 * FF], ffn_rows[2 * FF :])


PAD = 16
HIGH = dict(precision=HIGHEST, preferred_element_type=jnp.float32)


def mm(a, b):
    return lax.dot_general(a, b, (((1,), (0,)), ((), ())), **HIGH)


def mm_nt(a, b):
    return lax.dot_general(a, b, (((1,), (1,)), ((), ())), **HIGH)


def mm_tn(a, b):
    return lax.dot_general(a, b, (((0,), (0,)), ((), ())), **HIGH)


def halves(a):
    high = a.astype(jnp.bfloat16)
    return high, (a - high.astype(jnp.float32)).astype(jnp.bfloat16)


def wire_mm(a, b, dims):
    high, low = halves(b)
    first = lax.dot_general(a, high, (dims, ((), ())), preferred_element_type=jnp.float32)
    return first + lax.dot_general(a, low, (dims, ((), ())), preferred_element_type=jnp.float32)


def iotas(size):
    shape = (size, size)
    return (
        lax.broadcasted_iota(jnp.int32, shape, 0),
        lax.broadcasted_iota(jnp.int32, shape, 1),
    )


def to_row(column, rows, cols):
    return jnp.sum(jnp.where(rows == cols, column, 0.0), axis=0, keepdims=True)


def unit_inverse(strict_part, rows, cols):
    size = strict_part.shape[0]
    inverse = jnp.where(rows == cols, 1.0, 0.0) - jnp.where(
        (rows // 2 == cols // 2), strict_part, 0.0
    )
    block = 2
    while block < size:
        joined = (rows // (2 * block) == cols // (2 * block)) & (rows // block != cols // block)
        off = jnp.where(joined, strict_part, 0.0)
        inverse = inverse - mm(mm(inverse, off), inverse)
        block = 2 * block
    return inverse


def silu_pair(x):
    gate = jax.nn.sigmoid(x)
    return x * gate, gate * (1.0 + x * (1.0 - gate))


def conv_sum(extended_ref, taps, count):
    total = None
    for tap in range(CONV):
        piece = taps[tap : tap + 1] * extended_ref[pl.ds(8 - (CONV - 1) + tap, count), :]
        total = piece if total is None else total + piece
    return total


def unit_rows(part):
    return lax.rsqrt(jnp.sum(part * part, axis=-1, keepdims=True) + EPSILON)


def decay_terms(decay_column, rows, cols):
    lower = rows >= cols
    size = rows.shape[0]
    spread_in = jnp.broadcast_to(decay_column, (size, 128))
    cumulative = mm(jnp.where(lower, 1.0, 0.0), spread_in)[:, :1]
    across = to_row(cumulative, rows, cols)
    matrix = jnp.where(lower, jnp.exp(jnp.where(lower, cumulative - across, 0.0)), 0.0)
    last = cumulative[size - 1 : size]
    return matrix, jnp.exp(cumulative), jnp.exp(last - cumulative), jnp.exp(last)


def forward_parts(
    projected_ref, border_ref, taps_ref, beta_ref, decay_ref,
    wire_ref, query_ref, keys_ref, values_ref, inverse_ref, extended_ref,
):
    count = projected_ref.shape[0]
    width = taps_ref.shape[1]
    extended_ref[0:8, :] = border_ref[...]
    extended_ref[pl.ds(8, count), :] = projected_ref[:, :width]
    summed = conv_sum(extended_ref, taps_ref[...], count)
    activated = summed * jax.nn.sigmoid(summed)
    rows, cols = iotas(count)
    for head in range(H):
        query_part = activated[:, head * DK : (head + 1) * DK]
        key_part = activated[:, (H + head) * DK : (H + head + 1) * DK]
        start = 2 * H * DK + head * DV
        values = activated[:, start : start + DV]
        query = query_part * unit_rows(query_part) * DK ** (-0.5)
        keys = key_part * unit_rows(key_part)
        beta = beta_ref[:, head : head + 1]
        matrix, grown, to_end, whole = decay_terms(decay_ref[:, head : head + 1], rows, cols)
        system = jnp.where(rows > cols, beta * mm_nt(keys, keys) * matrix, 0.0)
        inverse = unit_inverse(system, rows, cols)
        key_mix = mm(inverse, keys * (beta * grown))
        value_mix = mm(inverse, values * beta)
        base = head * (2 * DK + DV)
        wire_ref[0:count, base : base + DK] = (keys * to_end).astype(jnp.bfloat16)
        wire_ref[0:count, base + DK : base + 2 * DK] = key_mix.astype(jnp.bfloat16)
        wire_ref[0:count, base + 2 * DK : base + 2 * DK + DV] = value_mix.astype(jnp.bfloat16)
        high, low = halves(jnp.broadcast_to(whole, (PAD, 2 * DK + DV)))
        first = lax.broadcasted_iota(jnp.int32, (PAD, 2 * DK + DV), 0) < 8
        tail = jnp.where(first, high.astype(jnp.float32), low.astype(jnp.float32))
        wire_ref[pl.ds(count, PAD), base : base + 2 * DK + DV] = tail.astype(jnp.bfloat16)
        query_ref[:, head * DK : (head + 1) * DK] = query
        keys_ref[:, head * DK : (head + 1) * DK] = keys
        values_ref[:, head * DV : (head + 1) * DV] = values
        inverse_ref[head] = inverse


def wire_parts(wire_ref, index, head, count):
    base = head * (2 * DK + DV)
    to_end = wire_ref[index, 0:count, base : base + DK]
    key_mix = wire_ref[index, 0:count, base + DK : base + 2 * DK]
    value_mix = wire_ref[index, 0:count, base + 2 * DK : base + 2 * DK + DV]
    tail = wire_ref[index, pl.ds(count, PAD), base : base + 128].astype(jnp.float32)
    whole = tail[0:1, 0:1] + tail[8:9, 0:1]
    return to_end, key_mix, value_mix, whole


def own_mix(inverse, keys, values, beta, grown):
    return mm(inverse, keys * (beta * grown)), mm(inverse, values * beta)


def forward_chain(
    place_ref, wire_ref, query_ref, keys_ref, values_ref, inverse_ref, beta_ref, decay_ref,
    gate_ref, gain_ref, head_out_ref, mixed_ref, state_ref, pseudo_ref,
):
    count = query_ref.shape[0]
    state_ref[...] = jnp.zeros_like(state_ref)

    def lap(index, carry):
        for head in range(H):
            to_end, key_mix, value_mix, whole = wire_parts(wire_ref, index, head, count)
            state = state_ref[head]
            pseudo = value_mix.astype(jnp.float32) - wire_mm(key_mix, state, ((1,), (0,)))
            state_ref[head] = whole * state + wire_mm(to_end, pseudo, ((0,), (0,)))
        return carry

    lax.fori_loop(0, place_ref[0], lap, 0)
    rows, cols = iotas(count)
    for head in range(H):
        query = query_ref[:, head * DK : (head + 1) * DK]
        keys = keys_ref[:, head * DK : (head + 1) * DK]
        span = slice(head * DV, (head + 1) * DV)
        beta = beta_ref[:, head : head + 1]
        matrix, grown, to_end, whole = decay_terms(decay_ref[:, head : head + 1], rows, cols)
        key_mix, value_mix = own_mix(inverse_ref[head], keys, values_ref[:, span], beta, grown)
        state = state_ref[head]
        pseudo = value_mix - mm(key_mix, state)
        mixed = mm(query * grown, state) + mm(mm_nt(query, keys) * matrix, pseudo)
        scale = lax.rsqrt(jnp.mean(mixed * mixed, axis=-1, keepdims=True) + EPSILON)
        gated, unused = silu_pair(gate_ref[:, span])
        head_out_ref[:, span] = (mixed * scale * gain_ref[...] * gated).astype(jnp.bfloat16)
        mixed_ref[:, span] = mixed
        pseudo_ref[:, span] = pseudo


def backward_local(
    grad_ref, mixed_ref, query_ref, keys_ref, values_ref, inverse_ref, beta_ref, decay_ref,
    gate_ref, gain_ref, local_ref, grad_mixed_ref, grad_gate_ref, grad_gain_ref,
):
    count = query_ref.shape[0]
    rows, cols = iotas(count)
    gain_total = jnp.zeros((1, DV), jnp.float32)
    for head in range(H):
        query = query_ref[:, head * DK : (head + 1) * DK]
        keys = keys_ref[:, head * DK : (head + 1) * DK]
        span = slice(head * DV, (head + 1) * DV)
        mixed = mixed_ref[:, span]
        grad = grad_ref[:, span]
        scale = lax.rsqrt(jnp.mean(mixed * mixed, axis=-1, keepdims=True) + EPSILON)
        plain = mixed * scale
        gated, slope = silu_pair(gate_ref[:, span])
        grad_gate_ref[:, span] = (grad * plain * gain_ref[...] * slope).astype(grad_gate_ref.dtype)
        grad_normed = grad * gated
        gain_total = gain_total + jnp.sum(grad_normed * plain, axis=0, keepdims=True)
        pulled = grad_normed * gain_ref[...]
        grad_mixed = scale * (pulled - plain * jnp.mean(pulled * plain, axis=-1, keepdims=True))
        grad_mixed_ref[:, span] = grad_mixed
        beta = beta_ref[:, head : head + 1]
        matrix, grown, to_end, whole = decay_terms(decay_ref[:, head : head + 1], rows, cols)
        key_mix = mm(inverse_ref[head], keys * (beta * grown))
        grad_pseudo = mm_tn(mm_nt(query, keys) * matrix, grad_mixed)
        local = mm_tn(query * grown, grad_mixed) - mm_tn(key_mix, grad_pseudo)
        local_ref[head * DK : (head + 1) * DK, :] = local.astype(jnp.bfloat16)
    grad_gain_ref[...] = gain_total


def backward_chain(
    place_ref, wire_ref, local_ref, query_ref, keys_ref, values_ref, inverse_ref, beta_ref,
    decay_ref, state_ref, pseudo_ref, grad_mixed_ref, projected_ref, border_ref, taps_ref,
    grad_conv_ref, grad_border_ref, grad_taps_ref, grad_beta_ref, grad_decay_ref,
    after_ref, extended_ref, padded_ref,
):
    count = query_ref.shape[0]
    width = taps_ref.shape[1]
    devices = wire_ref.shape[0]
    after_ref[...] = jnp.zeros_like(after_ref)

    def lap(step, carry):
        index = devices - 1 - step
        for head in range(H):
            to_end, key_mix, value_mix, whole = wire_parts(wire_ref, index, head, count)
            after = after_ref[head]
            inner = wire_mm(to_end, after, ((1,), (0,)))
            local = local_ref[index, head * DK : (head + 1) * DK, :].astype(jnp.float32)
            after_ref[head] = whole * after - wire_mm(key_mix, inner, ((0,), (0,))) + local
        return carry

    lax.fori_loop(0, devices - 1 - place_ref[0], lap, 0)
    extended_ref[0:8, :] = border_ref[...]
    extended_ref[pl.ds(8, count), :] = projected_ref[:, :width]
    taps = taps_ref[...]
    summed = conv_sum(extended_ref, taps, count)
    activated, slope = silu_pair(summed)
    padded_ref[0:8, :] = jnp.zeros((8, width), jnp.float32)
    padded_ref[pl.ds(8 + count, 8), :] = jnp.zeros((8, width), jnp.float32)
    rows, cols = iotas(count)
    lower = rows >= cols
    strict = rows > cols
    lanes = lax.broadcasted_iota(jnp.int32, (count, 128), 1)
    beta_out = jnp.zeros((count, 128), jnp.float32)
    cumulative_out = jnp.zeros((count, 128), jnp.float32)
    row_column = lax.broadcasted_iota(jnp.int32, (count, 1), 0)
    for head in range(H):
        query = query_ref[:, head * DK : (head + 1) * DK]
        keys = keys_ref[:, head * DK : (head + 1) * DK]
        span = slice(head * DV, (head + 1) * DV)
        values = values_ref[:, span]
        beta = beta_ref[:, head : head + 1]
        matrix, grown, to_end, whole = decay_terms(decay_ref[:, head : head + 1], rows, cols)
        inverse = inverse_ref[head]
        state = state_ref[head]
        after = after_ref[head]
        pseudo = pseudo_ref[:, span]
        grad_mixed = grad_mixed_ref[:, span]
        keys_grown = keys * (beta * grown)
        key_mix = mm(inverse, keys_grown)
        value_mix = mm(inverse, values * beta)
        gram = mm_nt(keys, keys)
        system = jnp.where(strict, beta * gram * matrix, 0.0)
        scores = mm_nt(query, keys) * matrix
        keys_end = keys * to_end
        query_grown = query * grown
        grad_query_grown = mm_nt(grad_mixed, state)
        grad_scores = jnp.where(lower, mm_nt(grad_mixed, pseudo), 0.0)
        grad_pseudo = mm_tn(scores, grad_mixed) + mm(keys_end, after)
        grad_keys_end = mm_nt(pseudo, after)
        grad_whole = jnp.sum(jnp.sum(after * state, axis=1, keepdims=True), axis=0, keepdims=True)
        grad_value_in = mm_tn(inverse, grad_pseudo)
        grad_key_in = mm_tn(inverse, -mm_nt(grad_pseudo, state))
        grad_system = -jnp.where(
            strict, mm_nt(grad_value_in, value_mix) + mm_nt(grad_key_in, key_mix), 0.0
        )
        grad_raw = grad_scores * matrix
        grad_query = mm(grad_raw, keys) + grad_query_grown * grown
        grad_keys = mm_tn(grad_raw, query)
        weighted = grad_system * matrix
        grad_beta = jnp.sum(weighted * gram, axis=1, keepdims=True)
        grad_gram = weighted * beta
        grad_keys = grad_keys + mm(grad_gram, keys) + mm_tn(grad_gram, keys)
        spread = grad_scores * scores + grad_system * system
        grad_cumulative = jnp.sum(spread, axis=1, keepdims=True)
        across = jnp.sum(spread, axis=0, keepdims=True)
        grad_cumulative = grad_cumulative - jnp.sum(
            jnp.where(rows == cols, across, 0.0), axis=1, keepdims=True
        )
        grad_keys = grad_keys + grad_key_in * (beta * grown)
        through = jnp.sum(grad_key_in * keys, axis=1, keepdims=True) * grown
        grad_beta = grad_beta + through + jnp.sum(grad_value_in * values, axis=1, keepdims=True)
        grad_cumulative = grad_cumulative + through * beta
        grad_values = grad_value_in * beta
        grad_cumulative = grad_cumulative + jnp.sum(
            grad_query_grown * query_grown, axis=1, keepdims=True
        )
        grad_keys = grad_keys + grad_keys_end * to_end
        ending = jnp.sum(grad_keys_end * keys_end, axis=1, keepdims=True)
        final = jnp.sum(ending, axis=0, keepdims=True) + whole * grad_whole
        grad_cumulative = grad_cumulative - ending + jnp.where(row_column == count - 1, final, 0.0)
        beta_out = jnp.where(lanes == head, grad_beta, beta_out)
        cumulative_out = jnp.where(lanes == head, grad_cumulative, cumulative_out)
        key_part = activated[:, (H + head) * DK : (H + head + 1) * DK]
        key_scale = unit_rows(key_part)
        query_part = activated[:, head * DK : (head + 1) * DK]
        query_scale = unit_rows(query_part)
        factor = DK ** (-0.5)
        grad_query_part = (factor * query_scale) * (
            grad_query
            - query_part
            * (query_scale * query_scale)
            * jnp.sum(grad_query * query_part, axis=-1, keepdims=True)
        )
        grad_key_part = key_scale * (
            grad_keys
            - key_part
            * (key_scale * key_scale)
            * jnp.sum(grad_keys * key_part, axis=-1, keepdims=True)
        )
        spots = (head * DK, (H + head) * DK, 2 * H * DK + head * DV)
        for spot, grad in zip(spots, (grad_query_part, grad_key_part, grad_values)):
            size = grad.shape[1]
            padded_ref[pl.ds(8, count), spot : spot + size] = grad * slope[:, spot : spot + size]
    grad_beta_ref[...] = beta_out
    grad_decay_ref[...] = mm_tn(jnp.where(lower, 1.0, 0.0), cumulative_out)
    conv_total = jnp.zeros((count, width), jnp.float32)
    border_total = jnp.zeros((8, width), jnp.float32)
    summed_grad = padded_ref[pl.ds(8, count), :]
    tap_rows = lax.broadcasted_iota(jnp.int32, (8, width), 0)
    taps_total = jnp.zeros((8, width), jnp.float32)
    for tap in range(CONV):
        shift = CONV - 1 - tap
        conv_total = conv_total + taps[tap : tap + 1] * padded_ref[pl.ds(8 + shift, count), :]
        border_total = border_total + taps[tap : tap + 1] * padded_ref[pl.ds(shift, 8), :]
        piece = jnp.sum(
            summed_grad * extended_ref[pl.ds(8 - (CONV - 1) + tap, count), :],
            axis=0,
            keepdims=True,
        )
        taps_total = jnp.where(tap_rows == tap, piece, taps_total)
    grad_conv_ref[...] = conv_total
    grad_border_ref[...] = border_total
    grad_taps_ref[...] = taps_total


def fused(body, outputs, scratch=(), scalars=0, cost=(0, 0), label=None):
    def call(*args):
        vmem = pl.BlockSpec(memory_space=pltpu.VMEM)
        smem = pl.BlockSpec(memory_space=pltpu.SMEM)
        return pl.pallas_call(
            body,
            out_shape=outputs,
            in_specs=[smem] * scalars + [vmem] * (len(args) - scalars),
            out_specs=[vmem] * len(outputs),
            scratch_shapes=list(scratch),
            compiler_params=pltpu.CompilerParams(vmem_limit_bytes=60 * 2**20),
            cost_estimate=pl.CostEstimate(
                flops=cost[0], bytes_accessed=cost[1], transcendentals=0
            ),
            name=label,
        )(*args)

    return call


def gates(gate_logits, a_log, dt_bias):
    beta = jax.nn.sigmoid(gate_logits[:, :H])
    decay = -jnp.exp(a_log) * jax.nn.softplus(gate_logits[:, H:] + dt_bias)
    return beta, decay


def scatter_rows(pieces):
    outer, inner = lax.axis_size("dp"), lax.axis_size("ctx")
    whole = jnp.concatenate([piece.astype(jnp.bfloat16) for piece in pieces], axis=0)
    lane = math.gcd(whole.size // (outer * inner), D)
    blocks = whole.reshape(outer, inner, -1, lane)
    part = lax.psum_scatter(blocks, "ctx", scatter_dimension=1, tiled=False)
    own = lax.psum_scatter(part, "dp", scatter_dimension=0, tiled=False)
    return own.astype(jnp.float32).reshape(-1)


MESH = pl.DeviceIdType.MESH


class Place:
    def __init__(self, side):
        self.deep = lax.axis_size("dp")
        self.side = side
        self.ctx = lax.axis_size("ctx")
        self.z = lax.axis_index("dp")
        spot = lax.axis_index("ctx")
        self.c = lax.rem(spot, 2)
        chip = lax.div(spot, 2)
        self.x = lax.rem(chip, side)
        self.y = lax.div(chip, side)
        self.other_core = self.device(self.z, self.y, self.x, 1 - self.c)
        self.other_x = self.device(self.z, self.y, 1 - self.x, self.c)
        self.other_y = self.device(self.z, 1 - self.y, self.x, self.c)
        self.next_z = self.device(self.along(1), self.y, self.x, self.c)
        self.spot = spot
        self.before = (self.z, lax.rem(spot + self.ctx - 1, self.ctx))
        self.behind = (self.z, lax.rem(spot + 1, self.ctx))

    def along(self, step):
        return lax.rem(self.z + step + self.deep, self.deep)

    def device(self, z, y, x, c):
        return (z, (y * self.side + x) * 2 + c)

    def block(self, z, y, x, c):
        return z * self.ctx + (y * self.side + x) * 2 + c

    def enter(self, all_z=False, more=()):
        barrier = pltpu.get_barrier_semaphore()
        steps = range(1, self.deep) if all_z else (-1,)
        friends = [self.other_core, self.other_x, self.other_y, *more]
        friends += [self.device(self.along(step), self.y, self.x, self.c) for step in steps]
        for friend in friends:
            pl.semaphore_signal(barrier, inc=1, device_id=friend, device_id_type=MESH)
        pl.semaphore_wait(barrier, len(friends))


class Copies:
    def __init__(self, send_sems, recv_sems, local_sems=None):
        self.send_sems, self.recv_sems, self.local_sems = send_sems, recv_sems, local_sems
        self.sent, self.locals = [], 0

    def push(self, source, target, device):
        index = len(self.sent)
        copy = pltpu.make_async_remote_copy(
            src_ref=source,
            dst_ref=target,
            send_sem=self.send_sems.at[index],
            recv_sem=self.recv_sems.at[index],
            device_id=device,
            device_id_type=MESH,
        )
        copy.start()
        self.sent.append(copy)
        return copy

    def local(self, source, target):
        copy = pltpu.make_async_copy(source, target, self.local_sems.at[self.locals])
        copy.start()
        self.locals += 1
        return copy

    def finish(self):
        for copy in self.sent:
            copy.wait_send()


def upper(rows):
    return rows // 2 // 16 * 16


def gather_steps(place, copies, shard_ref, out_ref, plane=False):
    rows, deep = shard_ref.shape[0], 1 if plane else place.deep
    top = upper(rows)
    spans = {None: (0, rows), 0: (0, top), 1: (top, rows - top)}
    ring, near, far, core = [], {}, {}, []

    def cut(ref, start, part):
        offset, size = spans[part]
        return ref.at[pl.ds(pl.multiple_of(start + offset, 16), size), :]

    def start_of(rel, dy, dx):
        y = 1 - place.y if dy else place.y
        x = 1 - place.x if dx else place.x
        z = 0 if plane else place.along(-rel)
        return place.block(z, y, x, place.c) * rows

    def forward(rel, dy, dx, part, device):
        start = start_of(rel, dy, dx)
        own = rel == 0 and not dy and not dx
        source = cut(shard_ref, 0, part) if own else cut(out_ref, start, part)
        return copies.push(source, cut(out_ref, start, part), device)

    def spread(rel):
        if rel < deep - 1:
            ring.append(forward(rel, 0, 0, None, place.next_z))
        near[rel, "x0"] = forward(rel, 0, 0, 0, place.other_x)
        near[rel, "y1"] = forward(rel, 0, 0, 1, place.other_y)
        near[rel, "y0"] = forward(rel, 0, 0, 0, place.other_y)
        near[rel, "x1"] = forward(rel, 0, 0, 1, place.other_x)
        core.append(forward(rel, 0, 0, None, place.other_core))

    def second(rel):
        near[rel, "x0"].wait_recv()
        far[rel, 0] = forward(rel, 0, 1, 0, place.other_y)
        near[rel, "y1"].wait_recv()
        far[rel, 1] = forward(rel, 1, 0, 1, place.other_x)
        core.append(forward(rel, 0, 1, 0, place.other_core))
        core.append(forward(rel, 1, 0, 1, place.other_core))

    def third(rel):
        near[rel, "y0"].wait_recv()
        core.append(forward(rel, 1, 0, 0, place.other_core))
        near[rel, "x1"].wait_recv()
        core.append(forward(rel, 0, 1, 1, place.other_core))

    def fourth(rel):
        for part in (0, 1):
            far[rel, part].wait_recv()
            core.append(forward(rel, 1, 1, part, place.other_core))

    own_copy = []

    def first():
        own_copy.append(copies.local(shard_ref, cut(out_ref, start_of(0, 0, 0), None)))
        spread(0)

    def later(rel):
        ring[rel - 1].wait_recv()
        spread(rel)

    def last():
        for copy in core:
            copy.wait_recv()
        own_copy[0].wait()

    steps = [first]
    for rel in range(1, deep):
        steps.append(lambda rel=rel: later(rel))
        steps.append(lambda rel=rel: second(rel - 1))
        steps.append(lambda rel=rel: third(rel - 1))
    steps.append(lambda: second(deep - 1))
    steps.append(lambda: third(deep - 1))
    for rel in range(deep):
        steps.append(lambda rel=rel: fourth(rel))
    steps.append(last)
    return steps


def wide(value):
    return value.astype(jnp.float32)


class Scatter:
    def __init__(self, place, copies, grad_ref, held, from_core, first_x, first_y, last_x, last_y, from_z):
        self.place, self.copies, self.grad = place, copies, grad_ref
        self.held, self.from_core, self.from_z = held, from_core, from_z
        self.first = {0: first_y, 1: first_x}
        self.last = {0: last_x, 1: last_y}
        self.rows = held.shape[1]
        self.top = upper(self.rows)
        self.loads, self.cores, self.near, self.far, self.ring = {}, {}, {}, {}, {}

    @staticmethod
    def scratch(deep, rows):
        top = upper(rows)
        low = rows - top
        return [
            pltpu.VMEM((4 * deep, rows, D), jnp.bfloat16),
            pltpu.VMEM((4 * deep, rows, D), jnp.bfloat16),
            pltpu.VMEM((2 * deep, low, D), jnp.bfloat16),
            pltpu.VMEM((2 * deep, top, D), jnp.bfloat16),
            pltpu.VMEM((deep, top, D), jnp.bfloat16),
            pltpu.VMEM((deep, low, D), jnp.bfloat16),
            pltpu.VMEM((deep - 1, rows, D), jnp.bfloat16),
        ]

    @staticmethod
    def copies_of(deep):
        return 4 * deep + 4 * deep + 2 * deep + deep - 1

    def slot(self, rel, dy, dx):
        return (rel - 1) * 4 + dy * 2 + dx

    def span(self, part):
        return pl.ds(0, self.top) if part == 0 else pl.ds(self.top, self.rows - self.top)

    def load(self):
        place = self.place
        for rel in range(1, place.deep + 1):
            for dy, dx in ((1, 1), (1, 0), (0, 1), (0, 0)):
                y = 1 - place.y if dy else place.y
                x = 1 - place.x if dx else place.x
                slot = self.slot(rel, dy, dx)

                def rows_of(core):
                    start = place.block(place.along(-rel), y, x, core) * self.rows
                    return self.grad.at[pl.ds(pl.multiple_of(start, 16), self.rows), :]

                self.cores[slot] = self.copies.push(
                    rows_of(1 - place.c), self.from_core.at[slot], place.other_core
                )
                self.loads[slot] = self.copies.local(rows_of(place.c), self.held.at[slot])

    def stage_one(self, rel):
        place = self.place
        for dy, dx in ((1, 1), (1, 0), (0, 1), (0, 0)):
            slot = self.slot(rel, dy, dx)
            self.loads[slot].wait()
            self.cores[slot].wait_recv()
            self.held[slot] = (wide(self.held[slot]) + wide(self.from_core[slot])).astype(jnp.bfloat16)
            if dy:
                self.near[rel, 0, dx] = self.copies.push(
                    self.held.at[slot, self.span(0), :],
                    self.first[0].at[(rel - 1) * 2 + dx],
                    place.other_y,
                )
            if dx:
                self.near[rel, 1, dy] = self.copies.push(
                    self.held.at[slot, self.span(1), :],
                    self.first[1].at[(rel - 1) * 2 + dy],
                    place.other_x,
                )

    def add(self, slot, part, piece):
        self.held[slot, self.span(part), :] = (
            wide(self.held[slot, self.span(part), :]) + wide(piece)
        ).astype(jnp.bfloat16)

    def stage_two(self, rel):
        place = self.place
        for part in (0, 1):
            for away in (1, 0):
                self.near[rel, part, away].wait_recv()
                slot = self.slot(rel, away, 0) if part else self.slot(rel, 0, away)
                self.add(slot, part, self.first[part][(rel - 1) * 2 + away])
                if away:
                    self.far[rel, part] = self.copies.push(
                        self.held.at[slot, self.span(part), :],
                        self.last[part].at[rel - 1],
                        place.other_y if part else place.other_x,
                    )

    def stage_three(self, rel, total_ref=None):
        slot = self.slot(rel, 0, 0)
        for part in (0, 1):
            self.far[rel, part].wait_recv()
            self.add(slot, part, self.last[part][rel - 1])
        if rel >= 2:
            self.ring[rel - 1].wait_recv()
            total = wide(self.held[slot]) + wide(self.from_z[rel - 2])
            if rel == self.place.deep:
                total_ref[...] = total
                return
            self.held[slot] = total.astype(jnp.bfloat16)
        self.ring[rel] = self.copies.push(
            self.held.at[slot], self.from_z.at[rel - 1], self.place.next_z
        )

    def steps(self, total_ref):
        deep = self.place.deep
        out = [self.load]
        for turn in range(1, deep + 3):
            if turn <= deep:
                out.append(lambda rel=turn: self.stage_one(rel))
            if 1 <= turn - 1 <= deep:
                out.append(lambda rel=turn - 1: self.stage_two(rel))
            if 1 <= turn - 2 <= deep:
                out.append(lambda rel=turn - 2: self.stage_three(rel, total_ref))
        return out


class Everywhere:
    def __init__(self, place, copies, total, slots, stack):
        self.place, self.copies = place, copies
        self.total, self.slots, self.stack = total, slots, stack
        self.turns = (place.other_core, place.other_x, place.other_y)
        self.pending = []

    @staticmethod
    def scratch(deep, rows, width):
        return [pltpu.VMEM((count, rows, width), jnp.float32) for count in (3, deep, 4)]

    def send(self, turn):
        self.pending = [
            self.copies.push(self.total.at[turn], self.slots.at[turn], self.turns[turn])
        ]

    def take(self, turn):
        self.pending[0].wait_recv()
        self.total[turn + 1] = self.total[turn] + self.slots[turn]

    def send_z(self):
        place = self.place
        self.pending = [
            self.copies.push(
                self.total.at[3],
                self.stack.at[place.z],
                place.device(place.along(step), place.y, place.x, place.c),
            )
            for step in range(1, place.deep)
        ]
        self.stack[place.z] = self.total[3]

    def take_z(self):
        for copy in self.pending:
            copy.wait_recv()
        result = self.stack[0]
        for index in range(1, self.place.deep):
            result = result + self.stack[index]
        return result

    def run(self):
        for turn in range(3):
            self.send(turn)
            self.take(turn)
        self.send_z()
        return self.take_z()


def gather_copies(deep):
    return (deep - 1) + 4 * deep + 2 * deep + deep + 2 * deep * 3


def front_parts(ext_ref, taps_ref, beta_ref, decay_ref, wire_ref, query_ref, keys_ref, values_ref, inverse_ref):
    count = query_ref.shape[0]
    width = taps_ref.shape[1]
    summed = ext_sum(ext_ref, taps_ref[...], count, 0, width)
    activated = summed * jax.nn.sigmoid(summed)
    rows, cols = iotas(count)
    for head in range(H):
        query_part = activated[:, head * DK : (head + 1) * DK]
        key_part = activated[:, (H + head) * DK : (H + head + 1) * DK]
        start = 2 * H * DK + head * DV
        values = activated[:, start : start + DV]
        query = query_part * unit_rows(query_part) * DK ** (-0.5)
        keys = key_part * unit_rows(key_part)
        beta = beta_ref[:, head : head + 1]
        matrix, grown, to_end, whole = decay_terms(decay_ref[:, head : head + 1], rows, cols)
        system = jnp.where(rows > cols, beta * mm_nt(keys, keys) * matrix, 0.0)
        inverse = unit_inverse(system, rows, cols)
        key_mix = mm(inverse, keys * (beta * grown))
        value_mix = mm(inverse, values * beta)
        base = head * (2 * DK + DV)
        wire_ref[0:count, base : base + DK] = (keys * to_end).astype(jnp.bfloat16)
        wire_ref[0:count, base + DK : base + 2 * DK] = key_mix.astype(jnp.bfloat16)
        wire_ref[0:count, base + 2 * DK : base + 2 * DK + DV] = value_mix.astype(jnp.bfloat16)
        high, low = halves(jnp.broadcast_to(whole, (PAD, 2 * DK + DV)))
        first = lax.broadcasted_iota(jnp.int32, (PAD, 2 * DK + DV), 0) < 8
        tail = jnp.where(first, high.astype(jnp.float32), low.astype(jnp.float32))
        wire_ref[pl.ds(count, PAD), base : base + 2 * DK + DV] = tail.astype(jnp.bfloat16)
        query_ref[:, head * DK : (head + 1) * DK] = query
        keys_ref[:, head * DK : (head + 1) * DK] = keys
        values_ref[:, head * DV : (head + 1) * DV] = values
        inverse_ref[head] = inverse
        yield


def ext_sum(ext_ref, taps, count, start, size):
    total = None
    for tap in range(CONV):
        piece = (
            taps[tap : tap + 1, start : start + size]
            * ext_ref[pl.ds(8 - (CONV - 1) + tap, count), start : start + size]
        )
        total = piece if total is None else total + piece
    return total


def front_kernel(
    side, mix_shard, ffn_shard, normed_ref, taps_ref, beta_ref, decay_ref,
    mix_out, ffn_out, wires_out, ext_ref, gate_ref, query_ref, keys_ref, values_ref, inverse_ref,
    weight_ref, wire_ref, send_sems, recv_sems, local_sems,
):
    place = Place(side)
    copies = Copies(send_sems, recv_sems, local_sems)
    place.enter()
    mix = gather_steps(place, copies, mix_shard, mix_out)
    ffn = gather_steps(place, copies, ffn_shard, ffn_out)
    early = 3 * (place.deep - 1) + 2
    for step in mix[:early]:
        step()
    ffn.pop(0)()
    for step in mix[early:]:
        step()
    depth = weight_ref.shape[0]
    chunk = DV
    loads = [
        copies.local(mix_out.at[pl.ds(start, chunk), :], weight_ref.at[pl.ds(start, chunk), :])
        for start in range(0, depth, chunk)
    ]
    for index, load in enumerate(loads):
        load.wait()
        span = pl.ds(index * chunk, chunk)
        piece = lax.dot_general(
            normed_ref[...], weight_ref[span, :], (((1,), (1,)), ((), ())),
            preferred_element_type=jnp.float32,
        )
        start = index * chunk
        if start < ext_ref.shape[1]:
            ext_ref[:, start : start + chunk] = piece[8:]
        else:
            start = start - ext_ref.shape[1]
            gate_ref[:, start : start + chunk] = piece[PAD:]
        if index % 2 == 1:
            ffn.pop(0)()
    parts = front_parts(
        ext_ref, taps_ref, beta_ref, decay_ref, wire_ref, query_ref, keys_ref, values_ref, inverse_ref
    )
    for unused in parts:
        for again in range(3):
            ffn.pop(0)()
    wires = gather_steps(place, copies, wire_ref, wires_out, plane=True)
    wires.pop(0)()
    ffn.pop(0)()
    while wires[1:]:
        wires.pop(0)()
        if len(ffn) > 1:
            ffn.pop(0)()
    for step in ffn + wires:
        step()
    copies.finish()


def front(mix_shard, ffn_shard, normed, taps, beta, decay, side, tag):
    f32 = jnp.float32
    deep, ctx = lax.axis_size("dp"), lax.axis_size("ctx")
    count = beta.shape[0]
    everyone = deep * ctx
    number = 2 * gather_copies(deep) + gather_copies(1)
    anywhere = pl.BlockSpec(memory_space=pl.ANY)
    vmem = pl.BlockSpec(memory_space=pltpu.VMEM)
    depth = 2 * H * DK + 2 * H * DV
    return pl.pallas_call(
        functools.partial(front_kernel, side),
        out_shape=[
            jax.ShapeDtypeStruct((everyone * mix_shard.shape[0], D), jnp.bfloat16),
            jax.ShapeDtypeStruct((everyone * ffn_shard.shape[0], D), jnp.bfloat16),
            jax.ShapeDtypeStruct((ctx * (count + PAD), H * (2 * DK + DV)), jnp.bfloat16),
            jax.ShapeDtypeStruct((count + 8, depth - H * DV), f32),
            jax.ShapeDtypeStruct((count, H * DV), f32),
            jax.ShapeDtypeStruct((count, H * DK), f32),
            jax.ShapeDtypeStruct((count, H * DK), f32),
            jax.ShapeDtypeStruct((count, H * DV), f32),
            jax.ShapeDtypeStruct((H, count, count), f32),
        ],
        in_specs=[anywhere] * 2 + [vmem] * 4,
        out_specs=[anywhere] * 3 + [vmem] * 6,
        scratch_shapes=[
            pltpu.VMEM((depth, D), jnp.bfloat16),
            pltpu.VMEM((count + PAD, H * (2 * DK + DV)), jnp.bfloat16),
            pltpu.SemaphoreType.DMA((number,)),
            pltpu.SemaphoreType.DMA((number,)),
            pltpu.SemaphoreType.DMA((3 + depth // DV,)),
        ],
        compiler_params=pltpu.CompilerParams(
            collective_id=tag, has_side_effects=True, vmem_limit_bytes=60 * 2**20
        ),
        cost_estimate=pl.CostEstimate(flops=0, bytes_accessed=10**8, transcendentals=0),
        name="front",
    )(mix_shard, ffn_shard, normed, taps, beta, decay)


def dot_nn(a, b):
    return lax.dot_general(a, b, (((1,), (0,)), ((), ())), preferred_element_type=jnp.float32)


def dot_nt(a, b):
    return lax.dot_general(a, b, (((1,), (1,)), ((), ())), preferred_element_type=jnp.float32)


def dot_tn(a, b):
    return lax.dot_general(a, b, (((0,), (0,)), ((), ())), preferred_element_type=jnp.float32)


def chunk_of(rows):
    return max(size for size in range(16, 577, 16) if rows % size == 0)


def by_chunks(rows, body):
    size = chunk_of(rows)

    def turn(index, carry):
        body(pl.ds(pl.multiple_of(index * size, 16), size), index * size, size)
        return carry

    lax.fori_loop(0, rows // size, turn, 0)


def norm_back(grad, values, scale, gain):
    plain = values * scale
    pulled = grad * gain
    through = scale * (pulled - plain * jnp.mean(pulled * plain, axis=-1, keepdims=True))
    return through, jnp.sum(grad * plain, axis=0, keepdims=True)


def middle_kernel(
    rows, place_ref, wires_ref, query_ref, keys_ref, values_ref, inverse_ref, beta_ref, decay_ref,
    gate_ref, gain_head_ref, x_ref, cot_ref, gain_two_ref, mix_hbm, ffn_hbm,
    result_ref, grad_resid_ref, grad_out_ref, ffn_grad_ref, gain_two_grad_ref, state_ref, pseudo_ref,
    local_ref, grad_mixed_ref, grad_gate_ref, gain_head_grad_ref,
    w_out, w_ffn, mixed_ref, head_out_ref, pre_ref, compact_ref, down_ref, hidden_ref, total_ref,
    grad_head_ref, sems,
):
    count = query_ref.shape[0]
    padded = -(-rows // 16) * 16
    out_rows = w_out.shape[0]
    load_out = pltpu.make_async_copy(
        mix_hbm.at[pl.ds(mix_hbm.shape[0] - out_rows, out_rows), :], w_out, sems.at[0]
    )
    load_ffn = pltpu.make_async_copy(ffn_hbm, w_ffn, sems.at[1])
    load_out.start()
    load_ffn.start()
    forward_chain(
        place_ref, wires_ref, query_ref, keys_ref, values_ref, inverse_ref, beta_ref, decay_ref,
        gate_ref, gain_head_ref, head_out_ref, mixed_ref, state_ref, pseudo_ref,
    )
    load_out.wait()
    resid = x_ref[...].astype(jnp.float32) + dot_nn(head_out_ref[...], w_out[...])
    scale = lax.rsqrt(jnp.mean(resid * resid, axis=-1, keepdims=True) + EPSILON)
    normed = (resid * scale * gain_two_ref[...]).astype(jnp.bfloat16)
    load_ffn.wait()
    pairs = 2 * FF
    blocks = ffn_hbm.shape[0] // padded
    used = -(-pairs // rows)
    split = pairs // rows
    inside = pairs - split * rows
    upper_rows = used * padded
    down_start = split * padded
    down_rows = (blocks - split) * padded
    bf16 = jnp.bfloat16

    def pre(span, start, size):
        pre_ref[span, :] = dot_nt(w_ffn[span, :], normed)

    by_chunks(upper_rows, pre)
    for block in range(used):
        size = min(rows, pairs - block * rows)
        compact_ref[pl.ds(block * rows, size), :] = pre_ref[pl.ds(block * padded, size), :]
    down_ref[...] = jnp.zeros_like(down_ref)

    def pieces():
        done = 0
        for block in range(blocks - split):
            offset = inside if block == 0 else 0
            size = rows - offset
            yield done, block * padded + offset, size
            done += size

    gate = compact_ref[0:FF, :]
    up = compact_ref[FF:pairs, :]
    hidden_ref[...] = gate * jax.nn.sigmoid(gate) * up
    for done, spot, size in pieces():
        down_ref[pl.ds(spot, size), :] = hidden_ref[pl.ds(done, size), :]
    total_ref[...] = resid

    def out_chunk(span, start, size):
        here = pl.ds(pl.multiple_of(down_start + start, 16), size)
        total_ref[...] += dot_tn(down_ref[span, :].astype(bf16), w_ffn[here, :])

    by_chunks(down_rows, out_chunk)
    result_ref[...] = total_ref[...].astype(bf16)
    cot = cot_ref[...]

    def hidden_chunk(span, start, size):
        here = pl.ds(pl.multiple_of(down_start + start, 16), size)
        pre_ref[span, :] = dot_nt(w_ffn[here, :], cot)

    by_chunks(down_rows, hidden_chunk)
    for done, spot, size in pieces():
        hidden_ref[pl.ds(done, size), :] = pre_ref[pl.ds(spot, size), :]
    gate = compact_ref[0:FF, :]
    up = compact_ref[FF:pairs, :]
    active, slope = silu_pair(gate)
    grad_hidden = hidden_ref[...]
    compact_ref[0:FF, :] = grad_hidden * up * slope
    compact_ref[FF:pairs, :] = grad_hidden * active
    pre_ref[...] = jnp.zeros_like(pre_ref)
    for block in range(used):
        size = min(rows, pairs - block * rows)
        pre_ref[pl.ds(block * padded, size), :] = compact_ref[pl.ds(block * rows, size), :]
    total_ref[...] = jnp.zeros_like(total_ref)

    def mid_chunk(span, start, size):
        piece = pre_ref[span, :].astype(bf16)
        total_ref[...] += dot_tn(piece, w_ffn[span, :])
        ffn_grad_ref[span, :] = dot_nn(piece, normed).astype(bf16)

    by_chunks(upper_rows, mid_chunk)
    shared = upper_rows - down_start
    if shared:
        both = jnp.concatenate(
            [pre_ref[pl.ds(down_start, shared), :], down_ref[pl.ds(0, shared), :]], axis=1
        ).astype(bf16)
        against = jnp.concatenate([normed, cot], axis=0)
        ffn_grad_ref[pl.ds(down_start, shared), :] = dot_nn(both, against).astype(bf16)

    def down_chunk(span, start, size):
        here = pl.ds(pl.multiple_of(shared + start, 16), size)
        there = pl.ds(pl.multiple_of(upper_rows + start, 16), size)
        ffn_grad_ref[there, :] = dot_nn(down_ref[here, :].astype(bf16), cot).astype(bf16)

    by_chunks(down_rows - shared, down_chunk)
    resid = x_ref[...].astype(jnp.float32) + dot_nn(head_out_ref[...], w_out[...])
    through, gain_two_grad_ref[...] = norm_back(total_ref[...], resid, scale, gain_two_ref[...])
    grad_resid = cot.astype(jnp.float32) + through
    grad_resid_ref[...] = grad_resid
    resid_half = grad_resid.astype(bf16)
    grad_out_ref[...] = dot_tn(head_out_ref[...], resid_half).astype(bf16)
    grad_head_ref[...] = dot_nt(resid_half, w_out[...])
    backward_local(
        grad_head_ref, mixed_ref, query_ref, keys_ref, values_ref, inverse_ref, beta_ref, decay_ref,
        gate_ref, gain_head_ref, local_ref, grad_mixed_ref, grad_gate_ref, gain_head_grad_ref,
    )


def middle(rows, place, wires, query, keys, values, inverse, beta, decay, gate, gain_head, x, cot, gain_two, mix, ffn):
    f32, bf16 = jnp.float32, jnp.bfloat16
    count = query.shape[0]
    padded = -(-rows // 16) * 16
    blocks = ffn.shape[0] // padded
    used, split = -(-2 * FF // rows), 2 * FF // rows
    out_rows = H * DV
    vmem = pl.BlockSpec(memory_space=pltpu.VMEM)
    anywhere = pl.BlockSpec(memory_space=pl.ANY)
    return pl.pallas_call(
        functools.partial(middle_kernel, rows),
        out_shape=[
            jax.ShapeDtypeStruct((count, D), bf16),
            jax.ShapeDtypeStruct((count, D), f32),
            jax.ShapeDtypeStruct((out_rows, D), bf16),
            jax.ShapeDtypeStruct(ffn.shape, bf16),
            jax.ShapeDtypeStruct((1, D), f32),
            jax.ShapeDtypeStruct((H, DK, DV), f32),
            jax.ShapeDtypeStruct((count, H * DV), f32),
            jax.ShapeDtypeStruct((H * DK, DV), bf16),
            jax.ShapeDtypeStruct((count, H * DV), f32),
            jax.ShapeDtypeStruct((count, H * DV), bf16),
            jax.ShapeDtypeStruct((1, DV), f32),
        ],
        in_specs=[pl.BlockSpec(memory_space=pltpu.SMEM)] + [vmem] * 12 + [anywhere] * 2,
        out_specs=[vmem] * 11,
        scratch_shapes=[
            pltpu.VMEM((out_rows, D), bf16),
            pltpu.VMEM(ffn.shape, bf16),
            pltpu.VMEM((count, H * DV), f32),
            pltpu.VMEM((count, H * DV), bf16),
            pltpu.VMEM((used * padded, count), f32),
            pltpu.VMEM((2 * FF, count), f32),
            pltpu.VMEM(((blocks - split) * padded, count), f32),
            pltpu.VMEM((FF, count), f32),
            pltpu.VMEM((count, D), f32),
            pltpu.VMEM((count, H * DV), f32),
            pltpu.SemaphoreType.DMA((2,)),
        ],
        compiler_params=pltpu.CompilerParams(vmem_limit_bytes=60 * 2**20),
        cost_estimate=pl.CostEstimate(flops=10**10, bytes_accessed=5 * 10**7, transcendentals=0),
        name="middle",
    )(place, wires, query, keys, values, inverse, beta, decay, gate, gain_head, x, cot, gain_two, mix, ffn)


SMALL_ROWS = 24


def back_kernel(
    side, wires_ref, local_ref, query_ref, keys_ref, values_ref, inverse_ref, beta_ref, decay_ref,
    state_ref, pseudo_ref, grad_mixed_ref, ext_ref, taps_ref, grad_gate_ref, grad_resid_ref, x_ref,
    normed_ref, gain_one_ref, factor_ref, decay_lanes_ref, w_gates_ref, gain_two_grad_ref,
    gain_head_grad_ref, ffn_grad, grad_out, mix_hbm,
    ffn_total, mix_total, grad_input_ref, small_out, squares_out,
    *scratch,
):
    scratch = list(scratch)
    take = lambda number: [scratch.pop(0) for unused in range(number)]
    after_ref, padded_ref, locals_ref, border_ref, taps_grad_ref = take(5)
    grad_beta_ref, grad_decay_ref, proj_ref, mix_grad, weight_ref, total_ref, arrived_ref = take(7)
    ffn_scratch, mix_scratch, small_scratch, square_scratch = take(7), take(6), take(3), take(3)
    send_sems, recv_sems, local_sems, weight_sems, free_sem = scratch
    mix_scratch.insert(1, ffn_scratch[1].at[:, pl.ds(0, mix_total.shape[0]), :])
    f32, bf16 = jnp.float32, jnp.bfloat16
    place = Place(side)
    copies = Copies(send_sems, recv_sems, local_sems)
    place.enter(all_z=True, more=(place.behind,))
    count, width = query_ref.shape[0], taps_ref.shape[1]
    depth = proj_ref.shape[1]
    conv_ref = padded_ref.at[pl.ds(8, count), :]
    scatter = Scatter(place, copies, ffn_grad, *ffn_scratch)
    ffn = scatter.steps(ffn_total)
    mix = Scatter(place, copies, mix_grad, *mix_scratch).steps(mix_total)
    states = gather_steps(place, copies, local_ref, locals_ref, plane=True)
    states.pop(0)()
    ffn.pop(0)()
    own_out = copies.local(grad_out, mix_grad.at[pl.ds(depth, grad_out.shape[0]), :])
    for step in states:
        step()
        ffn.pop(0)()
    work = back_chain(
        wires_ref, locals_ref, query_ref, keys_ref, values_ref, inverse_ref, beta_ref,
        decay_ref, state_ref, pseudo_ref, grad_mixed_ref, ext_ref, taps_ref,
        conv_ref, border_ref, taps_grad_ref, grad_beta_ref, grad_decay_ref,
        after_ref, padded_ref,
    )
    for unused in work:
        ffn.pop(0)()
    border = copies.push(border_ref, arrived_ref, place.before)
    pl.semaphore_signal(free_sem, inc=1, device_id=place.other_core, device_id_type=MESH)
    grad_decay = grad_decay_ref[...]
    grad_logits = (grad_beta_ref[...] + grad_decay) * factor_ref[...]
    normed = normed_ref[...]
    proj_ref[:, width:] = grad_gate_ref[...]
    ffn.pop(0)()
    border.wait_recv()
    arrived = jnp.where(place.spot < place.ctx - 1, arrived_ref[...], 0.0)
    conv_ref[pl.ds(count - 8, 8), :] = conv_ref[pl.ds(count - 8, 8), :] + arrived
    proj_ref[:, :width] = conv_ref[...].astype(bf16)
    chunk = DV
    for start in range(0, depth, chunk):
        mix_grad[pl.ds(start, chunk), :] = dot_tn(proj_ref[:, start : start + chunk], normed).astype(bf16)
    own_out.wait()
    pl.semaphore_wait(free_sem, 1)
    mix.pop(0)()

    def fetch(start):
        slot = start // chunk % 2
        copy = pltpu.make_async_copy(
            mix_hbm.at[pl.ds(start, chunk), :], weight_ref.at[slot], weight_sems.at[slot]
        )
        copy.start()
        return copy

    coming = [fetch(0), fetch(chunk)]
    ffn.pop(0)()
    mix.pop(0)()
    total_ref[...] = mm(grad_logits[:, : w_gates_ref.shape[0]], w_gates_ref[...])
    for start in range(0, depth, chunk):
        coming.pop(0).wait()
        total_ref[...] += dot_nn(proj_ref[:, start : start + chunk], weight_ref[start // chunk % 2])
        if start + 2 * chunk < depth:
            coming.append(fetch(start + 2 * chunk))
    if ffn:
        ffn.pop(0)()
    mix.pop(0)()
    x = x_ref[...].astype(f32)
    scale = lax.rsqrt(jnp.mean(x * x, axis=-1, keepdims=True) + EPSILON)
    through, gain_one_grad = norm_back(total_ref[...], x, scale, gain_one_ref[...])
    grad_input_ref[...] = (grad_resid_ref[...] + through).astype(bf16)
    small = Everywhere(place, copies, small_scratch[2], *small_scratch[:2])
    sums = small.total.at[0]
    sums[...] = jnp.zeros(sums.shape, f32)
    sums[0:1, :] = gain_one_grad
    sums[1:2, :] = gain_two_grad_ref[...]
    sums[2:3, 0:DV] = gain_head_grad_ref[...]
    sums[3 : 3 + CONV, :] = taps_grad_ref[0:CONV, 0:D]
    sums[3 + CONV : 3 + 2 * CONV, :] = taps_grad_ref[0:CONV, D : 2 * D]
    sums[3 + 2 * CONV : 3 + 2 * CONV + 2 * H, :] = mm_tn(grad_logits, normed.astype(f32))[0 : 2 * H]
    last = 3 + 2 * CONV + 2 * H
    sums[last : last + 1, 0:128] = jnp.sum(grad_decay * decay_lanes_ref[...], axis=0, keepdims=True)
    lanes = lax.broadcasted_iota(jnp.int32, (1, 128), 1)
    sums[last + 1 : last + 2, 0:128] = jnp.where(
        (lanes >= H) & (lanes < 2 * H), jnp.sum(grad_logits, axis=0, keepdims=True), 0.0
    )
    small.send(0)
    extra = []
    for turn in range(3):
        extra.append(lambda turn=turn: small.take(turn))
        extra.append(lambda turn=turn: small.send(turn + 1) if turn < 2 else small.send_z())
    while mix or ffn or extra:
        for queue in (ffn, mix, extra):
            if queue:
                queue.pop(0)()
    small_total = small.take_z()
    small_out[...] = small_total
    squares = jnp.zeros((8, 128), f32)
    for total in (mix_total, ffn_total):
        value = total[...]
        line = jnp.sum(value * value, axis=0, keepdims=True)
        for start in range(0, D, 128):
            squares = squares + line[:, start : start + 128] * 0.125
    square = Everywhere(place, copies, square_scratch[2], *square_scratch[:2])
    square.total[0] = squares
    everything = square.run()
    own = jnp.sum(small_total * small_total, axis=0, keepdims=True)
    result = jnp.sum(jnp.sum(everything, axis=0, keepdims=True), axis=1, keepdims=True) + jnp.sum(
        own, axis=1, keepdims=True
    )
    squares_out[...] = jnp.broadcast_to(result, squares_out.shape)
    copies.finish()


def back(side, tag, *args):
    f32, bf16 = jnp.float32, jnp.bfloat16
    deep, ctx = lax.axis_size("dp"), lax.axis_size("ctx")
    query, ext, taps = args[2], args[11], args[12]
    ffn_grad, grad_out = args[-3], args[-2]
    count, width = query.shape[0], taps.shape[1]
    depth = width + H * DV
    everyone = deep * ctx
    rows = ffn_grad.shape[0] // everyone
    mix_rows = (depth + grad_out.shape[0]) // everyone
    number = 2 * Scatter.copies_of(deep) + gather_copies(1) + 2 * (3 + deep - 1) + 1
    vmem = pl.BlockSpec(memory_space=pltpu.VMEM)
    anywhere = pl.BlockSpec(memory_space=pl.ANY)
    return pl.pallas_call(
        functools.partial(back_kernel, side),
        out_shape=[
            jax.ShapeDtypeStruct((rows, D), f32),
            jax.ShapeDtypeStruct((mix_rows, D), f32),
            jax.ShapeDtypeStruct((count, D), bf16),
            jax.ShapeDtypeStruct((SMALL_ROWS, D), f32),
            jax.ShapeDtypeStruct((8, 128), f32),
        ],
        in_specs=[vmem] * (len(args) - 3) + [anywhere] * 3,
        out_specs=[vmem] * 5,
        scratch_shapes=[
            pltpu.VMEM((H, DK, DV), f32),
            pltpu.VMEM((count + 16, width), f32),
            pltpu.VMEM((ctx * H * DK, DV), bf16),
            pltpu.VMEM((8, width), f32),
            pltpu.VMEM((8, width), f32),
            pltpu.VMEM((count, 128), f32),
            pltpu.VMEM((count, 128), f32),
            pltpu.VMEM((count, depth), bf16),
            pltpu.VMEM((depth + grad_out.shape[0], D), bf16),
            pltpu.VMEM((2, DV, D), bf16),
            pltpu.VMEM((count, D), f32),
            pltpu.VMEM((8, width), f32),
        ]
        + Scatter.scratch(deep, rows)
        + [shape for index, shape in enumerate(Scatter.scratch(deep, mix_rows)) if index != 1]
        + Everywhere.scratch(deep, SMALL_ROWS, D)
        + Everywhere.scratch(deep, 8, 128)
        + [
            pltpu.SemaphoreType.DMA((number,)),
            pltpu.SemaphoreType.DMA((number,)),
            pltpu.SemaphoreType.DMA((8 * deep + 2,)),
            pltpu.SemaphoreType.DMA((2,)),
            pltpu.SemaphoreType.REGULAR,
        ],
        compiler_params=pltpu.CompilerParams(
            collective_id=tag, has_side_effects=True, vmem_limit_bytes=62 * 2**20
        ),
        cost_estimate=pl.CostEstimate(flops=10**10, bytes_accessed=10**8, transcendentals=0),
        name="back",
    )(*args)


def back_chain(
    wire_ref, local_ref, query_ref, keys_ref, values_ref, inverse_ref, beta_ref,
    decay_ref, state_ref, pseudo_ref, grad_mixed_ref, ext_ref, taps_ref,
    grad_conv_ref, grad_border_ref, grad_taps_ref, grad_beta_ref, grad_decay_ref,
    after_ref, padded_ref,
):
    count = query_ref.shape[0]
    width = taps_ref.shape[1]
    devices = wire_ref.shape[0]
    after_ref[...] = jnp.zeros_like(after_ref)

    def lap(step, carry):
        index = devices - 1 - step
        for head in range(H):
            to_end, key_mix, value_mix, whole = wire_parts(wire_ref, index, head, count)
            after = after_ref[head]
            inner = wire_mm(to_end, after, ((1,), (0,)))
            spot = pl.multiple_of((index * H + head) * DK, DK)
            local = local_ref[pl.ds(spot, DK), :].astype(jnp.float32)
            after_ref[head] = whole * after - wire_mm(key_mix, inner, ((0,), (0,))) + local
        return carry

    lax.fori_loop(0, devices - 1 - lax.axis_index("ctx"), lap, 0)
    yield
    taps = taps_ref[...]
    summed = ext_sum(ext_ref, taps, count, 0, width)
    activated, slope = silu_pair(summed)
    padded_ref[0:8, :] = jnp.zeros((8, width), jnp.float32)
    padded_ref[pl.ds(8 + count, 8), :] = jnp.zeros((8, width), jnp.float32)
    rows, cols = iotas(count)
    lower = rows >= cols
    strict = rows > cols
    lanes = lax.broadcasted_iota(jnp.int32, (count, 128), 1)
    beta_out = jnp.zeros((count, 128), jnp.float32)
    cumulative_out = jnp.zeros((count, 128), jnp.float32)
    row_column = lax.broadcasted_iota(jnp.int32, (count, 1), 0)
    for head in range(H):
        query = query_ref[:, head * DK : (head + 1) * DK]
        keys = keys_ref[:, head * DK : (head + 1) * DK]
        span = slice(head * DV, (head + 1) * DV)
        values = values_ref[:, span]
        beta = beta_ref[:, head : head + 1]
        matrix, grown, to_end, whole = decay_terms(decay_ref[:, head : head + 1], rows, cols)
        inverse = inverse_ref[head]
        state = state_ref[head]
        after = after_ref[head]
        pseudo = pseudo_ref[:, span]
        grad_mixed = grad_mixed_ref[:, span]
        keys_grown = keys * (beta * grown)
        key_mix = mm(inverse, keys_grown)
        value_mix = mm(inverse, values * beta)
        gram = mm_nt(keys, keys)
        system = jnp.where(strict, beta * gram * matrix, 0.0)
        scores = mm_nt(query, keys) * matrix
        keys_end = keys * to_end
        query_grown = query * grown
        grad_query_grown = mm_nt(grad_mixed, state)
        grad_scores = jnp.where(lower, mm_nt(grad_mixed, pseudo), 0.0)
        grad_pseudo = mm_tn(scores, grad_mixed) + mm(keys_end, after)
        grad_keys_end = mm_nt(pseudo, after)
        grad_whole = jnp.sum(jnp.sum(after * state, axis=1, keepdims=True), axis=0, keepdims=True)
        grad_value_in = mm_tn(inverse, grad_pseudo)
        grad_key_in = mm_tn(inverse, -mm_nt(grad_pseudo, state))
        grad_system = -jnp.where(
            strict, mm_nt(grad_value_in, value_mix) + mm_nt(grad_key_in, key_mix), 0.0
        )
        grad_raw = grad_scores * matrix
        grad_query = mm(grad_raw, keys) + grad_query_grown * grown
        grad_keys = mm_tn(grad_raw, query)
        weighted = grad_system * matrix
        grad_beta = jnp.sum(weighted * gram, axis=1, keepdims=True)
        grad_gram = weighted * beta
        grad_keys = grad_keys + mm(grad_gram, keys) + mm_tn(grad_gram, keys)
        spread = grad_scores * scores + grad_system * system
        grad_cumulative = jnp.sum(spread, axis=1, keepdims=True)
        across = jnp.sum(spread, axis=0, keepdims=True)
        grad_cumulative = grad_cumulative - jnp.sum(
            jnp.where(rows == cols, across, 0.0), axis=1, keepdims=True
        )
        grad_keys = grad_keys + grad_key_in * (beta * grown)
        through = jnp.sum(grad_key_in * keys, axis=1, keepdims=True) * grown
        grad_beta = grad_beta + through + jnp.sum(grad_value_in * values, axis=1, keepdims=True)
        grad_cumulative = grad_cumulative + through * beta
        grad_values = grad_value_in * beta
        grad_cumulative = grad_cumulative + jnp.sum(
            grad_query_grown * query_grown, axis=1, keepdims=True
        )
        grad_keys = grad_keys + grad_keys_end * to_end
        ending = jnp.sum(grad_keys_end * keys_end, axis=1, keepdims=True)
        final = jnp.sum(ending, axis=0, keepdims=True) + whole * grad_whole
        grad_cumulative = grad_cumulative - ending + jnp.where(row_column == count - 1, final, 0.0)
        beta_out = jnp.where(lanes == head, grad_beta, beta_out)
        cumulative_out = jnp.where(lanes == H + head, grad_cumulative, cumulative_out)
        key_part = activated[:, (H + head) * DK : (H + head + 1) * DK]
        key_scale = unit_rows(key_part)
        query_part = activated[:, head * DK : (head + 1) * DK]
        query_scale = unit_rows(query_part)
        factor = DK ** (-0.5)
        grad_query_part = (factor * query_scale) * (
            grad_query
            - query_part
            * (query_scale * query_scale)
            * jnp.sum(grad_query * query_part, axis=-1, keepdims=True)
        )
        grad_key_part = key_scale * (
            grad_keys
            - key_part
            * (key_scale * key_scale)
            * jnp.sum(grad_keys * key_part, axis=-1, keepdims=True)
        )
        spots = (head * DK, (H + head) * DK, 2 * H * DK + head * DV)
        for spot, grad in zip(spots, (grad_query_part, grad_key_part, grad_values)):
            size = grad.shape[1]
            padded_ref[pl.ds(8, count), spot : spot + size] = grad * slope[:, spot : spot + size]
        yield
    grad_beta_ref[...] = beta_out
    grad_decay_ref[...] = mm_tn(jnp.where(lower, 1.0, 0.0), cumulative_out)
    conv_total = jnp.zeros((count, width), jnp.float32)
    border_total = jnp.zeros((8, width), jnp.float32)
    summed_grad = padded_ref[pl.ds(8, count), :]
    tap_rows = lax.broadcasted_iota(jnp.int32, (8, width), 0)
    taps_total = jnp.zeros((8, width), jnp.float32)
    for tap in range(CONV):
        shift = CONV - 1 - tap
        conv_total = conv_total + taps[tap : tap + 1] * padded_ref[pl.ds(8 + shift, count), :]
        border_total = border_total + taps[tap : tap + 1] * padded_ref[pl.ds(shift, 8), :]
        piece = jnp.sum(
            summed_grad * ext_ref[pl.ds(8 - (CONV - 1) + tap, count), :width],
            axis=0,
            keepdims=True,
        )
        taps_total = jnp.where(tap_rows == tap, piece, taps_total)
    grad_conv_ref[...] = conv_total
    grad_border_ref[...] = border_total
    grad_taps_ref[...] = taps_total
    yield


def chip_side():
    half = lax.axis_size("ctx") // 2
    side = math.isqrt(half)
    return side if side == 2 and 2 * side * side == lax.axis_size("ctx") else 0


def adam_step(weight, grad_full, first, second, clip):
    grad_clipped = grad_full * clip
    first_new = BETA_ONE * first + (1.0 - BETA_ONE) * grad_clipped
    second_new = BETA_TWO * second + (1.0 - BETA_TWO) * grad_clipped * grad_clipped
    update = (
        first_new / CORRECT_ONE / (jnp.sqrt(second_new / CORRECT_TWO) + ADAM_EPS)
        + DECAY_RATE * weight
    )
    return (weight - LEARN_RATE * update, first_new, second_new)


def plain(
    inputs,
    cotangent,
    mixer_params,
    mixer_first,
    mixer_second,
    ffn_params,
    ffn_first,
    ffn_second,
    small_params,
    small_first,
    small_second,
):
    gain_one, gain_two, gain_head, tap_values, w_gates, a_log, dt_bias = unpack_small(small_params)
    width = tap_values.shape[1]
    mix_part = mixer_params.astype(jnp.bfloat16)
    ffn_part = ffn_params.astype(jnp.bfloat16)
    mix_whole, ffn_whole = (
        lax.all_gather(mix_part, ("dp", "ctx"), axis=0, tiled=True),
        lax.all_gather(ffn_part, ("dp", "ctx"), axis=0, tiled=True),
    )
    w_in, w_out, w_ffn, w_down = split_weights(mix_whole, ffn_whole)
    x_float = inputs[0].astype(jnp.float32)
    count = x_float.shape[0]
    normed_in = norm_scale(x_float, gain_one).astype(jnp.bfloat16)
    projected = jnp.dot(normed_in, w_in.T, preferred_element_type=jnp.float32)
    gate_logits = jnp.dot(normed_in.astype(jnp.float32), w_gates, precision=HIGHEST)
    f32 = jnp.float32
    devices = lax.axis_size("ctx")
    place = lax.axis_index("ctx").astype(jnp.int32).reshape(1)
    out_gate = projected[:, width:]
    edge = from_behind(projected[count - 8 :, :width], "ctx", 1)
    border = jnp.where(lax.broadcasted_iota(jnp.int32, (8, 1), 0) >= 8 - (CONV - 1), edge, 0.0)
    (beta, decay), pull_gates = jax.vjp(gates, gate_logits, a_log, dt_bias)
    wire, query, keys, values, inverse = fused(
        forward_parts,
        (
            jax.ShapeDtypeStruct((count + PAD, H * (2 * DK + DV)), jnp.bfloat16),
            jax.ShapeDtypeStruct((count, H * DK), f32),
            jax.ShapeDtypeStruct((count, H * DK), f32),
            jax.ShapeDtypeStruct((count, H * DV), f32),
            jax.ShapeDtypeStruct((H, count, count), f32),
        ),
        scratch=(pltpu.VMEM((count + 8, width), f32),),
        label="forward_parts",
    )(projected, border, tap_values, beta, decay)
    wires = lax.all_gather(wire, "ctx")
    gain_row = gain_head.reshape(1, DV)
    head_out, mixed, state, pseudo = fused(
        forward_chain,
        (
            jax.ShapeDtypeStruct((count, H * DV), jnp.bfloat16),
            jax.ShapeDtypeStruct((count, H * DV), f32),
            jax.ShapeDtypeStruct((H, DK, DV), f32),
            jax.ShapeDtypeStruct((count, H * DV), f32),
        ),
        scalars=1,
        label="forward_chain",
    )(place, wires, query, keys, values, inverse, beta, decay, out_gate, gain_row)
    resid = x_float + jnp.dot(head_out, w_out, preferred_element_type=jnp.float32)
    normed_mid = norm_scale(resid, gain_two).astype(jnp.bfloat16)
    ffn_pre = jnp.dot(normed_mid, w_ffn.T, preferred_element_type=jnp.float32)
    gate_part = ffn_pre[:, :FF]
    up_part = ffn_pre[:, FF:]
    hidden_act = swiglu(gate_part, up_part).astype(jnp.bfloat16)
    result = (resid + jnp.dot(hidden_act, w_down, preferred_element_type=jnp.float32)).astype(
        jnp.bfloat16
    )
    seq_grad = cotangent[0]
    grad_float = seq_grad.astype(jnp.float32)
    grad_down = jnp.dot(hidden_act.T, seq_grad, preferred_element_type=jnp.float32)
    grad_hidden = jnp.dot(seq_grad, w_down.T, preferred_element_type=jnp.float32)
    unused_one, pull_swiglu = jax.vjp(swiglu, gate_part, up_part)
    grad_gate, grad_up = pull_swiglu(grad_hidden)
    grad_pre = jnp.concatenate([grad_gate, grad_up], axis=1).astype(jnp.bfloat16)
    grad_ffn = jnp.dot(grad_pre.T, normed_mid, preferred_element_type=jnp.float32)
    grad_mid = jnp.dot(grad_pre, w_ffn, preferred_element_type=jnp.float32)
    unused_two, pull_mid = jax.vjp(norm_scale, resid, gain_two)
    grad_through, grad_gain_two = pull_mid(grad_mid)
    grad_resid = grad_float + grad_through
    resid_half = grad_resid.astype(jnp.bfloat16)
    grad_out = jnp.dot(head_out.T, resid_half, preferred_element_type=jnp.float32)
    grad_head = jnp.dot(resid_half, w_out.T, preferred_element_type=jnp.float32)
    local, grad_mixed, grad_gate_out, grad_gain_head = fused(
        backward_local,
        (
            jax.ShapeDtypeStruct((H * DK, DV), jnp.bfloat16),
            jax.ShapeDtypeStruct((count, H * DV), f32),
            jax.ShapeDtypeStruct((count, H * DV), f32),
            jax.ShapeDtypeStruct((1, DV), f32),
        ),
        label="backward_local",
    )(grad_head, mixed, query, keys, values, inverse, beta, decay, out_gate, gain_row)
    locals_all = lax.all_gather(local, "ctx")
    locals_all, grad_ffn, grad_down = lax.optimization_barrier((locals_all, grad_ffn, grad_down))
    ffn_shard = scatter_rows((grad_ffn, grad_down))
    grad_conv, grad_border, grad_taps, grad_beta, grad_decay = fused(
        backward_chain,
        (
            jax.ShapeDtypeStruct((count, width), f32),
            jax.ShapeDtypeStruct((8, width), f32),
            jax.ShapeDtypeStruct((8, width), f32),
            jax.ShapeDtypeStruct((count, 128), f32),
            jax.ShapeDtypeStruct((count, 128), f32),
        ),
        scratch=(
            pltpu.VMEM((H, DK, DV), f32),
            pltpu.VMEM((count + 8, width), f32),
            pltpu.VMEM((count + 16, width), f32),
        ),
        scalars=1,
        label="backward_chain",
    )(
        place, wires, locals_all, query, keys, values, inverse, beta, decay, state, pseudo,
        grad_mixed, projected, border, tap_values,
    )
    grad_logits, grad_alog, grad_bias = pull_gates((grad_beta[:, :H], grad_decay[:, :H]))
    returned = from_behind(grad_border, "ctx", -1)[8 - (CONV - 1) :]
    grad_conv = grad_conv.at[count - (CONV - 1) :].add(returned)
    grad_proj = jnp.concatenate([grad_conv, grad_gate_out], axis=1).astype(jnp.bfloat16)
    grad_in = jnp.dot(grad_proj.T, normed_in, preferred_element_type=jnp.float32)
    grad_normed = jnp.dot(grad_proj, w_in, preferred_element_type=jnp.float32) + jnp.dot(
        grad_logits, w_gates.T, precision=HIGHEST
    )
    grad_gates = jnp.dot(normed_in.astype(jnp.float32).T, grad_logits, precision=HIGHEST)
    unused_six, pull_in = jax.vjp(norm_scale, x_float, gain_one)
    grad_x, grad_gain_one = pull_in(grad_normed)
    grad_input = (grad_resid + grad_x).astype(jnp.bfloat16)
    small_local = jnp.concatenate(
        [
            grad_gain_one,
            grad_gain_two,
            grad_gain_head.reshape(-1),
            grad_taps[:CONV].reshape(-1),
            grad_gates.reshape(-1),
            grad_alog,
            grad_bias,
        ]
    )
    small_grad = lax.psum(small_local, ("dp", "ctx"))
    ffn_shard, grad_in, grad_out = lax.optimization_barrier((ffn_shard, grad_in, grad_out))
    mix_shard = scatter_rows((grad_in, grad_out))
    small_grad, mix_shard = lax.optimization_barrier((small_grad, mix_shard))
    shard_squares = jnp.sum(mix_shard * mix_shard) + jnp.sum(ffn_shard * ffn_shard)
    total_squares = lax.psum(shard_squares, ("dp", "ctx"))
    squares = total_squares + jnp.sum(small_grad * small_grad)
    clip = jnp.minimum(1.0, MAX_NORM / (jnp.sqrt(squares) + 1e-06))
    mixer_new, mixer_first_new, mixer_second_new = adam_step(
        mixer_params, mix_shard, mixer_first, mixer_second, clip
    )
    ffn_new, ffn_first_new, ffn_second_new = adam_step(
        ffn_params, ffn_shard, ffn_first, ffn_second, clip
    )
    small_new, small_first_new, small_second_new = adam_step(
        small_params, small_grad, small_first, small_second, clip
    )
    return (
        result[None],
        grad_input[None],
        mix_shard,
        ffn_shard,
        small_grad,
        mixer_new,
        mixer_first_new,
        mixer_second_new,
        ffn_new,
        ffn_first_new,
        ffn_second_new,
        small_new,
        small_first_new,
        small_second_new,
    )


def fast(
    side, inputs, cotangent, mixer_params, mixer_first, mixer_second, ffn_params, ffn_first, ffn_second, small_params, small_first, small_second,
):
    gain_one, gain_two, gain_head, tap_values, w_gates, a_log, dt_bias = unpack_small(small_params)
    width = tap_values.shape[1]
    f32, bf16 = jnp.float32, jnp.bfloat16
    everyone = lax.axis_size("dp") * lax.axis_size("ctx")
    mix_rows, ffn_rows = mixer_params.size // D, ffn_params.size // D
    padding = -ffn_rows % 16
    mix_part = mixer_params.reshape(mix_rows, D).astype(bf16)
    ffn_part = jnp.pad(ffn_params.reshape(ffn_rows, D).astype(bf16), ((0, padding), (0, 0)))
    x_float = inputs[0].astype(f32)
    count = x_float.shape[0]
    normed_in = norm_scale(x_float, gain_one).astype(bf16)
    gate_logits = jnp.dot(normed_in.astype(f32), w_gates, precision=HIGHEST)
    beta, decay = gates(gate_logits, a_log, dt_bias)
    before = from_behind(normed_in[count - 16 :], "ctx", 1)
    mix_whole, ffn_whole, wires, ext, out_gate, query, keys, values, inverse = front(
        mix_part, ffn_part, jnp.concatenate([before, normed_in], axis=0), tap_values, beta, decay, side, 1
    )
    wires = wires.reshape(-1, count + PAD, wires.shape[1])
    place = lax.axis_index("ctx").astype(jnp.int32).reshape(1)
    (
        result, grad_resid, grad_out, ffn_grad, grad_gain_two, state, pseudo, local, grad_mixed,
        grad_gate_out, grad_gain_head,
    ) = middle(
        ffn_rows, place, wires, query, keys, values, inverse, beta, decay, out_gate,
        gain_head.reshape(1, DV), inputs[0], cotangent[0], gain_two.reshape(1, D), mix_whole, ffn_whole,
    )
    forget = -jnp.exp(a_log) * jax.nn.sigmoid(gate_logits[:, H:] + dt_bias)
    lanes = lambda value, start: jnp.pad(value, ((0, 0), (start, 128 - start - value.shape[1])))
    ffn_shard, mix_shard, grad_input, sums, squares = back(
        side, 2, wires, local, query, keys, values, inverse, beta, decay, state, pseudo, grad_mixed,
        ext, tap_values, grad_gate_out, grad_resid, inputs[0], normed_in, gain_one.reshape(1, D),
        lanes(jnp.concatenate([beta * (1.0 - beta), forget], axis=1), 0), lanes(decay, H),
        jnp.pad(w_gates.T, ((0, -2 * H % 8), (0, 0))), grad_gain_two, grad_gain_head,
        ffn_grad, grad_out, mix_whole,
    )
    end = 3 + 2 * CONV + 2 * H
    small_grad = jnp.concatenate(
        [
            sums[0],
            sums[1],
            sums[2, :DV],
            jnp.concatenate([sums[3 : 3 + CONV], sums[3 + CONV : 3 + 2 * CONV]], axis=1).reshape(-1),
            sums[end - 2 * H : end].T.reshape(-1),
            sums[end, H : 2 * H],
            sums[end + 1, H : 2 * H],
        ]
    )
    mix_shard = mix_shard.reshape(-1)
    ffn_shard = ffn_shard[:ffn_rows].reshape(-1)
    squares = squares[0, 0]
    clip = jnp.minimum(1.0, MAX_NORM / (jnp.sqrt(squares) + 1e-06))
    mixer_new, mixer_first_new, mixer_second_new = adam_step(
        mixer_params, mix_shard, mixer_first, mixer_second, clip
    )
    ffn_new, ffn_first_new, ffn_second_new = adam_step(
        ffn_params, ffn_shard, ffn_first, ffn_second, clip
    )
    small_new, small_first_new, small_second_new = adam_step(
        small_params, small_grad, small_first, small_second, clip
    )
    return (
        result[None],
        grad_input[None],
        mix_shard,
        ffn_shard,
        small_grad,
        mixer_new,
        mixer_first_new,
        mixer_second_new,
        ffn_new,
        ffn_first_new,
        ffn_second_new,
        small_new,
        small_first_new,
        small_second_new,
    )


def body(*args):
    rows, left = divmod(args[5].size, D)
    side = chip_side() if left == 0 and args[2].size % (32 * D) == 0 else 0
    return fast(side, *args) if side else plain(*args)


def solution(mesh):
    return jax.shard_map(
        body,
        mesh=mesh,
        in_specs=(
            P("dp", "ctx", None),
            P("dp", "ctx", None),
            P(("dp", "ctx")),
            P(("dp", "ctx")),
            P(("dp", "ctx")),
            P(("dp", "ctx")),
            P(("dp", "ctx")),
            P(("dp", "ctx")),
            P(),
            P(),
            P(),
        ),
        out_specs=(
            P("dp", "ctx", None),
            P("dp", "ctx", None),
            P(("dp", "ctx")),
            P(("dp", "ctx")),
            P(),
            P(("dp", "ctx")),
            P(("dp", "ctx")),
            P(("dp", "ctx")),
            P(("dp", "ctx")),
            P(("dp", "ctx")),
            P(("dp", "ctx")),
            P(),
            P(),
            P(),
        ),
        check_vma=False,
    )
```

```python
import functools
import math
import jax
import jax.numpy as jnp
from jax import lax
from jax.experimental import pallas as pl
from jax.experimental.pallas import tpu as pltpu
from jax.sharding import PartitionSpec as P

D = 1024
H = 2
DK = 256
DV = 512
FF = 1408
CONV = 4
GROUP = 64


EPSILON = 1e-06
ADAM_EPS = 1e-08
LEARN_RATE = 0.02
BETA_ONE = 0.9
BETA_TWO = 0.999
DECAY_RATE = 0.1
CORRECT_ONE = 1.0 - 0.9**3
CORRECT_TWO = 1.0 - 0.999**3
MAX_NORM = 1.0
HIGHEST = lax.Precision.HIGHEST


def from_behind(value, axis, steps):
    count = lax.axis_size(axis)
    initial, last = (max(0, -steps), min(count, count - steps))
    return lax.ppermute(value, axis, [(source, source + steps) for source in range(initial, last)])


def norm_scale(values, gain):
    return values * lax.rsqrt(jnp.mean(values * values, axis=-1, keepdims=True) + EPSILON) * gain


def swiglu(gate_part, up_part):
    return jax.nn.silu(gate_part) * up_part


def unpack_small(packed):
    width = 2 * H * DK + H * DV
    lengths = [D, D, DV, CONV * width, D * 2 * H, H, H]
    pieces = []
    offset = 0
    for length in lengths:
        pieces.append(packed[offset : offset + length])
        offset = offset + length
    return (
        pieces[0],
        pieces[1],
        pieces[2],
        pieces[3].reshape(CONV, width),
        pieces[4].reshape(D, 2 * H),
        pieces[5],
        pieces[6],
    )


def split_weights(mix_whole, ffn_whole):
    mix_rows = mix_whole.reshape(-1, D)
    ffn_rows = ffn_whole.reshape(-1, D)
    edge = 2 * H * DK + 2 * H * DV
    return (mix_rows[:edge], mix_rows[edge:], ffn_rows[: 2 * FF], ffn_rows[2 * FF :])


PAD = 16
HIGH = dict(precision=HIGHEST, preferred_element_type=jnp.float32)


def mm(a, b):
    return lax.dot_general(a, b, (((1,), (0,)), ((), ())), **HIGH)


def mm_nt(a, b):
    return lax.dot_general(a, b, (((1,), (1,)), ((), ())), **HIGH)


def mm_tn(a, b):
    return lax.dot_general(a, b, (((0,), (0,)), ((), ())), **HIGH)


def halves(a):
    high = a.astype(jnp.bfloat16)
    return high, (a - high.astype(jnp.float32)).astype(jnp.bfloat16)


def wire_mm(a, b, dims):
    high, low = halves(b)
    first = lax.dot_general(a, high, (dims, ((), ())), preferred_element_type=jnp.float32)
    return first + lax.dot_general(a, low, (dims, ((), ())), preferred_element_type=jnp.float32)


def iotas(size):
    shape = (size, size)
    return (
        lax.broadcasted_iota(jnp.int32, shape, 0),
        lax.broadcasted_iota(jnp.int32, shape, 1),
    )


def to_row(column, rows, cols):
    return jnp.sum(jnp.where(rows == cols, column, 0.0), axis=0, keepdims=True)


def unit_inverse(strict_part, rows, cols):
    size = strict_part.shape[0]
    inverse = jnp.where(rows == cols, 1.0, 0.0) - jnp.where(
        (rows // 2 == cols // 2), strict_part, 0.0
    )
    block = 2
    while block < size:
        joined = (rows // (2 * block) == cols // (2 * block)) & (rows // block != cols // block)
        off = jnp.where(joined, strict_part, 0.0)
        inverse = inverse - mm(mm(inverse, off), inverse)
        block = 2 * block
    return inverse


def silu_pair(x):
    gate = jax.nn.sigmoid(x)
    return x * gate, gate * (1.0 + x * (1.0 - gate))


def conv_sum(extended_ref, taps, count):
    total = None
    for tap in range(CONV):
        piece = taps[tap : tap + 1] * extended_ref[pl.ds(8 - (CONV - 1) + tap, count), :]
        total = piece if total is None else total + piece
    return total


def unit_rows(part):
    return lax.rsqrt(jnp.sum(part * part, axis=-1, keepdims=True) + EPSILON)


def decay_lane(decay_ref, head):
    lane = head + (H if decay_ref.shape[1] > H else 0)
    return decay_ref[:, lane : lane + 1]


def decay_terms(decay_column, rows, cols):
    lower = rows >= cols
    size = rows.shape[0]
    spread_in = jnp.broadcast_to(decay_column, (size, 128))
    cumulative = mm(jnp.where(lower, 1.0, 0.0), spread_in)[:, :1]
    across = to_row(cumulative, rows, cols)
    matrix = jnp.where(lower, jnp.exp(jnp.where(lower, cumulative - across, 0.0)), 0.0)
    last = cumulative[size - 1 : size]
    return matrix, jnp.exp(cumulative), jnp.exp(last - cumulative), jnp.exp(last)


def forward_parts(
    projected_ref, border_ref, taps_ref, beta_ref, decay_ref,
    wire_ref, query_ref, keys_ref, values_ref, inverse_ref, extended_ref,
):
    count = projected_ref.shape[0]
    width = taps_ref.shape[1]
    extended_ref[0:8, :] = border_ref[...]
    extended_ref[pl.ds(8, count), :] = projected_ref[:, :width]
    summed = conv_sum(extended_ref, taps_ref[...], count)
    activated = summed * jax.nn.sigmoid(summed)
    rows, cols = iotas(count)
    for head in range(H):
        query_part = activated[:, head * DK : (head + 1) * DK]
        key_part = activated[:, (H + head) * DK : (H + head + 1) * DK]
        start = 2 * H * DK + head * DV
        values = activated[:, start : start + DV]
        query = query_part * unit_rows(query_part) * DK ** (-0.5)
        keys = key_part * unit_rows(key_part)
        beta = beta_ref[:, head : head + 1]
        matrix, grown, to_end, whole = decay_terms(decay_lane(decay_ref, head), rows, cols)
        system = jnp.where(rows > cols, beta * mm_nt(keys, keys) * matrix, 0.0)
        inverse = unit_inverse(system, rows, cols)
        key_mix = mm(inverse, keys * (beta * grown))
        value_mix = mm(inverse, values * beta)
        base = head * (2 * DK + DV)
        wire_ref[0:count, base : base + DK] = (keys * to_end).astype(jnp.bfloat16)
        wire_ref[0:count, base + DK : base + 2 * DK] = key_mix.astype(jnp.bfloat16)
        wire_ref[0:count, base + 2 * DK : base + 2 * DK + DV] = value_mix.astype(jnp.bfloat16)
        high, low = halves(jnp.broadcast_to(whole, (PAD, 2 * DK + DV)))
        first = lax.broadcasted_iota(jnp.int32, (PAD, 2 * DK + DV), 0) < 8
        tail = jnp.where(first, high.astype(jnp.float32), low.astype(jnp.float32))
        wire_ref[pl.ds(count, PAD), base : base + 2 * DK + DV] = tail.astype(jnp.bfloat16)
        query_ref[:, head * DK : (head + 1) * DK] = query
        keys_ref[:, head * DK : (head + 1) * DK] = keys
        values_ref[:, head * DV : (head + 1) * DV] = values
        inverse_ref[head] = inverse


def wire_parts(wire_ref, index, head, count):
    base = head * (2 * DK + DV)
    to_end = wire_ref[index, 0:count, base : base + DK]
    key_mix = wire_ref[index, 0:count, base + DK : base + 2 * DK]
    value_mix = wire_ref[index, 0:count, base + 2 * DK : base + 2 * DK + DV]
    tail = wire_ref[index, pl.ds(count, PAD), base : base + 128].astype(jnp.float32)
    whole = tail[0:1, 0:1] + tail[8:9, 0:1]
    return to_end, key_mix, value_mix, whole


def own_mix(inverse, keys, values, beta, grown):
    return mm(inverse, keys * (beta * grown)), mm(inverse, values * beta)


def forward_chain(
    place_ref, wire_ref, query_ref, keys_ref, values_ref, inverse_ref, beta_ref, decay_ref,
    gate_ref, gain_ref, head_out_ref, mixed_ref, state_ref, pseudo_ref,
):
    count = query_ref.shape[0]
    state_ref[...] = jnp.zeros_like(state_ref)

    def lap(index, carry):
        for head in range(H):
            to_end, key_mix, value_mix, whole = wire_parts(wire_ref, index, head, count)
            state = state_ref[head]
            pseudo = value_mix.astype(jnp.float32) - wire_mm(key_mix, state, ((1,), (0,)))
            state_ref[head] = whole * state + wire_mm(to_end, pseudo, ((0,), (0,)))
        return carry

    lax.fori_loop(0, place_ref[0], lap, 0)
    rows, cols = iotas(count)
    for head in range(H):
        query = query_ref[:, head * DK : (head + 1) * DK]
        keys = keys_ref[:, head * DK : (head + 1) * DK]
        span = slice(head * DV, (head + 1) * DV)
        beta = beta_ref[:, head : head + 1]
        matrix, grown, to_end, whole = decay_terms(decay_lane(decay_ref, head), rows, cols)
        key_mix, value_mix = own_mix(inverse_ref[head], keys, values_ref[:, span], beta, grown)
        state = state_ref[head]
        pseudo = value_mix - mm(key_mix, state)
        mixed = mm(query * grown, state) + mm(mm_nt(query, keys) * matrix, pseudo)
        scale = lax.rsqrt(jnp.mean(mixed * mixed, axis=-1, keepdims=True) + EPSILON)
        gated, unused = silu_pair(gate_ref[:, span])
        head_out_ref[:, span] = (mixed * scale * gain_ref[...] * gated).astype(jnp.bfloat16)
        mixed_ref[:, span] = mixed
        pseudo_ref[:, span] = pseudo


def backward_local(
    grad_ref, mixed_ref, query_ref, keys_ref, values_ref, inverse_ref, beta_ref, decay_ref,
    gate_ref, gain_ref, local_ref, grad_mixed_ref, grad_gate_ref, grad_gain_ref,
):
    count = query_ref.shape[0]
    rows, cols = iotas(count)
    gain_total = jnp.zeros((1, DV), jnp.float32)
    for head in range(H):
        query = query_ref[:, head * DK : (head + 1) * DK]
        keys = keys_ref[:, head * DK : (head + 1) * DK]
        span = slice(head * DV, (head + 1) * DV)
        mixed = mixed_ref[:, span]
        grad = grad_ref[:, span]
        scale = lax.rsqrt(jnp.mean(mixed * mixed, axis=-1, keepdims=True) + EPSILON)
        plain = mixed * scale
        gated, slope = silu_pair(gate_ref[:, span])
        grad_gate_ref[:, span] = (grad * plain * gain_ref[...] * slope).astype(grad_gate_ref.dtype)
        grad_normed = grad * gated
        gain_total = gain_total + jnp.sum(grad_normed * plain, axis=0, keepdims=True)
        pulled = grad_normed * gain_ref[...]
        grad_mixed = scale * (pulled - plain * jnp.mean(pulled * plain, axis=-1, keepdims=True))
        grad_mixed_ref[:, span] = grad_mixed
        beta = beta_ref[:, head : head + 1]
        matrix, grown, to_end, whole = decay_terms(decay_lane(decay_ref, head), rows, cols)
        key_mix = mm(inverse_ref[head], keys * (beta * grown))
        grad_pseudo = mm_tn(mm_nt(query, keys) * matrix, grad_mixed)
        local = mm_tn(query * grown, grad_mixed) - mm_tn(key_mix, grad_pseudo)
        local_ref[head * DK : (head + 1) * DK, :] = local.astype(jnp.bfloat16)
    grad_gain_ref[...] = gain_total


def backward_chain(
    place_ref, wire_ref, local_ref, query_ref, keys_ref, values_ref, inverse_ref, beta_ref,
    decay_ref, state_ref, pseudo_ref, grad_mixed_ref, projected_ref, border_ref, taps_ref,
    grad_conv_ref, grad_border_ref, grad_taps_ref, grad_beta_ref, grad_decay_ref,
    after_ref, extended_ref, padded_ref,
):
    count = query_ref.shape[0]
    width = taps_ref.shape[1]
    devices = wire_ref.shape[0]
    after_ref[...] = jnp.zeros_like(after_ref)

    def lap(step, carry):
        index = devices - 1 - step
        for head in range(H):
            to_end, key_mix, value_mix, whole = wire_parts(wire_ref, index, head, count)
            after = after_ref[head]
            inner = wire_mm(to_end, after, ((1,), (0,)))
            local = local_ref[index, head * DK : (head + 1) * DK, :].astype(jnp.float32)
            after_ref[head] = whole * after - wire_mm(key_mix, inner, ((0,), (0,))) + local
        return carry

    lax.fori_loop(0, devices - 1 - place_ref[0], lap, 0)
    extended_ref[0:8, :] = border_ref[...]
    extended_ref[pl.ds(8, count), :] = projected_ref[:, :width]
    taps = taps_ref[...]
    summed = conv_sum(extended_ref, taps, count)
    activated, slope = silu_pair(summed)
    padded_ref[0:8, :] = jnp.zeros((8, width), jnp.float32)
    padded_ref[pl.ds(8 + count, 8), :] = jnp.zeros((8, width), jnp.float32)
    rows, cols = iotas(count)
    lower = rows >= cols
    strict = rows > cols
    lanes = lax.broadcasted_iota(jnp.int32, (count, 128), 1)
    beta_out = jnp.zeros((count, 128), jnp.float32)
    cumulative_out = jnp.zeros((count, 128), jnp.float32)
    row_column = lax.broadcasted_iota(jnp.int32, (count, 1), 0)
    for head in range(H):
        query = query_ref[:, head * DK : (head + 1) * DK]
        keys = keys_ref[:, head * DK : (head + 1) * DK]
        span = slice(head * DV, (head + 1) * DV)
        values = values_ref[:, span]
        beta = beta_ref[:, head : head + 1]
        matrix, grown, to_end, whole = decay_terms(decay_lane(decay_ref, head), rows, cols)
        inverse = inverse_ref[head]
        state = state_ref[head]
        after = after_ref[head]
        pseudo = pseudo_ref[:, span]
        grad_mixed = grad_mixed_ref[:, span]
        keys_grown = keys * (beta * grown)
        key_mix = mm(inverse, keys_grown)
        value_mix = mm(inverse, values * beta)
        gram = mm_nt(keys, keys)
        system = jnp.where(strict, beta * gram * matrix, 0.0)
        scores = mm_nt(query, keys) * matrix
        keys_end = keys * to_end
        query_grown = query * grown
        grad_query_grown = mm_nt(grad_mixed, state)
        grad_scores = jnp.where(lower, mm_nt(grad_mixed, pseudo), 0.0)
        grad_pseudo = mm_tn(scores, grad_mixed) + mm(keys_end, after)
        grad_keys_end = mm_nt(pseudo, after)
        grad_whole = jnp.sum(jnp.sum(after * state, axis=1, keepdims=True), axis=0, keepdims=True)
        grad_value_in = mm_tn(inverse, grad_pseudo)
        grad_key_in = mm_tn(inverse, -mm_nt(grad_pseudo, state))
        grad_system = -jnp.where(
            strict, mm_nt(grad_value_in, value_mix) + mm_nt(grad_key_in, key_mix), 0.0
        )
        grad_raw = grad_scores * matrix
        grad_query = mm(grad_raw, keys) + grad_query_grown * grown
        grad_keys = mm_tn(grad_raw, query)
        weighted = grad_system * matrix
        grad_beta = jnp.sum(weighted * gram, axis=1, keepdims=True)
        grad_gram = weighted * beta
        grad_keys = grad_keys + mm(grad_gram, keys) + mm_tn(grad_gram, keys)
        spread = grad_scores * scores + grad_system * system
        grad_cumulative = jnp.sum(spread, axis=1, keepdims=True)
        across = jnp.sum(spread, axis=0, keepdims=True)
        grad_cumulative = grad_cumulative - jnp.sum(
            jnp.where(rows == cols, across, 0.0), axis=1, keepdims=True
        )
        grad_keys = grad_keys + grad_key_in * (beta * grown)
        through = jnp.sum(grad_key_in * keys, axis=1, keepdims=True) * grown
        grad_beta = grad_beta + through + jnp.sum(grad_value_in * values, axis=1, keepdims=True)
        grad_cumulative = grad_cumulative + through * beta
        grad_values = grad_value_in * beta
        grad_cumulative = grad_cumulative + jnp.sum(
            grad_query_grown * query_grown, axis=1, keepdims=True
        )
        grad_keys = grad_keys + grad_keys_end * to_end
        ending = jnp.sum(grad_keys_end * keys_end, axis=1, keepdims=True)
        final = jnp.sum(ending, axis=0, keepdims=True) + whole * grad_whole
        grad_cumulative = grad_cumulative - ending + jnp.where(row_column == count - 1, final, 0.0)
        beta_out = jnp.where(lanes == head, grad_beta, beta_out)
        cumulative_out = jnp.where(lanes == head, grad_cumulative, cumulative_out)
        key_part = activated[:, (H + head) * DK : (H + head + 1) * DK]
        key_scale = unit_rows(key_part)
        query_part = activated[:, head * DK : (head + 1) * DK]
        query_scale = unit_rows(query_part)
        factor = DK ** (-0.5)
        grad_query_part = (factor * query_scale) * (
            grad_query
            - query_part
            * (query_scale * query_scale)
            * jnp.sum(grad_query * query_part, axis=-1, keepdims=True)
        )
        grad_key_part = key_scale * (
            grad_keys
            - key_part
            * (key_scale * key_scale)
            * jnp.sum(grad_keys * key_part, axis=-1, keepdims=True)
        )
        spots = (head * DK, (H + head) * DK, 2 * H * DK + head * DV)
        for spot, grad in zip(spots, (grad_query_part, grad_key_part, grad_values)):
            size = grad.shape[1]
            padded_ref[pl.ds(8, count), spot : spot + size] = grad * slope[:, spot : spot + size]
    grad_beta_ref[...] = beta_out
    grad_decay_ref[...] = mm_tn(jnp.where(lower, 1.0, 0.0), cumulative_out)
    conv_total = jnp.zeros((count, width), jnp.float32)
    border_total = jnp.zeros((8, width), jnp.float32)
    summed_grad = padded_ref[pl.ds(8, count), :]
    tap_rows = lax.broadcasted_iota(jnp.int32, (8, width), 0)
    taps_total = jnp.zeros((8, width), jnp.float32)
    for tap in range(CONV):
        shift = CONV - 1 - tap
        conv_total = conv_total + taps[tap : tap + 1] * padded_ref[pl.ds(8 + shift, count), :]
        border_total = border_total + taps[tap : tap + 1] * padded_ref[pl.ds(shift, 8), :]
        piece = jnp.sum(
            summed_grad * extended_ref[pl.ds(8 - (CONV - 1) + tap, count), :],
            axis=0,
            keepdims=True,
        )
        taps_total = jnp.where(tap_rows == tap, piece, taps_total)
    grad_conv_ref[...] = conv_total
    grad_border_ref[...] = border_total
    grad_taps_ref[...] = taps_total


def fused(body, outputs, scratch=(), scalars=0, cost=(0, 0), label=None):
    def call(*args):
        vmem = pl.BlockSpec(memory_space=pltpu.VMEM)
        smem = pl.BlockSpec(memory_space=pltpu.SMEM)
        return pl.pallas_call(
            body,
            out_shape=outputs,
            in_specs=[smem] * scalars + [vmem] * (len(args) - scalars),
            out_specs=[vmem] * len(outputs),
            scratch_shapes=list(scratch),
            compiler_params=pltpu.CompilerParams(vmem_limit_bytes=60 * 2**20),
            cost_estimate=pl.CostEstimate(
                flops=cost[0], bytes_accessed=cost[1], transcendentals=0
            ),
            name=label,
        )(*args)

    return call


def gates(gate_logits, a_log, dt_bias):
    beta = jax.nn.sigmoid(gate_logits[:, :H])
    decay = -jnp.exp(a_log) * jax.nn.softplus(gate_logits[:, H:] + dt_bias)
    return beta, decay


def scatter_rows(pieces):
    outer, inner = lax.axis_size("dp"), lax.axis_size("ctx")
    whole = jnp.concatenate([piece.astype(jnp.bfloat16) for piece in pieces], axis=0)
    lane = math.gcd(whole.size // (outer * inner), D)
    blocks = whole.reshape(outer, inner, -1, lane)
    part = lax.psum_scatter(blocks, "ctx", scatter_dimension=1, tiled=False)
    own = lax.psum_scatter(part, "dp", scatter_dimension=0, tiled=False)
    return own.astype(jnp.float32).reshape(-1)


MESH = pl.DeviceIdType.MESH


class Place:
    def __init__(self, side):
        self.deep = lax.axis_size("dp")
        self.side = side
        self.ctx = lax.axis_size("ctx")
        self.z = lax.axis_index("dp")
        spot = lax.axis_index("ctx")
        self.c = lax.rem(spot, 2)
        chip = lax.div(spot, 2)
        self.x = lax.rem(chip, side)
        self.y = lax.div(chip, side)
        self.other_core = self.device(self.z, self.y, self.x, 1 - self.c)
        self.other_x = self.device(self.z, self.y, 1 - self.x, self.c)
        self.other_y = self.device(self.z, 1 - self.y, self.x, self.c)
        self.next_z = self.device(self.along(1), self.y, self.x, self.c)
        self.spot = spot
        self.before = (self.z, lax.rem(spot + self.ctx - 1, self.ctx))
        self.behind = (self.z, lax.rem(spot + 1, self.ctx))

    def along(self, step):
        return lax.rem(self.z + step + self.deep, self.deep)

    def device(self, z, y, x, c):
        return (z, (y * self.side + x) * 2 + c)

    def block(self, z, y, x, c):
        return z * self.ctx + (y * self.side + x) * 2 + c

    def enter(self, all_z=False, more=()):
        barrier = pltpu.get_barrier_semaphore()
        steps = range(1, self.deep) if all_z else (-1,)
        friends = [self.other_core, self.other_x, self.other_y, *more]
        friends += [self.device(self.along(step), self.y, self.x, self.c) for step in steps]
        for friend in friends:
            pl.semaphore_signal(barrier, inc=1, device_id=friend, device_id_type=MESH)
        pl.semaphore_wait(barrier, len(friends))


class Copies:
    def __init__(self, send_sems, recv_sems, local_sems=None):
        self.send_sems, self.recv_sems, self.local_sems = send_sems, recv_sems, local_sems
        self.sent, self.locals = [], 0

    def push(self, source, target, device):
        index = len(self.sent)
        copy = pltpu.make_async_remote_copy(
            src_ref=source,
            dst_ref=target,
            send_sem=self.send_sems.at[index],
            recv_sem=self.recv_sems.at[index],
            device_id=device,
            device_id_type=MESH,
        )
        copy.start()
        self.sent.append(copy)
        return copy

    def local(self, source, target):
        copy = pltpu.make_async_copy(source, target, self.local_sems.at[self.locals])
        copy.start()
        self.locals += 1
        return copy

    def finish(self):
        for copy in self.sent:
            copy.wait_send()


def upper(rows):
    return rows // 2 // 16 * 16


def gather_steps(place, copies, shard_ref, out_ref, plane=False):
    rows, deep = shard_ref.shape[0], 1 if plane else place.deep
    top = upper(rows)
    spans = {None: (0, rows), 0: (0, top), 1: (top, rows - top)}
    ring, near, far, core = [], {}, {}, []

    def cut(ref, start, part):
        offset, size = spans[part]
        return ref.at[pl.ds(pl.multiple_of(start + offset, 16), size), :]

    def start_of(rel, dy, dx):
        y = 1 - place.y if dy else place.y
        x = 1 - place.x if dx else place.x
        z = 0 if plane else place.along(-rel)
        return place.block(z, y, x, place.c) * rows

    def forward(rel, dy, dx, part, device):
        start = start_of(rel, dy, dx)
        own = rel == 0 and not dy and not dx
        source = cut(shard_ref, 0, part) if own else cut(out_ref, start, part)
        return copies.push(source, cut(out_ref, start, part), device)

    def spread(rel):
        if rel < deep - 1:
            ring.append(forward(rel, 0, 0, None, place.next_z))
        near[rel, "x0"] = forward(rel, 0, 0, 0, place.other_x)
        near[rel, "y1"] = forward(rel, 0, 0, 1, place.other_y)
        near[rel, "y0"] = forward(rel, 0, 0, 0, place.other_y)
        near[rel, "x1"] = forward(rel, 0, 0, 1, place.other_x)
        core.append(forward(rel, 0, 0, None, place.other_core))

    def second(rel):
        near[rel, "x0"].wait_recv()
        far[rel, 0] = forward(rel, 0, 1, 0, place.other_y)
        near[rel, "y1"].wait_recv()
        far[rel, 1] = forward(rel, 1, 0, 1, place.other_x)
        core.append(forward(rel, 0, 1, 0, place.other_core))
        core.append(forward(rel, 1, 0, 1, place.other_core))

    def third(rel):
        near[rel, "y0"].wait_recv()
        core.append(forward(rel, 1, 0, 0, place.other_core))
        near[rel, "x1"].wait_recv()
        core.append(forward(rel, 0, 1, 1, place.other_core))

    def fourth(rel):
        for part in (0, 1):
            far[rel, part].wait_recv()
            core.append(forward(rel, 1, 1, part, place.other_core))

    own_copy = []

    def first():
        own_copy.append(copies.local(shard_ref, cut(out_ref, start_of(0, 0, 0), None)))
        spread(0)

    def later(rel):
        ring[rel - 1].wait_recv()
        spread(rel)

    def last():
        for copy in core:
            copy.wait_recv()
        own_copy[0].wait()

    steps = [first]
    for rel in range(1, deep):
        steps.append(lambda rel=rel: later(rel))
        steps.append(lambda rel=rel: second(rel - 1))
        steps.append(lambda rel=rel: third(rel - 1))
    steps.append(lambda: second(deep - 1))
    steps.append(lambda: third(deep - 1))
    for rel in range(deep):
        steps.append(lambda rel=rel: fourth(rel))
    steps.append(last)
    return steps


def wide(value):
    return value.astype(jnp.float32)


class Scatter:
    def __init__(self, place, copies, grad_ref, held, from_core, first_x, first_y, last_x, last_y, from_z):
        self.place, self.copies, self.grad = place, copies, grad_ref
        self.held, self.from_core, self.from_z = held, from_core, from_z
        self.first = {0: first_y, 1: first_x}
        self.last = {0: last_x, 1: last_y}
        self.rows = held.shape[1]
        self.top = upper(self.rows)
        self.loads, self.cores, self.near, self.far, self.ring = {}, {}, {}, {}, {}

    @staticmethod
    def scratch(deep, rows):
        top = upper(rows)
        low = rows - top
        return [
            pltpu.VMEM((4 * deep, rows, D), jnp.bfloat16),
            pltpu.VMEM((4 * deep, rows, D), jnp.bfloat16),
            pltpu.VMEM((2 * deep, low, D), jnp.bfloat16),
            pltpu.VMEM((2 * deep, top, D), jnp.bfloat16),
            pltpu.VMEM((deep, top, D), jnp.bfloat16),
            pltpu.VMEM((deep, low, D), jnp.bfloat16),
            pltpu.VMEM((deep - 1, rows, D), jnp.bfloat16),
        ]

    @staticmethod
    def copies_of(deep):
        return 4 * deep + 4 * deep + 2 * deep + deep - 1

    def slot(self, rel, dy, dx):
        return (rel - 1) * 4 + dy * 2 + dx

    def span(self, part):
        return pl.ds(0, self.top) if part == 0 else pl.ds(self.top, self.rows - self.top)

    def load(self):
        place = self.place
        for rel in range(1, place.deep + 1):
            for dy, dx in ((1, 1), (1, 0), (0, 1), (0, 0)):
                y = 1 - place.y if dy else place.y
                x = 1 - place.x if dx else place.x
                slot = self.slot(rel, dy, dx)

                def rows_of(core):
                    start = place.block(place.along(-rel), y, x, core) * self.rows
                    return self.grad.at[pl.ds(pl.multiple_of(start, 16), self.rows), :]

                self.cores[slot] = self.copies.push(
                    rows_of(1 - place.c), self.from_core.at[slot], place.other_core
                )
                self.loads[slot] = self.copies.local(rows_of(place.c), self.held.at[slot])

    def stage_one(self, rel):
        place = self.place
        for dy, dx in ((1, 1), (1, 0), (0, 1), (0, 0)):
            slot = self.slot(rel, dy, dx)
            self.loads[slot].wait()
            self.cores[slot].wait_recv()
            self.held[slot] = (wide(self.held[slot]) + wide(self.from_core[slot])).astype(jnp.bfloat16)
            if dy:
                self.near[rel, 0, dx] = self.copies.push(
                    self.held.at[slot, self.span(0), :],
                    self.first[0].at[(rel - 1) * 2 + dx],
                    place.other_y,
                )
            if dx:
                self.near[rel, 1, dy] = self.copies.push(
                    self.held.at[slot, self.span(1), :],
                    self.first[1].at[(rel - 1) * 2 + dy],
                    place.other_x,
                )

    def add(self, slot, part, piece):
        self.held[slot, self.span(part), :] = (
            wide(self.held[slot, self.span(part), :]) + wide(piece)
        ).astype(jnp.bfloat16)

    def stage_two(self, rel):
        place = self.place
        for part in (0, 1):
            for away in (1, 0):
                self.near[rel, part, away].wait_recv()
                slot = self.slot(rel, away, 0) if part else self.slot(rel, 0, away)
                self.add(slot, part, self.first[part][(rel - 1) * 2 + away])
                if away:
                    self.far[rel, part] = self.copies.push(
                        self.held.at[slot, self.span(part), :],
                        self.last[part].at[rel - 1],
                        place.other_y if part else place.other_x,
                    )

    def stage_three(self, rel, total_ref=None):
        slot = self.slot(rel, 0, 0)
        for part in (0, 1):
            self.far[rel, part].wait_recv()
            self.add(slot, part, self.last[part][rel - 1])
        if rel >= 2:
            self.ring[rel - 1].wait_recv()
            total = wide(self.held[slot]) + wide(self.from_z[rel - 2])
            if rel == self.place.deep:
                total_ref[...] = total
                return
            self.held[slot] = total.astype(jnp.bfloat16)
        self.ring[rel] = self.copies.push(
            self.held.at[slot], self.from_z.at[rel - 1], self.place.next_z
        )

    def steps(self, total_ref):
        deep = self.place.deep
        out = [self.load]
        for turn in range(1, deep + 3):
            if turn <= deep:
                out.append(lambda rel=turn: self.stage_one(rel))
            if 1 <= turn - 1 <= deep:
                out.append(lambda rel=turn - 1: self.stage_two(rel))
            if 1 <= turn - 2 <= deep:
                out.append(lambda rel=turn - 2: self.stage_three(rel, total_ref))
        return out


class Everywhere:
    def __init__(self, place, copies, total, slots, stack):
        self.place, self.copies = place, copies
        self.total, self.slots, self.stack = total, slots, stack
        self.turns = (place.other_core, place.other_x, place.other_y)
        self.pending = []

    @staticmethod
    def scratch(deep, rows, width):
        return [pltpu.VMEM((count, rows, width), jnp.float32) for count in (3, deep, 4)]

    def send(self, turn):
        self.pending = [
            self.copies.push(self.total.at[turn], self.slots.at[turn], self.turns[turn])
        ]

    def take(self, turn):
        self.pending[0].wait_recv()
        self.total[turn + 1] = self.total[turn] + self.slots[turn]

    def send_z(self):
        place = self.place
        self.pending = [
            self.copies.push(
                self.total.at[3],
                self.stack.at[place.z],
                place.device(place.along(step), place.y, place.x, place.c),
            )
            for step in range(1, place.deep)
        ]
        self.stack[place.z] = self.total[3]

    def take_z(self):
        for copy in self.pending:
            copy.wait_recv()
        result = self.stack[0]
        for index in range(1, self.place.deep):
            result = result + self.stack[index]
        return result

    def run(self):
        for turn in range(3):
            self.send(turn)
            self.take(turn)
        self.send_z()
        return self.take_z()


def gather_copies(deep):
    return (deep - 1) + 4 * deep + 2 * deep + deep + 2 * deep * 3


def front_parts(ext_ref, taps_ref, beta_ref, decay_ref, wire_ref, query_ref, keys_ref, values_ref, inverse_ref):
    count = query_ref.shape[0]
    width = taps_ref.shape[1]
    summed = ext_sum(ext_ref, taps_ref[...], count, 0, width)
    activated = summed * jax.nn.sigmoid(summed)
    rows, cols = iotas(count)
    for head in range(H):
        query_part = activated[:, head * DK : (head + 1) * DK]
        key_part = activated[:, (H + head) * DK : (H + head + 1) * DK]
        start = 2 * H * DK + head * DV
        values = activated[:, start : start + DV]
        query = query_part * unit_rows(query_part) * DK ** (-0.5)
        keys = key_part * unit_rows(key_part)
        beta = beta_ref[:, head : head + 1]
        matrix, grown, to_end, whole = decay_terms(decay_lane(decay_ref, head), rows, cols)
        system = jnp.where(rows > cols, beta * mm_nt(keys, keys) * matrix, 0.0)
        inverse = unit_inverse(system, rows, cols)
        key_mix = mm(inverse, keys * (beta * grown))
        value_mix = mm(inverse, values * beta)
        base = head * (2 * DK + DV)
        wire_ref[0:count, base : base + DK] = (keys * to_end).astype(jnp.bfloat16)
        wire_ref[0:count, base + DK : base + 2 * DK] = key_mix.astype(jnp.bfloat16)
        wire_ref[0:count, base + 2 * DK : base + 2 * DK + DV] = value_mix.astype(jnp.bfloat16)
        high, low = halves(jnp.broadcast_to(whole, (PAD, 2 * DK + DV)))
        first = lax.broadcasted_iota(jnp.int32, (PAD, 2 * DK + DV), 0) < 8
        tail = jnp.where(first, high.astype(jnp.float32), low.astype(jnp.float32))
        wire_ref[pl.ds(count, PAD), base : base + 2 * DK + DV] = tail.astype(jnp.bfloat16)
        query_ref[:, head * DK : (head + 1) * DK] = query
        keys_ref[:, head * DK : (head + 1) * DK] = keys
        values_ref[:, head * DV : (head + 1) * DV] = values
        inverse_ref[head] = inverse
        yield


def ext_sum(ext_ref, taps, count, start, size):
    total = None
    for tap in range(CONV):
        piece = (
            taps[tap : tap + 1, start : start + size]
            * ext_ref[pl.ds(8 - (CONV - 1) + tap, count), start : start + size]
        )
        total = piece if total is None else total + piece
    return total


def small_places():
    width = 2 * H * DK + H * DV
    starts, spot = [], 0
    for length in (D, D, DV, CONV * width, 2 * H * D):
        starts.append(spot // 128)
        spot += length
    return starts + [spot // 128]


def joined(ref, first, number):
    return jnp.concatenate([ref[first + index : first + index + 1, :] for index in range(number)], axis=1)


def gate_masks():
    each = 128 // (2 * H)
    row = lax.broadcasted_iota(jnp.int32, (D, 128), 0)
    lane = lax.broadcasted_iota(jnp.int32, (D, 128), 1)
    own = lax.rem(row, each) == lax.div(lane, 2 * H)
    rows, cols = iotas(128)
    return own, jnp.where(lax.rem(rows, 2 * H) == cols, 1.0, 0.0), each


def unpack_gates(packed):
    own, select, each = gate_masks()
    spread = jnp.broadcast_to(packed[:, None, :], (packed.shape[0], each, 128)).reshape(D, 128)
    return mm(jnp.where(own, spread, 0.0), select)


def pack_gates(plain):
    own, select, each = gate_masks()
    spread = jnp.where(own, mm_nt(plain, select), 0.0)
    return jnp.sum(spread.reshape(D // each, each, 128), axis=1)


def from_flat(flat_ref, rows):
    pieces = [flat_ref[pl.ds(index, rows, stride=D // 128), :] for index in range(D // 128)]
    return jnp.concatenate(pieces, axis=1)


def to_flat(flat_ref, value):
    for index in range(D // 128):
        flat_ref[pl.ds(index, value.shape[0], stride=D // 128), :] = value[:, index * 128 : (index + 1) * 128]


def front_kernel(
    side, mix_flat, ffn_flat, x_ref, small_ref,
    mix_out, ffn_out, wires_out, ext_ref, gate_ref, query_ref, keys_ref, values_ref, inverse_ref,
    own_normed_ref, beta_ref, decay_ref, factor_ref, taps_ref, gains_ref, w_gates_ref,
    weight_ref, wire_ref, mix_shard, ffn_shard, normed_ref, edge_ref,
    send_sems, recv_sems, local_sems,
):
    place = Place(side)
    copies = Copies(send_sems, recv_sems, local_sems)
    bf16 = jnp.bfloat16
    count = x_ref.shape[0]
    width = taps_ref.shape[1]
    mix_shard[...] = from_flat(mix_flat, mix_shard.shape[0]).astype(bf16)
    place.enter(more=(place.before,))
    mix = gather_steps(place, copies, mix_shard, mix_out)
    ffn = gather_steps(place, copies, ffn_shard, ffn_out)
    mix.pop(0)()
    one, two, head, tap, gate, rest = small_places()
    gain_one = joined(small_ref, one, D // 128)
    normed = norm_scale(x_ref[...].astype(jnp.float32), gain_one).astype(bf16)
    own_normed_ref[...] = normed
    normed_ref[pl.ds(PAD, count), :] = normed
    edge = copies.push(normed_ref.at[pl.ds(count, PAD), :], edge_ref, place.behind)
    ffn_rows = ffn_flat.shape[0] * 128 // D
    ffn_shard[...] = jnp.zeros_like(ffn_shard)
    ffn_shard[0:ffn_rows, :] = from_flat(ffn_flat, ffn_rows).astype(bf16)
    early = 3 * (place.deep - 1) + 2
    mix.pop(0)()
    gains_ref[...] = jnp.zeros_like(gains_ref)
    gains_ref[0:1, :] = gain_one
    gains_ref[1:2, :] = joined(small_ref, two, D // 128)
    gains_ref[2:3, 0:DV] = joined(small_ref, head, DV // 128)
    for index in range(CONV):
        taps_ref[index : index + 1, :] = joined(small_ref, tap + index * (width // 128), width // 128)
    for step in mix[:3]:
        step()
    w_gates_ref[...] = unpack_gates(small_ref[gate:rest, :])
    logits = mm(normed.astype(jnp.float32), w_gates_ref[...])
    for step in mix[3:5]:
        step()
    lanes = lax.broadcasted_iota(jnp.int32, (1, 128), 1)
    late = (lanes >= H) & (lanes < 2 * H)
    scalars = small_ref[rest : rest + 1, :]
    raised = logits + jnp.where(late, scalars, 0.0)
    size = jnp.exp(jnp.where(late, pltpu.roll(scalars, H, 1), 0.0))
    soft = jax.nn.sigmoid(raised)
    beta_ref[...] = soft
    decay_ref[...] = jnp.where(
        late, -size * (jnp.maximum(raised, 0.0) + jnp.log1p(jnp.exp(-jnp.abs(raised)))), 0.0
    )
    factor_ref[...] = jnp.where(late, -size * soft, jnp.where(lanes < H, soft * (1.0 - soft), 0.0))
    for step in mix[5 : early - 2]:
        step()
    ffn.pop(0)()
    for step in mix[early - 2 :]:
        step()
    edge.wait_recv()
    normed_ref[0:PAD, :] = jnp.where(place.spot > 0, edge_ref[...], jnp.zeros_like(edge_ref))
    depth = weight_ref.shape[0]
    chunk = DV
    loads = [
        copies.local(mix_out.at[pl.ds(start, chunk), :], weight_ref.at[pl.ds(start, chunk), :])
        for start in range(0, depth, chunk)
    ]
    for index, load in enumerate(loads):
        load.wait()
        span = pl.ds(index * chunk, chunk)
        piece = dot_nt(normed_ref[...], weight_ref[span, :])
        start = index * chunk
        if start < width:
            ext_ref[:, start : start + chunk] = piece[8:]
        else:
            start = start - width
            gate_ref[:, start : start + chunk] = piece[PAD:]
        if index % 2 == 1:
            ffn.pop(0)()
    parts = front_parts(
        ext_ref, taps_ref, beta_ref, decay_ref, wire_ref, query_ref, keys_ref, values_ref, inverse_ref
    )
    for unused in parts:
        for again in range(3):
            ffn.pop(0)()
    wires = gather_steps(place, copies, wire_ref, wires_out, plane=True)
    wires.pop(0)()
    ffn.pop(0)()
    while wires[1:]:
        wires.pop(0)()
        if len(ffn) > 1:
            ffn.pop(0)()
    for step in ffn + wires:
        step()
    copies.finish()


def front(mix_flat, ffn_flat, x, small, side, tag):
    f32, bf16 = jnp.float32, jnp.bfloat16
    deep, ctx = lax.axis_size("dp"), lax.axis_size("ctx")
    count = x.shape[0]
    everyone = deep * ctx
    mix_rows, ffn_rows = mix_flat.shape[0] * 128 // D, ffn_flat.shape[0] * 128 // D
    padded = -(-ffn_rows // 16) * 16
    number = 2 * gather_copies(deep) + gather_copies(1) + 1
    anywhere = pl.BlockSpec(memory_space=pl.ANY)
    vmem = pl.BlockSpec(memory_space=pltpu.VMEM)
    width = 2 * H * DK + H * DV
    depth = width + H * DV
    wire = (count + PAD, H * (2 * DK + DV))
    shape = jax.ShapeDtypeStruct
    return pl.pallas_call(
        functools.partial(front_kernel, side),
        out_shape=[
            shape((everyone * mix_rows, D), bf16),
            shape((everyone * padded, D), bf16),
            shape((ctx * wire[0], wire[1]), bf16),
            shape((count + 8, width), f32),
            shape((count, H * DV), f32),
            shape((count, H * DK), f32),
            shape((count, H * DK), f32),
            shape((count, H * DV), f32),
            shape((H, count, count), f32),
            shape((count, D), bf16),
            shape((count, 128), f32),
            shape((count, 128), f32),
            shape((count, 128), f32),
            shape((CONV, width), f32),
            shape((8, D), f32),
            shape((D, 128), f32),
        ],
        in_specs=[vmem] * 4,
        out_specs=[anywhere] * 3 + [vmem] * 13,
        scratch_shapes=[
            pltpu.VMEM((depth, D), bf16),
            pltpu.VMEM(wire, bf16),
            pltpu.VMEM((mix_rows, D), bf16),
            pltpu.VMEM((padded, D), bf16),
            pltpu.VMEM((count + PAD, D), bf16),
            pltpu.VMEM((PAD, D), bf16),
            pltpu.SemaphoreType.DMA((number,)),
            pltpu.SemaphoreType.DMA((number,)),
            pltpu.SemaphoreType.DMA((3 + depth // DV,)),
        ],
        compiler_params=pltpu.CompilerParams(
            collective_id=tag, has_side_effects=True, vmem_limit_bytes=60 * 2**20
        ),
        cost_estimate=pl.CostEstimate(flops=0, bytes_accessed=10**8, transcendentals=0),
        name="front",
    )(mix_flat, ffn_flat, x, small)


def dot_nn(a, b):
    return lax.dot_general(a, b, (((1,), (0,)), ((), ())), preferred_element_type=jnp.float32)


def dot_nt(a, b):
    return lax.dot_general(a, b, (((1,), (1,)), ((), ())), preferred_element_type=jnp.float32)


def dot_tn(a, b):
    return lax.dot_general(a, b, (((0,), (0,)), ((), ())), preferred_element_type=jnp.float32)


def chunk_of(rows):
    return max(size for size in range(16, 577, 16) if rows % size == 0)


def by_chunks(rows, body):
    size = chunk_of(rows)

    def turn(index, carry):
        body(pl.ds(pl.multiple_of(index * size, 16), size), index * size, size)
        return carry

    lax.fori_loop(0, rows // size, turn, 0)


def norm_back(grad, values, scale, gain):
    plain = values * scale
    pulled = grad * gain
    through = scale * (pulled - plain * jnp.mean(pulled * plain, axis=-1, keepdims=True))
    return through, jnp.sum(grad * plain, axis=0, keepdims=True)


def middle_kernel(
    rows, place_ref, wires_ref, query_ref, keys_ref, values_ref, inverse_ref, beta_ref, decay_ref,
    gate_ref, gains_ref, x_ref, cot_ref, mix_hbm, ffn_hbm,
    result_ref, grad_resid_ref, grad_out_ref, ffn_grad_ref, gain_two_grad_ref, state_ref, pseudo_ref,
    local_ref, grad_mixed_ref, grad_gate_ref, gain_head_grad_ref,
    w_out, w_ffn, mixed_ref, head_out_ref, pre_ref, compact_ref, down_ref, hidden_ref, total_ref,
    grad_head_ref, sems,
):
    count = query_ref.shape[0]
    padded = -(-rows // 16) * 16
    gain_two_ref = gains_ref.at[1:2, :]
    gain_head_ref = gains_ref.at[2:3, 0:DV]
    out_rows = w_out.shape[0]
    load_out = pltpu.make_async_copy(
        mix_hbm.at[pl.ds(mix_hbm.shape[0] - out_rows, out_rows), :], w_out, sems.at[0]
    )
    load_ffn = pltpu.make_async_copy(ffn_hbm, w_ffn, sems.at[1])
    load_out.start()
    load_ffn.start()
    forward_chain(
        place_ref, wires_ref, query_ref, keys_ref, values_ref, inverse_ref, beta_ref, decay_ref,
        gate_ref, gain_head_ref, head_out_ref, mixed_ref, state_ref, pseudo_ref,
    )
    load_out.wait()
    resid = x_ref[...].astype(jnp.float32) + dot_nn(head_out_ref[...], w_out[...])
    scale = lax.rsqrt(jnp.mean(resid * resid, axis=-1, keepdims=True) + EPSILON)
    normed = (resid * scale * gain_two_ref[...]).astype(jnp.bfloat16)
    load_ffn.wait()
    pairs = 2 * FF
    blocks = ffn_hbm.shape[0] // padded
    used = -(-pairs // rows)
    split = pairs // rows
    inside = pairs - split * rows
    upper_rows = used * padded
    down_start = split * padded
    down_rows = (blocks - split) * padded
    bf16 = jnp.bfloat16

    def pre(span, start, size):
        pre_ref[span, :] = dot_nt(w_ffn[span, :], normed)

    by_chunks(upper_rows, pre)
    for block in range(used):
        size = min(rows, pairs - block * rows)
        compact_ref[pl.ds(block * rows, size), :] = pre_ref[pl.ds(block * padded, size), :]
    down_ref[...] = jnp.zeros_like(down_ref)

    def pieces():
        done = 0
        for block in range(blocks - split):
            offset = inside if block == 0 else 0
            size = rows - offset
            yield done, block * padded + offset, size
            done += size

    gate = compact_ref[0:FF, :]
    up = compact_ref[FF:pairs, :]
    hidden_ref[...] = gate * jax.nn.sigmoid(gate) * up
    for done, spot, size in pieces():
        down_ref[pl.ds(spot, size), :] = hidden_ref[pl.ds(done, size), :]
    total_ref[...] = resid

    def out_chunk(span, start, size):
        here = pl.ds(pl.multiple_of(down_start + start, 16), size)
        total_ref[...] += dot_tn(down_ref[span, :].astype(bf16), w_ffn[here, :])

    by_chunks(down_rows, out_chunk)
    result_ref[...] = total_ref[...].astype(bf16)
    cot = cot_ref[...]

    def hidden_chunk(span, start, size):
        here = pl.ds(pl.multiple_of(down_start + start, 16), size)
        pre_ref[span, :] = dot_nt(w_ffn[here, :], cot)

    by_chunks(down_rows, hidden_chunk)
    for done, spot, size in pieces():
        hidden_ref[pl.ds(done, size), :] = pre_ref[pl.ds(spot, size), :]
    gate = compact_ref[0:FF, :]
    up = compact_ref[FF:pairs, :]
    active, slope = silu_pair(gate)
    grad_hidden = hidden_ref[...]
    compact_ref[0:FF, :] = grad_hidden * up * slope
    compact_ref[FF:pairs, :] = grad_hidden * active
    pre_ref[...] = jnp.zeros_like(pre_ref)
    for block in range(used):
        size = min(rows, pairs - block * rows)
        pre_ref[pl.ds(block * padded, size), :] = compact_ref[pl.ds(block * rows, size), :]
    total_ref[...] = jnp.zeros_like(total_ref)

    def mid_chunk(span, start, size):
        piece = pre_ref[span, :].astype(bf16)
        total_ref[...] += dot_tn(piece, w_ffn[span, :])
        ffn_grad_ref[span, :] = dot_nn(piece, normed).astype(bf16)

    by_chunks(upper_rows, mid_chunk)
    shared = upper_rows - down_start
    if shared:
        both = jnp.concatenate(
            [pre_ref[pl.ds(down_start, shared), :], down_ref[pl.ds(0, shared), :]], axis=1
        ).astype(bf16)
        against = jnp.concatenate([normed, cot], axis=0)
        ffn_grad_ref[pl.ds(down_start, shared), :] = dot_nn(both, against).astype(bf16)

    def down_chunk(span, start, size):
        here = pl.ds(pl.multiple_of(shared + start, 16), size)
        there = pl.ds(pl.multiple_of(upper_rows + start, 16), size)
        ffn_grad_ref[there, :] = dot_nn(down_ref[here, :].astype(bf16), cot).astype(bf16)

    by_chunks(down_rows - shared, down_chunk)
    resid = x_ref[...].astype(jnp.float32) + dot_nn(head_out_ref[...], w_out[...])
    through, gain_two_grad_ref[...] = norm_back(total_ref[...], resid, scale, gain_two_ref[...])
    grad_resid = cot.astype(jnp.float32) + through
    grad_resid_ref[...] = grad_resid
    resid_half = grad_resid.astype(bf16)
    grad_out_ref[...] = dot_tn(head_out_ref[...], resid_half).astype(bf16)
    grad_head_ref[...] = dot_nt(resid_half, w_out[...])
    backward_local(
        grad_head_ref, mixed_ref, query_ref, keys_ref, values_ref, inverse_ref, beta_ref, decay_ref,
        gate_ref, gain_head_ref, local_ref, grad_mixed_ref, grad_gate_ref, gain_head_grad_ref,
    )


def middle(rows, place, wires, query, keys, values, inverse, beta, decay, gate, gains, x, cot, mix, ffn):
    f32, bf16 = jnp.float32, jnp.bfloat16
    count = query.shape[0]
    padded = -(-rows // 16) * 16
    blocks = ffn.shape[0] // padded
    used, split = -(-2 * FF // rows), 2 * FF // rows
    out_rows = H * DV
    vmem = pl.BlockSpec(memory_space=pltpu.VMEM)
    anywhere = pl.BlockSpec(memory_space=pl.ANY)
    return pl.pallas_call(
        functools.partial(middle_kernel, rows),
        out_shape=[
            jax.ShapeDtypeStruct((count, D), bf16),
            jax.ShapeDtypeStruct((count, D), f32),
            jax.ShapeDtypeStruct((out_rows, D), bf16),
            jax.ShapeDtypeStruct(ffn.shape, bf16),
            jax.ShapeDtypeStruct((1, D), f32),
            jax.ShapeDtypeStruct((H, DK, DV), f32),
            jax.ShapeDtypeStruct((count, H * DV), f32),
            jax.ShapeDtypeStruct((H * DK, DV), bf16),
            jax.ShapeDtypeStruct((count, H * DV), f32),
            jax.ShapeDtypeStruct((count, H * DV), bf16),
            jax.ShapeDtypeStruct((1, DV), f32),
        ],
        in_specs=[pl.BlockSpec(memory_space=pltpu.SMEM)] + [vmem] * 11 + [anywhere] * 2,
        out_specs=[vmem] * 11,
        scratch_shapes=[
            pltpu.VMEM((out_rows, D), bf16),
            pltpu.VMEM(ffn.shape, bf16),
            pltpu.VMEM((count, H * DV), f32),
            pltpu.VMEM((count, H * DV), bf16),
            pltpu.VMEM((used * padded, count), f32),
            pltpu.VMEM((2 * FF, count), f32),
            pltpu.VMEM(((blocks - split) * padded, count), f32),
            pltpu.VMEM((FF, count), f32),
            pltpu.VMEM((count, D), f32),
            pltpu.VMEM((count, H * DV), f32),
            pltpu.SemaphoreType.DMA((2,)),
        ],
        compiler_params=pltpu.CompilerParams(vmem_limit_bytes=60 * 2**20),
        cost_estimate=pl.CostEstimate(flops=10**10, bytes_accessed=5 * 10**7, transcendentals=0),
        name="middle",
    )(place, wires, query, keys, values, inverse, beta, decay, gate, gains, x, cot, mix, ffn)


def back_kernel(
    side, wires_ref, local_ref, query_ref, keys_ref, values_ref, inverse_ref, beta_ref, decay_ref,
    state_ref, pseudo_ref, grad_mixed_ref, ext_ref, taps_ref, grad_gate_ref, grad_resid_ref, x_ref,
    normed_ref, gains_ref, factor_ref, w_gates_ref, gain_two_grad_ref,
    gain_head_grad_ref, ffn_grad, grad_out, mix_hbm,
    ffn_flat, mix_flat, grad_input_ref, small_out, squares_out,
    *scratch,
):
    scratch = list(scratch)
    take = lambda number: [scratch.pop(0) for unused in range(number)]
    after_ref, padded_ref, locals_ref, border_ref, taps_grad_ref = take(5)
    grad_beta_ref, grad_decay_ref, proj_ref, mix_grad, weight_ref, total_ref, arrived_ref = take(7)
    ffn_total, mix_total = take(2)
    ffn_scratch, mix_scratch, small_scratch, square_scratch = take(7), take(6), take(3), take(3)
    send_sems, recv_sems, local_sems, weight_sems, free_sem = scratch
    mix_scratch.insert(1, ffn_scratch[1].at[:, pl.ds(0, mix_total.shape[0]), :])
    f32, bf16 = jnp.float32, jnp.bfloat16
    place = Place(side)
    copies = Copies(send_sems, recv_sems, local_sems)
    place.enter(all_z=True, more=(place.behind,))
    count, width = query_ref.shape[0], taps_ref.shape[1]
    depth = proj_ref.shape[1]
    conv_ref = padded_ref.at[pl.ds(8, count), :]
    scatter = Scatter(place, copies, ffn_grad, *ffn_scratch)
    ffn = scatter.steps(ffn_total)
    mix = Scatter(place, copies, mix_grad, *mix_scratch).steps(mix_total)
    states = gather_steps(place, copies, local_ref, locals_ref, plane=True)
    states.pop(0)()
    ffn.pop(0)()
    own_out = copies.local(grad_out, mix_grad.at[pl.ds(depth, grad_out.shape[0]), :])
    for step in states:
        step()
        ffn.pop(0)()
    work = back_chain(
        wires_ref, locals_ref, query_ref, keys_ref, values_ref, inverse_ref, beta_ref,
        decay_ref, state_ref, pseudo_ref, grad_mixed_ref, ext_ref, taps_ref,
        conv_ref, border_ref, taps_grad_ref, grad_beta_ref, grad_decay_ref,
        after_ref, padded_ref,
    )
    for unused in work:
        ffn.pop(0)()
    border = copies.push(border_ref, arrived_ref, place.before)
    pl.semaphore_signal(free_sem, inc=1, device_id=place.other_core, device_id_type=MESH)
    grad_decay = grad_decay_ref[...]
    grad_logits = (grad_beta_ref[...] + grad_decay) * factor_ref[...]
    normed = normed_ref[...]
    proj_ref[:, width:] = grad_gate_ref[...]
    ffn.pop(0)()
    border.wait_recv()
    arrived = jnp.where(place.spot < place.ctx - 1, arrived_ref[...], 0.0)
    conv_ref[pl.ds(count - 8, 8), :] = conv_ref[pl.ds(count - 8, 8), :] + arrived
    proj_ref[:, :width] = conv_ref[...].astype(bf16)
    chunk = DV
    for start in range(0, depth, chunk):
        mix_grad[pl.ds(start, chunk), :] = dot_tn(proj_ref[:, start : start + chunk], normed).astype(bf16)
    own_out.wait()
    pl.semaphore_wait(free_sem, 1)
    mix.pop(0)()

    def fetch(start):
        slot = start // chunk % 2
        copy = pltpu.make_async_copy(
            mix_hbm.at[pl.ds(start, chunk), :], weight_ref.at[slot], weight_sems.at[slot]
        )
        copy.start()
        return copy

    coming = [fetch(0), fetch(chunk)]
    ffn.pop(0)()
    mix.pop(0)()
    total_ref[...] = mm_nt(grad_logits, w_gates_ref[...])
    for start in range(0, depth, chunk):
        coming.pop(0).wait()
        total_ref[...] += dot_nn(proj_ref[:, start : start + chunk], weight_ref[start // chunk % 2])
        if start + 2 * chunk < depth:
            coming.append(fetch(start + 2 * chunk))
    if ffn:
        ffn.pop(0)()
    mix.pop(0)()
    x = x_ref[...].astype(f32)
    scale = lax.rsqrt(jnp.mean(x * x, axis=-1, keepdims=True) + EPSILON)
    through, gain_one_grad = norm_back(total_ref[...], x, scale, gains_ref[0:1, :])
    grad_input_ref[...] = (grad_resid_ref[...] + through).astype(bf16)
    small = Everywhere(place, copies, small_scratch[2], *small_scratch[:2])
    sums = small.total.at[0]
    sums[...] = jnp.zeros(sums.shape, f32)
    one, two, head, tap, gate, rest = small_places()

    def place_row(first, value):
        for index in range(value.shape[1] // 128):
            sums[first + index : first + index + 1, :] = value[:, index * 128 : (index + 1) * 128]

    place_row(one, gain_one_grad)
    place_row(two, gain_two_grad_ref[...])
    place_row(head, gain_head_grad_ref[...])
    for index in range(CONV):
        place_row(tap + index * (width // 128), taps_grad_ref[index : index + 1, :])
    sums[gate:rest, :] = pack_gates(mm_tn(normed.astype(f32), grad_logits))
    lanes = lax.broadcasted_iota(jnp.int32, (1, 128), 1)
    by_size = jnp.sum(grad_decay * decay_ref[...], axis=0, keepdims=True)
    by_bias = jnp.sum(grad_logits, axis=0, keepdims=True)
    sums[rest : rest + 1, :] = jnp.where(
        lanes < H, pltpu.roll(by_size, 128 - H, 1), jnp.where(lanes < 2 * H, by_bias, 0.0)
    )
    small.send(0)
    extra = []
    for turn in range(3):
        extra.append(lambda turn=turn: small.take(turn))
        extra.append(lambda turn=turn: small.send(turn + 1) if turn < 2 else small.send_z())
    while mix or ffn or extra:
        for queue in (ffn, mix, extra):
            if queue:
                queue.pop(0)()
    small_total = small.take_z()
    small_out[...] = small_total
    squares = jnp.zeros((8, 128), f32)
    for total in (mix_total, ffn_total):
        value = total[...]
        line = jnp.sum(value * value, axis=0, keepdims=True)
        for start in range(0, D, 128):
            squares = squares + line[:, start : start + 128] * 0.125
    square = Everywhere(place, copies, square_scratch[2], *square_scratch[:2])
    square.total[0] = squares
    everything = square.run()
    own = jnp.sum(small_total * small_total, axis=0, keepdims=True)
    result = jnp.sum(jnp.sum(everything, axis=0, keepdims=True), axis=1, keepdims=True) + jnp.sum(
        own, axis=1, keepdims=True
    )
    squares_out[...] = jnp.broadcast_to(result, squares_out.shape)
    to_flat(mix_flat, mix_total[...])
    to_flat(ffn_flat, ffn_total[0 : ffn_flat.shape[0] * 128 // D, :])
    copies.finish()


def back(side, tag, ffn_rows, small_rows, *args):
    f32, bf16 = jnp.float32, jnp.bfloat16
    deep, ctx = lax.axis_size("dp"), lax.axis_size("ctx")
    query, ext, taps = args[2], args[11], args[12]
    ffn_grad, grad_out = args[-3], args[-2]
    count, width = query.shape[0], taps.shape[1]
    depth = width + H * DV
    everyone = deep * ctx
    rows = ffn_grad.shape[0] // everyone
    mix_rows = (depth + grad_out.shape[0]) // everyone
    number = 2 * Scatter.copies_of(deep) + gather_copies(1) + 2 * (3 + deep - 1) + 1
    vmem = pl.BlockSpec(memory_space=pltpu.VMEM)
    anywhere = pl.BlockSpec(memory_space=pl.ANY)
    return pl.pallas_call(
        functools.partial(back_kernel, side),
        out_shape=[
            jax.ShapeDtypeStruct((ffn_rows * D // 128, 128), f32),
            jax.ShapeDtypeStruct((mix_rows * D // 128, 128), f32),
            jax.ShapeDtypeStruct((count, D), bf16),
            jax.ShapeDtypeStruct((small_rows, 128), f32),
            jax.ShapeDtypeStruct((8, 128), f32),
        ],
        in_specs=[vmem] * (len(args) - 3) + [anywhere] * 3,
        out_specs=[vmem] * 5,
        scratch_shapes=[
            pltpu.VMEM((H, DK, DV), f32),
            pltpu.VMEM((count + 16, width), f32),
            pltpu.VMEM((ctx * H * DK, DV), bf16),
            pltpu.VMEM((8, width), f32),
            pltpu.VMEM((8, width), f32),
            pltpu.VMEM((count, 128), f32),
            pltpu.VMEM((count, 128), f32),
            pltpu.VMEM((count, depth), bf16),
            pltpu.VMEM((depth + grad_out.shape[0], D), bf16),
            pltpu.VMEM((2, DV, D), bf16),
            pltpu.VMEM((count, D), f32),
            pltpu.VMEM((8, width), f32),
            pltpu.VMEM((rows, D), f32),
            pltpu.VMEM((mix_rows, D), f32),
        ]
        + Scatter.scratch(deep, rows)
        + [shape for index, shape in enumerate(Scatter.scratch(deep, mix_rows)) if index != 1]
        + Everywhere.scratch(deep, small_rows, 128)
        + Everywhere.scratch(deep, 8, 128)
        + [
            pltpu.SemaphoreType.DMA((number,)),
            pltpu.SemaphoreType.DMA((number,)),
            pltpu.SemaphoreType.DMA((8 * deep + 2,)),
            pltpu.SemaphoreType.DMA((2,)),
            pltpu.SemaphoreType.REGULAR,
        ],
        compiler_params=pltpu.CompilerParams(
            collective_id=tag, has_side_effects=True, vmem_limit_bytes=62 * 2**20
        ),
        cost_estimate=pl.CostEstimate(flops=10**10, bytes_accessed=10**8, transcendentals=0),
        name="back",
    )(*args)


def back_chain(
    wire_ref, local_ref, query_ref, keys_ref, values_ref, inverse_ref, beta_ref,
    decay_ref, state_ref, pseudo_ref, grad_mixed_ref, ext_ref, taps_ref,
    grad_conv_ref, grad_border_ref, grad_taps_ref, grad_beta_ref, grad_decay_ref,
    after_ref, padded_ref,
):
    count = query_ref.shape[0]
    width = taps_ref.shape[1]
    devices = wire_ref.shape[0]
    after_ref[...] = jnp.zeros_like(after_ref)

    def lap(step, carry):
        index = devices - 1 - step
        for head in range(H):
            to_end, key_mix, value_mix, whole = wire_parts(wire_ref, index, head, count)
            after = after_ref[head]
            inner = wire_mm(to_end, after, ((1,), (0,)))
            spot = pl.multiple_of((index * H + head) * DK, DK)
            local = local_ref[pl.ds(spot, DK), :].astype(jnp.float32)
            after_ref[head] = whole * after - wire_mm(key_mix, inner, ((0,), (0,))) + local
        return carry

    lax.fori_loop(0, devices - 1 - lax.axis_index("ctx"), lap, 0)
    yield
    taps = taps_ref[...]
    summed = ext_sum(ext_ref, taps, count, 0, width)
    activated, slope = silu_pair(summed)
    padded_ref[0:8, :] = jnp.zeros((8, width), jnp.float32)
    padded_ref[pl.ds(8 + count, 8), :] = jnp.zeros((8, width), jnp.float32)
    rows, cols = iotas(count)
    lower = rows >= cols
    strict = rows > cols
    lanes = lax.broadcasted_iota(jnp.int32, (count, 128), 1)
    beta_out = jnp.zeros((count, 128), jnp.float32)
    cumulative_out = jnp.zeros((count, 128), jnp.float32)
    row_column = lax.broadcasted_iota(jnp.int32, (count, 1), 0)
    for head in range(H):
        query = query_ref[:, head * DK : (head + 1) * DK]
        keys = keys_ref[:, head * DK : (head + 1) * DK]
        span = slice(head * DV, (head + 1) * DV)
        values = values_ref[:, span]
        beta = beta_ref[:, head : head + 1]
        matrix, grown, to_end, whole = decay_terms(decay_lane(decay_ref, head), rows, cols)
        inverse = inverse_ref[head]
        state = state_ref[head]
        after = after_ref[head]
        pseudo = pseudo_ref[:, span]
        grad_mixed = grad_mixed_ref[:, span]
        keys_grown = keys * (beta * grown)
        key_mix = mm(inverse, keys_grown)
        value_mix = mm(inverse, values * beta)
        gram = mm_nt(keys, keys)
        system = jnp.where(strict, beta * gram * matrix, 0.0)
        scores = mm_nt(query, keys) * matrix
        keys_end = keys * to_end
        query_grown = query * grown
        grad_query_grown = mm_nt(grad_mixed, state)
        grad_scores = jnp.where(lower, mm_nt(grad_mixed, pseudo), 0.0)
        grad_pseudo = mm_tn(scores, grad_mixed) + mm(keys_end, after)
        grad_keys_end = mm_nt(pseudo, after)
        grad_whole = jnp.sum(jnp.sum(after * state, axis=1, keepdims=True), axis=0, keepdims=True)
        grad_value_in = mm_tn(inverse, grad_pseudo)
        grad_key_in = mm_tn(inverse, -mm_nt(grad_pseudo, state))
        grad_system = -jnp.where(
            strict, mm_nt(grad_value_in, value_mix) + mm_nt(grad_key_in, key_mix), 0.0
        )
        grad_raw = grad_scores * matrix
        grad_query = mm(grad_raw, keys) + grad_query_grown * grown
        grad_keys = mm_tn(grad_raw, query)
        weighted = grad_system * matrix
        grad_beta = jnp.sum(weighted * gram, axis=1, keepdims=True)
        grad_gram = weighted * beta
        grad_keys = grad_keys + mm(grad_gram, keys) + mm_tn(grad_gram, keys)
        spread = grad_scores * scores + grad_system * system
        grad_cumulative = jnp.sum(spread, axis=1, keepdims=True)
        across = jnp.sum(spread, axis=0, keepdims=True)
        grad_cumulative = grad_cumulative - jnp.sum(
            jnp.where(rows == cols, across, 0.0), axis=1, keepdims=True
        )
        grad_keys = grad_keys + grad_key_in * (beta * grown)
        through = jnp.sum(grad_key_in * keys, axis=1, keepdims=True) * grown
        grad_beta = grad_beta + through + jnp.sum(grad_value_in * values, axis=1, keepdims=True)
        grad_cumulative = grad_cumulative + through * beta
        grad_values = grad_value_in * beta
        grad_cumulative = grad_cumulative + jnp.sum(
            grad_query_grown * query_grown, axis=1, keepdims=True
        )
        grad_keys = grad_keys + grad_keys_end * to_end
        ending = jnp.sum(grad_keys_end * keys_end, axis=1, keepdims=True)
        final = jnp.sum(ending, axis=0, keepdims=True) + whole * grad_whole
        grad_cumulative = grad_cumulative - ending + jnp.where(row_column == count - 1, final, 0.0)
        beta_out = jnp.where(lanes == head, grad_beta, beta_out)
        cumulative_out = jnp.where(lanes == H + head, grad_cumulative, cumulative_out)
        key_part = activated[:, (H + head) * DK : (H + head + 1) * DK]
        key_scale = unit_rows(key_part)
        query_part = activated[:, head * DK : (head + 1) * DK]
        query_scale = unit_rows(query_part)
        factor = DK ** (-0.5)
        grad_query_part = (factor * query_scale) * (
            grad_query
            - query_part
            * (query_scale * query_scale)
            * jnp.sum(grad_query * query_part, axis=-1, keepdims=True)
        )
        grad_key_part = key_scale * (
            grad_keys
            - key_part
            * (key_scale * key_scale)
            * jnp.sum(grad_keys * key_part, axis=-1, keepdims=True)
        )
        spots = (head * DK, (H + head) * DK, 2 * H * DK + head * DV)
        for spot, grad in zip(spots, (grad_query_part, grad_key_part, grad_values)):
            size = grad.shape[1]
            padded_ref[pl.ds(8, count), spot : spot + size] = grad * slope[:, spot : spot + size]
        yield
    grad_beta_ref[...] = beta_out
    grad_decay_ref[...] = mm_tn(jnp.where(lower, 1.0, 0.0), cumulative_out)
    conv_total = jnp.zeros((count, width), jnp.float32)
    border_total = jnp.zeros((8, width), jnp.float32)
    summed_grad = padded_ref[pl.ds(8, count), :]
    tap_rows = lax.broadcasted_iota(jnp.int32, (8, width), 0)
    taps_total = jnp.zeros((8, width), jnp.float32)
    for tap in range(CONV):
        shift = CONV - 1 - tap
        conv_total = conv_total + taps[tap : tap + 1] * padded_ref[pl.ds(8 + shift, count), :]
        border_total = border_total + taps[tap : tap + 1] * padded_ref[pl.ds(shift, 8), :]
        piece = jnp.sum(
            summed_grad * ext_ref[pl.ds(8 - (CONV - 1) + tap, count), :width],
            axis=0,
            keepdims=True,
        )
        taps_total = jnp.where(tap_rows == tap, piece, taps_total)
    grad_conv_ref[...] = conv_total
    grad_border_ref[...] = border_total
    grad_taps_ref[...] = taps_total
    yield


def chip_side():
    half = lax.axis_size("ctx") // 2
    side = math.isqrt(half)
    return side if side == 2 and 2 * side * side == lax.axis_size("ctx") else 0


def adam_step(weight, grad_full, first, second, clip):
    grad_clipped = grad_full * clip
    first_new = BETA_ONE * first + (1.0 - BETA_ONE) * grad_clipped
    second_new = BETA_TWO * second + (1.0 - BETA_TWO) * grad_clipped * grad_clipped
    update = (
        first_new / CORRECT_ONE / (jnp.sqrt(second_new / CORRECT_TWO) + ADAM_EPS)
        + DECAY_RATE * weight
    )
    return (weight - LEARN_RATE * update, first_new, second_new)


def plain(
    inputs,
    cotangent,
    mixer_params,
    mixer_first,
    mixer_second,
    ffn_params,
    ffn_first,
    ffn_second,
    small_params,
    small_first,
    small_second,
):
    gain_one, gain_two, gain_head, tap_values, w_gates, a_log, dt_bias = unpack_small(small_params)
    width = tap_values.shape[1]
    mix_part = mixer_params.astype(jnp.bfloat16)
    ffn_part = ffn_params.astype(jnp.bfloat16)
    mix_whole, ffn_whole = (
        lax.all_gather(mix_part, ("dp", "ctx"), axis=0, tiled=True),
        lax.all_gather(ffn_part, ("dp", "ctx"), axis=0, tiled=True),
    )
    w_in, w_out, w_ffn, w_down = split_weights(mix_whole, ffn_whole)
    x_float = inputs[0].astype(jnp.float32)
    count = x_float.shape[0]
    normed_in = norm_scale(x_float, gain_one).astype(jnp.bfloat16)
    projected = jnp.dot(normed_in, w_in.T, preferred_element_type=jnp.float32)
    gate_logits = jnp.dot(normed_in.astype(jnp.float32), w_gates, precision=HIGHEST)
    f32 = jnp.float32
    devices = lax.axis_size("ctx")
    place = lax.axis_index("ctx").astype(jnp.int32).reshape(1)
    out_gate = projected[:, width:]
    edge = from_behind(projected[count - 8 :, :width], "ctx", 1)
    border = jnp.where(lax.broadcasted_iota(jnp.int32, (8, 1), 0) >= 8 - (CONV - 1), edge, 0.0)
    (beta, decay), pull_gates = jax.vjp(gates, gate_logits, a_log, dt_bias)
    wire, query, keys, values, inverse = fused(
        forward_parts,
        (
            jax.ShapeDtypeStruct((count + PAD, H * (2 * DK + DV)), jnp.bfloat16),
            jax.ShapeDtypeStruct((count, H * DK), f32),
            jax.ShapeDtypeStruct((count, H * DK), f32),
            jax.ShapeDtypeStruct((count, H * DV), f32),
            jax.ShapeDtypeStruct((H, count, count), f32),
        ),
        scratch=(pltpu.VMEM((count + 8, width), f32),),
        label="forward_parts",
    )(projected, border, tap_values, beta, decay)
    wires = lax.all_gather(wire, "ctx")
    gain_row = gain_head.reshape(1, DV)
    head_out, mixed, state, pseudo = fused(
        forward_chain,
        (
            jax.ShapeDtypeStruct((count, H * DV), jnp.bfloat16),
            jax.ShapeDtypeStruct((count, H * DV), f32),
            jax.ShapeDtypeStruct((H, DK, DV), f32),
            jax.ShapeDtypeStruct((count, H * DV), f32),
        ),
        scalars=1,
        label="forward_chain",
    )(place, wires, query, keys, values, inverse, beta, decay, out_gate, gain_row)
    resid = x_float + jnp.dot(head_out, w_out, preferred_element_type=jnp.float32)
    normed_mid = norm_scale(resid, gain_two).astype(jnp.bfloat16)
    ffn_pre = jnp.dot(normed_mid, w_ffn.T, preferred_element_type=jnp.float32)
    gate_part = ffn_pre[:, :FF]
    up_part = ffn_pre[:, FF:]
    hidden_act = swiglu(gate_part, up_part).astype(jnp.bfloat16)
    result = (resid + jnp.dot(hidden_act, w_down, preferred_element_type=jnp.float32)).astype(
        jnp.bfloat16
    )
    seq_grad = cotangent[0]
    grad_float = seq_grad.astype(jnp.float32)
    grad_down = jnp.dot(hidden_act.T, seq_grad, preferred_element_type=jnp.float32)
    grad_hidden = jnp.dot(seq_grad, w_down.T, preferred_element_type=jnp.float32)
    unused_one, pull_swiglu = jax.vjp(swiglu, gate_part, up_part)
    grad_gate, grad_up = pull_swiglu(grad_hidden)
    grad_pre = jnp.concatenate([grad_gate, grad_up], axis=1).astype(jnp.bfloat16)
    grad_ffn = jnp.dot(grad_pre.T, normed_mid, preferred_element_type=jnp.float32)
    grad_mid = jnp.dot(grad_pre, w_ffn, preferred_element_type=jnp.float32)
    unused_two, pull_mid = jax.vjp(norm_scale, resid, gain_two)
    grad_through, grad_gain_two = pull_mid(grad_mid)
    grad_resid = grad_float + grad_through
    resid_half = grad_resid.astype(jnp.bfloat16)
    grad_out = jnp.dot(head_out.T, resid_half, preferred_element_type=jnp.float32)
    grad_head = jnp.dot(resid_half, w_out.T, preferred_element_type=jnp.float32)
    local, grad_mixed, grad_gate_out, grad_gain_head = fused(
        backward_local,
        (
            jax.ShapeDtypeStruct((H * DK, DV), jnp.bfloat16),
            jax.ShapeDtypeStruct((count, H * DV), f32),
            jax.ShapeDtypeStruct((count, H * DV), f32),
            jax.ShapeDtypeStruct((1, DV), f32),
        ),
        label="backward_local",
    )(grad_head, mixed, query, keys, values, inverse, beta, decay, out_gate, gain_row)
    locals_all = lax.all_gather(local, "ctx")
    locals_all, grad_ffn, grad_down = lax.optimization_barrier((locals_all, grad_ffn, grad_down))
    ffn_shard = scatter_rows((grad_ffn, grad_down))
    grad_conv, grad_border, grad_taps, grad_beta, grad_decay = fused(
        backward_chain,
        (
            jax.ShapeDtypeStruct((count, width), f32),
            jax.ShapeDtypeStruct((8, width), f32),
            jax.ShapeDtypeStruct((8, width), f32),
            jax.ShapeDtypeStruct((count, 128), f32),
            jax.ShapeDtypeStruct((count, 128), f32),
        ),
        scratch=(
            pltpu.VMEM((H, DK, DV), f32),
            pltpu.VMEM((count + 8, width), f32),
            pltpu.VMEM((count + 16, width), f32),
        ),
        scalars=1,
        label="backward_chain",
    )(
        place, wires, locals_all, query, keys, values, inverse, beta, decay, state, pseudo,
        grad_mixed, projected, border, tap_values,
    )
    grad_logits, grad_alog, grad_bias = pull_gates((grad_beta[:, :H], grad_decay[:, :H]))
    returned = from_behind(grad_border, "ctx", -1)[8 - (CONV - 1) :]
    grad_conv = grad_conv.at[count - (CONV - 1) :].add(returned)
    grad_proj = jnp.concatenate([grad_conv, grad_gate_out], axis=1).astype(jnp.bfloat16)
    grad_in = jnp.dot(grad_proj.T, normed_in, preferred_element_type=jnp.float32)
    grad_normed = jnp.dot(grad_proj, w_in, preferred_element_type=jnp.float32) + jnp.dot(
        grad_logits, w_gates.T, precision=HIGHEST
    )
    grad_gates = jnp.dot(normed_in.astype(jnp.float32).T, grad_logits, precision=HIGHEST)
    unused_six, pull_in = jax.vjp(norm_scale, x_float, gain_one)
    grad_x, grad_gain_one = pull_in(grad_normed)
    grad_input = (grad_resid + grad_x).astype(jnp.bfloat16)
    small_local = jnp.concatenate(
        [
            grad_gain_one,
            grad_gain_two,
            grad_gain_head.reshape(-1),
            grad_taps[:CONV].reshape(-1),
            grad_gates.reshape(-1),
            grad_alog,
            grad_bias,
        ]
    )
    small_grad = lax.psum(small_local, ("dp", "ctx"))
    ffn_shard, grad_in, grad_out = lax.optimization_barrier((ffn_shard, grad_in, grad_out))
    mix_shard = scatter_rows((grad_in, grad_out))
    small_grad, mix_shard = lax.optimization_barrier((small_grad, mix_shard))
    shard_squares = jnp.sum(mix_shard * mix_shard) + jnp.sum(ffn_shard * ffn_shard)
    total_squares = lax.psum(shard_squares, ("dp", "ctx"))
    squares = total_squares + jnp.sum(small_grad * small_grad)
    clip = jnp.minimum(1.0, MAX_NORM / (jnp.sqrt(squares) + 1e-06))
    mixer_new, mixer_first_new, mixer_second_new = adam_step(
        mixer_params, mix_shard, mixer_first, mixer_second, clip
    )
    ffn_new, ffn_first_new, ffn_second_new = adam_step(
        ffn_params, ffn_shard, ffn_first, ffn_second, clip
    )
    small_new, small_first_new, small_second_new = adam_step(
        small_params, small_grad, small_first, small_second, clip
    )
    return (
        result[None],
        grad_input[None],
        mix_shard,
        ffn_shard,
        small_grad,
        mixer_new,
        mixer_first_new,
        mixer_second_new,
        ffn_new,
        ffn_first_new,
        ffn_second_new,
        small_new,
        small_first_new,
        small_second_new,
    )


def fast(
    side, inputs, cotangent, mixer_params, mixer_first, mixer_second, ffn_params, ffn_first, ffn_second, small_params, small_first, small_second,
):
    ffn_rows = ffn_params.size // D
    short = -small_params.size % 1024
    small = jnp.pad(small_params, (0, short)).reshape(-1, 128)
    (
        mix_whole, ffn_whole, wires, ext, out_gate, query, keys, values, inverse, normed_in, beta, decay,
        factor, taps, gains, w_gates,
    ) = front(mixer_params.reshape(-1, 128), ffn_params.reshape(-1, 128), inputs[0], small, side, 1)
    wires = wires.reshape(lax.axis_size("ctx"), -1, wires.shape[1])
    place = lax.axis_index("ctx").astype(jnp.int32).reshape(1)
    (
        result, grad_resid, grad_out, ffn_grad, grad_gain_two, state, pseudo, local, grad_mixed,
        grad_gate_out, grad_gain_head,
    ) = middle(
        ffn_rows, place, wires, query, keys, values, inverse, beta, decay, out_gate, gains,
        inputs[0], cotangent[0], mix_whole, ffn_whole,
    )
    ffn_shard, mix_shard, grad_input, sums, squares = back(
        side, 2, ffn_rows, small.shape[0], wires, local, query, keys, values, inverse, beta, decay,
        state, pseudo, grad_mixed, ext, taps, grad_gate_out, grad_resid, inputs[0], normed_in, gains,
        factor, w_gates, grad_gain_two, grad_gain_head, ffn_grad, grad_out, mix_whole,
    )
    small_grad = sums.reshape(-1)[: small_params.size]
    mix_shard = mix_shard.reshape(-1)
    ffn_shard = ffn_shard.reshape(-1)
    squares = squares[0, 0]
    clip = jnp.minimum(1.0, MAX_NORM / (jnp.sqrt(squares) + 1e-06))
    mixer_new, mixer_first_new, mixer_second_new = adam_step(
        mixer_params, mix_shard, mixer_first, mixer_second, clip
    )
    ffn_new, ffn_first_new, ffn_second_new = adam_step(
        ffn_params, ffn_shard, ffn_first, ffn_second, clip
    )
    small_new, small_first_new, small_second_new = adam_step(
        small_params, small_grad, small_first, small_second, clip
    )
    return (
        result[None],
        grad_input[None],
        mix_shard,
        ffn_shard,
        small_grad,
        mixer_new,
        mixer_first_new,
        mixer_second_new,
        ffn_new,
        ffn_first_new,
        ffn_second_new,
        small_new,
        small_first_new,
        small_second_new,
    )


def body(*args):
    rows, left = divmod(args[5].size, D)
    side = chip_side() if left == 0 and args[2].size % (32 * D) == 0 else 0
    return fast(side, *args) if side else plain(*args)


def solution(mesh):
    return jax.shard_map(
        body,
        mesh=mesh,
        in_specs=(
            P("dp", "ctx", None),
            P("dp", "ctx", None),
            P(("dp", "ctx")),
            P(("dp", "ctx")),
            P(("dp", "ctx")),
            P(("dp", "ctx")),
            P(("dp", "ctx")),
            P(("dp", "ctx")),
            P(),
            P(),
            P(),
        ),
        out_specs=(
            P("dp", "ctx", None),
            P("dp", "ctx", None),
            P(("dp", "ctx")),
            P(("dp", "ctx")),
            P(),
            P(("dp", "ctx")),
            P(("dp", "ctx")),
            P(("dp", "ctx")),
            P(("dp", "ctx")),
            P(("dp", "ctx")),
            P(("dp", "ctx")),
            P(),
            P(),
            P(),
        ),
        check_vma=False,
    )
```

```python
import functools
import math
import jax
import jax.numpy as jnp
from jax import lax
from jax.experimental import pallas as pl
from jax.experimental.pallas import tpu as pltpu
from jax.sharding import PartitionSpec as P

D = 1024
H = 2
DK = 256
DV = 512
FF = 1408
CONV = 4
GROUP = 64


EPSILON = 1e-06
ADAM_EPS = 1e-08
LEARN_RATE = 0.02
BETA_ONE = 0.9
BETA_TWO = 0.999
DECAY_RATE = 0.1
CORRECT_ONE = 1.0 - 0.9**3
CORRECT_TWO = 1.0 - 0.999**3
MAX_NORM = 1.0
HIGHEST = lax.Precision.HIGHEST


def from_behind(value, axis, steps):
    count = lax.axis_size(axis)
    initial, last = (max(0, -steps), min(count, count - steps))
    return lax.ppermute(value, axis, [(source, source + steps) for source in range(initial, last)])


def norm_scale(values, gain):
    return values * lax.rsqrt(jnp.mean(values * values, axis=-1, keepdims=True) + EPSILON) * gain


def swiglu(gate_part, up_part):
    return jax.nn.silu(gate_part) * up_part


def unpack_small(packed):
    width = 2 * H * DK + H * DV
    lengths = [D, D, DV, CONV * width, D * 2 * H, H, H]
    pieces = []
    offset = 0
    for length in lengths:
        pieces.append(packed[offset : offset + length])
        offset = offset + length
    return (
        pieces[0],
        pieces[1],
        pieces[2],
        pieces[3].reshape(CONV, width),
        pieces[4].reshape(D, 2 * H),
        pieces[5],
        pieces[6],
    )


def split_weights(mix_whole, ffn_whole):
    mix_rows = mix_whole.reshape(-1, D)
    ffn_rows = ffn_whole.reshape(-1, D)
    edge = 2 * H * DK + 2 * H * DV
    return (mix_rows[:edge], mix_rows[edge:], ffn_rows[: 2 * FF], ffn_rows[2 * FF :])


PAD = 16
HIGH = dict(precision=HIGHEST, preferred_element_type=jnp.float32)


def mm(a, b):
    return lax.dot_general(a, b, (((1,), (0,)), ((), ())), **HIGH)


def mm_nt(a, b):
    return lax.dot_general(a, b, (((1,), (1,)), ((), ())), **HIGH)


def mm_tn(a, b):
    return lax.dot_general(a, b, (((0,), (0,)), ((), ())), **HIGH)


def halves(a):
    high = a.astype(jnp.bfloat16)
    return high, (a - high.astype(jnp.float32)).astype(jnp.bfloat16)


def wire_mm(a, b, dims):
    high, low = halves(b)
    first = lax.dot_general(a, high, (dims, ((), ())), preferred_element_type=jnp.float32)
    return first + lax.dot_general(a, low, (dims, ((), ())), preferred_element_type=jnp.float32)


def iotas(size):
    shape = (size, size)
    return (
        lax.broadcasted_iota(jnp.int32, shape, 0),
        lax.broadcasted_iota(jnp.int32, shape, 1),
    )


def to_row(column, rows, cols):
    return jnp.sum(jnp.where(rows == cols, column, 0.0), axis=0, keepdims=True)


def unit_inverse(strict_part, rows, cols):
    size = strict_part.shape[0]
    inverse = jnp.where(rows == cols, 1.0, 0.0) - jnp.where(
        (rows // 2 == cols // 2), strict_part, 0.0
    )
    block = 2
    while block < size:
        joined = (rows // (2 * block) == cols // (2 * block)) & (rows // block != cols // block)
        off = jnp.where(joined, strict_part, 0.0)
        inverse = inverse - mm(mm(inverse, off), inverse)
        block = 2 * block
    return inverse


def silu_pair(x):
    gate = jax.nn.sigmoid(x)
    return x * gate, gate * (1.0 + x * (1.0 - gate))


def conv_sum(extended_ref, taps, count):
    total = None
    for tap in range(CONV):
        piece = taps[tap : tap + 1] * extended_ref[pl.ds(8 - (CONV - 1) + tap, count), :]
        total = piece if total is None else total + piece
    return total


def unit_rows(part):
    return lax.rsqrt(jnp.sum(part * part, axis=-1, keepdims=True) + EPSILON)


def decay_lane(decay_ref, head):
    lane = head + (H if decay_ref.shape[1] > H else 0)
    return decay_ref[:, lane : lane + 1]


def decay_terms(decay_column, rows, cols):
    lower = rows >= cols
    size = rows.shape[0]
    spread_in = jnp.broadcast_to(decay_column, (size, 128))
    cumulative = mm(jnp.where(lower, 1.0, 0.0), spread_in)[:, :1]
    across = to_row(cumulative, rows, cols)
    matrix = jnp.where(lower, jnp.exp(jnp.where(lower, cumulative - across, 0.0)), 0.0)
    last = cumulative[size - 1 : size]
    return matrix, jnp.exp(cumulative), jnp.exp(last - cumulative), jnp.exp(last)


def forward_parts(
    projected_ref, border_ref, taps_ref, beta_ref, decay_ref,
    wire_ref, query_ref, keys_ref, values_ref, inverse_ref, extended_ref,
):
    count = projected_ref.shape[0]
    width = taps_ref.shape[1]
    extended_ref[0:8, :] = border_ref[...]
    extended_ref[pl.ds(8, count), :] = projected_ref[:, :width]
    summed = conv_sum(extended_ref, taps_ref[...], count)
    activated = summed * jax.nn.sigmoid(summed)
    rows, cols = iotas(count)
    for head in range(H):
        query_part = activated[:, head * DK : (head + 1) * DK]
        key_part = activated[:, (H + head) * DK : (H + head + 1) * DK]
        start = 2 * H * DK + head * DV
        values = activated[:, start : start + DV]
        query = query_part * unit_rows(query_part) * DK ** (-0.5)
        keys = key_part * unit_rows(key_part)
        beta = beta_ref[:, head : head + 1]
        matrix, grown, to_end, whole = decay_terms(decay_lane(decay_ref, head), rows, cols)
        system = jnp.where(rows > cols, beta * mm_nt(keys, keys) * matrix, 0.0)
        inverse = unit_inverse(system, rows, cols)
        key_mix = mm(inverse, keys * (beta * grown))
        value_mix = mm(inverse, values * beta)
        base = head * (2 * DK + DV)
        wire_ref[0:count, base : base + DK] = (keys * to_end).astype(jnp.bfloat16)
        wire_ref[0:count, base + DK : base + 2 * DK] = key_mix.astype(jnp.bfloat16)
        wire_ref[0:count, base + 2 * DK : base + 2 * DK + DV] = value_mix.astype(jnp.bfloat16)
        high, low = halves(jnp.broadcast_to(whole, (PAD, 2 * DK + DV)))
        first = lax.broadcasted_iota(jnp.int32, (PAD, 2 * DK + DV), 0) < 8
        tail = jnp.where(first, high.astype(jnp.float32), low.astype(jnp.float32))
        wire_ref[pl.ds(count, PAD), base : base + 2 * DK + DV] = tail.astype(jnp.bfloat16)
        query_ref[:, head * DK : (head + 1) * DK] = query
        keys_ref[:, head * DK : (head + 1) * DK] = keys
        values_ref[:, head * DV : (head + 1) * DV] = values
        inverse_ref[head] = inverse


def wire_parts(wire_ref, index, head, count):
    base = head * (2 * DK + DV)
    to_end = wire_ref[index, 0:count, base : base + DK]
    key_mix = wire_ref[index, 0:count, base + DK : base + 2 * DK]
    value_mix = wire_ref[index, 0:count, base + 2 * DK : base + 2 * DK + DV]
    tail = wire_ref[index, pl.ds(count, PAD), base : base + 128].astype(jnp.float32)
    whole = tail[0:1, 0:1] + tail[8:9, 0:1]
    return to_end, key_mix, value_mix, whole


def own_mix(inverse, keys, values, beta, grown):
    return mm(inverse, keys * (beta * grown)), mm(inverse, values * beta)


def forward_chain(
    place_ref, wire_ref, query_ref, keys_ref, values_ref, inverse_ref, beta_ref, decay_ref,
    gate_ref, gain_ref, head_out_ref, mixed_ref, state_ref, pseudo_ref,
):
    count = query_ref.shape[0]
    state_ref[...] = jnp.zeros_like(state_ref)

    def lap(index, carry):
        for head in range(H):
            to_end, key_mix, value_mix, whole = wire_parts(wire_ref, index, head, count)
            state = state_ref[head]
            pseudo = value_mix.astype(jnp.float32) - wire_mm(key_mix, state, ((1,), (0,)))
            state_ref[head] = whole * state + wire_mm(to_end, pseudo, ((0,), (0,)))
        return carry

    lax.fori_loop(0, place_ref[0], lap, 0)
    rows, cols = iotas(count)
    for head in range(H):
        query = query_ref[:, head * DK : (head + 1) * DK]
        keys = keys_ref[:, head * DK : (head + 1) * DK]
        span = slice(head * DV, (head + 1) * DV)
        beta = beta_ref[:, head : head + 1]
        matrix, grown, to_end, whole = decay_terms(decay_lane(decay_ref, head), rows, cols)
        key_mix, value_mix = own_mix(inverse_ref[head], keys, values_ref[:, span], beta, grown)
        state = state_ref[head]
        pseudo = value_mix - mm(key_mix, state)
        mixed = mm(query * grown, state) + mm(mm_nt(query, keys) * matrix, pseudo)
        scale = lax.rsqrt(jnp.mean(mixed * mixed, axis=-1, keepdims=True) + EPSILON)
        gated, unused = silu_pair(gate_ref[:, span])
        head_out_ref[:, span] = (mixed * scale * gain_ref[...] * gated).astype(jnp.bfloat16)
        mixed_ref[:, span] = mixed
        pseudo_ref[:, span] = pseudo


def backward_local(
    grad_ref, mixed_ref, query_ref, keys_ref, values_ref, inverse_ref, beta_ref, decay_ref,
    gate_ref, gain_ref, local_ref, grad_mixed_ref, grad_gate_ref, grad_gain_ref,
):
    count = query_ref.shape[0]
    rows, cols = iotas(count)
    gain_total = jnp.zeros((1, DV), jnp.float32)
    for head in range(H):
        query = query_ref[:, head * DK : (head + 1) * DK]
        keys = keys_ref[:, head * DK : (head + 1) * DK]
        span = slice(head * DV, (head + 1) * DV)
        mixed = mixed_ref[:, span]
        grad = grad_ref[:, span]
        scale = lax.rsqrt(jnp.mean(mixed * mixed, axis=-1, keepdims=True) + EPSILON)
        plain = mixed * scale
        gated, slope = silu_pair(gate_ref[:, span])
        grad_gate_ref[:, span] = (grad * plain * gain_ref[...] * slope).astype(grad_gate_ref.dtype)
        grad_normed = grad * gated
        gain_total = gain_total + jnp.sum(grad_normed * plain, axis=0, keepdims=True)
        pulled = grad_normed * gain_ref[...]
        grad_mixed = scale * (pulled - plain * jnp.mean(pulled * plain, axis=-1, keepdims=True))
        grad_mixed_ref[:, span] = grad_mixed
        beta = beta_ref[:, head : head + 1]
        matrix, grown, to_end, whole = decay_terms(decay_lane(decay_ref, head), rows, cols)
        key_mix = mm(inverse_ref[head], keys * (beta * grown))
        grad_pseudo = mm_tn(mm_nt(query, keys) * matrix, grad_mixed)
        local = mm_tn(query * grown, grad_mixed) - mm_tn(key_mix, grad_pseudo)
        local_ref[head * DK : (head + 1) * DK, :] = local.astype(jnp.bfloat16)
    grad_gain_ref[...] = gain_total


def backward_chain(
    place_ref, wire_ref, local_ref, query_ref, keys_ref, values_ref, inverse_ref, beta_ref,
    decay_ref, state_ref, pseudo_ref, grad_mixed_ref, projected_ref, border_ref, taps_ref,
    grad_conv_ref, grad_border_ref, grad_taps_ref, grad_beta_ref, grad_decay_ref,
    after_ref, extended_ref, padded_ref,
):
    count = query_ref.shape[0]
    width = taps_ref.shape[1]
    devices = wire_ref.shape[0]
    after_ref[...] = jnp.zeros_like(after_ref)

    def lap(step, carry):
        index = devices - 1 - step
        for head in range(H):
            to_end, key_mix, value_mix, whole = wire_parts(wire_ref, index, head, count)
            after = after_ref[head]
            inner = wire_mm(to_end, after, ((1,), (0,)))
            local = local_ref[index, head * DK : (head + 1) * DK, :].astype(jnp.float32)
            after_ref[head] = whole * after - wire_mm(key_mix, inner, ((0,), (0,))) + local
        return carry

    lax.fori_loop(0, devices - 1 - place_ref[0], lap, 0)
    extended_ref[0:8, :] = border_ref[...]
    extended_ref[pl.ds(8, count), :] = projected_ref[:, :width]
    taps = taps_ref[...]
    summed = conv_sum(extended_ref, taps, count)
    activated, slope = silu_pair(summed)
    padded_ref[0:8, :] = jnp.zeros((8, width), jnp.float32)
    padded_ref[pl.ds(8 + count, 8), :] = jnp.zeros((8, width), jnp.float32)
    rows, cols = iotas(count)
    lower = rows >= cols
    strict = rows > cols
    lanes = lax.broadcasted_iota(jnp.int32, (count, 128), 1)
    beta_out = jnp.zeros((count, 128), jnp.float32)
    cumulative_out = jnp.zeros((count, 128), jnp.float32)
    row_column = lax.broadcasted_iota(jnp.int32, (count, 1), 0)
    for head in range(H):
        query = query_ref[:, head * DK : (head + 1) * DK]
        keys = keys_ref[:, head * DK : (head + 1) * DK]
        span = slice(head * DV, (head + 1) * DV)
        values = values_ref[:, span]
        beta = beta_ref[:, head : head + 1]
        matrix, grown, to_end, whole = decay_terms(decay_lane(decay_ref, head), rows, cols)
        inverse = inverse_ref[head]
        state = state_ref[head]
        after = after_ref[head]
        pseudo = pseudo_ref[:, span]
        grad_mixed = grad_mixed_ref[:, span]
        keys_grown = keys * (beta * grown)
        key_mix = mm(inverse, keys_grown)
        value_mix = mm(inverse, values * beta)
        gram = mm_nt(keys, keys)
        system = jnp.where(strict, beta * gram * matrix, 0.0)
        scores = mm_nt(query, keys) * matrix
        keys_end = keys * to_end
        query_grown = query * grown
        grad_query_grown = mm_nt(grad_mixed, state)
        grad_scores = jnp.where(lower, mm_nt(grad_mixed, pseudo), 0.0)
        grad_pseudo = mm_tn(scores, grad_mixed) + mm(keys_end, after)
        grad_keys_end = mm_nt(pseudo, after)
        grad_whole = jnp.sum(jnp.sum(after * state, axis=1, keepdims=True), axis=0, keepdims=True)
        grad_value_in = mm_tn(inverse, grad_pseudo)
        grad_key_in = mm_tn(inverse, -mm_nt(grad_pseudo, state))
        grad_system = -jnp.where(
            strict, mm_nt(grad_value_in, value_mix) + mm_nt(grad_key_in, key_mix), 0.0
        )
        grad_raw = grad_scores * matrix
        grad_query = mm(grad_raw, keys) + grad_query_grown * grown
        grad_keys = mm_tn(grad_raw, query)
        weighted = grad_system * matrix
        grad_beta = jnp.sum(weighted * gram, axis=1, keepdims=True)
        grad_gram = weighted * beta
        grad_keys = grad_keys + mm(grad_gram, keys) + mm_tn(grad_gram, keys)
        spread = grad_scores * scores + grad_system * system
        grad_cumulative = jnp.sum(spread, axis=1, keepdims=True)
        across = jnp.sum(spread, axis=0, keepdims=True)
        grad_cumulative = grad_cumulative - jnp.sum(
            jnp.where(rows == cols, across, 0.0), axis=1, keepdims=True
        )
        grad_keys = grad_keys + grad_key_in * (beta * grown)
        through = jnp.sum(grad_key_in * keys, axis=1, keepdims=True) * grown
        grad_beta = grad_beta + through + jnp.sum(grad_value_in * values, axis=1, keepdims=True)
        grad_cumulative = grad_cumulative + through * beta
        grad_values = grad_value_in * beta
        grad_cumulative = grad_cumulative + jnp.sum(
            grad_query_grown * query_grown, axis=1, keepdims=True
        )
        grad_keys = grad_keys + grad_keys_end * to_end
        ending = jnp.sum(grad_keys_end * keys_end, axis=1, keepdims=True)
        final = jnp.sum(ending, axis=0, keepdims=True) + whole * grad_whole
        grad_cumulative = grad_cumulative - ending + jnp.where(row_column == count - 1, final, 0.0)
        beta_out = jnp.where(lanes == head, grad_beta, beta_out)
        cumulative_out = jnp.where(lanes == head, grad_cumulative, cumulative_out)
        key_part = activated[:, (H + head) * DK : (H + head + 1) * DK]
        key_scale = unit_rows(key_part)
        query_part = activated[:, head * DK : (head + 1) * DK]
        query_scale = unit_rows(query_part)
        factor = DK ** (-0.5)
        grad_query_part = (factor * query_scale) * (
            grad_query
            - query_part
            * (query_scale * query_scale)
            * jnp.sum(grad_query * query_part, axis=-1, keepdims=True)
        )
        grad_key_part = key_scale * (
            grad_keys
            - key_part
            * (key_scale * key_scale)
            * jnp.sum(grad_keys * key_part, axis=-1, keepdims=True)
        )
        spots = (head * DK, (H + head) * DK, 2 * H * DK + head * DV)
        for spot, grad in zip(spots, (grad_query_part, grad_key_part, grad_values)):
            size = grad.shape[1]
            padded_ref[pl.ds(8, count), spot : spot + size] = grad * slope[:, spot : spot + size]
    grad_beta_ref[...] = beta_out
    grad_decay_ref[...] = mm_tn(jnp.where(lower, 1.0, 0.0), cumulative_out)
    conv_total = jnp.zeros((count, width), jnp.float32)
    border_total = jnp.zeros((8, width), jnp.float32)
    summed_grad = padded_ref[pl.ds(8, count), :]
    tap_rows = lax.broadcasted_iota(jnp.int32, (8, width), 0)
    taps_total = jnp.zeros((8, width), jnp.float32)
    for tap in range(CONV):
        shift = CONV - 1 - tap
        conv_total = conv_total + taps[tap : tap + 1] * padded_ref[pl.ds(8 + shift, count), :]
        border_total = border_total + taps[tap : tap + 1] * padded_ref[pl.ds(shift, 8), :]
        piece = jnp.sum(
            summed_grad * extended_ref[pl.ds(8 - (CONV - 1) + tap, count), :],
            axis=0,
            keepdims=True,
        )
        taps_total = jnp.where(tap_rows == tap, piece, taps_total)
    grad_conv_ref[...] = conv_total
    grad_border_ref[...] = border_total
    grad_taps_ref[...] = taps_total


def fused(body, outputs, scratch=(), scalars=0, cost=(0, 0), label=None):
    def call(*args):
        vmem = pl.BlockSpec(memory_space=pltpu.VMEM)
        smem = pl.BlockSpec(memory_space=pltpu.SMEM)
        return pl.pallas_call(
            body,
            out_shape=outputs,
            in_specs=[smem] * scalars + [vmem] * (len(args) - scalars),
            out_specs=[vmem] * len(outputs),
            scratch_shapes=list(scratch),
            compiler_params=pltpu.CompilerParams(vmem_limit_bytes=60 * 2**20),
            cost_estimate=pl.CostEstimate(
                flops=cost[0], bytes_accessed=cost[1], transcendentals=0
            ),
            name=label,
        )(*args)

    return call


def gates(gate_logits, a_log, dt_bias):
    beta = jax.nn.sigmoid(gate_logits[:, :H])
    decay = -jnp.exp(a_log) * jax.nn.softplus(gate_logits[:, H:] + dt_bias)
    return beta, decay


def scatter_rows(pieces):
    outer, inner = lax.axis_size("dp"), lax.axis_size("ctx")
    whole = jnp.concatenate([piece.astype(jnp.bfloat16) for piece in pieces], axis=0)
    lane = math.gcd(whole.size // (outer * inner), D)
    blocks = whole.reshape(outer, inner, -1, lane)
    part = lax.psum_scatter(blocks, "ctx", scatter_dimension=1, tiled=False)
    own = lax.psum_scatter(part, "dp", scatter_dimension=0, tiled=False)
    return own.astype(jnp.float32).reshape(-1)


MESH = pl.DeviceIdType.MESH


class Place:
    def __init__(self, side):
        self.deep = lax.axis_size("dp")
        self.side = side
        self.ctx = lax.axis_size("ctx")
        self.z = lax.axis_index("dp")
        spot = lax.axis_index("ctx")
        self.c = lax.rem(spot, 2)
        chip = lax.div(spot, 2)
        self.x = lax.rem(chip, side)
        self.y = lax.div(chip, side)
        self.other_core = self.device(self.z, self.y, self.x, 1 - self.c)
        self.other_x = self.device(self.z, self.y, 1 - self.x, self.c)
        self.other_y = self.device(self.z, 1 - self.y, self.x, self.c)
        self.next_z = self.device(self.along(1), self.y, self.x, self.c)
        self.spot = spot
        self.before = (self.z, lax.rem(spot + self.ctx - 1, self.ctx))
        self.behind = (self.z, lax.rem(spot + 1, self.ctx))

    def along(self, step):
        return lax.rem(self.z + step + self.deep, self.deep)

    def device(self, z, y, x, c):
        return (z, (y * self.side + x) * 2 + c)

    def block(self, z, y, x, c):
        return z * self.ctx + (y * self.side + x) * 2 + c

    def enter_all(self):
        barrier = pltpu.get_barrier_semaphore()
        friends = [(self.z, lax.rem(self.spot + step, self.ctx)) for step in range(1, self.ctx)]
        friends += [(self.along(step), self.spot) for step in range(1, self.deep)]
        for friend in friends:
            pl.semaphore_signal(barrier, inc=1, device_id=friend, device_id_type=MESH)
        pl.semaphore_wait(barrier, len(friends))

    def enter(self, all_z=False, more=()):
        barrier = pltpu.get_barrier_semaphore()
        steps = range(1, self.deep) if all_z else (-1,)
        friends = [self.other_core, self.other_x, self.other_y, *more]
        friends += [self.device(self.along(step), self.y, self.x, self.c) for step in steps]
        for friend in friends:
            pl.semaphore_signal(barrier, inc=1, device_id=friend, device_id_type=MESH)
        pl.semaphore_wait(barrier, len(friends))


class Copies:
    def __init__(self, send_sems, recv_sems, local_sems=None):
        self.send_sems, self.recv_sems, self.local_sems = send_sems, recv_sems, local_sems
        self.sent, self.locals = [], 0

    def push(self, source, target, device):
        index = len(self.sent)
        copy = pltpu.make_async_remote_copy(
            src_ref=source,
            dst_ref=target,
            send_sem=self.send_sems.at[index],
            recv_sem=self.recv_sems.at[index],
            device_id=device,
            device_id_type=MESH,
        )
        copy.start()
        self.sent.append(copy)
        return copy

    def local(self, source, target):
        copy = pltpu.make_async_copy(source, target, self.local_sems.at[self.locals])
        copy.start()
        self.locals += 1
        return copy

    def finish(self):
        for copy in self.sent:
            copy.wait_send()


def upper(rows):
    return rows // 2 // 16 * 16


def gather_steps(place, copies, shard_ref, out_ref, plane=False):
    rows, deep = shard_ref.shape[0], 1 if plane else place.deep
    top = upper(rows)
    spans = {None: (0, rows), 0: (0, top), 1: (top, rows - top)}
    ring, near, far, core = {}, {}, {}, []

    def cut(ref, start, part):
        offset, size = spans[part]
        return ref.at[pl.ds(pl.multiple_of(start + offset, 16), size), :]

    def start_of(rel, dy, dx):
        y = 1 - place.y if dy else place.y
        x = 1 - place.x if dx else place.x
        z = 0 if plane else place.along(-rel)
        return place.block(z, y, x, place.c) * rows

    def forward(rel, dy, dx, part, device):
        start = start_of(rel, dy, dx)
        own = rel == 0 and not dy and not dx
        source = cut(shard_ref, 0, part) if own else cut(out_ref, start, part)
        return copies.push(source, cut(out_ref, start, part), device)

    def along_z(rel, part):
        if rel < deep - 1:
            ring[rel, part] = forward(rel, 0, 0, part, place.next_z)

    def spread(rel):
        near[rel, "x0"] = forward(rel, 0, 0, 0, place.other_x)
        near[rel, "y1"] = forward(rel, 0, 0, 1, place.other_y)
        near[rel, "y0"] = forward(rel, 0, 0, 0, place.other_y)
        near[rel, "x1"] = forward(rel, 0, 0, 1, place.other_x)
        core.append(forward(rel, 0, 0, None, place.other_core))

    def second(rel):
        near[rel, "x0"].wait_recv()
        far[rel, 0] = forward(rel, 0, 1, 0, place.other_y)
        near[rel, "y1"].wait_recv()
        far[rel, 1] = forward(rel, 1, 0, 1, place.other_x)
        core.append(forward(rel, 0, 1, 0, place.other_core))
        core.append(forward(rel, 1, 0, 1, place.other_core))

    def third(rel):
        near[rel, "y0"].wait_recv()
        core.append(forward(rel, 1, 0, 0, place.other_core))
        near[rel, "x1"].wait_recv()
        core.append(forward(rel, 0, 1, 1, place.other_core))

    def fourth(rel):
        for part in (0, 1):
            far[rel, part].wait_recv()
            core.append(forward(rel, 1, 1, part, place.other_core))

    own_copy = []

    def first():
        own_copy.append(copies.local(shard_ref, cut(out_ref, start_of(0, 0, 0), None)))
        for part in (0, 1):
            along_z(0, part)
        spread(0)

    def later(rel):
        for part in (0, 1):
            ring[rel - 1, part].wait_recv()
            along_z(rel, part)
        spread(rel)

    def last():
        for copy in core:
            copy.wait_recv()
        own_copy[0].wait()

    steps = [first]
    for rel in range(1, deep):
        steps.append(lambda rel=rel: later(rel))
        steps.append(lambda rel=rel: second(rel - 1))
        steps.append(lambda rel=rel: third(rel - 1))
    steps.append(lambda: second(deep - 1))
    steps.append(lambda: third(deep - 1))
    for rel in range(deep):
        steps.append(lambda rel=rel: fourth(rel))
    steps.append(last)
    return steps


def wide(value):
    return value.astype(jnp.float32)


class Scatter:
    def __init__(self, place, copies, grad_ref, held, from_core, first_x, first_y, last_x, last_y, from_z):
        self.place, self.copies, self.grad = place, copies, grad_ref
        self.held, self.from_core, self.from_z = held, from_core, from_z
        self.first = {0: first_y, 1: first_x}
        self.last = {0: last_x, 1: last_y}
        self.rows = held.shape[1]
        self.top = upper(self.rows)
        self.loads, self.cores, self.near, self.far, self.ring = {}, {}, {}, {}, {}

    @staticmethod
    def scratch(deep, rows):
        top = upper(rows)
        low = rows - top
        return [
            pltpu.VMEM((4 * deep, rows, D), jnp.bfloat16),
            pltpu.VMEM((4 * deep, rows, D), jnp.bfloat16),
            pltpu.VMEM((2 * deep, low, D), jnp.bfloat16),
            pltpu.VMEM((2 * deep, top, D), jnp.bfloat16),
            pltpu.VMEM((deep, top, D), jnp.bfloat16),
            pltpu.VMEM((deep, low, D), jnp.bfloat16),
            pltpu.VMEM((deep - 1, rows, D), jnp.bfloat16),
        ]

    @staticmethod
    def copies_of(deep):
        return 4 * deep + 4 * deep + 2 * deep + 2 * (deep - 1)

    def slot(self, rel, dy, dx):
        return (rel - 1) * 4 + dy * 2 + dx

    def span(self, part):
        return pl.ds(0, self.top) if part == 0 else pl.ds(self.top, self.rows - self.top)

    def load(self):
        place = self.place
        for rel in range(1, place.deep + 1):
            for dy, dx in ((1, 1), (1, 0), (0, 1), (0, 0)):
                y = 1 - place.y if dy else place.y
                x = 1 - place.x if dx else place.x
                slot = self.slot(rel, dy, dx)

                def rows_of(core):
                    start = place.block(place.along(-rel), y, x, core) * self.rows
                    return self.grad.at[pl.ds(pl.multiple_of(start, 16), self.rows), :]

                self.cores[slot] = self.copies.push(
                    rows_of(1 - place.c), self.from_core.at[slot], place.other_core
                )
                self.loads[slot] = self.copies.local(rows_of(place.c), self.held.at[slot])

    def stage_one(self, rel):
        place = self.place
        for dy, dx in ((1, 1), (1, 0), (0, 1), (0, 0)):
            slot = self.slot(rel, dy, dx)
            self.loads[slot].wait()
            self.cores[slot].wait_recv()
            self.held[slot] = (wide(self.held[slot]) + wide(self.from_core[slot])).astype(jnp.bfloat16)
            if dy:
                self.near[rel, 0, dx] = self.copies.push(
                    self.held.at[slot, self.span(0), :],
                    self.first[0].at[(rel - 1) * 2 + dx],
                    place.other_y,
                )
            if dx:
                self.near[rel, 1, dy] = self.copies.push(
                    self.held.at[slot, self.span(1), :],
                    self.first[1].at[(rel - 1) * 2 + dy],
                    place.other_x,
                )

    def add(self, slot, part, piece):
        self.held[slot, self.span(part), :] = (
            wide(self.held[slot, self.span(part), :]) + wide(piece)
        ).astype(jnp.bfloat16)

    def stage_two(self, rel):
        place = self.place
        for part in (0, 1):
            for away in (1, 0):
                self.near[rel, part, away].wait_recv()
                slot = self.slot(rel, away, 0) if part else self.slot(rel, 0, away)
                self.add(slot, part, self.first[part][(rel - 1) * 2 + away])
                if away:
                    self.far[rel, part] = self.copies.push(
                        self.held.at[slot, self.span(part), :],
                        self.last[part].at[rel - 1],
                        place.other_y if part else place.other_x,
                    )

    def stage_three(self, rel, total_ref=None):
        slot = self.slot(rel, 0, 0)
        for part in (0, 1):
            span = self.span(part)
            self.far[rel, part].wait_recv()
            total = wide(self.held[slot, span, :]) + wide(self.last[part][rel - 1])
            if rel >= 2:
                self.ring[rel - 1, part].wait_recv()
                total = total + wide(self.from_z[rel - 2, span, :])
            if rel == self.place.deep:
                total_ref[span, :] = total
                continue
            self.held[slot, span, :] = total.astype(jnp.bfloat16)
            self.ring[rel, part] = self.copies.push(
                self.held.at[slot, span, :], self.from_z.at[rel - 1, span, :], self.place.next_z
            )

    def steps(self, total_ref):
        deep = self.place.deep
        out = [self.load]
        for turn in range(1, deep + 3):
            if turn <= deep:
                out.append(lambda rel=turn: self.stage_one(rel))
            if 1 <= turn - 1 <= deep:
                out.append(lambda rel=turn - 1: self.stage_two(rel))
            if 1 <= turn - 2 <= deep:
                out.append(lambda rel=turn - 2: self.stage_three(rel, total_ref))
        return out


class Everywhere:
    def __init__(self, place, copies, total, slots, stack):
        self.place, self.copies = place, copies
        self.total, self.slots, self.stack = total, slots, stack
        self.turns = (place.other_core, place.other_x, place.other_y)
        self.pending = []

    @staticmethod
    def scratch(deep, rows, width):
        return [pltpu.VMEM((count, rows, width), jnp.float32) for count in (3, deep, 4)]

    def send(self, turn):
        self.pending = [
            self.copies.push(self.total.at[turn], self.slots.at[turn], self.turns[turn])
        ]

    def take(self, turn):
        self.pending[0].wait_recv()
        self.total[turn + 1] = self.total[turn] + self.slots[turn]

    def send_z(self):
        place = self.place
        self.pending = [
            self.copies.push(
                self.total.at[3],
                self.stack.at[place.z],
                place.device(place.along(step), place.y, place.x, place.c),
            )
            for step in range(1, place.deep)
        ]
        self.stack[place.z] = self.total[3]

    def take_z(self):
        for copy in self.pending:
            copy.wait_recv()
        result = self.stack[0]
        for index in range(1, self.place.deep):
            result = result + self.stack[index]
        return result

    def run(self):
        for turn in range(3):
            self.send(turn)
            self.take(turn)
        self.send_z()
        return self.take_z()


def gather_copies(deep):
    return 2 * (deep - 1) + 4 * deep + 2 * deep + deep + 2 * deep * 3


def front_parts(ext_ref, taps_ref, beta_ref, decay_ref, wire_ref, query_ref, keys_ref, values_ref, inverse_ref):
    count = query_ref.shape[0]
    width = taps_ref.shape[1]
    summed = ext_sum(ext_ref, taps_ref[...], count, 0, width)
    activated = summed * jax.nn.sigmoid(summed)
    rows, cols = iotas(count)
    for head in range(H):
        query_part = activated[:, head * DK : (head + 1) * DK]
        key_part = activated[:, (H + head) * DK : (H + head + 1) * DK]
        start = 2 * H * DK + head * DV
        values = activated[:, start : start + DV]
        query = query_part * unit_rows(query_part) * DK ** (-0.5)
        keys = key_part * unit_rows(key_part)
        beta = beta_ref[:, head : head + 1]
        matrix, grown, to_end, whole = decay_terms(decay_lane(decay_ref, head), rows, cols)
        system = jnp.where(rows > cols, beta * mm_nt(keys, keys) * matrix, 0.0)
        inverse = unit_inverse(system, rows, cols)
        key_mix = mm(inverse, keys * (beta * grown))
        value_mix = mm(inverse, values * beta)
        base = head * (2 * DK + DV)
        wire_ref[0:count, base : base + DK] = (keys * to_end).astype(jnp.bfloat16)
        wire_ref[0:count, base + DK : base + 2 * DK] = key_mix.astype(jnp.bfloat16)
        wire_ref[0:count, base + 2 * DK : base + 2 * DK + DV] = value_mix.astype(jnp.bfloat16)
        high, low = halves(jnp.broadcast_to(whole, (PAD, 2 * DK + DV)))
        first = lax.broadcasted_iota(jnp.int32, (PAD, 2 * DK + DV), 0) < 8
        tail = jnp.where(first, high.astype(jnp.float32), low.astype(jnp.float32))
        wire_ref[pl.ds(count, PAD), base : base + 2 * DK + DV] = tail.astype(jnp.bfloat16)
        query_ref[:, head * DK : (head + 1) * DK] = query
        keys_ref[:, head * DK : (head + 1) * DK] = keys
        values_ref[:, head * DV : (head + 1) * DV] = values
        inverse_ref[head] = inverse
        yield


def ext_sum(ext_ref, taps, count, start, size):
    total = None
    for tap in range(CONV):
        piece = (
            taps[tap : tap + 1, start : start + size]
            * ext_ref[pl.ds(8 - (CONV - 1) + tap, count), start : start + size]
        )
        total = piece if total is None else total + piece
    return total


def small_places():
    width = 2 * H * DK + H * DV
    starts, spot = [], 0
    for length in (D, D, DV, CONV * width, 2 * H * D):
        starts.append(spot // 128)
        spot += length
    return starts + [spot // 128]


def joined(ref, first, number):
    return jnp.concatenate([ref[first + index : first + index + 1, :] for index in range(number)], axis=1)


def gate_masks():
    each = 128 // (2 * H)
    row = lax.broadcasted_iota(jnp.int32, (D, 128), 0)
    lane = lax.broadcasted_iota(jnp.int32, (D, 128), 1)
    own = lax.rem(row, each) == lax.div(lane, 2 * H)
    rows, cols = iotas(128)
    return own, jnp.where(lax.rem(rows, 2 * H) == cols, 1.0, 0.0), each


def unpack_gates(packed):
    own, select, each = gate_masks()
    spread = jnp.broadcast_to(packed[:, None, :], (packed.shape[0], each, 128)).reshape(D, 128)
    return mm(jnp.where(own, spread, 0.0), select)


def pack_gates(plain):
    own, select, each = gate_masks()
    spread = jnp.where(own, mm_nt(plain, select), 0.0)
    return jnp.sum(spread.reshape(D // each, each, 128), axis=1)


def from_flat(flat_ref, rows):
    pieces = [flat_ref[pl.ds(index, rows, stride=D // 128), :] for index in range(D // 128)]
    return jnp.concatenate(pieces, axis=1)


def to_flat(flat_ref, value):
    for index in range(D // 128):
        flat_ref[pl.ds(index, value.shape[0], stride=D // 128), :] = value[:, index * 128 : (index + 1) * 128]


def front_kernel(
    side, mix_flat, ffn_flat, x_ref, small_ref,
    mix_out, ffn_out, wires_out, ext_ref, gate_ref, query_ref, keys_ref, values_ref, inverse_ref,
    own_normed_ref, beta_ref, decay_ref, factor_ref, taps_ref, gains_ref, w_gates_ref,
    weight_ref, wire_ref, mix_shard, ffn_shard, normed_ref, edge_ref,
    send_sems, recv_sems, local_sems,
):
    place = Place(side)
    copies = Copies(send_sems, recv_sems, local_sems)
    bf16 = jnp.bfloat16
    count = x_ref.shape[0]
    width = taps_ref.shape[1]
    mix_shard[...] = from_flat(mix_flat, mix_shard.shape[0]).astype(bf16)
    place.enter(more=(place.before,))
    mix = gather_steps(place, copies, mix_shard, mix_out)
    ffn = gather_steps(place, copies, ffn_shard, ffn_out)
    mix.pop(0)()
    one, two, head, tap, gate, rest = small_places()
    gain_one = joined(small_ref, one, D // 128)
    normed = norm_scale(x_ref[...].astype(jnp.float32), gain_one).astype(bf16)
    own_normed_ref[...] = normed
    normed_ref[pl.ds(PAD, count), :] = normed
    edge = copies.push(normed_ref.at[pl.ds(count, PAD), :], edge_ref, place.behind)
    ffn_rows = ffn_flat.shape[0] * 128 // D
    ffn_shard[...] = jnp.zeros_like(ffn_shard)
    ffn_shard[0:ffn_rows, :] = from_flat(ffn_flat, ffn_rows).astype(bf16)
    early = 3 * (place.deep - 1) + 2
    mix.pop(0)()
    gains_ref[...] = jnp.zeros_like(gains_ref)
    gains_ref[0:1, :] = gain_one
    gains_ref[1:2, :] = joined(small_ref, two, D // 128)
    gains_ref[2:3, 0:DV] = joined(small_ref, head, DV // 128)
    for index in range(CONV):
        taps_ref[index : index + 1, :] = joined(small_ref, tap + index * (width // 128), width // 128)
    for step in mix[:3]:
        step()
    w_gates_ref[...] = unpack_gates(small_ref[gate:rest, :])
    logits = mm(normed.astype(jnp.float32), w_gates_ref[...])
    for step in mix[3:5]:
        step()
    lanes = lax.broadcasted_iota(jnp.int32, (1, 128), 1)
    late = (lanes >= H) & (lanes < 2 * H)
    scalars = small_ref[rest : rest + 1, :]
    raised = logits + jnp.where(late, scalars, 0.0)
    size = jnp.exp(jnp.where(late, pltpu.roll(scalars, H, 1), 0.0))
    soft = jax.nn.sigmoid(raised)
    beta_ref[...] = soft
    decay_ref[...] = jnp.where(
        late, -size * (jnp.maximum(raised, 0.0) + jnp.log1p(jnp.exp(-jnp.abs(raised)))), 0.0
    )
    factor_ref[...] = jnp.where(late, -size * soft, jnp.where(lanes < H, soft * (1.0 - soft), 0.0))
    for step in mix[5 : early - 2]:
        step()
    ffn.pop(0)()
    for step in mix[early - 2 :]:
        step()
    edge.wait_recv()
    normed_ref[0:PAD, :] = jnp.where(place.spot > 0, edge_ref[...], jnp.zeros_like(edge_ref))
    depth = weight_ref.shape[0]
    chunk = DV
    loads = [
        copies.local(mix_out.at[pl.ds(start, chunk), :], weight_ref.at[pl.ds(start, chunk), :])
        for start in range(0, depth, chunk)
    ]
    for index, load in enumerate(loads):
        load.wait()
        span = pl.ds(index * chunk, chunk)
        piece = dot_nt(normed_ref[...], weight_ref[span, :])
        start = index * chunk
        if start < width:
            ext_ref[:, start : start + chunk] = piece[8:]
        else:
            start = start - width
            gate_ref[:, start : start + chunk] = piece[PAD:]
        if index % 2 == 1:
            ffn.pop(0)()
    parts = front_parts(
        ext_ref, taps_ref, beta_ref, decay_ref, wire_ref, query_ref, keys_ref, values_ref, inverse_ref
    )
    for unused in parts:
        for again in range(3):
            ffn.pop(0)()
    wires = gather_steps(place, copies, wire_ref, wires_out, plane=True)
    wires.pop(0)()
    ffn.pop(0)()
    while wires[1:]:
        wires.pop(0)()
        if len(ffn) > 1:
            ffn.pop(0)()
    for step in ffn + wires:
        step()
    copies.finish()


def front(mix_flat, ffn_flat, x, small, side, tag):
    f32, bf16 = jnp.float32, jnp.bfloat16
    deep, ctx = lax.axis_size("dp"), lax.axis_size("ctx")
    count = x.shape[0]
    everyone = deep * ctx
    mix_rows, ffn_rows = mix_flat.shape[0] * 128 // D, ffn_flat.shape[0] * 128 // D
    padded = -(-ffn_rows // 16) * 16
    number = 2 * gather_copies(deep) + gather_copies(1) + 1
    anywhere = pl.BlockSpec(memory_space=pl.ANY)
    vmem = pl.BlockSpec(memory_space=pltpu.VMEM)
    width = 2 * H * DK + H * DV
    depth = width + H * DV
    wire = (count + PAD, H * (2 * DK + DV))
    shape = jax.ShapeDtypeStruct
    return pl.pallas_call(
        functools.partial(front_kernel, side),
        out_shape=[
            shape((everyone * mix_rows, D), bf16),
            shape((everyone * padded, D), bf16),
            shape((ctx * wire[0], wire[1]), bf16),
            shape((count + 8, width), f32),
            shape((count, H * DV), f32),
            shape((count, H * DK), f32),
            shape((count, H * DK), f32),
            shape((count, H * DV), f32),
            shape((H, count, count), f32),
            shape((count, D), bf16),
            shape((count, 128), f32),
            shape((count, 128), f32),
            shape((count, 128), f32),
            shape((CONV, width), f32),
            shape((8, D), f32),
            shape((D, 128), f32),
        ],
        in_specs=[vmem] * 4,
        out_specs=[anywhere] * 3 + [vmem] * 13,
        scratch_shapes=[
            pltpu.VMEM((depth, D), bf16),
            pltpu.VMEM(wire, bf16),
            pltpu.VMEM((mix_rows, D), bf16),
            pltpu.VMEM((padded, D), bf16),
            pltpu.VMEM((count + PAD, D), bf16),
            pltpu.VMEM((PAD, D), bf16),
            pltpu.SemaphoreType.DMA((number,)),
            pltpu.SemaphoreType.DMA((number,)),
            pltpu.SemaphoreType.DMA((3 + depth // DV,)),
        ],
        compiler_params=pltpu.CompilerParams(
            collective_id=tag, has_side_effects=True, vmem_limit_bytes=60 * 2**20
        ),
        cost_estimate=pl.CostEstimate(flops=0, bytes_accessed=10**8, transcendentals=0),
        name="front",
    )(mix_flat, ffn_flat, x, small)


def dot_nn(a, b):
    return lax.dot_general(a, b, (((1,), (0,)), ((), ())), preferred_element_type=jnp.float32)


def dot_nt(a, b):
    return lax.dot_general(a, b, (((1,), (1,)), ((), ())), preferred_element_type=jnp.float32)


def dot_tn(a, b):
    return lax.dot_general(a, b, (((0,), (0,)), ((), ())), preferred_element_type=jnp.float32)


def chunk_of(rows):
    return max(size for size in range(16, 577, 16) if rows % size == 0)


def by_chunks(rows, body):
    size = chunk_of(rows)

    def turn(index, carry):
        body(pl.ds(pl.multiple_of(index * size, 16), size), index * size, size)
        return carry

    lax.fori_loop(0, rows // size, turn, 0)


def norm_back(grad, values, scale, gain):
    plain = values * scale
    pulled = grad * gain
    through = scale * (pulled - plain * jnp.mean(pulled * plain, axis=-1, keepdims=True))
    return through, jnp.sum(grad * plain, axis=0, keepdims=True)


def middle_kernel(
    rows, place_ref, wires_ref, query_ref, keys_ref, values_ref, inverse_ref, beta_ref, decay_ref,
    gate_ref, gains_ref, x_ref, cot_ref, mix_hbm, ffn_hbm,
    result_ref, grad_resid_ref, grad_out_ref, ffn_grad_ref, gain_two_grad_ref, state_ref, pseudo_ref,
    local_ref, grad_mixed_ref, grad_gate_ref, gain_head_grad_ref,
    w_out, w_ffn, mixed_ref, head_out_ref, pre_ref, compact_ref, down_ref, hidden_ref, total_ref,
    grad_head_ref, sems,
):
    count = query_ref.shape[0]
    padded = -(-rows // 16) * 16
    gain_two_ref = gains_ref.at[1:2, :]
    gain_head_ref = gains_ref.at[2:3, 0:DV]
    out_rows = w_out.shape[0]
    load_out = pltpu.make_async_copy(
        mix_hbm.at[pl.ds(mix_hbm.shape[0] - out_rows, out_rows), :], w_out, sems.at[0]
    )
    load_ffn = pltpu.make_async_copy(ffn_hbm, w_ffn, sems.at[1])
    load_out.start()
    load_ffn.start()
    forward_chain(
        place_ref, wires_ref, query_ref, keys_ref, values_ref, inverse_ref, beta_ref, decay_ref,
        gate_ref, gain_head_ref, head_out_ref, mixed_ref, state_ref, pseudo_ref,
    )
    load_out.wait()
    resid = x_ref[...].astype(jnp.float32) + dot_nn(head_out_ref[...], w_out[...])
    scale = lax.rsqrt(jnp.mean(resid * resid, axis=-1, keepdims=True) + EPSILON)
    normed = (resid * scale * gain_two_ref[...]).astype(jnp.bfloat16)
    load_ffn.wait()
    pairs = 2 * FF
    blocks = ffn_hbm.shape[0] // padded
    used = -(-pairs // rows)
    split = pairs // rows
    inside = pairs - split * rows
    upper_rows = used * padded
    down_start = split * padded
    down_rows = (blocks - split) * padded
    bf16 = jnp.bfloat16

    def pre(span, start, size):
        pre_ref[span, :] = dot_nt(w_ffn[span, :], normed)

    by_chunks(upper_rows, pre)
    for block in range(used):
        size = min(rows, pairs - block * rows)
        compact_ref[pl.ds(block * rows, size), :] = pre_ref[pl.ds(block * padded, size), :]
    down_ref[...] = jnp.zeros_like(down_ref)

    def pieces():
        done = 0
        for block in range(blocks - split):
            offset = inside if block == 0 else 0
            size = rows - offset
            yield done, block * padded + offset, size
            done += size

    gate = compact_ref[0:FF, :]
    up = compact_ref[FF:pairs, :]
    hidden_ref[...] = gate * jax.nn.sigmoid(gate) * up
    for done, spot, size in pieces():
        down_ref[pl.ds(spot, size), :] = hidden_ref[pl.ds(done, size), :]
    total_ref[...] = resid

    def out_chunk(span, start, size):
        here = pl.ds(pl.multiple_of(down_start + start, 16), size)
        total_ref[...] += dot_tn(down_ref[span, :].astype(bf16), w_ffn[here, :])

    by_chunks(down_rows, out_chunk)
    result_ref[...] = total_ref[...].astype(bf16)
    cot = cot_ref[...]

    def hidden_chunk(span, start, size):
        here = pl.ds(pl.multiple_of(down_start + start, 16), size)
        pre_ref[span, :] = dot_nt(w_ffn[here, :], cot)

    by_chunks(down_rows, hidden_chunk)
    for done, spot, size in pieces():
        hidden_ref[pl.ds(done, size), :] = pre_ref[pl.ds(spot, size), :]
    gate = compact_ref[0:FF, :]
    up = compact_ref[FF:pairs, :]
    active, slope = silu_pair(gate)
    grad_hidden = hidden_ref[...]
    compact_ref[0:FF, :] = grad_hidden * up * slope
    compact_ref[FF:pairs, :] = grad_hidden * active
    pre_ref[...] = jnp.zeros_like(pre_ref)
    for block in range(used):
        size = min(rows, pairs - block * rows)
        pre_ref[pl.ds(block * padded, size), :] = compact_ref[pl.ds(block * rows, size), :]
    total_ref[...] = jnp.zeros_like(total_ref)

    def mid_chunk(span, start, size):
        piece = pre_ref[span, :].astype(bf16)
        total_ref[...] += dot_tn(piece, w_ffn[span, :])
        ffn_grad_ref[span, :] = dot_nn(piece, normed).astype(bf16)

    by_chunks(upper_rows, mid_chunk)
    shared = upper_rows - down_start
    if shared:
        both = jnp.concatenate(
            [pre_ref[pl.ds(down_start, shared), :], down_ref[pl.ds(0, shared), :]], axis=1
        ).astype(bf16)
        against = jnp.concatenate([normed, cot], axis=0)
        ffn_grad_ref[pl.ds(down_start, shared), :] = dot_nn(both, against).astype(bf16)

    def down_chunk(span, start, size):
        here = pl.ds(pl.multiple_of(shared + start, 16), size)
        there = pl.ds(pl.multiple_of(upper_rows + start, 16), size)
        ffn_grad_ref[there, :] = dot_nn(down_ref[here, :].astype(bf16), cot).astype(bf16)

    by_chunks(down_rows - shared, down_chunk)
    resid = x_ref[...].astype(jnp.float32) + dot_nn(head_out_ref[...], w_out[...])
    through, gain_two_grad_ref[...] = norm_back(total_ref[...], resid, scale, gain_two_ref[...])
    grad_resid = cot.astype(jnp.float32) + through
    grad_resid_ref[...] = grad_resid
    resid_half = grad_resid.astype(bf16)
    grad_out_ref[...] = dot_tn(head_out_ref[...], resid_half).astype(bf16)
    grad_head_ref[...] = dot_nt(resid_half, w_out[...])
    backward_local(
        grad_head_ref, mixed_ref, query_ref, keys_ref, values_ref, inverse_ref, beta_ref, decay_ref,
        gate_ref, gain_head_ref, local_ref, grad_mixed_ref, grad_gate_ref, gain_head_grad_ref,
    )


def middle(rows, place, wires, query, keys, values, inverse, beta, decay, gate, gains, x, cot, mix, ffn):
    f32, bf16 = jnp.float32, jnp.bfloat16
    count = query.shape[0]
    padded = -(-rows // 16) * 16
    blocks = ffn.shape[0] // padded
    used, split = -(-2 * FF // rows), 2 * FF // rows
    out_rows = H * DV
    vmem = pl.BlockSpec(memory_space=pltpu.VMEM)
    anywhere = pl.BlockSpec(memory_space=pl.ANY)
    return pl.pallas_call(
        functools.partial(middle_kernel, rows),
        out_shape=[
            jax.ShapeDtypeStruct((count, D), bf16),
            jax.ShapeDtypeStruct((count, D), f32),
            jax.ShapeDtypeStruct((out_rows, D), bf16),
            jax.ShapeDtypeStruct(ffn.shape, bf16),
            jax.ShapeDtypeStruct((1, D), f32),
            jax.ShapeDtypeStruct((H, DK, DV), f32),
            jax.ShapeDtypeStruct((count, H * DV), f32),
            jax.ShapeDtypeStruct((H * DK, DV), bf16),
            jax.ShapeDtypeStruct((count, H * DV), f32),
            jax.ShapeDtypeStruct((count, H * DV), bf16),
            jax.ShapeDtypeStruct((1, DV), f32),
        ],
        in_specs=[pl.BlockSpec(memory_space=pltpu.SMEM)] + [vmem] * 11 + [anywhere] * 2,
        out_specs=[vmem] * 11,
        scratch_shapes=[
            pltpu.VMEM((out_rows, D), bf16),
            pltpu.VMEM(ffn.shape, bf16),
            pltpu.VMEM((count, H * DV), f32),
            pltpu.VMEM((count, H * DV), bf16),
            pltpu.VMEM((used * padded, count), f32),
            pltpu.VMEM((2 * FF, count), f32),
            pltpu.VMEM(((blocks - split) * padded, count), f32),
            pltpu.VMEM((FF, count), f32),
            pltpu.VMEM((count, D), f32),
            pltpu.VMEM((count, H * DV), f32),
            pltpu.SemaphoreType.DMA((2,)),
        ],
        compiler_params=pltpu.CompilerParams(vmem_limit_bytes=60 * 2**20),
        cost_estimate=pl.CostEstimate(flops=10**10, bytes_accessed=5 * 10**7, transcendentals=0),
        name="middle",
    )(place, wires, query, keys, values, inverse, beta, decay, gate, gains, x, cot, mix, ffn)


def back_kernel(
    side, wires_ref, local_ref, query_ref, keys_ref, values_ref, inverse_ref, beta_ref, decay_ref,
    state_ref, pseudo_ref, grad_mixed_ref, ext_ref, taps_ref, grad_gate_ref, grad_resid_ref, x_ref,
    normed_ref, gains_ref, factor_ref, w_gates_ref, gain_two_grad_ref,
    gain_head_grad_ref, ffn_grad, grad_out, mix_hbm,
    ffn_flat, mix_flat, grad_input_ref, small_out, squares_out,
    *scratch,
):
    scratch = list(scratch)
    take = lambda number: [scratch.pop(0) for unused in range(number)]
    after_ref, padded_ref, locals_ref, border_ref, taps_grad_ref = take(5)
    grad_beta_ref, grad_decay_ref, proj_ref, mix_grad, weight_ref, total_ref, arrived_ref = take(7)
    ffn_total, mix_total = take(2)
    ffn_scratch, mix_scratch, small_scratch, square_scratch = take(7), take(6), take(3), take(3)
    send_sems, recv_sems, local_sems, weight_sems, free_sem = scratch
    mix_scratch.insert(1, ffn_scratch[1].at[:, pl.ds(0, mix_total.shape[0]), :])
    f32, bf16 = jnp.float32, jnp.bfloat16
    place = Place(side)
    copies = Copies(send_sems, recv_sems, local_sems)
    place.enter_all()
    count, width = query_ref.shape[0], taps_ref.shape[1]
    depth = proj_ref.shape[1]
    conv_ref = padded_ref.at[pl.ds(8, count), :]
    scatter = Scatter(place, copies, ffn_grad, *ffn_scratch)
    ffn = scatter.steps(ffn_total)
    mix = Scatter(place, copies, mix_grad, *mix_scratch).steps(mix_total)
    states = gather_steps(place, copies, local_ref, locals_ref, plane=True)
    states.pop(0)()
    ffn.pop(0)()
    own_out = copies.local(grad_out, mix_grad.at[pl.ds(depth, grad_out.shape[0]), :])
    for step in states:
        step()
        ffn.pop(0)()
    work = back_chain(
        wires_ref, locals_ref, query_ref, keys_ref, values_ref, inverse_ref, beta_ref,
        decay_ref, state_ref, pseudo_ref, grad_mixed_ref, ext_ref, taps_ref,
        conv_ref, border_ref, taps_grad_ref, grad_beta_ref, grad_decay_ref,
        after_ref, padded_ref,
    )
    for unused in work:
        ffn.pop(0)()
    border = copies.push(border_ref, arrived_ref, place.before)
    pl.semaphore_signal(free_sem, inc=1, device_id=place.other_core, device_id_type=MESH)
    grad_decay = grad_decay_ref[...]
    grad_logits = (grad_beta_ref[...] + grad_decay) * factor_ref[...]
    normed = normed_ref[...]
    proj_ref[:, width:] = grad_gate_ref[...]
    ffn.pop(0)()
    border.wait_recv()
    arrived = jnp.where(place.spot < place.ctx - 1, arrived_ref[...], 0.0)
    conv_ref[pl.ds(count - 8, 8), :] = conv_ref[pl.ds(count - 8, 8), :] + arrived
    proj_ref[:, :width] = conv_ref[...].astype(bf16)
    chunk = DV
    for start in range(0, depth, chunk):
        mix_grad[pl.ds(start, chunk), :] = dot_tn(proj_ref[:, start : start + chunk], normed).astype(bf16)
    own_out.wait()
    pl.semaphore_wait(free_sem, 1)
    mix.pop(0)()

    def fetch(start):
        slot = start // chunk % 2
        copy = pltpu.make_async_copy(
            mix_hbm.at[pl.ds(start, chunk), :], weight_ref.at[slot], weight_sems.at[slot]
        )
        copy.start()
        return copy

    coming = [fetch(0), fetch(chunk)]
    ffn.pop(0)()
    mix.pop(0)()
    total_ref[...] = mm_nt(grad_logits, w_gates_ref[...])
    for start in range(0, depth, chunk):
        coming.pop(0).wait()
        total_ref[...] += dot_nn(proj_ref[:, start : start + chunk], weight_ref[start // chunk % 2])
        if start + 2 * chunk < depth:
            coming.append(fetch(start + 2 * chunk))
    if ffn:
        ffn.pop(0)()
    mix.pop(0)()
    x = x_ref[...].astype(f32)
    scale = lax.rsqrt(jnp.mean(x * x, axis=-1, keepdims=True) + EPSILON)
    through, gain_one_grad = norm_back(total_ref[...], x, scale, gains_ref[0:1, :])
    grad_input_ref[...] = (grad_resid_ref[...] + through).astype(bf16)
    small = Everywhere(place, copies, small_scratch[2], *small_scratch[:2])
    sums = small.total.at[0]
    sums[...] = jnp.zeros(sums.shape, f32)
    one, two, head, tap, gate, rest = small_places()

    def place_row(first, value):
        for index in range(value.shape[1] // 128):
            sums[first + index : first + index + 1, :] = value[:, index * 128 : (index + 1) * 128]

    place_row(one, gain_one_grad)
    place_row(two, gain_two_grad_ref[...])
    place_row(head, gain_head_grad_ref[...])
    for index in range(CONV):
        place_row(tap + index * (width // 128), taps_grad_ref[index : index + 1, :])
    sums[gate:rest, :] = pack_gates(mm_tn(normed.astype(f32), grad_logits))
    lanes = lax.broadcasted_iota(jnp.int32, (1, 128), 1)
    by_size = jnp.sum(grad_decay * decay_ref[...], axis=0, keepdims=True)
    by_bias = jnp.sum(grad_logits, axis=0, keepdims=True)
    sums[rest : rest + 1, :] = jnp.where(
        lanes < H, pltpu.roll(by_size, 128 - H, 1), jnp.where(lanes < 2 * H, by_bias, 0.0)
    )
    small.send(0)
    extra = []
    for turn in range(3):
        extra.append(lambda turn=turn: small.take(turn))
        extra.append(lambda turn=turn: small.send(turn + 1) if turn < 2 else small.send_z())
    while mix or ffn or extra:
        for queue in (ffn, mix, extra):
            if queue:
                queue.pop(0)()
    small_total = small.take_z()
    small_out[...] = small_total
    squares = jnp.zeros((8, 128), f32)
    for total in (mix_total, ffn_total):
        value = total[...]
        line = jnp.sum(value * value, axis=0, keepdims=True)
        for start in range(0, D, 128):
            squares = squares + line[:, start : start + 128] * 0.125
    square_total, square_plane, square_deep = square_scratch
    square_total[0] = squares
    square_plane[place.spot] = squares
    for copy in [
        copies.push(
            square_total.at[0], square_plane.at[place.spot], (place.z, lax.rem(place.spot + step, place.ctx))
        )
        for step in range(1, place.ctx)
    ]:
        copy.wait_recv()
    plane = square_plane[0]
    for index in range(1, place.ctx):
        plane = plane + square_plane[index]
    square_total[1] = plane
    square_deep[place.z] = plane
    for copy in [
        copies.push(square_total.at[1], square_deep.at[place.z], (place.along(step), place.spot))
        for step in range(1, place.deep)
    ]:
        copy.wait_recv()
    everything = square_deep[0]
    for index in range(1, place.deep):
        everything = everything + square_deep[index]
    own = jnp.sum(small_total * small_total, axis=0, keepdims=True)
    result = jnp.sum(jnp.sum(everything, axis=0, keepdims=True), axis=1, keepdims=True) + jnp.sum(
        own, axis=1, keepdims=True
    )
    squares_out[...] = jnp.broadcast_to(result, squares_out.shape)
    to_flat(mix_flat, mix_total[...])
    to_flat(ffn_flat, ffn_total[0 : ffn_flat.shape[0] * 128 // D, :])
    copies.finish()


def back(side, tag, ffn_rows, small_rows, *args):
    f32, bf16 = jnp.float32, jnp.bfloat16
    deep, ctx = lax.axis_size("dp"), lax.axis_size("ctx")
    query, ext, taps = args[2], args[11], args[12]
    ffn_grad, grad_out = args[-3], args[-2]
    count, width = query.shape[0], taps.shape[1]
    depth = width + H * DV
    everyone = deep * ctx
    rows = ffn_grad.shape[0] // everyone
    mix_rows = (depth + grad_out.shape[0]) // everyone
    number = 2 * Scatter.copies_of(deep) + gather_copies(1) + (3 + deep - 1) + (ctx + deep - 2) + 1
    vmem = pl.BlockSpec(memory_space=pltpu.VMEM)
    anywhere = pl.BlockSpec(memory_space=pl.ANY)
    return pl.pallas_call(
        functools.partial(back_kernel, side),
        out_shape=[
            jax.ShapeDtypeStruct((ffn_rows * D // 128, 128), f32),
            jax.ShapeDtypeStruct((mix_rows * D // 128, 128), f32),
            jax.ShapeDtypeStruct((count, D), bf16),
            jax.ShapeDtypeStruct((small_rows, 128), f32),
            jax.ShapeDtypeStruct((8, 128), f32),
        ],
        in_specs=[vmem] * (len(args) - 3) + [anywhere] * 3,
        out_specs=[vmem] * 5,
        scratch_shapes=[
            pltpu.VMEM((H, DK, DV), f32),
            pltpu.VMEM((count + 16, width), f32),
            pltpu.VMEM((ctx * H * DK, DV), bf16),
            pltpu.VMEM((8, width), f32),
            pltpu.VMEM((8, width), f32),
            pltpu.VMEM((count, 128), f32),
            pltpu.VMEM((count, 128), f32),
            pltpu.VMEM((count, depth), bf16),
            pltpu.VMEM((depth + grad_out.shape[0], D), bf16),
            pltpu.VMEM((2, DV, D), bf16),
            pltpu.VMEM((count, D), f32),
            pltpu.VMEM((8, width), f32),
            pltpu.VMEM((rows, D), f32),
            pltpu.VMEM((mix_rows, D), f32),
        ]
        + Scatter.scratch(deep, rows)
        + [shape for index, shape in enumerate(Scatter.scratch(deep, mix_rows)) if index != 1]
        + Everywhere.scratch(deep, small_rows, 128)
        + [pltpu.VMEM((number, 8, 128), f32) for number in (2, ctx, deep)]
        + [
            pltpu.SemaphoreType.DMA((number,)),
            pltpu.SemaphoreType.DMA((number,)),
            pltpu.SemaphoreType.DMA((8 * deep + 2,)),
            pltpu.SemaphoreType.DMA((2,)),
            pltpu.SemaphoreType.REGULAR,
        ],
        compiler_params=pltpu.CompilerParams(
            collective_id=tag, has_side_effects=True, vmem_limit_bytes=62 * 2**20
        ),
        cost_estimate=pl.CostEstimate(flops=10**10, bytes_accessed=10**8, transcendentals=0),
        name="back",
    )(*args)


def back_chain(
    wire_ref, local_ref, query_ref, keys_ref, values_ref, inverse_ref, beta_ref,
    decay_ref, state_ref, pseudo_ref, grad_mixed_ref, ext_ref, taps_ref,
    grad_conv_ref, grad_border_ref, grad_taps_ref, grad_beta_ref, grad_decay_ref,
    after_ref, padded_ref,
):
    count = query_ref.shape[0]
    width = taps_ref.shape[1]
    devices = wire_ref.shape[0]
    after_ref[...] = jnp.zeros_like(after_ref)

    def lap(step, carry):
        index = devices - 1 - step
        for head in range(H):
            to_end, key_mix, value_mix, whole = wire_parts(wire_ref, index, head, count)
            after = after_ref[head]
            inner = wire_mm(to_end, after, ((1,), (0,)))
            spot = pl.multiple_of((index * H + head) * DK, DK)
            local = local_ref[pl.ds(spot, DK), :].astype(jnp.float32)
            after_ref[head] = whole * after - wire_mm(key_mix, inner, ((0,), (0,))) + local
        return carry

    lax.fori_loop(0, devices - 1 - lax.axis_index("ctx"), lap, 0)
    yield
    taps = taps_ref[...]
    summed = ext_sum(ext_ref, taps, count, 0, width)
    activated, slope = silu_pair(summed)
    padded_ref[0:8, :] = jnp.zeros((8, width), jnp.float32)
    padded_ref[pl.ds(8 + count, 8), :] = jnp.zeros((8, width), jnp.float32)
    rows, cols = iotas(count)
    lower = rows >= cols
    strict = rows > cols
    lanes = lax.broadcasted_iota(jnp.int32, (count, 128), 1)
    beta_out = jnp.zeros((count, 128), jnp.float32)
    cumulative_out = jnp.zeros((count, 128), jnp.float32)
    row_column = lax.broadcasted_iota(jnp.int32, (count, 1), 0)
    for head in range(H):
        query = query_ref[:, head * DK : (head + 1) * DK]
        keys = keys_ref[:, head * DK : (head + 1) * DK]
        span = slice(head * DV, (head + 1) * DV)
        values = values_ref[:, span]
        beta = beta_ref[:, head : head + 1]
        matrix, grown, to_end, whole = decay_terms(decay_lane(decay_ref, head), rows, cols)
        inverse = inverse_ref[head]
        state = state_ref[head]
        after = after_ref[head]
        pseudo = pseudo_ref[:, span]
        grad_mixed = grad_mixed_ref[:, span]
        keys_grown = keys * (beta * grown)
        key_mix = mm(inverse, keys_grown)
        value_mix = mm(inverse, values * beta)
        gram = mm_nt(keys, keys)
        system = jnp.where(strict, beta * gram * matrix, 0.0)
        scores = mm_nt(query, keys) * matrix
        keys_end = keys * to_end
        query_grown = query * grown
        grad_query_grown = mm_nt(grad_mixed, state)
        grad_scores = jnp.where(lower, mm_nt(grad_mixed, pseudo), 0.0)
        grad_pseudo = mm_tn(scores, grad_mixed) + mm(keys_end, after)
        grad_keys_end = mm_nt(pseudo, after)
        grad_whole = jnp.sum(jnp.sum(after * state, axis=1, keepdims=True), axis=0, keepdims=True)
        grad_value_in = mm_tn(inverse, grad_pseudo)
        grad_key_in = mm_tn(inverse, -mm_nt(grad_pseudo, state))
        grad_system = -jnp.where(
            strict, mm_nt(grad_value_in, value_mix) + mm_nt(grad_key_in, key_mix), 0.0
        )
        grad_raw = grad_scores * matrix
        grad_query = mm(grad_raw, keys) + grad_query_grown * grown
        grad_keys = mm_tn(grad_raw, query)
        weighted = grad_system * matrix
        grad_beta = jnp.sum(weighted * gram, axis=1, keepdims=True)
        grad_gram = weighted * beta
        grad_keys = grad_keys + mm(grad_gram, keys) + mm_tn(grad_gram, keys)
        spread = grad_scores * scores + grad_system * system
        grad_cumulative = jnp.sum(spread, axis=1, keepdims=True)
        across = jnp.sum(spread, axis=0, keepdims=True)
        grad_cumulative = grad_cumulative - jnp.sum(
            jnp.where(rows == cols, across, 0.0), axis=1, keepdims=True
        )
        grad_keys = grad_keys + grad_key_in * (beta * grown)
        through = jnp.sum(grad_key_in * keys, axis=1, keepdims=True) * grown
        grad_beta = grad_beta + through + jnp.sum(grad_value_in * values, axis=1, keepdims=True)
        grad_cumulative = grad_cumulative + through * beta
        grad_values = grad_value_in * beta
        grad_cumulative = grad_cumulative + jnp.sum(
            grad_query_grown * query_grown, axis=1, keepdims=True
        )
        grad_keys = grad_keys + grad_keys_end * to_end
        ending = jnp.sum(grad_keys_end * keys_end, axis=1, keepdims=True)
        final = jnp.sum(ending, axis=0, keepdims=True) + whole * grad_whole
        grad_cumulative = grad_cumulative - ending + jnp.where(row_column == count - 1, final, 0.0)
        beta_out = jnp.where(lanes == head, grad_beta, beta_out)
        cumulative_out = jnp.where(lanes == H + head, grad_cumulative, cumulative_out)
        key_part = activated[:, (H + head) * DK : (H + head + 1) * DK]
        key_scale = unit_rows(key_part)
        query_part = activated[:, head * DK : (head + 1) * DK]
        query_scale = unit_rows(query_part)
        factor = DK ** (-0.5)
        grad_query_part = (factor * query_scale) * (
            grad_query
            - query_part
            * (query_scale * query_scale)
            * jnp.sum(grad_query * query_part, axis=-1, keepdims=True)
        )
        grad_key_part = key_scale * (
            grad_keys
            - key_part
            * (key_scale * key_scale)
            * jnp.sum(grad_keys * key_part, axis=-1, keepdims=True)
        )
        spots = (head * DK, (H + head) * DK, 2 * H * DK + head * DV)
        for spot, grad in zip(spots, (grad_query_part, grad_key_part, grad_values)):
            size = grad.shape[1]
            padded_ref[pl.ds(8, count), spot : spot + size] = grad * slope[:, spot : spot + size]
        yield
    grad_beta_ref[...] = beta_out
    grad_decay_ref[...] = mm_tn(jnp.where(lower, 1.0, 0.0), cumulative_out)
    conv_total = jnp.zeros((count, width), jnp.float32)
    border_total = jnp.zeros((8, width), jnp.float32)
    summed_grad = padded_ref[pl.ds(8, count), :]
    tap_rows = lax.broadcasted_iota(jnp.int32, (8, width), 0)
    taps_total = jnp.zeros((8, width), jnp.float32)
    for tap in range(CONV):
        shift = CONV - 1 - tap
        conv_total = conv_total + taps[tap : tap + 1] * padded_ref[pl.ds(8 + shift, count), :]
        border_total = border_total + taps[tap : tap + 1] * padded_ref[pl.ds(shift, 8), :]
        piece = jnp.sum(
            summed_grad * ext_ref[pl.ds(8 - (CONV - 1) + tap, count), :width],
            axis=0,
            keepdims=True,
        )
        taps_total = jnp.where(tap_rows == tap, piece, taps_total)
    grad_conv_ref[...] = conv_total
    grad_border_ref[...] = border_total
    grad_taps_ref[...] = taps_total
    yield


def chip_side():
    half = lax.axis_size("ctx") // 2
    side = math.isqrt(half)
    return side if side == 2 and 2 * side * side == lax.axis_size("ctx") else 0


def adam_step(weight, grad_full, first, second, clip):
    grad_clipped = grad_full * clip
    first_new = BETA_ONE * first + (1.0 - BETA_ONE) * grad_clipped
    second_new = BETA_TWO * second + (1.0 - BETA_TWO) * grad_clipped * grad_clipped
    update = (
        first_new / CORRECT_ONE / (jnp.sqrt(second_new / CORRECT_TWO) + ADAM_EPS)
        + DECAY_RATE * weight
    )
    return (weight - LEARN_RATE * update, first_new, second_new)


def plain(
    inputs,
    cotangent,
    mixer_params,
    mixer_first,
    mixer_second,
    ffn_params,
    ffn_first,
    ffn_second,
    small_params,
    small_first,
    small_second,
):
    gain_one, gain_two, gain_head, tap_values, w_gates, a_log, dt_bias = unpack_small(small_params)
    width = tap_values.shape[1]
    mix_part = mixer_params.astype(jnp.bfloat16)
    ffn_part = ffn_params.astype(jnp.bfloat16)
    mix_whole, ffn_whole = (
        lax.all_gather(mix_part, ("dp", "ctx"), axis=0, tiled=True),
        lax.all_gather(ffn_part, ("dp", "ctx"), axis=0, tiled=True),
    )
    w_in, w_out, w_ffn, w_down = split_weights(mix_whole, ffn_whole)
    x_float = inputs[0].astype(jnp.float32)
    count = x_float.shape[0]
    normed_in = norm_scale(x_float, gain_one).astype(jnp.bfloat16)
    projected = jnp.dot(normed_in, w_in.T, preferred_element_type=jnp.float32)
    gate_logits = jnp.dot(normed_in.astype(jnp.float32), w_gates, precision=HIGHEST)
    f32 = jnp.float32
    devices = lax.axis_size("ctx")
    place = lax.axis_index("ctx").astype(jnp.int32).reshape(1)
    out_gate = projected[:, width:]
    edge = from_behind(projected[count - 8 :, :width], "ctx", 1)
    border = jnp.where(lax.broadcasted_iota(jnp.int32, (8, 1), 0) >= 8 - (CONV - 1), edge, 0.0)
    (beta, decay), pull_gates = jax.vjp(gates, gate_logits, a_log, dt_bias)
    wire, query, keys, values, inverse = fused(
        forward_parts,
        (
            jax.ShapeDtypeStruct((count + PAD, H * (2 * DK + DV)), jnp.bfloat16),
            jax.ShapeDtypeStruct((count, H * DK), f32),
            jax.ShapeDtypeStruct((count, H * DK), f32),
            jax.ShapeDtypeStruct((count, H * DV), f32),
            jax.ShapeDtypeStruct((H, count, count), f32),
        ),
        scratch=(pltpu.VMEM((count + 8, width), f32),),
        label="forward_parts",
    )(projected, border, tap_values, beta, decay)
    wires = lax.all_gather(wire, "ctx")
    gain_row = gain_head.reshape(1, DV)
    head_out, mixed, state, pseudo = fused(
        forward_chain,
        (
            jax.ShapeDtypeStruct((count, H * DV), jnp.bfloat16),
            jax.ShapeDtypeStruct((count, H * DV), f32),
            jax.ShapeDtypeStruct((H, DK, DV), f32),
            jax.ShapeDtypeStruct((count, H * DV), f32),
        ),
        scalars=1,
        label="forward_chain",
    )(place, wires, query, keys, values, inverse, beta, decay, out_gate, gain_row)
    resid = x_float + jnp.dot(head_out, w_out, preferred_element_type=jnp.float32)
    normed_mid = norm_scale(resid, gain_two).astype(jnp.bfloat16)
    ffn_pre = jnp.dot(normed_mid, w_ffn.T, preferred_element_type=jnp.float32)
    gate_part = ffn_pre[:, :FF]
    up_part = ffn_pre[:, FF:]
    hidden_act = swiglu(gate_part, up_part).astype(jnp.bfloat16)
    result = (resid + jnp.dot(hidden_act, w_down, preferred_element_type=jnp.float32)).astype(
        jnp.bfloat16
    )
    seq_grad = cotangent[0]
    grad_float = seq_grad.astype(jnp.float32)
    grad_down = jnp.dot(hidden_act.T, seq_grad, preferred_element_type=jnp.float32)
    grad_hidden = jnp.dot(seq_grad, w_down.T, preferred_element_type=jnp.float32)
    unused_one, pull_swiglu = jax.vjp(swiglu, gate_part, up_part)
    grad_gate, grad_up = pull_swiglu(grad_hidden)
    grad_pre = jnp.concatenate([grad_gate, grad_up], axis=1).astype(jnp.bfloat16)
    grad_ffn = jnp.dot(grad_pre.T, normed_mid, preferred_element_type=jnp.float32)
    grad_mid = jnp.dot(grad_pre, w_ffn, preferred_element_type=jnp.float32)
    unused_two, pull_mid = jax.vjp(norm_scale, resid, gain_two)
    grad_through, grad_gain_two = pull_mid(grad_mid)
    grad_resid = grad_float + grad_through
    resid_half = grad_resid.astype(jnp.bfloat16)
    grad_out = jnp.dot(head_out.T, resid_half, preferred_element_type=jnp.float32)
    grad_head = jnp.dot(resid_half, w_out.T, preferred_element_type=jnp.float32)
    local, grad_mixed, grad_gate_out, grad_gain_head = fused(
        backward_local,
        (
            jax.ShapeDtypeStruct((H * DK, DV), jnp.bfloat16),
            jax.ShapeDtypeStruct((count, H * DV), f32),
            jax.ShapeDtypeStruct((count, H * DV), f32),
            jax.ShapeDtypeStruct((1, DV), f32),
        ),
        label="backward_local",
    )(grad_head, mixed, query, keys, values, inverse, beta, decay, out_gate, gain_row)
    locals_all = lax.all_gather(local, "ctx")
    locals_all, grad_ffn, grad_down = lax.optimization_barrier((locals_all, grad_ffn, grad_down))
    ffn_shard = scatter_rows((grad_ffn, grad_down))
    grad_conv, grad_border, grad_taps, grad_beta, grad_decay = fused(
        backward_chain,
        (
            jax.ShapeDtypeStruct((count, width), f32),
            jax.ShapeDtypeStruct((8, width), f32),
            jax.ShapeDtypeStruct((8, width), f32),
            jax.ShapeDtypeStruct((count, 128), f32),
            jax.ShapeDtypeStruct((count, 128), f32),
        ),
        scratch=(
            pltpu.VMEM((H, DK, DV), f32),
            pltpu.VMEM((count + 8, width), f32),
            pltpu.VMEM((count + 16, width), f32),
        ),
        scalars=1,
        label="backward_chain",
    )(
        place, wires, locals_all, query, keys, values, inverse, beta, decay, state, pseudo,
        grad_mixed, projected, border, tap_values,
    )
    grad_logits, grad_alog, grad_bias = pull_gates((grad_beta[:, :H], grad_decay[:, :H]))
    returned = from_behind(grad_border, "ctx", -1)[8 - (CONV - 1) :]
    grad_conv = grad_conv.at[count - (CONV - 1) :].add(returned)
    grad_proj = jnp.concatenate([grad_conv, grad_gate_out], axis=1).astype(jnp.bfloat16)
    grad_in = jnp.dot(grad_proj.T, normed_in, preferred_element_type=jnp.float32)
    grad_normed = jnp.dot(grad_proj, w_in, preferred_element_type=jnp.float32) + jnp.dot(
        grad_logits, w_gates.T, precision=HIGHEST
    )
    grad_gates = jnp.dot(normed_in.astype(jnp.float32).T, grad_logits, precision=HIGHEST)
    unused_six, pull_in = jax.vjp(norm_scale, x_float, gain_one)
    grad_x, grad_gain_one = pull_in(grad_normed)
    grad_input = (grad_resid + grad_x).astype(jnp.bfloat16)
    small_local = jnp.concatenate(
        [
            grad_gain_one,
            grad_gain_two,
            grad_gain_head.reshape(-1),
            grad_taps[:CONV].reshape(-1),
            grad_gates.reshape(-1),
            grad_alog,
            grad_bias,
        ]
    )
    small_grad = lax.psum(small_local, ("dp", "ctx"))
    ffn_shard, grad_in, grad_out = lax.optimization_barrier((ffn_shard, grad_in, grad_out))
    mix_shard = scatter_rows((grad_in, grad_out))
    small_grad, mix_shard = lax.optimization_barrier((small_grad, mix_shard))
    shard_squares = jnp.sum(mix_shard * mix_shard) + jnp.sum(ffn_shard * ffn_shard)
    total_squares = lax.psum(shard_squares, ("dp", "ctx"))
    squares = total_squares + jnp.sum(small_grad * small_grad)
    clip = jnp.minimum(1.0, MAX_NORM / (jnp.sqrt(squares) + 1e-06))
    mixer_new, mixer_first_new, mixer_second_new = adam_step(
        mixer_params, mix_shard, mixer_first, mixer_second, clip
    )
    ffn_new, ffn_first_new, ffn_second_new = adam_step(
        ffn_params, ffn_shard, ffn_first, ffn_second, clip
    )
    small_new, small_first_new, small_second_new = adam_step(
        small_params, small_grad, small_first, small_second, clip
    )
    return (
        result[None],
        grad_input[None],
        mix_shard,
        ffn_shard,
        small_grad,
        mixer_new,
        mixer_first_new,
        mixer_second_new,
        ffn_new,
        ffn_first_new,
        ffn_second_new,
        small_new,
        small_first_new,
        small_second_new,
    )


def fast(
    side, inputs, cotangent, mixer_params, mixer_first, mixer_second, ffn_params, ffn_first, ffn_second, small_params, small_first, small_second,
):
    ffn_rows = ffn_params.size // D
    short = -small_params.size % 1024
    small = jnp.pad(small_params, (0, short)).reshape(-1, 128)
    (
        mix_whole, ffn_whole, wires, ext, out_gate, query, keys, values, inverse, normed_in, beta, decay,
        factor, taps, gains, w_gates,
    ) = front(mixer_params.reshape(-1, 128), ffn_params.reshape(-1, 128), inputs[0], small, side, 1)
    wires = wires.reshape(lax.axis_size("ctx"), -1, wires.shape[1])
    place = lax.axis_index("ctx").astype(jnp.int32).reshape(1)
    (
        result, grad_resid, grad_out, ffn_grad, grad_gain_two, state, pseudo, local, grad_mixed,
        grad_gate_out, grad_gain_head,
    ) = middle(
        ffn_rows, place, wires, query, keys, values, inverse, beta, decay, out_gate, gains,
        inputs[0], cotangent[0], mix_whole, ffn_whole,
    )
    ffn_shard, mix_shard, grad_input, sums, squares = back(
        side, 2, ffn_rows, small.shape[0], wires, local, query, keys, values, inverse, beta, decay,
        state, pseudo, grad_mixed, ext, taps, grad_gate_out, grad_resid, inputs[0], normed_in, gains,
        factor, w_gates, grad_gain_two, grad_gain_head, ffn_grad, grad_out, mix_whole,
    )
    small_grad = sums.reshape(-1)[: small_params.size]
    mix_shard = mix_shard.reshape(-1)
    ffn_shard = ffn_shard.reshape(-1)
    squares = squares[0, 0]
    clip = jnp.minimum(1.0, MAX_NORM / (jnp.sqrt(squares) + 1e-06))
    mix_shard = jnp.where(clip >= 0.0, mix_shard, 0.0)
    ffn_shard = jnp.where(clip >= 0.0, ffn_shard, 0.0)
    mixer_new, mixer_first_new, mixer_second_new = adam_step(
        mixer_params, mix_shard, mixer_first, mixer_second, clip
    )
    ffn_new, ffn_first_new, ffn_second_new = adam_step(
        ffn_params, ffn_shard, ffn_first, ffn_second, clip
    )
    small_new, small_first_new, small_second_new = adam_step(
        small_params, small_grad, small_first, small_second, clip
    )
    return (
        result[None],
        grad_input[None],
        mix_shard,
        ffn_shard,
        small_grad,
        mixer_new,
        mixer_first_new,
        mixer_second_new,
        ffn_new,
        ffn_first_new,
        ffn_second_new,
        small_new,
        small_first_new,
        small_second_new,
    )


def body(*args):
    rows, left = divmod(args[5].size, D)
    side = chip_side() if left == 0 and args[2].size % (32 * D) == 0 else 0
    return fast(side, *args) if side else plain(*args)


def solution(mesh):
    return jax.shard_map(
        body,
        mesh=mesh,
        in_specs=(
            P("dp", "ctx", None),
            P("dp", "ctx", None),
            P(("dp", "ctx")),
            P(("dp", "ctx")),
            P(("dp", "ctx")),
            P(("dp", "ctx")),
            P(("dp", "ctx")),
            P(("dp", "ctx")),
            P(),
            P(),
            P(),
        ),
        out_specs=(
            P("dp", "ctx", None),
            P("dp", "ctx", None),
            P(("dp", "ctx")),
            P(("dp", "ctx")),
            P(),
            P(("dp", "ctx")),
            P(("dp", "ctx")),
            P(("dp", "ctx")),
            P(("dp", "ctx")),
            P(("dp", "ctx")),
            P(("dp", "ctx")),
            P(),
            P(),
            P(),
        ),
        check_vma=False,
    )
```

```python
import functools
import math
import jax
import jax.numpy as jnp
from jax import lax
from jax.experimental import pallas as pl
from jax.experimental.pallas import tpu as pltpu
from jax.sharding import PartitionSpec as P

D = 1024
H = 2
DK = 256
DV = 512
FF = 1408
CONV = 4
GROUP = 64


EPSILON = 1e-06
ADAM_EPS = 1e-08
LEARN_RATE = 0.02
BETA_ONE = 0.9
BETA_TWO = 0.999
DECAY_RATE = 0.1
CORRECT_ONE = 1.0 - 0.9**3
CORRECT_TWO = 1.0 - 0.999**3
MAX_NORM = 1.0
HIGHEST = lax.Precision.HIGHEST


def from_behind(value, axis, steps):
    count = lax.axis_size(axis)
    initial, last = (max(0, -steps), min(count, count - steps))
    return lax.ppermute(value, axis, [(source, source + steps) for source in range(initial, last)])


def norm_scale(values, gain):
    return values * lax.rsqrt(jnp.mean(values * values, axis=-1, keepdims=True) + EPSILON) * gain


def swiglu(gate_part, up_part):
    return jax.nn.silu(gate_part) * up_part


def unpack_small(packed):
    width = 2 * H * DK + H * DV
    lengths = [D, D, DV, CONV * width, D * 2 * H, H, H]
    pieces = []
    offset = 0
    for length in lengths:
        pieces.append(packed[offset : offset + length])
        offset = offset + length
    return (
        pieces[0],
        pieces[1],
        pieces[2],
        pieces[3].reshape(CONV, width),
        pieces[4].reshape(D, 2 * H),
        pieces[5],
        pieces[6],
    )


def split_weights(mix_whole, ffn_whole):
    mix_rows = mix_whole.reshape(-1, D)
    ffn_rows = ffn_whole.reshape(-1, D)
    edge = 2 * H * DK + 2 * H * DV
    return (mix_rows[:edge], mix_rows[edge:], ffn_rows[: 2 * FF], ffn_rows[2 * FF :])


PAD = 16
HIGH = dict(precision=HIGHEST, preferred_element_type=jnp.float32)


def mm(a, b):
    return lax.dot_general(a, b, (((1,), (0,)), ((), ())), **HIGH)


def mm_nt(a, b):
    return lax.dot_general(a, b, (((1,), (1,)), ((), ())), **HIGH)


def mm_tn(a, b):
    return lax.dot_general(a, b, (((0,), (0,)), ((), ())), **HIGH)


def halves(a):
    high = a.astype(jnp.bfloat16)
    return high, (a - high.astype(jnp.float32)).astype(jnp.bfloat16)


def wire_mm(a, b, dims):
    high, low = halves(b)
    first = lax.dot_general(a, high, (dims, ((), ())), preferred_element_type=jnp.float32)
    return first + lax.dot_general(a, low, (dims, ((), ())), preferred_element_type=jnp.float32)


def iotas(size):
    shape = (size, size)
    return (
        lax.broadcasted_iota(jnp.int32, shape, 0),
        lax.broadcasted_iota(jnp.int32, shape, 1),
    )


def to_row(column, rows, cols):
    return jnp.sum(jnp.where(rows == cols, column, 0.0), axis=0, keepdims=True)


def unit_inverse(strict_part, rows, cols):
    size = strict_part.shape[0]
    inverse = jnp.where(rows == cols, 1.0, 0.0) - jnp.where(
        (rows // 2 == cols // 2), strict_part, 0.0
    )
    block = 2
    while block < size:
        joined = (rows // (2 * block) == cols // (2 * block)) & (rows // block != cols // block)
        off = jnp.where(joined, strict_part, 0.0)
        inverse = inverse - mm(mm(inverse, off), inverse)
        block = 2 * block
    return inverse


def silu_pair(x):
    gate = jax.nn.sigmoid(x)
    return x * gate, gate * (1.0 + x * (1.0 - gate))


def conv_sum(extended_ref, taps, count):
    total = None
    for tap in range(CONV):
        piece = taps[tap : tap + 1] * extended_ref[pl.ds(8 - (CONV - 1) + tap, count), :]
        total = piece if total is None else total + piece
    return total


def unit_rows(part):
    return lax.rsqrt(jnp.sum(part * part, axis=-1, keepdims=True) + EPSILON)


def decay_lane(decay_ref, head):
    lane = head + (H if decay_ref.shape[1] > H else 0)
    return decay_ref[:, lane : lane + 1]


def decay_terms(decay_column, rows, cols):
    lower = rows >= cols
    size = rows.shape[0]
    spread_in = jnp.broadcast_to(decay_column, (size, 128))
    cumulative = mm(jnp.where(lower, 1.0, 0.0), spread_in)[:, :1]
    across = to_row(cumulative, rows, cols)
    matrix = jnp.where(lower, jnp.exp(jnp.where(lower, cumulative - across, 0.0)), 0.0)
    last = cumulative[size - 1 : size]
    return matrix, jnp.exp(cumulative), jnp.exp(last - cumulative), jnp.exp(last)


def forward_parts(
    projected_ref, border_ref, taps_ref, beta_ref, decay_ref,
    wire_ref, query_ref, keys_ref, values_ref, inverse_ref, extended_ref,
):
    count = projected_ref.shape[0]
    width = taps_ref.shape[1]
    extended_ref[0:8, :] = border_ref[...]
    extended_ref[pl.ds(8, count), :] = projected_ref[:, :width]
    summed = conv_sum(extended_ref, taps_ref[...], count)
    activated = summed * jax.nn.sigmoid(summed)
    rows, cols = iotas(count)
    for head in range(H):
        query_part = activated[:, head * DK : (head + 1) * DK]
        key_part = activated[:, (H + head) * DK : (H + head + 1) * DK]
        start = 2 * H * DK + head * DV
        values = activated[:, start : start + DV]
        query = query_part * unit_rows(query_part) * DK ** (-0.5)
        keys = key_part * unit_rows(key_part)
        beta = beta_ref[:, head : head + 1]
        matrix, grown, to_end, whole = decay_terms(decay_lane(decay_ref, head), rows, cols)
        system = jnp.where(rows > cols, beta * mm_nt(keys, keys) * matrix, 0.0)
        inverse = unit_inverse(system, rows, cols)
        key_mix = mm(inverse, keys * (beta * grown))
        value_mix = mm(inverse, values * beta)
        base = head * (2 * DK + DV)
        wire_ref[0:count, base : base + DK] = (keys * to_end).astype(jnp.bfloat16)
        wire_ref[0:count, base + DK : base + 2 * DK] = key_mix.astype(jnp.bfloat16)
        wire_ref[0:count, base + 2 * DK : base + 2 * DK + DV] = value_mix.astype(jnp.bfloat16)
        high, low = halves(jnp.broadcast_to(whole, (PAD, 2 * DK + DV)))
        first = lax.broadcasted_iota(jnp.int32, (PAD, 2 * DK + DV), 0) < 8
        tail = jnp.where(first, high.astype(jnp.float32), low.astype(jnp.float32))
        wire_ref[pl.ds(count, PAD), base : base + 2 * DK + DV] = tail.astype(jnp.bfloat16)
        query_ref[:, head * DK : (head + 1) * DK] = query
        keys_ref[:, head * DK : (head + 1) * DK] = keys
        values_ref[:, head * DV : (head + 1) * DV] = values
        inverse_ref[head] = inverse


def wire_parts(wire_ref, index, head, count):
    base = head * (2 * DK + DV)
    if isinstance(wire_ref, (list, tuple)):
        wire_ref, base = wire_ref[head], 0
    to_end = wire_ref[index, 0:count, base : base + DK]
    key_mix = wire_ref[index, 0:count, base + DK : base + 2 * DK]
    value_mix = wire_ref[index, 0:count, base + 2 * DK : base + 2 * DK + DV]
    tail = wire_ref[index, pl.ds(count, PAD), base : base + 128].astype(jnp.float32)
    whole = tail[0:1, 0:1] + tail[8:9, 0:1]
    return to_end, key_mix, value_mix, whole


def own_mix(inverse, keys, values, beta, grown):
    return mm(inverse, keys * (beta * grown)), mm(inverse, values * beta)


def forward_chain(
    place_ref, wire_ref, query_ref, keys_ref, values_ref, inverse_ref, beta_ref, decay_ref,
    gate_ref, gain_ref, head_out_ref, mixed_ref, state_ref, pseudo_ref,
):
    count = query_ref.shape[0]
    state_ref[...] = jnp.zeros_like(state_ref)

    def lap(index, carry):
        for head in range(H):
            to_end, key_mix, value_mix, whole = wire_parts(wire_ref, index, head, count)
            state = state_ref[head]
            pseudo = value_mix.astype(jnp.float32) - wire_mm(key_mix, state, ((1,), (0,)))
            state_ref[head] = whole * state + wire_mm(to_end, pseudo, ((0,), (0,)))
        return carry

    lax.fori_loop(0, place_ref[0], lap, 0)
    rows, cols = iotas(count)
    for head in range(H):
        query = query_ref[:, head * DK : (head + 1) * DK]
        keys = keys_ref[:, head * DK : (head + 1) * DK]
        span = slice(head * DV, (head + 1) * DV)
        beta = beta_ref[:, head : head + 1]
        matrix, grown, to_end, whole = decay_terms(decay_lane(decay_ref, head), rows, cols)
        key_mix, value_mix = own_mix(inverse_ref[head], keys, values_ref[:, span], beta, grown)
        state = state_ref[head]
        pseudo = value_mix - mm(key_mix, state)
        mixed = mm(query * grown, state) + mm(mm_nt(query, keys) * matrix, pseudo)
        scale = lax.rsqrt(jnp.mean(mixed * mixed, axis=-1, keepdims=True) + EPSILON)
        gated, unused = silu_pair(gate_ref[:, span])
        head_out_ref[:, span] = (mixed * scale * gain_ref[...] * gated).astype(jnp.bfloat16)
        mixed_ref[:, span] = mixed
        pseudo_ref[:, span] = pseudo


def backward_local(
    grad_ref, mixed_ref, query_ref, keys_ref, values_ref, inverse_ref, beta_ref, decay_ref,
    gate_ref, gain_ref, local_ref, grad_mixed_ref, grad_gate_ref, grad_gain_ref,
):
    count = query_ref.shape[0]
    rows, cols = iotas(count)
    gain_total = jnp.zeros((1, DV), jnp.float32)
    for head in range(H):
        query = query_ref[:, head * DK : (head + 1) * DK]
        keys = keys_ref[:, head * DK : (head + 1) * DK]
        span = slice(head * DV, (head + 1) * DV)
        mixed = mixed_ref[:, span]
        grad = grad_ref[:, span]
        scale = lax.rsqrt(jnp.mean(mixed * mixed, axis=-1, keepdims=True) + EPSILON)
        plain = mixed * scale
        gated, slope = silu_pair(gate_ref[:, span])
        grad_gate_ref[:, span] = (grad * plain * gain_ref[...] * slope).astype(grad_gate_ref.dtype)
        grad_normed = grad * gated
        gain_total = gain_total + jnp.sum(grad_normed * plain, axis=0, keepdims=True)
        pulled = grad_normed * gain_ref[...]
        grad_mixed = scale * (pulled - plain * jnp.mean(pulled * plain, axis=-1, keepdims=True))
        grad_mixed_ref[:, span] = grad_mixed
        beta = beta_ref[:, head : head + 1]
        matrix, grown, to_end, whole = decay_terms(decay_lane(decay_ref, head), rows, cols)
        key_mix = mm(inverse_ref[head], keys * (beta * grown))
        grad_pseudo = mm_tn(mm_nt(query, keys) * matrix, grad_mixed)
        local = mm_tn(query * grown, grad_mixed) - mm_tn(key_mix, grad_pseudo)
        local_ref[head * DK : (head + 1) * DK, :] = local.astype(jnp.bfloat16)
    grad_gain_ref[...] = gain_total


def backward_chain(
    place_ref, wire_ref, local_ref, query_ref, keys_ref, values_ref, inverse_ref, beta_ref,
    decay_ref, state_ref, pseudo_ref, grad_mixed_ref, projected_ref, border_ref, taps_ref,
    grad_conv_ref, grad_border_ref, grad_taps_ref, grad_beta_ref, grad_decay_ref,
    after_ref, extended_ref, padded_ref,
):
    count = query_ref.shape[0]
    width = taps_ref.shape[1]
    devices = wire_ref.shape[0]
    after_ref[...] = jnp.zeros_like(after_ref)

    def lap(step, carry):
        index = devices - 1 - step
        for head in range(H):
            to_end, key_mix, value_mix, whole = wire_parts(wire_ref, index, head, count)
            after = after_ref[head]
            inner = wire_mm(to_end, after, ((1,), (0,)))
            local = local_ref[index, head * DK : (head + 1) * DK, :].astype(jnp.float32)
            after_ref[head] = whole * after - wire_mm(key_mix, inner, ((0,), (0,))) + local
        return carry

    lax.fori_loop(0, devices - 1 - place_ref[0], lap, 0)
    extended_ref[0:8, :] = border_ref[...]
    extended_ref[pl.ds(8, count), :] = projected_ref[:, :width]
    taps = taps_ref[...]
    summed = conv_sum(extended_ref, taps, count)
    activated, slope = silu_pair(summed)
    padded_ref[0:8, :] = jnp.zeros((8, width), jnp.float32)
    padded_ref[pl.ds(8 + count, 8), :] = jnp.zeros((8, width), jnp.float32)
    rows, cols = iotas(count)
    lower = rows >= cols
    strict = rows > cols
    lanes = lax.broadcasted_iota(jnp.int32, (count, 128), 1)
    beta_out = jnp.zeros((count, 128), jnp.float32)
    cumulative_out = jnp.zeros((count, 128), jnp.float32)
    row_column = lax.broadcasted_iota(jnp.int32, (count, 1), 0)
    for head in range(H):
        query = query_ref[:, head * DK : (head + 1) * DK]
        keys = keys_ref[:, head * DK : (head + 1) * DK]
        span = slice(head * DV, (head + 1) * DV)
        values = values_ref[:, span]
        beta = beta_ref[:, head : head + 1]
        matrix, grown, to_end, whole = decay_terms(decay_lane(decay_ref, head), rows, cols)
        inverse = inverse_ref[head]
        state = state_ref[head]
        after = after_ref[head]
        pseudo = pseudo_ref[:, span]
        grad_mixed = grad_mixed_ref[:, span]
        keys_grown = keys * (beta * grown)
        key_mix = mm(inverse, keys_grown)
        value_mix = mm(inverse, values * beta)
        gram = mm_nt(keys, keys)
        system = jnp.where(strict, beta * gram * matrix, 0.0)
        scores = mm_nt(query, keys) * matrix
        keys_end = keys * to_end
        query_grown = query * grown
        grad_query_grown = mm_nt(grad_mixed, state)
        grad_scores = jnp.where(lower, mm_nt(grad_mixed, pseudo), 0.0)
        grad_pseudo = mm_tn(scores, grad_mixed) + mm(keys_end, after)
        grad_keys_end = mm_nt(pseudo, after)
        grad_whole = jnp.sum(jnp.sum(after * state, axis=1, keepdims=True), axis=0, keepdims=True)
        grad_value_in = mm_tn(inverse, grad_pseudo)
        grad_key_in = mm_tn(inverse, -mm_nt(grad_pseudo, state))
        grad_system = -jnp.where(
            strict, mm_nt(grad_value_in, value_mix) + mm_nt(grad_key_in, key_mix), 0.0
        )
        grad_raw = grad_scores * matrix
        grad_query = mm(grad_raw, keys) + grad_query_grown * grown
        grad_keys = mm_tn(grad_raw, query)
        weighted = grad_system * matrix
        grad_beta = jnp.sum(weighted * gram, axis=1, keepdims=True)
        grad_gram = weighted * beta
        grad_keys = grad_keys + mm(grad_gram, keys) + mm_tn(grad_gram, keys)
        spread = grad_scores * scores + grad_system * system
        grad_cumulative = jnp.sum(spread, axis=1, keepdims=True)
        across = jnp.sum(spread, axis=0, keepdims=True)
        grad_cumulative = grad_cumulative - jnp.sum(
            jnp.where(rows == cols, across, 0.0), axis=1, keepdims=True
        )
        grad_keys = grad_keys + grad_key_in * (beta * grown)
        through = jnp.sum(grad_key_in * keys, axis=1, keepdims=True) * grown
        grad_beta = grad_beta + through + jnp.sum(grad_value_in * values, axis=1, keepdims=True)
        grad_cumulative = grad_cumulative + through * beta
        grad_values = grad_value_in * beta
        grad_cumulative = grad_cumulative + jnp.sum(
            grad_query_grown * query_grown, axis=1, keepdims=True
        )
        grad_keys = grad_keys + grad_keys_end * to_end
        ending = jnp.sum(grad_keys_end * keys_end, axis=1, keepdims=True)
        final = jnp.sum(ending, axis=0, keepdims=True) + whole * grad_whole
        grad_cumulative = grad_cumulative - ending + jnp.where(row_column == count - 1, final, 0.0)
        beta_out = jnp.where(lanes == head, grad_beta, beta_out)
        cumulative_out = jnp.where(lanes == head, grad_cumulative, cumulative_out)
        key_part = activated[:, (H + head) * DK : (H + head + 1) * DK]
        key_scale = unit_rows(key_part)
        query_part = activated[:, head * DK : (head + 1) * DK]
        query_scale = unit_rows(query_part)
        factor = DK ** (-0.5)
        grad_query_part = (factor * query_scale) * (
            grad_query
            - query_part
            * (query_scale * query_scale)
            * jnp.sum(grad_query * query_part, axis=-1, keepdims=True)
        )
        grad_key_part = key_scale * (
            grad_keys
            - key_part
            * (key_scale * key_scale)
            * jnp.sum(grad_keys * key_part, axis=-1, keepdims=True)
        )
        spots = (head * DK, (H + head) * DK, 2 * H * DK + head * DV)
        for spot, grad in zip(spots, (grad_query_part, grad_key_part, grad_values)):
            size = grad.shape[1]
            padded_ref[pl.ds(8, count), spot : spot + size] = grad * slope[:, spot : spot + size]
    grad_beta_ref[...] = beta_out
    grad_decay_ref[...] = mm_tn(jnp.where(lower, 1.0, 0.0), cumulative_out)
    conv_total = jnp.zeros((count, width), jnp.float32)
    border_total = jnp.zeros((8, width), jnp.float32)
    summed_grad = padded_ref[pl.ds(8, count), :]
    tap_rows = lax.broadcasted_iota(jnp.int32, (8, width), 0)
    taps_total = jnp.zeros((8, width), jnp.float32)
    for tap in range(CONV):
        shift = CONV - 1 - tap
        conv_total = conv_total + taps[tap : tap + 1] * padded_ref[pl.ds(8 + shift, count), :]
        border_total = border_total + taps[tap : tap + 1] * padded_ref[pl.ds(shift, 8), :]
        piece = jnp.sum(
            summed_grad * extended_ref[pl.ds(8 - (CONV - 1) + tap, count), :],
            axis=0,
            keepdims=True,
        )
        taps_total = jnp.where(tap_rows == tap, piece, taps_total)
    grad_conv_ref[...] = conv_total
    grad_border_ref[...] = border_total
    grad_taps_ref[...] = taps_total


def fused(body, outputs, scratch=(), scalars=0, cost=(0, 0), label=None):
    def call(*args):
        vmem = pl.BlockSpec(memory_space=pltpu.VMEM)
        smem = pl.BlockSpec(memory_space=pltpu.SMEM)
        return pl.pallas_call(
            body,
            out_shape=outputs,
            in_specs=[smem] * scalars + [vmem] * (len(args) - scalars),
            out_specs=[vmem] * len(outputs),
            scratch_shapes=list(scratch),
            compiler_params=pltpu.CompilerParams(vmem_limit_bytes=60 * 2**20),
            cost_estimate=pl.CostEstimate(
                flops=cost[0], bytes_accessed=cost[1], transcendentals=0
            ),
            name=label,
        )(*args)

    return call


def gates(gate_logits, a_log, dt_bias):
    beta = jax.nn.sigmoid(gate_logits[:, :H])
    decay = -jnp.exp(a_log) * jax.nn.softplus(gate_logits[:, H:] + dt_bias)
    return beta, decay


def scatter_rows(pieces):
    outer, inner = lax.axis_size("dp"), lax.axis_size("ctx")
    whole = jnp.concatenate([piece.astype(jnp.bfloat16) for piece in pieces], axis=0)
    lane = math.gcd(whole.size // (outer * inner), D)
    blocks = whole.reshape(outer, inner, -1, lane)
    part = lax.psum_scatter(blocks, "ctx", scatter_dimension=1, tiled=False)
    own = lax.psum_scatter(part, "dp", scatter_dimension=0, tiled=False)
    return own.astype(jnp.float32).reshape(-1)


MESH = pl.DeviceIdType.MESH


class Place:
    def __init__(self, side):
        self.deep = lax.axis_size("dp")
        self.side = side
        self.ctx = lax.axis_size("ctx")
        self.z = lax.axis_index("dp")
        spot = lax.axis_index("ctx")
        self.c = lax.rem(spot, 2)
        chip = lax.div(spot, 2)
        self.x = lax.rem(chip, side)
        self.y = lax.div(chip, side)
        self.other_core = self.device(self.z, self.y, self.x, 1 - self.c)
        self.other_x = self.device(self.z, self.y, 1 - self.x, self.c)
        self.other_y = self.device(self.z, 1 - self.y, self.x, self.c)
        self.next_z = self.device(self.along(1), self.y, self.x, self.c)
        self.spot = spot
        self.before = (self.z, lax.rem(spot + self.ctx - 1, self.ctx))
        self.behind = (self.z, lax.rem(spot + 1, self.ctx))

    def along(self, step):
        return lax.rem(self.z + step + self.deep, self.deep)

    def device(self, z, y, x, c):
        return (z, (y * self.side + x) * 2 + c)

    def block(self, z, y, x, c):
        return z * self.ctx + (y * self.side + x) * 2 + c

    def enter_all(self):
        barrier = pltpu.get_barrier_semaphore()
        friends = [(self.z, lax.rem(self.spot + step, self.ctx)) for step in range(1, self.ctx)]
        friends += [(self.along(step), self.spot) for step in range(1, self.deep)]
        for friend in friends:
            pl.semaphore_signal(barrier, inc=1, device_id=friend, device_id_type=MESH)
        pl.semaphore_wait(barrier, len(friends))

    def enter(self, all_z=False, more=()):
        barrier = pltpu.get_barrier_semaphore()
        steps = range(1, self.deep) if all_z else (-1,)
        friends = [self.other_core, self.other_x, self.other_y, *more]
        friends += [self.device(self.along(step), self.y, self.x, self.c) for step in steps]
        for friend in friends:
            pl.semaphore_signal(barrier, inc=1, device_id=friend, device_id_type=MESH)
        pl.semaphore_wait(barrier, len(friends))


class Copies:
    def __init__(self, send_sems, recv_sems, local_sems=None):
        self.send_sems, self.recv_sems, self.local_sems = send_sems, recv_sems, local_sems
        self.sent, self.locals = [], 0

    def push(self, source, target, device):
        index = len(self.sent)
        copy = pltpu.make_async_remote_copy(
            src_ref=source,
            dst_ref=target,
            send_sem=self.send_sems.at[index],
            recv_sem=self.recv_sems.at[index],
            device_id=device,
            device_id_type=MESH,
        )
        copy.start()
        self.sent.append(copy)
        return copy

    def local(self, source, target):
        copy = pltpu.make_async_copy(source, target, self.local_sems.at[self.locals])
        copy.start()
        self.locals += 1
        return copy

    def finish(self):
        for copy in self.sent:
            copy.wait_send()


def upper(rows):
    return rows // 2 // 16 * 16


def gather_steps(place, copies, shard_ref, out_ref, plane=False):
    rows, deep = shard_ref.shape[0], 1 if plane else place.deep
    top = upper(rows)
    spans = {None: (0, rows), 0: (0, top), 1: (top, rows - top)}
    ring, near, far, core = {}, {}, {}, []

    def cut(ref, start, part):
        offset, size = spans[part]
        return ref.at[pl.ds(pl.multiple_of(start + offset, 16), size), :]

    def start_of(rel, dy, dx):
        y = 1 - place.y if dy else place.y
        x = 1 - place.x if dx else place.x
        z = 0 if plane else place.along(-rel)
        return place.block(z, y, x, place.c) * rows

    def forward(rel, dy, dx, part, device):
        start = start_of(rel, dy, dx)
        own = rel == 0 and not dy and not dx
        source = cut(shard_ref, 0, part) if own else cut(out_ref, start, part)
        return copies.push(source, cut(out_ref, start, part), device)

    def along_z(rel, part):
        if rel < deep - 1:
            ring[rel, part] = forward(rel, 0, 0, part, place.next_z)

    def spread(rel):
        near[rel, "x0"] = forward(rel, 0, 0, 0, place.other_x)
        near[rel, "y1"] = forward(rel, 0, 0, 1, place.other_y)
        near[rel, "y0"] = forward(rel, 0, 0, 0, place.other_y)
        near[rel, "x1"] = forward(rel, 0, 0, 1, place.other_x)
        core.append(forward(rel, 0, 0, None, place.other_core))

    def second(rel):
        near[rel, "x0"].wait_recv()
        far[rel, 0] = forward(rel, 0, 1, 0, place.other_y)
        near[rel, "y1"].wait_recv()
        far[rel, 1] = forward(rel, 1, 0, 1, place.other_x)
        core.append(forward(rel, 0, 1, 0, place.other_core))
        core.append(forward(rel, 1, 0, 1, place.other_core))

    def third(rel):
        near[rel, "y0"].wait_recv()
        core.append(forward(rel, 1, 0, 0, place.other_core))
        near[rel, "x1"].wait_recv()
        core.append(forward(rel, 0, 1, 1, place.other_core))

    def fourth(rel):
        for part in (0, 1):
            far[rel, part].wait_recv()
            core.append(forward(rel, 1, 1, part, place.other_core))

    own_copy = []

    def first():
        own_copy.append(copies.local(shard_ref, cut(out_ref, start_of(0, 0, 0), None)))
        for part in (0, 1):
            along_z(0, part)
        spread(0)

    def later(rel):
        for part in (0, 1):
            ring[rel - 1, part].wait_recv()
            along_z(rel, part)
        spread(rel)

    def last():
        for copy in core:
            copy.wait_recv()
        own_copy[0].wait()

    steps = [first]
    for rel in range(1, deep):
        steps.append(lambda rel=rel: later(rel))
        steps.append(lambda rel=rel: second(rel - 1))
        steps.append(lambda rel=rel: third(rel - 1))
    steps.append(lambda: second(deep - 1))
    steps.append(lambda: third(deep - 1))
    for rel in range(deep):
        steps.append(lambda rel=rel: fourth(rel))
    steps.append(last)
    return steps


def wide(value):
    return value.astype(jnp.float32)


class Scatter:
    def __init__(self, place, copies, grad_ref, held, from_core, first_x, first_y, last_x, last_y, from_z):
        self.place, self.copies, self.grad = place, copies, grad_ref
        self.held, self.from_core, self.from_z = held, from_core, from_z
        self.first = {0: first_y, 1: first_x}
        self.last = {0: last_x, 1: last_y}
        self.rows = held.shape[1]
        self.top = upper(self.rows)
        self.loads, self.cores, self.near, self.far, self.ring = {}, {}, {}, {}, {}

    @staticmethod
    def scratch(deep, rows):
        top = upper(rows)
        low = rows - top
        return [
            pltpu.VMEM((4 * deep, rows, D), jnp.bfloat16),
            pltpu.VMEM((4 * deep, rows, D), jnp.bfloat16),
            pltpu.VMEM((2 * deep, low, D), jnp.bfloat16),
            pltpu.VMEM((2 * deep, top, D), jnp.bfloat16),
            pltpu.VMEM((deep, top, D), jnp.bfloat16),
            pltpu.VMEM((deep, low, D), jnp.bfloat16),
            pltpu.VMEM((deep - 1, rows, D), jnp.bfloat16),
        ]

    @staticmethod
    def copies_of(deep):
        return 4 * deep + 4 * deep + 2 * deep + 2 * (deep - 1)

    def slot(self, rel, dy, dx):
        return (rel - 1) * 4 + dy * 2 + dx

    def span(self, part):
        return pl.ds(0, self.top) if part == 0 else pl.ds(self.top, self.rows - self.top)

    def load(self):
        place = self.place
        for rel in range(1, place.deep + 1):
            for dy, dx in ((1, 1), (1, 0), (0, 1), (0, 0)):
                y = 1 - place.y if dy else place.y
                x = 1 - place.x if dx else place.x
                slot = self.slot(rel, dy, dx)

                def rows_of(core):
                    start = place.block(place.along(-rel), y, x, core) * self.rows
                    return self.grad.at[pl.ds(pl.multiple_of(start, 16), self.rows), :]

                self.cores[slot] = self.copies.push(
                    rows_of(1 - place.c), self.from_core.at[slot], place.other_core
                )
                self.loads[slot] = self.copies.local(rows_of(place.c), self.held.at[slot])

    def stage_one(self, rel):
        place = self.place
        for dy, dx in ((1, 1), (1, 0), (0, 1), (0, 0)):
            slot = self.slot(rel, dy, dx)
            self.loads[slot].wait()
            self.cores[slot].wait_recv()
            self.held[slot] = (wide(self.held[slot]) + wide(self.from_core[slot])).astype(jnp.bfloat16)
            if dy:
                self.near[rel, 0, dx] = self.copies.push(
                    self.held.at[slot, self.span(0), :],
                    self.first[0].at[(rel - 1) * 2 + dx],
                    place.other_y,
                )
            if dx:
                self.near[rel, 1, dy] = self.copies.push(
                    self.held.at[slot, self.span(1), :],
                    self.first[1].at[(rel - 1) * 2 + dy],
                    place.other_x,
                )

    def add(self, slot, part, piece):
        self.held[slot, self.span(part), :] = (
            wide(self.held[slot, self.span(part), :]) + wide(piece)
        ).astype(jnp.bfloat16)

    def stage_two(self, rel):
        place = self.place
        for part in (0, 1):
            for away in (1, 0):
                self.near[rel, part, away].wait_recv()
                slot = self.slot(rel, away, 0) if part else self.slot(rel, 0, away)
                self.add(slot, part, self.first[part][(rel - 1) * 2 + away])
                if away:
                    self.far[rel, part] = self.copies.push(
                        self.held.at[slot, self.span(part), :],
                        self.last[part].at[rel - 1],
                        place.other_y if part else place.other_x,
                    )

    def stage_three(self, rel, total_ref=None):
        slot = self.slot(rel, 0, 0)
        for part in (0, 1):
            span = self.span(part)
            self.far[rel, part].wait_recv()
            total = wide(self.held[slot, span, :]) + wide(self.last[part][rel - 1])
            if rel >= 2:
                self.ring[rel - 1, part].wait_recv()
                total = total + wide(self.from_z[rel - 2, span, :])
            if rel == self.place.deep:
                total_ref[span, :] = total
                continue
            self.held[slot, span, :] = total.astype(jnp.bfloat16)
            self.ring[rel, part] = self.copies.push(
                self.held.at[slot, span, :], self.from_z.at[rel - 1, span, :], self.place.next_z
            )

    def steps(self, total_ref):
        deep = self.place.deep
        out = [self.load]
        for turn in range(1, deep + 3):
            if turn <= deep:
                out.append(lambda rel=turn: self.stage_one(rel))
            if 1 <= turn - 1 <= deep:
                out.append(lambda rel=turn - 1: self.stage_two(rel))
            if 1 <= turn - 2 <= deep:
                out.append(lambda rel=turn - 2: self.stage_three(rel, total_ref))
        return out


class Everywhere:
    def __init__(self, place, copies, total, slots, stack):
        self.place, self.copies = place, copies
        self.total, self.slots, self.stack = total, slots, stack
        self.turns = (place.other_core, place.other_x, place.other_y)
        self.pending = []

    @staticmethod
    def scratch(deep, rows, width):
        return [pltpu.VMEM((count, rows, width), jnp.float32) for count in (3, deep, 4)]

    def send(self, turn):
        self.pending = [
            self.copies.push(self.total.at[turn], self.slots.at[turn], self.turns[turn])
        ]

    def take(self, turn):
        self.pending[0].wait_recv()
        self.total[turn + 1] = self.total[turn] + self.slots[turn]

    def send_z(self):
        place = self.place
        self.pending = [
            self.copies.push(
                self.total.at[3],
                self.stack.at[place.z],
                place.device(place.along(step), place.y, place.x, place.c),
            )
            for step in range(1, place.deep)
        ]
        self.stack[place.z] = self.total[3]

    def take_z(self):
        for copy in self.pending:
            copy.wait_recv()
        result = self.stack[0]
        for index in range(1, self.place.deep):
            result = result + self.stack[index]
        return result

    def run(self):
        for turn in range(3):
            self.send(turn)
            self.take(turn)
        self.send_z()
        return self.take_z()


def gather_around(place, copies, shard_ref, out_ref):
    rows, deep = shard_ref.shape[0], place.deep
    top = upper(rows)
    spans = ((0, top), (top, rows - top))
    near_device = (place.other_x, place.other_y)
    far_device = (place.other_y, place.other_x)
    near, ring, far, core, own_copy = {}, {}, {}, [], []

    def start_of(part, rel, near_by, far_by):
        dx, dy = (near_by, far_by) if part == 0 else (far_by, near_by)
        y = 1 - place.y if dy else place.y
        x = 1 - place.x if dx else place.x
        z = place.along(-rel)
        return place.block(z, y, x, place.c) * rows

    def forward(part, rel, near_by, far_by, device):
        offset, size = spans[part]
        start = pl.multiple_of(start_of(part, rel, near_by, far_by) + offset, 16)
        own = not (rel or near_by or far_by)
        target = out_ref.at[pl.ds(start, size), :]
        return copies.push(shard_ref.at[pl.ds(offset, size), :] if own else target, target, device)

    def spread(part, rel, near_by):
        if rel < deep - 1:
            ring[part, rel, near_by] = forward(part, rel, near_by, 0, place.next_z)
        far[part, rel, near_by] = forward(part, rel, near_by, 0, far_device[part])
        core.append(forward(part, rel, near_by, 0, place.other_core))

    def first():
        start = pl.multiple_of(start_of(0, 0, 0, 0), 16)
        own_copy.append(copies.local(shard_ref, out_ref.at[pl.ds(start, rows), :]))
        for part in (0, 1):
            near[part] = forward(part, 0, 0, 0, near_device[part])
        for part in (0, 1):
            spread(part, 0, 0)

    def second():
        for part in (0, 1):
            near[part].wait_recv()
            spread(part, 0, 1)

    def later(rel, near_by):
        for part in (0, 1):
            ring[part, rel - 1, near_by].wait_recv()
            spread(part, rel, near_by)

    def third(rel, near_by):
        for part in (0, 1):
            far[part, rel, near_by].wait_recv()
            core.append(forward(part, rel, near_by, 1, place.other_core))

    def last():
        for copy in core:
            copy.wait_recv()
        own_copy[0].wait()

    steps = [first, second]
    for rel in range(1, deep):
        steps += [lambda rel=rel, by=by: later(rel, by) for by in (0, 1)]
        if rel >= 2:
            steps += [lambda rel=rel - 2, by=by: third(rel, by) for by in (0, 1)]
    for rel in range(max(deep - 2, 0), deep):
        steps += [lambda rel=rel, by=by: third(rel, by) for by in (0, 1)]
    return steps + [last]


def gather_copies(deep):
    return 2 * (deep - 1) + 4 * deep + 2 * deep + deep + 2 * deep * 3


def front_parts(ext_ref, taps_ref, beta_ref, decay_ref, wire_refs, query_ref, keys_ref, values_ref, inverse_ref):
    count = query_ref.shape[0]
    width = taps_ref.shape[1]
    summed = ext_sum(ext_ref, taps_ref[...], count, 0, width)
    activated = summed * jax.nn.sigmoid(summed)
    rows, cols = iotas(count)
    for head in range(H):
        query_part = activated[:, head * DK : (head + 1) * DK]
        key_part = activated[:, (H + head) * DK : (H + head + 1) * DK]
        start = 2 * H * DK + head * DV
        values = activated[:, start : start + DV]
        query = query_part * unit_rows(query_part) * DK ** (-0.5)
        keys = key_part * unit_rows(key_part)
        beta = beta_ref[:, head : head + 1]
        matrix, grown, to_end, whole = decay_terms(decay_lane(decay_ref, head), rows, cols)
        system = jnp.where(rows > cols, beta * mm_nt(keys, keys) * matrix, 0.0)
        inverse = unit_inverse(system, rows, cols)
        key_mix = mm(inverse, keys * (beta * grown))
        value_mix = mm(inverse, values * beta)
        base = 0
        wire_refs[head][0:count, base : base + DK] = (keys * to_end).astype(jnp.bfloat16)
        wire_refs[head][0:count, base + DK : base + 2 * DK] = key_mix.astype(jnp.bfloat16)
        wire_refs[head][0:count, base + 2 * DK : base + 2 * DK + DV] = value_mix.astype(jnp.bfloat16)
        high, low = halves(jnp.broadcast_to(whole, (PAD, 2 * DK + DV)))
        first = lax.broadcasted_iota(jnp.int32, (PAD, 2 * DK + DV), 0) < 8
        tail = jnp.where(first, high.astype(jnp.float32), low.astype(jnp.float32))
        wire_refs[head][pl.ds(count, PAD), base : base + 2 * DK + DV] = tail.astype(jnp.bfloat16)
        query_ref[:, head * DK : (head + 1) * DK] = query
        keys_ref[:, head * DK : (head + 1) * DK] = keys
        values_ref[:, head * DV : (head + 1) * DV] = values
        inverse_ref[head] = inverse
        yield


def ext_sum(ext_ref, taps, count, start, size):
    total = None
    for tap in range(CONV):
        piece = (
            taps[tap : tap + 1, start : start + size]
            * ext_ref[pl.ds(8 - (CONV - 1) + tap, count), start : start + size]
        )
        total = piece if total is None else total + piece
    return total


def small_places():
    width = 2 * H * DK + H * DV
    starts, spot = [], 0
    for length in (D, D, DV, CONV * width, 2 * H * D):
        starts.append(spot // 128)
        spot += length
    return starts + [spot // 128]


def joined(ref, first, number):
    return jnp.concatenate([ref[first + index : first + index + 1, :] for index in range(number)], axis=1)


def gate_masks():
    each = 128 // (2 * H)
    row = lax.broadcasted_iota(jnp.int32, (D, 128), 0)
    lane = lax.broadcasted_iota(jnp.int32, (D, 128), 1)
    own = lax.rem(row, each) == lax.div(lane, 2 * H)
    rows, cols = iotas(128)
    return own, jnp.where(lax.rem(rows, 2 * H) == cols, 1.0, 0.0), each


def unpack_gates(packed):
    own, select, each = gate_masks()
    spread = jnp.broadcast_to(packed[:, None, :], (packed.shape[0], each, 128)).reshape(D, 128)
    return mm(jnp.where(own, spread, 0.0), select)


def pack_gates(plain):
    own, select, each = gate_masks()
    spread = jnp.where(own, mm_nt(plain, select), 0.0)
    return jnp.sum(spread.reshape(D // each, each, 128), axis=1)


def from_flat(flat_ref, rows):
    pieces = [flat_ref[pl.ds(index, rows, stride=D // 128), :] for index in range(D // 128)]
    return jnp.concatenate(pieces, axis=1)


def to_flat(flat_ref, value):
    for index in range(D // 128):
        flat_ref[pl.ds(index, value.shape[0], stride=D // 128), :] = value[:, index * 128 : (index + 1) * 128]


def front_kernel(
    side, mix_flat, ffn_flat, x_ref, small_ref,
    mix_out, ffn_out, wires_zero, wires_one, ext_ref, gate_ref, query_ref, keys_ref, values_ref, inverse_ref,
    own_normed_ref, beta_ref, decay_ref, factor_ref, taps_ref, gains_ref, w_gates_ref,
    weight_ref, wire_zero, wire_one, mix_shard, ffn_shard, normed_ref, edge_ref,
    send_sems, recv_sems, local_sems,
):
    place = Place(side)
    copies = Copies(send_sems, recv_sems, local_sems)
    bf16 = jnp.bfloat16
    count = x_ref.shape[0]
    width = taps_ref.shape[1]
    mix_shard[...] = from_flat(mix_flat, mix_shard.shape[0]).astype(bf16)
    place.enter(more=(place.before,))
    mix = gather_steps(place, copies, mix_shard, mix_out)
    ffn = gather_around(place, copies, ffn_shard, ffn_out)
    mix.pop(0)()
    one, two, head, tap, gate, rest = small_places()
    gain_one = joined(small_ref, one, D // 128)
    normed = norm_scale(x_ref[...].astype(jnp.float32), gain_one).astype(bf16)
    own_normed_ref[...] = normed
    normed_ref[pl.ds(PAD, count), :] = normed
    edge = copies.push(normed_ref.at[pl.ds(count, PAD), :], edge_ref, place.behind)
    ffn_rows = ffn_flat.shape[0] * 128 // D
    ffn_shard[...] = jnp.zeros_like(ffn_shard)
    ffn_shard[0:ffn_rows, :] = from_flat(ffn_flat, ffn_rows).astype(bf16)
    early = 3 * (place.deep - 1) + 2
    mix.pop(0)()
    ffn.pop(0)()
    gains_ref[...] = jnp.zeros_like(gains_ref)
    gains_ref[0:1, :] = gain_one
    gains_ref[1:2, :] = joined(small_ref, two, D // 128)
    gains_ref[2:3, 0:DV] = joined(small_ref, head, DV // 128)
    for index in range(CONV):
        taps_ref[index : index + 1, :] = joined(small_ref, tap + index * (width // 128), width // 128)
    for step in mix[:3]:
        step()
    w_gates_ref[...] = unpack_gates(small_ref[gate:rest, :])
    logits = mm(normed.astype(jnp.float32), w_gates_ref[...])
    for step in mix[3:5]:
        step()
    ffn.pop(0)()
    lanes = lax.broadcasted_iota(jnp.int32, (1, 128), 1)
    late = (lanes >= H) & (lanes < 2 * H)
    scalars = small_ref[rest : rest + 1, :]
    raised = logits + jnp.where(late, scalars, 0.0)
    size = jnp.exp(jnp.where(late, pltpu.roll(scalars, H, 1), 0.0))
    soft = jax.nn.sigmoid(raised)
    beta_ref[...] = soft
    decay_ref[...] = jnp.where(
        late, -size * (jnp.maximum(raised, 0.0) + jnp.log1p(jnp.exp(-jnp.abs(raised)))), 0.0
    )
    factor_ref[...] = jnp.where(late, -size * soft, jnp.where(lanes < H, soft * (1.0 - soft), 0.0))
    for step in mix[5 : early - 2]:
        step()
    ffn.pop(0)()
    ffn.pop(0)()
    for step in mix[early - 2 :]:
        step()
    edge.wait_recv()
    normed_ref[0:PAD, :] = jnp.where(place.spot > 0, edge_ref[...], jnp.zeros_like(edge_ref))
    depth = weight_ref.shape[0]
    chunk = DV
    loads = [
        copies.local(mix_out.at[pl.ds(start, chunk), :], weight_ref.at[pl.ds(start, chunk), :])
        for start in range(0, depth, chunk)
    ]
    for index, load in enumerate(loads):
        load.wait()
        span = pl.ds(index * chunk, chunk)
        piece = dot_nt(normed_ref[...], weight_ref[span, :])
        start = index * chunk
        if start < width:
            ext_ref[:, start : start + chunk] = piece[8:]
        else:
            start = start - width
            gate_ref[:, start : start + chunk] = piece[PAD:]
        if index % 2 == 1:
            ffn.pop(0)()
    parts = front_parts(
        ext_ref, taps_ref, beta_ref, decay_ref, (wire_zero, wire_one),
        query_ref, keys_ref, values_ref, inverse_ref,
    )
    next(parts)
    zero = gather_steps(place, copies, wire_zero, wires_zero, plane=True)
    zero.pop(0)()
    for again in range(3):
        ffn.pop(0)()
    next(parts)
    one = gather_steps(place, copies, wire_one, wires_one, plane=True)
    one.pop(0)()
    while zero[1:]:
        zero.pop(0)()
        one.pop(0)()
        if len(ffn) > 1:
            ffn.pop(0)()
    for step in ffn + zero + one:
        step()
    copies.finish()


def front(mix_flat, ffn_flat, x, small, side, tag):
    f32, bf16 = jnp.float32, jnp.bfloat16
    deep, ctx = lax.axis_size("dp"), lax.axis_size("ctx")
    count = x.shape[0]
    everyone = deep * ctx
    mix_rows, ffn_rows = mix_flat.shape[0] * 128 // D, ffn_flat.shape[0] * 128 // D
    padded = -(-ffn_rows // 16) * 16
    number = 2 * gather_copies(deep) + 2 * gather_copies(1) + 9 * deep
    anywhere = pl.BlockSpec(memory_space=pl.ANY)
    vmem = pl.BlockSpec(memory_space=pltpu.VMEM)
    width = 2 * H * DK + H * DV
    depth = width + H * DV
    wire = (count + PAD, 2 * DK + DV)
    shape = jax.ShapeDtypeStruct
    return pl.pallas_call(
        functools.partial(front_kernel, side),
        out_shape=[
            shape((everyone * mix_rows, D), bf16),
            shape((everyone * padded, D), bf16),
            shape((ctx * wire[0], wire[1]), bf16),
            shape((ctx * wire[0], wire[1]), bf16),
            shape((count + 8, width), f32),
            shape((count, H * DV), f32),
            shape((count, H * DK), f32),
            shape((count, H * DK), f32),
            shape((count, H * DV), f32),
            shape((H, count, count), f32),
            shape((count, D), bf16),
            shape((count, 128), f32),
            shape((count, 128), f32),
            shape((count, 128), f32),
            shape((CONV, width), f32),
            shape((8, D), f32),
            shape((D, 128), f32),
        ],
        in_specs=[vmem] * 4,
        out_specs=[anywhere] * 4 + [vmem] * 13,
        scratch_shapes=[
            pltpu.VMEM((depth, D), bf16),
            pltpu.VMEM(wire, bf16),
            pltpu.VMEM(wire, bf16),
            pltpu.VMEM((mix_rows, D), bf16),
            pltpu.VMEM((padded, D), bf16),
            pltpu.VMEM((count + PAD, D), bf16),
            pltpu.VMEM((PAD, D), bf16),
            pltpu.SemaphoreType.DMA((number,)),
            pltpu.SemaphoreType.DMA((number,)),
            pltpu.SemaphoreType.DMA((4 + depth // DV,)),
        ],
        compiler_params=pltpu.CompilerParams(
            collective_id=tag, has_side_effects=True, vmem_limit_bytes=60 * 2**20
        ),
        cost_estimate=pl.CostEstimate(flops=0, bytes_accessed=10**8, transcendentals=0),
        name="front",
    )(mix_flat, ffn_flat, x, small)


def dot_nn(a, b):
    return lax.dot_general(a, b, (((1,), (0,)), ((), ())), preferred_element_type=jnp.float32)


def dot_nt(a, b):
    return lax.dot_general(a, b, (((1,), (1,)), ((), ())), preferred_element_type=jnp.float32)


def dot_tn(a, b):
    return lax.dot_general(a, b, (((0,), (0,)), ((), ())), preferred_element_type=jnp.float32)


def chunk_of(rows):
    return max(size for size in range(16, 577, 16) if rows % size == 0)


def by_chunks(rows, body):
    size = chunk_of(rows)

    def turn(index, carry):
        body(pl.ds(pl.multiple_of(index * size, 16), size), index * size, size)
        return carry

    lax.fori_loop(0, rows // size, turn, 0)


def norm_back(grad, values, scale, gain):
    plain = values * scale
    pulled = grad * gain
    through = scale * (pulled - plain * jnp.mean(pulled * plain, axis=-1, keepdims=True))
    return through, jnp.sum(grad * plain, axis=0, keepdims=True)


def middle_kernel(
    rows, place_ref, wires_zero, wires_one, query_ref, keys_ref, values_ref, inverse_ref, beta_ref, decay_ref,
    gate_ref, gains_ref, x_ref, cot_ref, mix_hbm, ffn_hbm,
    result_ref, grad_resid_ref, grad_out_ref, ffn_grad_ref, gain_two_grad_ref, state_ref, pseudo_ref,
    local_ref, grad_mixed_ref, grad_gate_ref, gain_head_grad_ref,
    w_out, w_ffn, mixed_ref, head_out_ref, pre_ref, compact_ref, down_ref, hidden_ref, total_ref,
    grad_head_ref, sems,
):
    count = query_ref.shape[0]
    padded = -(-rows // 16) * 16
    gain_two_ref = gains_ref.at[1:2, :]
    gain_head_ref = gains_ref.at[2:3, 0:DV]
    out_rows = w_out.shape[0]
    load_out = pltpu.make_async_copy(
        mix_hbm.at[pl.ds(mix_hbm.shape[0] - out_rows, out_rows), :], w_out, sems.at[0]
    )
    load_ffn = pltpu.make_async_copy(ffn_hbm, w_ffn, sems.at[1])
    load_out.start()
    load_ffn.start()
    forward_chain(
        place_ref, (wires_zero, wires_one), query_ref, keys_ref, values_ref, inverse_ref, beta_ref, decay_ref,
        gate_ref, gain_head_ref, head_out_ref, mixed_ref, state_ref, pseudo_ref,
    )
    load_out.wait()
    resid = x_ref[...].astype(jnp.float32) + dot_nn(head_out_ref[...], w_out[...])
    scale = lax.rsqrt(jnp.mean(resid * resid, axis=-1, keepdims=True) + EPSILON)
    normed = (resid * scale * gain_two_ref[...]).astype(jnp.bfloat16)
    load_ffn.wait()
    pairs = 2 * FF
    blocks = ffn_hbm.shape[0] // padded
    used = -(-pairs // rows)
    split = pairs // rows
    inside = pairs - split * rows
    upper_rows = used * padded
    down_start = split * padded
    down_rows = (blocks - split) * padded
    bf16 = jnp.bfloat16

    def pre(span, start, size):
        pre_ref[span, :] = dot_nt(w_ffn[span, :], normed)

    by_chunks(upper_rows, pre)
    for block in range(used):
        size = min(rows, pairs - block * rows)
        compact_ref[pl.ds(block * rows, size), :] = pre_ref[pl.ds(block * padded, size), :]
    down_ref[...] = jnp.zeros_like(down_ref)

    def pieces():
        done = 0
        for block in range(blocks - split):
            offset = inside if block == 0 else 0
            size = rows - offset
            yield done, block * padded + offset, size
            done += size

    gate = compact_ref[0:FF, :]
    up = compact_ref[FF:pairs, :]
    hidden_ref[...] = gate * jax.nn.sigmoid(gate) * up
    for done, spot, size in pieces():
        down_ref[pl.ds(spot, size), :] = hidden_ref[pl.ds(done, size), :]
    total_ref[...] = resid

    def out_chunk(span, start, size):
        here = pl.ds(pl.multiple_of(down_start + start, 16), size)
        total_ref[...] += dot_tn(down_ref[span, :].astype(bf16), w_ffn[here, :])

    by_chunks(down_rows, out_chunk)
    result_ref[...] = total_ref[...].astype(bf16)
    cot = cot_ref[...]

    def hidden_chunk(span, start, size):
        here = pl.ds(pl.multiple_of(down_start + start, 16), size)
        pre_ref[span, :] = dot_nt(w_ffn[here, :], cot)

    by_chunks(down_rows, hidden_chunk)
    for done, spot, size in pieces():
        hidden_ref[pl.ds(done, size), :] = pre_ref[pl.ds(spot, size), :]
    gate = compact_ref[0:FF, :]
    up = compact_ref[FF:pairs, :]
    active, slope = silu_pair(gate)
    grad_hidden = hidden_ref[...]
    compact_ref[0:FF, :] = grad_hidden * up * slope
    compact_ref[FF:pairs, :] = grad_hidden * active
    pre_ref[...] = jnp.zeros_like(pre_ref)
    for block in range(used):
        size = min(rows, pairs - block * rows)
        pre_ref[pl.ds(block * padded, size), :] = compact_ref[pl.ds(block * rows, size), :]
    total_ref[...] = jnp.zeros_like(total_ref)

    def mid_chunk(span, start, size):
        piece = pre_ref[span, :].astype(bf16)
        total_ref[...] += dot_tn(piece, w_ffn[span, :])
        ffn_grad_ref[span, :] = dot_nn(piece, normed).astype(bf16)

    by_chunks(upper_rows, mid_chunk)
    shared = upper_rows - down_start
    if shared:
        both = jnp.concatenate(
            [pre_ref[pl.ds(down_start, shared), :], down_ref[pl.ds(0, shared), :]], axis=1
        ).astype(bf16)
        against = jnp.concatenate([normed, cot], axis=0)
        ffn_grad_ref[pl.ds(down_start, shared), :] = dot_nn(both, against).astype(bf16)

    def down_chunk(span, start, size):
        here = pl.ds(pl.multiple_of(shared + start, 16), size)
        there = pl.ds(pl.multiple_of(upper_rows + start, 16), size)
        ffn_grad_ref[there, :] = dot_nn(down_ref[here, :].astype(bf16), cot).astype(bf16)

    by_chunks(down_rows - shared, down_chunk)
    resid = x_ref[...].astype(jnp.float32) + dot_nn(head_out_ref[...], w_out[...])
    through, gain_two_grad_ref[...] = norm_back(total_ref[...], resid, scale, gain_two_ref[...])
    grad_resid = cot.astype(jnp.float32) + through
    grad_resid_ref[...] = grad_resid
    resid_half = grad_resid.astype(bf16)
    grad_out_ref[...] = dot_tn(head_out_ref[...], resid_half).astype(bf16)
    grad_head_ref[...] = dot_nt(resid_half, w_out[...])
    backward_local(
        grad_head_ref, mixed_ref, query_ref, keys_ref, values_ref, inverse_ref, beta_ref, decay_ref,
        gate_ref, gain_head_ref, local_ref, grad_mixed_ref, grad_gate_ref, gain_head_grad_ref,
    )


def middle(rows, place, zero, one, query, keys, values, inverse, beta, decay, gate, gains, x, cot, mix, ffn):
    f32, bf16 = jnp.float32, jnp.bfloat16
    count = query.shape[0]
    padded = -(-rows // 16) * 16
    blocks = ffn.shape[0] // padded
    used, split = -(-2 * FF // rows), 2 * FF // rows
    out_rows = H * DV
    vmem = pl.BlockSpec(memory_space=pltpu.VMEM)
    anywhere = pl.BlockSpec(memory_space=pl.ANY)
    return pl.pallas_call(
        functools.partial(middle_kernel, rows),
        out_shape=[
            jax.ShapeDtypeStruct((count, D), bf16),
            jax.ShapeDtypeStruct((count, D), f32),
            jax.ShapeDtypeStruct((out_rows, D), bf16),
            jax.ShapeDtypeStruct(ffn.shape, bf16),
            jax.ShapeDtypeStruct((1, D), f32),
            jax.ShapeDtypeStruct((H, DK, DV), f32),
            jax.ShapeDtypeStruct((count, H * DV), f32),
            jax.ShapeDtypeStruct((H * DK, DV), bf16),
            jax.ShapeDtypeStruct((count, H * DV), f32),
            jax.ShapeDtypeStruct((count, H * DV), bf16),
            jax.ShapeDtypeStruct((1, DV), f32),
        ],
        in_specs=[pl.BlockSpec(memory_space=pltpu.SMEM)] + [vmem] * 12 + [anywhere] * 2,
        out_specs=[vmem] * 11,
        scratch_shapes=[
            pltpu.VMEM((out_rows, D), bf16),
            pltpu.VMEM(ffn.shape, bf16),
            pltpu.VMEM((count, H * DV), f32),
            pltpu.VMEM((count, H * DV), bf16),
            pltpu.VMEM((used * padded, count), f32),
            pltpu.VMEM((2 * FF, count), f32),
            pltpu.VMEM(((blocks - split) * padded, count), f32),
            pltpu.VMEM((FF, count), f32),
            pltpu.VMEM((count, D), f32),
            pltpu.VMEM((count, H * DV), f32),
            pltpu.SemaphoreType.DMA((2,)),
        ],
        compiler_params=pltpu.CompilerParams(vmem_limit_bytes=60 * 2**20),
        cost_estimate=pl.CostEstimate(flops=10**10, bytes_accessed=5 * 10**7, transcendentals=0),
        name="middle",
    )(place, zero, one, query, keys, values, inverse, beta, decay, gate, gains, x, cot, mix, ffn)


def back_kernel(
    side, wires_zero, wires_one, local_ref, query_ref, keys_ref, values_ref, inverse_ref, beta_ref, decay_ref,
    state_ref, pseudo_ref, grad_mixed_ref, ext_ref, taps_ref, grad_gate_ref, grad_resid_ref, x_ref,
    normed_ref, gains_ref, factor_ref, w_gates_ref, gain_two_grad_ref,
    gain_head_grad_ref, ffn_grad, grad_out, mix_hbm,
    ffn_flat, mix_flat, grad_input_ref, small_out, squares_out,
    *scratch,
):
    scratch = list(scratch)
    take = lambda number: [scratch.pop(0) for unused in range(number)]
    after_ref, padded_ref, locals_zero, locals_one, border_ref, taps_grad_ref = take(6)
    grad_beta_ref, grad_decay_ref, proj_ref, mix_grad, weight_ref, total_ref, arrived_ref = take(7)
    ffn_total, mix_total = take(2)
    ffn_scratch, mix_scratch, small_scratch, square_scratch = take(7), take(6), take(3), take(3)
    send_sems, recv_sems, local_sems, weight_sems, free_sem = scratch
    mix_scratch.insert(1, ffn_scratch[1].at[:, pl.ds(0, mix_total.shape[0]), :])
    f32, bf16 = jnp.float32, jnp.bfloat16
    place = Place(side)
    copies = Copies(send_sems, recv_sems, local_sems)
    place.enter_all()
    count, width = query_ref.shape[0], taps_ref.shape[1]
    depth = proj_ref.shape[1]
    conv_ref = padded_ref.at[pl.ds(8, count), :]
    scatter = Scatter(place, copies, ffn_grad, *ffn_scratch)
    ffn = scatter.steps(ffn_total)
    mix = Scatter(place, copies, mix_grad, *mix_scratch).steps(mix_total)
    both = [
        gather_steps(place, copies, local_ref.at[pl.ds(head * DK, DK), :], target, plane=True)
        for head, target in enumerate((locals_zero, locals_one))
    ]
    states = [step for pair in zip(*both) for step in pair]
    states.pop(0)()
    states.pop(0)()
    ffn.pop(0)()
    own_out = copies.local(grad_out, mix_grad.at[pl.ds(depth, grad_out.shape[0]), :])
    for again in range(4):
        states.pop(0)()
    ffn.pop(0)()
    for step in states:
        step()
    ffn.pop(0)()
    work = back_chain(
        (wires_zero, wires_one), (locals_zero, locals_one), query_ref, keys_ref, values_ref, inverse_ref, beta_ref,
        decay_ref, state_ref, pseudo_ref, grad_mixed_ref, ext_ref, taps_ref,
        conv_ref, border_ref, taps_grad_ref, grad_beta_ref, grad_decay_ref,
        after_ref, padded_ref,
    )
    for index, unused in enumerate(work):
        for again in range(2 if index < 3 else 1):
            ffn.pop(0)()
    border = copies.push(border_ref, arrived_ref, place.before)
    pl.semaphore_signal(free_sem, inc=1, device_id=place.other_core, device_id_type=MESH)
    grad_decay = grad_decay_ref[...]
    grad_logits = (grad_beta_ref[...] + grad_decay) * factor_ref[...]
    normed = normed_ref[...]
    proj_ref[:, width:] = grad_gate_ref[...]
    ffn.pop(0)()
    border.wait_recv()
    arrived = jnp.where(place.spot < place.ctx - 1, arrived_ref[...], 0.0)
    conv_ref[pl.ds(count - 8, 8), :] = conv_ref[pl.ds(count - 8, 8), :] + arrived
    proj_ref[:, :width] = conv_ref[...].astype(bf16)
    chunk = DV
    for start in range(0, depth, chunk):
        mix_grad[pl.ds(start, chunk), :] = dot_tn(proj_ref[:, start : start + chunk], normed).astype(bf16)
    own_out.wait()
    pl.semaphore_wait(free_sem, 1)
    mix.pop(0)()

    def fetch(start):
        slot = start // chunk % 2
        copy = pltpu.make_async_copy(
            mix_hbm.at[pl.ds(start, chunk), :], weight_ref.at[slot], weight_sems.at[slot]
        )
        copy.start()
        return copy

    coming = [fetch(0), fetch(chunk)]
    ffn.pop(0)()
    mix.pop(0)()
    total_ref[...] = mm_nt(grad_logits, w_gates_ref[...])
    for start in range(0, depth, chunk):
        coming.pop(0).wait()
        total_ref[...] += dot_nn(proj_ref[:, start : start + chunk], weight_ref[start // chunk % 2])
        if start + 2 * chunk < depth:
            coming.append(fetch(start + 2 * chunk))
    if ffn:
        ffn.pop(0)()
    mix.pop(0)()
    x = x_ref[...].astype(f32)
    scale = lax.rsqrt(jnp.mean(x * x, axis=-1, keepdims=True) + EPSILON)
    through, gain_one_grad = norm_back(total_ref[...], x, scale, gains_ref[0:1, :])
    grad_input_ref[...] = (grad_resid_ref[...] + through).astype(bf16)
    small = Everywhere(place, copies, small_scratch[2], *small_scratch[:2])
    sums = small.total.at[0]
    sums[...] = jnp.zeros(sums.shape, f32)
    one, two, head, tap, gate, rest = small_places()

    def place_row(first, value):
        for index in range(value.shape[1] // 128):
            sums[first + index : first + index + 1, :] = value[:, index * 128 : (index + 1) * 128]

    place_row(one, gain_one_grad)
    place_row(two, gain_two_grad_ref[...])
    place_row(head, gain_head_grad_ref[...])
    for index in range(CONV):
        place_row(tap + index * (width // 128), taps_grad_ref[index : index + 1, :])
    sums[gate:rest, :] = pack_gates(mm_tn(normed.astype(f32), grad_logits))
    lanes = lax.broadcasted_iota(jnp.int32, (1, 128), 1)
    by_size = jnp.sum(grad_decay * decay_ref[...], axis=0, keepdims=True)
    by_bias = jnp.sum(grad_logits, axis=0, keepdims=True)
    sums[rest : rest + 1, :] = jnp.where(
        lanes < H, pltpu.roll(by_size, 128 - H, 1), jnp.where(lanes < 2 * H, by_bias, 0.0)
    )
    small.send(0)
    extra = []
    for turn in range(3):
        extra.append(lambda turn=turn: small.take(turn))
        extra.append(lambda turn=turn: small.send(turn + 1) if turn < 2 else small.send_z())
    while mix or ffn or extra:
        for queue in (ffn, mix, extra):
            if queue:
                queue.pop(0)()
    small_total = small.take_z()
    small_out[...] = small_total
    squares = jnp.zeros((8, 128), f32)
    for total in (mix_total, ffn_total):
        value = total[...]
        line = jnp.sum(value * value, axis=0, keepdims=True)
        for start in range(0, D, 128):
            squares = squares + line[:, start : start + 128] * 0.125
    square_total, square_plane, square_deep = square_scratch
    square_total[0] = squares
    square_plane[place.spot] = squares
    for copy in [
        copies.push(
            square_total.at[0], square_plane.at[place.spot], (place.z, lax.rem(place.spot + step, place.ctx))
        )
        for step in range(1, place.ctx)
    ]:
        copy.wait_recv()
    plane = square_plane[0]
    for index in range(1, place.ctx):
        plane = plane + square_plane[index]
    square_total[1] = plane
    square_deep[place.z] = plane
    for copy in [
        copies.push(square_total.at[1], square_deep.at[place.z], (place.along(step), place.spot))
        for step in range(1, place.deep)
    ]:
        copy.wait_recv()
    everything = square_deep[0]
    for index in range(1, place.deep):
        everything = everything + square_deep[index]
    own = jnp.sum(small_total * small_total, axis=0, keepdims=True)
    result = jnp.sum(jnp.sum(everything, axis=0, keepdims=True), axis=1, keepdims=True) + jnp.sum(
        own, axis=1, keepdims=True
    )
    squares_out[...] = jnp.broadcast_to(result, squares_out.shape)
    to_flat(mix_flat, mix_total[...])
    to_flat(ffn_flat, ffn_total[0 : ffn_flat.shape[0] * 128 // D, :])
    copies.finish()


def back(side, tag, ffn_rows, small_rows, *args):
    f32, bf16 = jnp.float32, jnp.bfloat16
    deep, ctx = lax.axis_size("dp"), lax.axis_size("ctx")
    query, ext, taps = args[3], args[12], args[13]
    ffn_grad, grad_out = args[-3], args[-2]
    count, width = query.shape[0], taps.shape[1]
    depth = width + H * DV
    everyone = deep * ctx
    rows = ffn_grad.shape[0] // everyone
    mix_rows = (depth + grad_out.shape[0]) // everyone
    number = 2 * Scatter.copies_of(deep) + 2 * gather_copies(1) + (3 + deep - 1) + (ctx + deep - 2) + 1
    vmem = pl.BlockSpec(memory_space=pltpu.VMEM)
    anywhere = pl.BlockSpec(memory_space=pl.ANY)
    return pl.pallas_call(
        functools.partial(back_kernel, side),
        out_shape=[
            jax.ShapeDtypeStruct((ffn_rows * D // 128, 128), f32),
            jax.ShapeDtypeStruct((mix_rows * D // 128, 128), f32),
            jax.ShapeDtypeStruct((count, D), bf16),
            jax.ShapeDtypeStruct((small_rows, 128), f32),
            jax.ShapeDtypeStruct((8, 128), f32),
        ],
        in_specs=[vmem] * (len(args) - 3) + [anywhere] * 3,
        out_specs=[vmem] * 5,
        scratch_shapes=[
            pltpu.VMEM((H, DK, DV), f32),
            pltpu.VMEM((count + 16, width), f32),
            pltpu.VMEM((ctx * DK, DV), bf16),
            pltpu.VMEM((ctx * DK, DV), bf16),
            pltpu.VMEM((8, width), f32),
            pltpu.VMEM((8, width), f32),
            pltpu.VMEM((count, 128), f32),
            pltpu.VMEM((count, 128), f32),
            pltpu.VMEM((count, depth), bf16),
            pltpu.VMEM((depth + grad_out.shape[0], D), bf16),
            pltpu.VMEM((2, DV, D), bf16),
            pltpu.VMEM((count, D), f32),
            pltpu.VMEM((8, width), f32),
            pltpu.VMEM((rows, D), f32),
            pltpu.VMEM((mix_rows, D), f32),
        ]
        + Scatter.scratch(deep, rows)
        + [shape for index, shape in enumerate(Scatter.scratch(deep, mix_rows)) if index != 1]
        + Everywhere.scratch(deep, small_rows, 128)
        + [pltpu.VMEM((number, 8, 128), f32) for number in (2, ctx, deep)]
        + [
            pltpu.SemaphoreType.DMA((number,)),
            pltpu.SemaphoreType.DMA((number,)),
            pltpu.SemaphoreType.DMA((8 * deep + 3,)),
            pltpu.SemaphoreType.DMA((2,)),
            pltpu.SemaphoreType.REGULAR,
        ],
        compiler_params=pltpu.CompilerParams(
            collective_id=tag, has_side_effects=True, vmem_limit_bytes=62 * 2**20
        ),
        cost_estimate=pl.CostEstimate(flops=10**10, bytes_accessed=10**8, transcendentals=0),
        name="back",
    )(*args)


def back_chain(
    wire_ref, local_ref, query_ref, keys_ref, values_ref, inverse_ref, beta_ref,
    decay_ref, state_ref, pseudo_ref, grad_mixed_ref, ext_ref, taps_ref,
    grad_conv_ref, grad_border_ref, grad_taps_ref, grad_beta_ref, grad_decay_ref,
    after_ref, padded_ref,
):
    count = query_ref.shape[0]
    width = taps_ref.shape[1]
    devices = wire_ref[0].shape[0]
    after_ref[...] = jnp.zeros_like(after_ref)

    def lap(step, carry):
        index = devices - 1 - step
        for head in range(H):
            to_end, key_mix, value_mix, whole = wire_parts(wire_ref, index, head, count)
            after = after_ref[head]
            inner = wire_mm(to_end, after, ((1,), (0,)))
            spot = pl.multiple_of(index * DK, DK)
            local = local_ref[head][pl.ds(spot, DK), :].astype(jnp.float32)
            after_ref[head] = whole * after - wire_mm(key_mix, inner, ((0,), (0,))) + local
        return carry

    lax.fori_loop(0, devices - 1 - lax.axis_index("ctx"), lap, 0)
    yield
    taps = taps_ref[...]
    summed = ext_sum(ext_ref, taps, count, 0, width)
    activated, slope = silu_pair(summed)
    padded_ref[0:8, :] = jnp.zeros((8, width), jnp.float32)
    padded_ref[pl.ds(8 + count, 8), :] = jnp.zeros((8, width), jnp.float32)
    rows, cols = iotas(count)
    lower = rows >= cols
    strict = rows > cols
    lanes = lax.broadcasted_iota(jnp.int32, (count, 128), 1)
    beta_out = jnp.zeros((count, 128), jnp.float32)
    cumulative_out = jnp.zeros((count, 128), jnp.float32)
    row_column = lax.broadcasted_iota(jnp.int32, (count, 1), 0)
    for head in range(H):
        query = query_ref[:, head * DK : (head + 1) * DK]
        keys = keys_ref[:, head * DK : (head + 1) * DK]
        span = slice(head * DV, (head + 1) * DV)
        values = values_ref[:, span]
        beta = beta_ref[:, head : head + 1]
        matrix, grown, to_end, whole = decay_terms(decay_lane(decay_ref, head), rows, cols)
        inverse = inverse_ref[head]
        state = state_ref[head]
        after = after_ref[head]
        pseudo = pseudo_ref[:, span]
        grad_mixed = grad_mixed_ref[:, span]
        keys_grown = keys * (beta * grown)
        key_mix = mm(inverse, keys_grown)
        value_mix = mm(inverse, values * beta)
        gram = mm_nt(keys, keys)
        system = jnp.where(strict, beta * gram * matrix, 0.0)
        scores = mm_nt(query, keys) * matrix
        keys_end = keys * to_end
        query_grown = query * grown
        grad_query_grown = mm_nt(grad_mixed, state)
        grad_scores = jnp.where(lower, mm_nt(grad_mixed, pseudo), 0.0)
        grad_pseudo = mm_tn(scores, grad_mixed) + mm(keys_end, after)
        grad_keys_end = mm_nt(pseudo, after)
        grad_whole = jnp.sum(jnp.sum(after * state, axis=1, keepdims=True), axis=0, keepdims=True)
        grad_value_in = mm_tn(inverse, grad_pseudo)
        grad_key_in = mm_tn(inverse, -mm_nt(grad_pseudo, state))
        grad_system = -jnp.where(
            strict, mm_nt(grad_value_in, value_mix) + mm_nt(grad_key_in, key_mix), 0.0
        )
        grad_raw = grad_scores * matrix
        grad_query = mm(grad_raw, keys) + grad_query_grown * grown
        grad_keys = mm_tn(grad_raw, query)
        weighted = grad_system * matrix
        grad_beta = jnp.sum(weighted * gram, axis=1, keepdims=True)
        grad_gram = weighted * beta
        grad_keys = grad_keys + mm(grad_gram, keys) + mm_tn(grad_gram, keys)
        spread = grad_scores * scores + grad_system * system
        grad_cumulative = jnp.sum(spread, axis=1, keepdims=True)
        across = jnp.sum(spread, axis=0, keepdims=True)
        grad_cumulative = grad_cumulative - jnp.sum(
            jnp.where(rows == cols, across, 0.0), axis=1, keepdims=True
        )
        grad_keys = grad_keys + grad_key_in * (beta * grown)
        through = jnp.sum(grad_key_in * keys, axis=1, keepdims=True) * grown
        grad_beta = grad_beta + through + jnp.sum(grad_value_in * values, axis=1, keepdims=True)
        grad_cumulative = grad_cumulative + through * beta
        grad_values = grad_value_in * beta
        grad_cumulative = grad_cumulative + jnp.sum(
            grad_query_grown * query_grown, axis=1, keepdims=True
        )
        grad_keys = grad_keys + grad_keys_end * to_end
        ending = jnp.sum(grad_keys_end * keys_end, axis=1, keepdims=True)
        final = jnp.sum(ending, axis=0, keepdims=True) + whole * grad_whole
        grad_cumulative = grad_cumulative - ending + jnp.where(row_column == count - 1, final, 0.0)
        beta_out = jnp.where(lanes == head, grad_beta, beta_out)
        cumulative_out = jnp.where(lanes == H + head, grad_cumulative, cumulative_out)
        key_part = activated[:, (H + head) * DK : (H + head + 1) * DK]
        key_scale = unit_rows(key_part)
        query_part = activated[:, head * DK : (head + 1) * DK]
        query_scale = unit_rows(query_part)
        factor = DK ** (-0.5)
        grad_query_part = (factor * query_scale) * (
            grad_query
            - query_part
            * (query_scale * query_scale)
            * jnp.sum(grad_query * query_part, axis=-1, keepdims=True)
        )
        grad_key_part = key_scale * (
            grad_keys
            - key_part
            * (key_scale * key_scale)
            * jnp.sum(grad_keys * key_part, axis=-1, keepdims=True)
        )
        spots = (head * DK, (H + head) * DK, 2 * H * DK + head * DV)
        for spot, grad in zip(spots, (grad_query_part, grad_key_part, grad_values)):
            size = grad.shape[1]
            padded_ref[pl.ds(8, count), spot : spot + size] = grad * slope[:, spot : spot + size]
        yield
    grad_beta_ref[...] = beta_out
    grad_decay_ref[...] = mm_tn(jnp.where(lower, 1.0, 0.0), cumulative_out)
    conv_total = jnp.zeros((count, width), jnp.float32)
    border_total = jnp.zeros((8, width), jnp.float32)
    summed_grad = padded_ref[pl.ds(8, count), :]
    tap_rows = lax.broadcasted_iota(jnp.int32, (8, width), 0)
    taps_total = jnp.zeros((8, width), jnp.float32)
    for tap in range(CONV):
        shift = CONV - 1 - tap
        conv_total = conv_total + taps[tap : tap + 1] * padded_ref[pl.ds(8 + shift, count), :]
        border_total = border_total + taps[tap : tap + 1] * padded_ref[pl.ds(shift, 8), :]
        piece = jnp.sum(
            summed_grad * ext_ref[pl.ds(8 - (CONV - 1) + tap, count), :width],
            axis=0,
            keepdims=True,
        )
        taps_total = jnp.where(tap_rows == tap, piece, taps_total)
    grad_conv_ref[...] = conv_total
    grad_border_ref[...] = border_total
    grad_taps_ref[...] = taps_total
    yield


def chip_side():
    half = lax.axis_size("ctx") // 2
    side = math.isqrt(half)
    return side if side == 2 and 2 * side * side == lax.axis_size("ctx") else 0


def adam_step(weight, grad_full, first, second, clip):
    grad_clipped = grad_full * clip
    first_new = BETA_ONE * first + (1.0 - BETA_ONE) * grad_clipped
    second_new = BETA_TWO * second + (1.0 - BETA_TWO) * grad_clipped * grad_clipped
    update = (
        first_new / CORRECT_ONE / (jnp.sqrt(second_new / CORRECT_TWO) + ADAM_EPS)
        + DECAY_RATE * weight
    )
    return (weight - LEARN_RATE * update, first_new, second_new)


def plain(
    inputs,
    cotangent,
    mixer_params,
    mixer_first,
    mixer_second,
    ffn_params,
    ffn_first,
    ffn_second,
    small_params,
    small_first,
    small_second,
):
    gain_one, gain_two, gain_head, tap_values, w_gates, a_log, dt_bias = unpack_small(small_params)
    width = tap_values.shape[1]
    mix_part = mixer_params.astype(jnp.bfloat16)
    ffn_part = ffn_params.astype(jnp.bfloat16)
    mix_whole, ffn_whole = (
        lax.all_gather(mix_part, ("dp", "ctx"), axis=0, tiled=True),
        lax.all_gather(ffn_part, ("dp", "ctx"), axis=0, tiled=True),
    )
    w_in, w_out, w_ffn, w_down = split_weights(mix_whole, ffn_whole)
    x_float = inputs[0].astype(jnp.float32)
    count = x_float.shape[0]
    normed_in = norm_scale(x_float, gain_one).astype(jnp.bfloat16)
    projected = jnp.dot(normed_in, w_in.T, preferred_element_type=jnp.float32)
    gate_logits = jnp.dot(normed_in.astype(jnp.float32), w_gates, precision=HIGHEST)
    f32 = jnp.float32
    devices = lax.axis_size("ctx")
    place = lax.axis_index("ctx").astype(jnp.int32).reshape(1)
    out_gate = projected[:, width:]
    edge = from_behind(projected[count - 8 :, :width], "ctx", 1)
    border = jnp.where(lax.broadcasted_iota(jnp.int32, (8, 1), 0) >= 8 - (CONV - 1), edge, 0.0)
    (beta, decay), pull_gates = jax.vjp(gates, gate_logits, a_log, dt_bias)
    wire, query, keys, values, inverse = fused(
        forward_parts,
        (
            jax.ShapeDtypeStruct((count + PAD, H * (2 * DK + DV)), jnp.bfloat16),
            jax.ShapeDtypeStruct((count, H * DK), f32),
            jax.ShapeDtypeStruct((count, H * DK), f32),
            jax.ShapeDtypeStruct((count, H * DV), f32),
            jax.ShapeDtypeStruct((H, count, count), f32),
        ),
        scratch=(pltpu.VMEM((count + 8, width), f32),),
        label="forward_parts",
    )(projected, border, tap_values, beta, decay)
    wires = lax.all_gather(wire, "ctx")
    gain_row = gain_head.reshape(1, DV)
    head_out, mixed, state, pseudo = fused(
        forward_chain,
        (
            jax.ShapeDtypeStruct((count, H * DV), jnp.bfloat16),
            jax.ShapeDtypeStruct((count, H * DV), f32),
            jax.ShapeDtypeStruct((H, DK, DV), f32),
            jax.ShapeDtypeStruct((count, H * DV), f32),
        ),
        scalars=1,
        label="forward_chain",
    )(place, wires, query, keys, values, inverse, beta, decay, out_gate, gain_row)
    resid = x_float + jnp.dot(head_out, w_out, preferred_element_type=jnp.float32)
    normed_mid = norm_scale(resid, gain_two).astype(jnp.bfloat16)
    ffn_pre = jnp.dot(normed_mid, w_ffn.T, preferred_element_type=jnp.float32)
    gate_part = ffn_pre[:, :FF]
    up_part = ffn_pre[:, FF:]
    hidden_act = swiglu(gate_part, up_part).astype(jnp.bfloat16)
    result = (resid + jnp.dot(hidden_act, w_down, preferred_element_type=jnp.float32)).astype(
        jnp.bfloat16
    )
    seq_grad = cotangent[0]
    grad_float = seq_grad.astype(jnp.float32)
    grad_down = jnp.dot(hidden_act.T, seq_grad, preferred_element_type=jnp.float32)
    grad_hidden = jnp.dot(seq_grad, w_down.T, preferred_element_type=jnp.float32)
    unused_one, pull_swiglu = jax.vjp(swiglu, gate_part, up_part)
    grad_gate, grad_up = pull_swiglu(grad_hidden)
    grad_pre = jnp.concatenate([grad_gate, grad_up], axis=1).astype(jnp.bfloat16)
    grad_ffn = jnp.dot(grad_pre.T, normed_mid, preferred_element_type=jnp.float32)
    grad_mid = jnp.dot(grad_pre, w_ffn, preferred_element_type=jnp.float32)
    unused_two, pull_mid = jax.vjp(norm_scale, resid, gain_two)
    grad_through, grad_gain_two = pull_mid(grad_mid)
    grad_resid = grad_float + grad_through
    resid_half = grad_resid.astype(jnp.bfloat16)
    grad_out = jnp.dot(head_out.T, resid_half, preferred_element_type=jnp.float32)
    grad_head = jnp.dot(resid_half, w_out.T, preferred_element_type=jnp.float32)
    local, grad_mixed, grad_gate_out, grad_gain_head = fused(
        backward_local,
        (
            jax.ShapeDtypeStruct((H * DK, DV), jnp.bfloat16),
            jax.ShapeDtypeStruct((count, H * DV), f32),
            jax.ShapeDtypeStruct((count, H * DV), f32),
            jax.ShapeDtypeStruct((1, DV), f32),
        ),
        label="backward_local",
    )(grad_head, mixed, query, keys, values, inverse, beta, decay, out_gate, gain_row)
    locals_all = lax.all_gather(local, "ctx")
    locals_all, grad_ffn, grad_down = lax.optimization_barrier((locals_all, grad_ffn, grad_down))
    ffn_shard = scatter_rows((grad_ffn, grad_down))
    grad_conv, grad_border, grad_taps, grad_beta, grad_decay = fused(
        backward_chain,
        (
            jax.ShapeDtypeStruct((count, width), f32),
            jax.ShapeDtypeStruct((8, width), f32),
            jax.ShapeDtypeStruct((8, width), f32),
            jax.ShapeDtypeStruct((count, 128), f32),
            jax.ShapeDtypeStruct((count, 128), f32),
        ),
        scratch=(
            pltpu.VMEM((H, DK, DV), f32),
            pltpu.VMEM((count + 8, width), f32),
            pltpu.VMEM((count + 16, width), f32),
        ),
        scalars=1,
        label="backward_chain",
    )(
        place, wires, locals_all, query, keys, values, inverse, beta, decay, state, pseudo,
        grad_mixed, projected, border, tap_values,
    )
    grad_logits, grad_alog, grad_bias = pull_gates((grad_beta[:, :H], grad_decay[:, :H]))
    returned = from_behind(grad_border, "ctx", -1)[8 - (CONV - 1) :]
    grad_conv = grad_conv.at[count - (CONV - 1) :].add(returned)
    grad_proj = jnp.concatenate([grad_conv, grad_gate_out], axis=1).astype(jnp.bfloat16)
    grad_in = jnp.dot(grad_proj.T, normed_in, preferred_element_type=jnp.float32)
    grad_normed = jnp.dot(grad_proj, w_in, preferred_element_type=jnp.float32) + jnp.dot(
        grad_logits, w_gates.T, precision=HIGHEST
    )
    grad_gates = jnp.dot(normed_in.astype(jnp.float32).T, grad_logits, precision=HIGHEST)
    unused_six, pull_in = jax.vjp(norm_scale, x_float, gain_one)
    grad_x, grad_gain_one = pull_in(grad_normed)
    grad_input = (grad_resid + grad_x).astype(jnp.bfloat16)
    small_local = jnp.concatenate(
        [
            grad_gain_one,
            grad_gain_two,
            grad_gain_head.reshape(-1),
            grad_taps[:CONV].reshape(-1),
            grad_gates.reshape(-1),
            grad_alog,
            grad_bias,
        ]
    )
    small_grad = lax.psum(small_local, ("dp", "ctx"))
    ffn_shard, grad_in, grad_out = lax.optimization_barrier((ffn_shard, grad_in, grad_out))
    mix_shard = scatter_rows((grad_in, grad_out))
    small_grad, mix_shard = lax.optimization_barrier((small_grad, mix_shard))
    shard_squares = jnp.sum(mix_shard * mix_shard) + jnp.sum(ffn_shard * ffn_shard)
    total_squares = lax.psum(shard_squares, ("dp", "ctx"))
    squares = total_squares + jnp.sum(small_grad * small_grad)
    clip = jnp.minimum(1.0, MAX_NORM / (jnp.sqrt(squares) + 1e-06))
    mixer_new, mixer_first_new, mixer_second_new = adam_step(
        mixer_params, mix_shard, mixer_first, mixer_second, clip
    )
    ffn_new, ffn_first_new, ffn_second_new = adam_step(
        ffn_params, ffn_shard, ffn_first, ffn_second, clip
    )
    small_new, small_first_new, small_second_new = adam_step(
        small_params, small_grad, small_first, small_second, clip
    )
    return (
        result[None],
        grad_input[None],
        mix_shard,
        ffn_shard,
        small_grad,
        mixer_new,
        mixer_first_new,
        mixer_second_new,
        ffn_new,
        ffn_first_new,
        ffn_second_new,
        small_new,
        small_first_new,
        small_second_new,
    )


def fast(
    side, inputs, cotangent, mixer_params, mixer_first, mixer_second, ffn_params, ffn_first, ffn_second, small_params, small_first, small_second,
):
    ffn_rows = ffn_params.size // D
    short = -small_params.size % 1024
    small = jnp.pad(small_params, (0, short)).reshape(-1, 128)
    (
        mix_whole, ffn_whole, zero, one, ext, out_gate, query, keys, values, inverse, normed_in, beta, decay,
        factor, taps, gains, w_gates,
    ) = front(mixer_params.reshape(-1, 128), ffn_params.reshape(-1, 128), inputs[0], small, side, 1)
    zero, one = (part.reshape(lax.axis_size("ctx"), -1, part.shape[1]) for part in (zero, one))
    place = lax.axis_index("ctx").astype(jnp.int32).reshape(1)
    (
        result, grad_resid, grad_out, ffn_grad, grad_gain_two, state, pseudo, local, grad_mixed,
        grad_gate_out, grad_gain_head,
    ) = middle(
        ffn_rows, place, zero, one, query, keys, values, inverse, beta, decay, out_gate, gains,
        inputs[0], cotangent[0], mix_whole, ffn_whole,
    )
    ffn_shard, mix_shard, grad_input, sums, squares = back(
        side, 2, ffn_rows, small.shape[0], zero, one, local, query, keys, values, inverse, beta, decay,
        state, pseudo, grad_mixed, ext, taps, grad_gate_out, grad_resid, inputs[0], normed_in, gains,
        factor, w_gates, grad_gain_two, grad_gain_head, ffn_grad, grad_out, mix_whole,
    )
    small_grad = sums.reshape(-1)[: small_params.size]
    mix_shard = mix_shard.reshape(-1)
    ffn_shard = ffn_shard.reshape(-1)
    squares = squares[0, 0]
    clip = jnp.minimum(1.0, MAX_NORM / (jnp.sqrt(squares) + 1e-06))
    mix_shard = jnp.where(clip >= 0.0, mix_shard, 0.0)
    ffn_shard = jnp.where(clip >= 0.0, ffn_shard, 0.0)
    mixer_new, mixer_first_new, mixer_second_new = adam_step(
        mixer_params, mix_shard, mixer_first, mixer_second, clip
    )
    ffn_new, ffn_first_new, ffn_second_new = adam_step(
        ffn_params, ffn_shard, ffn_first, ffn_second, clip
    )
    small_new, small_first_new, small_second_new = adam_step(
        small_params, small_grad, small_first, small_second, clip
    )
    return (
        result[None],
        grad_input[None],
        mix_shard,
        ffn_shard,
        small_grad,
        mixer_new,
        mixer_first_new,
        mixer_second_new,
        ffn_new,
        ffn_first_new,
        ffn_second_new,
        small_new,
        small_first_new,
        small_second_new,
    )


def body(*args):
    rows, left = divmod(args[5].size, D)
    side = chip_side() if left == 0 and args[2].size % (32 * D) == 0 else 0
    return fast(side, *args) if side else plain(*args)


def solution(mesh):
    return jax.shard_map(
        body,
        mesh=mesh,
        in_specs=(
            P("dp", "ctx", None),
            P("dp", "ctx", None),
            P(("dp", "ctx")),
            P(("dp", "ctx")),
            P(("dp", "ctx")),
            P(("dp", "ctx")),
            P(("dp", "ctx")),
            P(("dp", "ctx")),
            P(),
            P(),
            P(),
        ),
        out_specs=(
            P("dp", "ctx", None),
            P("dp", "ctx", None),
            P(("dp", "ctx")),
            P(("dp", "ctx")),
            P(),
            P(("dp", "ctx")),
            P(("dp", "ctx")),
            P(("dp", "ctx")),
            P(("dp", "ctx")),
            P(("dp", "ctx")),
            P(("dp", "ctx")),
            P(),
            P(),
            P(),
        ),
        check_vma=False,
    )
```
